32 devices in a mesh: seq: 8 (over z, y), fsdp: 4 (over x, core).
Axes of the slice: x: 2, y: 2, z: 4, core: 2. Of those that a mesh axis runs over, the one named last changes fastest.
Arguments:
- tokens: bfloat16 [4, 1024, 768], P('fsdp', 'seq'), may hold values from -6 to 6, as said below
- cotangent: bfloat16 [4, 1024, 768], P('fsdp', 'seq'), may hold values from -6 to 6
- doc_lengths: int32 [4, 4], P('fsdp'), may hold values from 64 to 512, as said below
- w_query: bfloat16 [768, 768], P(('seq', 'fsdp')), may hold values from -0.21875 to 0.21875
- b_query: bfloat16 [768], P(('seq', 'fsdp')), may hold values from -1.5 to 1.5
- w_key: bfloat16 [768, 768], P(('seq', 'fsdp')), may hold values from -0.21875 to 0.21875
- w_value: bfloat16 [768, 768], P(('seq', 'fsdp')), may hold values from -0.21875 to 0.21875
- b_value: bfloat16 [768], P(('seq', 'fsdp')), may hold values from -1.5 to 1.5
- w_out: bfloat16 [768, 768], P(('seq', 'fsdp')), may hold values from -0.21875 to 0.21875
- b_out: bfloat16 [768], P(('seq', 'fsdp')), may hold values from -1.5 to 1.5
- w_up: bfloat16 [768, 3072], P(('seq', 'fsdp')), may hold values from -0.21875 to 0.21875
- b_up: bfloat16 [3072], P(('seq', 'fsdp')), may hold values from -1.5 to 1.5
- w_down: bfloat16 [3072, 768], P(('seq', 'fsdp')), may hold values from -0.109375 to 0.109375
- b_down: bfloat16 [768], P(('seq', 'fsdp')), may hold values from -1.5 to 1.5
- g_attn: bfloat16 [768], P(('seq', 'fsdp')), may hold values from 0.5 to 1.5
- s_attn: bfloat16 [768], P(('seq', 'fsdp')), may hold values from -1.5 to 1.5
- g_mlp: bfloat16 [768], P(('seq', 'fsdp')), may hold values from 0.5 to 1.5
- s_mlp: bfloat16 [768], P(('seq', 'fsdp')), may hold values from -1.5 to 1.5
- conv_kernel: bfloat16 [33, 12], replicated, may hold values from -0.6796875 to 0.6796875
Outputs:
- output: bfloat16 [4, 1024, 768], P('fsdp', 'seq')
- d_tokens: bfloat16 [4, 1024, 768], P('fsdp', 'seq')
- dw_query: float32 [768, 768], P(('seq', 'fsdp'))
- db_query: float32 [768], P(('seq', 'fsdp'))
- dw_key: float32 [768, 768], P(('seq', 'fsdp'))
- dw_value: float32 [768, 768], P(('seq', 'fsdp'))
- db_value: float32 [768], P(('seq', 'fsdp'))
- dw_out: float32 [768, 768], P(('seq', 'fsdp'))
- db_out: float32 [768], P(('seq', 'fsdp'))
- dw_up: float32 [768, 3072], P(('seq', 'fsdp'))
- db_up: float32 [3072], P(('seq', 'fsdp'))
- dw_down: float32 [3072, 768], P(('seq', 'fsdp'))
- db_down: float32 [768], P(('seq', 'fsdp'))
- dg_attn: float32 [768], P(('seq', 'fsdp'))
- ds_attn: float32 [768], P(('seq', 'fsdp'))
- dg_mlp: float32 [768], P(('seq', 'fsdp'))
- ds_mlp: float32 [768], P(('seq', 'fsdp'))
- d_kernel: float32 [33, 12], replicated
The draws below stay inside these ranges and needn't reach their ends.
Inputs may be any that keep to these rules, and one draw needn't show every extreme that they name: `doc_lengths`: in each stream the 4 lengths sum to 1024, and one of them is exactly 512. `tokens`: token features with a slowly varying part along the stream.
All inputs are finite; a program needn't handle non-finite values.
Results may differ from the reference program's by a relative error of at most 0.015.
Values may be sent and summed in bfloat16 or wider, within the bound.
A program may use at most 320 MiB of HBM per device.

```python
import math
import jax
import jax.numpy as jnp
from jax import lax

D = 768
HEADS = 12
HD = 64
FF = 3072
NLAND = 64
NS_ITERS = 6
CONV = 33
DOCS = 4
STREAMS = 4
STREAM = 1024
SHORTEST = 64
LONGEST = 512
SLOTS = 256


def draw_tokens(key, part):
    key_noise, key_freq, key_phase = jax.random.split(key, 3)
    place = jnp.arange(STREAM, dtype=jnp.float32)[None, :, None]
    angular = jnp.exp(jax.random.uniform(key_freq, (1, 1, D), jnp.float32, math.log(0.002), math.log(0.2)))
    phase = jax.random.uniform(key_phase, (STREAMS, 1, D), jnp.float32, -math.pi, math.pi)
    wave = jnp.sin(place * angular + phase)
    noise = 0.6 * jnp.clip(jax.random.normal(key_noise, (STREAMS, STREAM, D), jnp.float32), -6.0, 6.0)
    amplitude = 1.1
    return (noise + amplitude * wave).astype(jnp.bfloat16)


def draw_doc_lengths(key, part):
    spare_total = STREAM - LONGEST - (DOCS - 1) * SHORTEST

    def one_stream(row_key):
        key_big, key_cut = jax.random.split(row_key)
        longest_at = jax.random.randint(key_big, (), 0, DOCS)
        cut_points = jnp.sort(jax.random.randint(key_cut, (DOCS - 2,), 0, spare_total + 1))
        boundaries = jnp.concatenate([jnp.zeros((1,), jnp.int32), cut_points.astype(jnp.int32), jnp.full((1,), spare_total, jnp.int32)])
        extras = boundaries[1:] - boundaries[:-1]
        places = jnp.arange(DOCS, dtype=jnp.int32)
        others = jnp.clip(places - (places > longest_at).astype(jnp.int32), 0, DOCS - 2)
        return jnp.where(places == longest_at, LONGEST, SHORTEST + extras[others]).astype(jnp.int32)
    return jax.vmap(one_stream)(jax.random.split(key, STREAMS))


def block_levels(key, extent, cuts, smallest, top_value):
    def one(dim, shards_of):
        heights = jax.random.uniform(jax.random.fold_in(jax.random.fold_in(key, 6), dim), (shards_of,), jnp.float32, smallest / len(cuts), top_value / len(cuts))
        return jnp.repeat(jnp.exp(heights), extent[dim] // shards_of).reshape((-1,) + (1,) * (len(extent) - dim - 1))

    factor_of = one(*cuts[0])
    for cut in cuts[1:]:
        factor_of = factor_of * one(*cut)
    return factor_of


def gaussian(own_key, dims, deviation, most, cuts=(), held_as=jnp.bfloat16):
    array = jax.random.normal(own_key, dims, jnp.float32) * deviation
    if len(cuts) > 0:
        array = block_levels(own_key, dims, cuts, -0.22, 0.18) * array
    return jnp.clip(array, min=-most, max=most).astype(held_as)


def setup_inputs(seed: int = 0) -> dict:
    seeds = jax.random.split(jax.random.key(seed), 20)
    tokens = draw_tokens(jax.random.fold_in(seeds[19], 71), 0)
    cotangent = gaussian(seeds[1], (STREAMS, STREAM, D), 1.0, 6.0, ((0, 4), (1, 8)))
    doc_lengths = draw_doc_lengths(jax.random.fold_in(seeds[19], 71), 0)
    w_query = gaussian(seeds[3], (D, D), D ** -0.5, 0.21875, ((0, 32),))
    b_query = gaussian(seeds[4], (D,), 0.3, 1.5, ((0, 32),))
    w_key = gaussian(seeds[5], (D, D), D ** -0.5, 0.21875, ((0, 32),))
    w_value = gaussian(seeds[6], (D, D), D ** -0.5, 0.21875, ((0, 32),))
    b_value = gaussian(seeds[7], (D,), 0.3, 1.5, ((0, 32),))
    w_out = gaussian(seeds[8], (D, D), D ** -0.5, 0.21875, ((0, 32),))
    b_out = gaussian(seeds[9], (D,), 0.3, 1.5, ((0, 32),))
    w_up = gaussian(seeds[10], (D, FF), D ** -0.5, 0.21875, ((0, 32),))
    b_up = gaussian(seeds[11], (FF,), 0.3, 1.5, ((0, 32),))
    w_down = gaussian(seeds[12], (FF, D), FF ** -0.5, 0.109375, ((0, 32),))
    b_down = gaussian(seeds[13], (D,), 0.3, 1.5, ((0, 32),))
    g_attn = jnp.clip(1.0 + 0.1 * jax.random.normal(seeds[14], (D,), jnp.float32), 0.5, 1.5).astype(jnp.bfloat16)
    s_attn = gaussian(seeds[15], (D,), 0.3, 1.5, ((0, 32),))
    g_mlp = jnp.clip(1.0 + 0.1 * jax.random.normal(seeds[16], (D,), jnp.float32), 0.5, 1.5).astype(jnp.bfloat16)
    s_mlp = gaussian(seeds[17], (D,), 0.3, 1.5, ((0, 32),))
    conv_kernel = gaussian(seeds[18], (CONV, HEADS), 0.17, 0.6796875)
    return {"tokens": tokens, "cotangent": cotangent, "doc_lengths": doc_lengths, "w_query": w_query, "b_query": b_query, "w_key": w_key, "w_value": w_value, "b_value": b_value, "w_out": w_out, "b_out": b_out, "w_up": w_up, "b_up": b_up, "w_down": w_down, "b_down": b_down, "g_attn": g_attn, "s_attn": s_attn, "g_mlp": g_mlp, "s_mlp": s_mlp, "conv_kernel": conv_kernel}


HIGHEST = lax.Precision.HIGHEST
epsilon = 1e-05
masked_score = -1e+30

@jax.custom_vjp
def low(v):
    return lax.optimization_barrier(v.astype(jnp.bfloat16)).astype(jnp.float32)

@jax.custom_vjp
def low_back(v):
    return v

def low_keep(v):
    return (low(v), None)

def low_pass(kept, grad):
    return (grad,)

def back_keep(v):
    return (v, None)

def back_low(kept, grad):
    return (low(grad),)
low.defvjp(low_keep, low_pass)
low_back.defvjp(back_keep, back_low)

def locate(positions, lengths):
    doc_ends = jnp.cumsum(lengths)
    doc_index = lax.optimization_barrier(jnp.sum((positions[:, None] >= doc_ends[None, :]).astype(jnp.int32), axis=1))
    doc_onehot = (doc_index[:, None] == jnp.arange(DOCS, dtype=jnp.int32)[None, :]).astype(jnp.int32)
    doc_start = lax.optimization_barrier(jnp.sum(doc_onehot * (doc_ends - lengths)[None, :], axis=1))
    doc_length = jnp.maximum(lax.optimization_barrier(jnp.sum(doc_onehot * lengths[None, :], axis=1)), 1)
    segment = (NLAND * (positions - doc_start) + NLAND - 1) // doc_length
    return (doc_index, doc_index * NLAND + segment)

def slot_counts(lengths):
    slot_length = jnp.repeat(lengths, NLAND)
    segment = jnp.tile(jnp.arange(NLAND, dtype=jnp.int32), DOCS)
    return ((segment + 1) * slot_length // NLAND - segment * slot_length // NLAND).astype(jnp.float32)

def layer_norm(inputs, gain_row, shifts):
    average = lax.optimization_barrier(jnp.mean(inputs, axis=-1, keepdims=True))
    centred = inputs - average
    variance = lax.optimization_barrier(jnp.mean(centred * centred, axis=-1, keepdims=True))
    return centred * lax.rsqrt(variance + epsilon) * gain_row + shifts

def newton_pinv(matrix):
    identity = jnp.eye(matrix.shape[-1], dtype=jnp.float32)
    approx = jnp.swapaxes(matrix, -1, -2) / lax.optimization_barrier(jnp.sum(matrix * matrix, axis=(-2, -1), keepdims=True))
    for repeat in range(NS_ITERS):
        product = jnp.einsum('...ij,...jk->...ik', matrix, approx, precision=HIGHEST)
        factor = 7.0 * identity - product
        factor = 15.0 * identity - jnp.einsum('...ij,...jk->...ik', product, factor, precision=HIGHEST)
        factor = 13.0 * identity - jnp.einsum('...ij,...jk->...ik', product, factor, precision=HIGHEST)
        approx = 0.25 * jnp.einsum('...ij,...jk->...ik', approx, factor, precision=HIGHEST)
    return approx

def stream_layer(tokens, w_query, b_query, w_key, w_value, b_value, w_out, b_out, w_up, b_up, w_down, b_down, g_attn, s_attn, g_mlp, s_mlp, conv_kernel, doc_index, slot_index, counts):
    score_scale = 1.0 / math.sqrt(HD)
    half_width = (CONV - 1) // 2
    stream_len = tokens.shape[0]
    queries = low_back(jnp.dot(tokens, w_query, precision=HIGHEST) + b_query)
    key_rows = low_back(jnp.dot(tokens, w_key, precision=HIGHEST))
    values = low_back(jnp.dot(tokens, w_value, precision=HIGHEST) + b_value)
    member = (slot_index[:, None] == jnp.arange(SLOTS, dtype=jnp.int32)[None, :]).astype(jnp.float32)
    q_land = jnp.dot(member.T, queries, precision=HIGHEST) / counts[:, None]
    k_land = jnp.dot(member.T, key_rows, precision=HIGHEST) / counts[:, None]
    slot_doc = jnp.arange(SLOTS, dtype=jnp.int32) // NLAND
    same_doc = doc_index[:, None] == slot_doc[None, :]

    def one_head(pieces):
        q_head, k_head, v_head, ql_head, kl_head = pieces
        f_scores = jnp.where(same_doc, jnp.dot(q_head, kl_head.T, precision=HIGHEST) * score_scale, masked_score)
        f_weights = jax.nn.softmax(f_scores, axis=-1)
        b_scores = jnp.where(same_doc.T, jnp.dot(ql_head, k_head.T, precision=HIGHEST) * score_scale, masked_score)
        key_mix = jnp.dot(jax.nn.softmax(b_scores, axis=-1), v_head, precision=HIGHEST)
        q_docs = ql_head.reshape(DOCS, NLAND, HD)
        k_docs = kl_head.reshape(DOCS, NLAND, HD)
        a_scores = jnp.einsum('aid,ajd->aij', q_docs, k_docs, precision=HIGHEST) * score_scale
        inverse = newton_pinv(jax.nn.softmax(a_scores, axis=-1))
        mixing = jnp.einsum('aij,ajd->aid', inverse, key_mix.reshape(DOCS, NLAND, HD), precision=HIGHEST).reshape(SLOTS, HD)
        return jnp.dot(f_weights, mixing, precision=HIGHEST)

    def to_heads(matrix_rows):
        return jnp.transpose(matrix_rows.reshape(matrix_rows.shape[0], HEADS, HD), (1, 0, 2))
    head_out = lax.map(jax.checkpoint(one_head), (to_heads(queries), to_heads(key_rows), to_heads(values), to_heads(q_land), to_heads(k_land)))
    nystrom = jnp.transpose(head_out, (1, 0, 2)).reshape(stream_len, D)
    value_heads = values.reshape(stream_len, HEADS, HD)
    padded = jnp.pad(value_heads, ((half_width, half_width), (0, 0), (0, 0)))
    padded_doc = jnp.pad(doc_index, (half_width, half_width), constant_values=-1)
    conv_out = jnp.zeros((stream_len, HEADS, HD), jnp.float32)
    for offset in range(CONV):
        same_mask = (padded_doc[offset:offset + stream_len] == doc_index).astype(jnp.float32)
        conv_out = conv_out + conv_kernel[offset][None, :, None] * padded[offset:offset + stream_len] * same_mask[:, None, None]
    attention = nystrom + conv_out.reshape(stream_len, D)
    out_proj = low_back(jnp.dot(low(attention), w_out, precision=HIGHEST) + b_out)
    hidden = layer_norm(tokens + out_proj, g_attn, s_attn)
    up_pre = low_back(jnp.dot(low(hidden), w_up, precision=HIGHEST) + b_up)
    gelu_out = low(jax.nn.gelu(up_pre, approximate=False))
    down_pre = low_back(jnp.dot(gelu_out, w_down, precision=HIGHEST) + b_down)
    return layer_norm(hidden + down_pre, g_mlp, s_mlp)

def reference(tokens, cotangent, doc_lengths, w_query, b_query, w_key, w_value, b_value, w_out, b_out, w_up, b_up, w_down, b_down, g_attn, s_attn, g_mlp, s_mlp, conv_kernel):
    params = tuple((weight_arr.astype(jnp.float32) for weight_arr in (w_query, b_query, w_key, w_value, b_value, w_out, b_out, w_up, b_up, w_down, b_down, g_attn, s_attn, g_mlp, s_mlp, conv_kernel)))

    def per_stream(totals, stream_items):
        row_tokens, row_cot, lengths = stream_items
        positions = jnp.arange(STREAM, dtype=jnp.int32)
        doc_index, slot_index = locate(positions, lengths)
        counts = slot_counts(lengths)

        def forward(*inputs):
            return stream_layer(*inputs, doc_index, slot_index, counts)
        result, pullback = jax.vjp(forward, row_tokens.astype(jnp.float32), *params)
        gradients = pullback(row_cot.astype(jnp.float32))
        new_totals = tuple((summed + added for summed, added in zip(totals, gradients[1:])))
        return (new_totals, (result.astype(jnp.bfloat16), gradients[0].astype(jnp.bfloat16)))
    zero_grads = tuple((jnp.zeros(weight_arr.shape, jnp.float32) for weight_arr in params))
    totals, stacked = lax.scan(per_stream, zero_grads, (tokens, cotangent, doc_lengths))
    return (stacked[0], stacked[1], totals[0], totals[1], totals[2], totals[3], totals[4], totals[5], totals[6], totals[7], totals[8], totals[9], totals[10], totals[11], totals[12], totals[13], totals[14], totals[15])
```

```python
from functools import partial
import math

import jax
import jax.numpy as jnp
from jax import lax
from jax.experimental import pallas as pl
from jax.experimental.pallas import tpu as pltpu
from jax.sharding import PartitionSpec as P

D = 768
HEADS = 12
HD = 64
FF = 3072
NLAND = 64
NS_ITERS = 6
CONV = 33
REACH = CONV // 2
DOCS = 4
SLOTS = 256
SCALE = 1.0 / math.sqrt(HD)

HIGHEST = lax.Precision.HIGHEST
epsilon = 1e-05
masked_score = -1e30
f32 = jnp.float32
bf16 = jnp.bfloat16
MESH = pl.DeviceIdType.MESH
VMEM_BYTES = 56 * 1024 * 1024


def greet(peers):
    barrier = pltpu.get_barrier_semaphore()
    for peer in peers:
        pl.semaphore_signal(barrier, inc=1, device_id=peer, device_id_type=MESH)
    pl.semaphore_wait(barrier, len(peers))


def remote(src, dst, send_sem, recv_sem, peer):
    return pltpu.make_async_remote_copy(
        src_ref=src, dst_ref=dst, send_sem=send_sem, recv_sem=recv_sem,
        device_id=peer, device_id_type=MESH,
    )


def push_kernel(sizes, channels, *refs):
    seq, fsdp = sizes
    count = len(channels)
    srcs, dsts = refs[:count], refs[count : 2 * count]
    send_sem, recv_sem, own_sem = refs[2 * count :]
    s, f = lax.axis_index("seq"), lax.axis_index("fsdp")
    whole = any(kind == "all" for kind, _ in channels)
    steps = [(j, i) for j in range(seq) for i in range(fsdp if whole else 1) if (j, i) != (0, 0)]
    greet([((s + j) % seq, (f + i) % fsdp) for j, i in steps])
    copies, n = [], 0
    for c, (kind, period) in enumerate(channels):
        slot = s * fsdp + f if kind == "all" else s
        for j, i in [(0, 0)] + steps:
            if kind != "all" and i:
                continue
            to_s, to_f = (s + j) % seq, (f + i) % fsdp
            if period is None:
                block = srcs[c]
            else:
                index = to_s % period if period else (to_s * fsdp + to_f if kind == "all" else to_s)
                block = srcs[c].at[index]
            if (j, i) == (0, 0):
                copy = pltpu.make_async_copy(block, dsts[c].at[slot], own_sem.at[c])
            else:
                copy = remote(block, dsts[c].at[slot], send_sem.at[n], recv_sem.at[n], (to_s, to_f))
                n += 1
            copy.start()
            copies.append(copy)
    for copy in copies:
        copy.wait()


def push(sizes, channels, arrays, collective_id):
    seq, fsdp = sizes
    shapes, total = [], 0
    for (kind, period), array in zip(channels, arrays):
        slots = seq * fsdp if kind == "all" else seq
        total += slots - 1
        block = array.shape if period is None else array.shape[1:]
        shapes.append(jax.ShapeDtypeStruct((slots, *block), array.dtype))
    return pl.pallas_call(
        partial(push_kernel, sizes, channels),
        out_shape=tuple(shapes),
        in_specs=[pl.BlockSpec(memory_space=pl.ANY)] * len(arrays),
        out_specs=tuple([pl.BlockSpec(memory_space=pl.ANY)] * len(arrays)),
        scratch_shapes=[
            pltpu.SemaphoreType.DMA((total,)),
            pltpu.SemaphoreType.DMA((total,)),
            pltpu.SemaphoreType.DMA((len(arrays),)),
        ],
        compiler_params=pltpu.CompilerParams(collective_id=collective_id, has_side_effects=True),
    )(*arrays)


def place():
    s, f = lax.axis_index("seq"), lax.axis_index("fsdp")
    z, y, x, c = s // 2, s % 2, f // 2, f % 2
    return s, f, z, y, x, c


def gather_kernel(half, own_ref, out_ref, own_sem, z_send, z_recv, y_send, y_recv, x_send, x_recv, c_send, c_recv):
    s, f, z, y, x, c = place()
    oy, ox, oc = 1 - y, 1 - x, 1 - c
    z_peers = [((z + j) % 4 * 2 + y, f) for j in range(1, 4)]
    y_peer, x_peer, c_peer = (z * 2 + oy, f), (s, ox * 2 + c), (s, x * 2 + oc)
    greet(z_peers + [y_peer, x_peer, c_peer])
    rows_a, rows_b = pl.ds(0, half), pl.ds(half, half)

    def slot(k, sy, sx, sc):
        return ((z + 4 - k) % 4 * 2 + sy) * 4 + sx * 2 + sc

    started = []

    def start(copy):
        copy.start()
        started.append(copy)
        return copy

    own = pltpu.make_async_copy(own_ref, out_ref.at[slot(0, y, x, c)], own_sem)
    own.start()
    z_copies = []
    for j in range(1, 4):
        z_copies.append(
            start(remote(own_ref, out_ref.at[slot(0, y, x, c)], z_send.at[j - 1], z_recv.at[j - 1], z_peers[j - 1]))
        )

    def send_half(src, rows, where, sems, n, peer):
        return start(remote(src.at[rows], out_ref.at[where, rows], sems[0].at[n], sems[1].at[n], peer))

    def send_core(src, where, n):
        start(remote(src, out_ref.at[where], c_send.at[n], c_recv.at[n], c_peer))

    ys, xs = (y_send, y_recv), (x_send, x_recv)
    from_y, from_x, last_y, last_x = {}, {}, {}, {}

    def spread(k):
        src = own_ref if k == 0 else out_ref.at[slot(k, y, x, c)]
        where = slot(k, y, x, c)
        from_y[k, 0] = send_half(src, rows_a, where, ys, 3 * k, y_peer)
        from_x[k, 1] = send_half(src, rows_b, where, xs, 3 * k, x_peer)
        from_x[k, 0] = send_half(src, rows_a, where, xs, 3 * k + 1, x_peer)
        from_y[k, 1] = send_half(src, rows_b, where, ys, 3 * k + 1, y_peer)
        send_core(src, where, 4 * k)

    def relay(k):
        from_y[k, 0].wait_recv()
        where = slot(k, oy, x, c)
        last_x[k] = send_half(out_ref.at[where], rows_a, where, xs, 3 * k + 2, x_peer)
        from_x[k, 1].wait_recv()
        where = slot(k, y, ox, c)
        last_y[k] = send_half(out_ref.at[where], rows_b, where, ys, 3 * k + 2, y_peer)

    def finish(k):
        from_y[k, 1].wait_recv()
        send_core(out_ref.at[slot(k, oy, x, c)], slot(k, oy, x, c), 4 * k + 1)
        from_x[k, 0].wait_recv()
        send_core(out_ref.at[slot(k, y, ox, c)], slot(k, y, ox, c), 4 * k + 2)

    def corner(k):
        last_x[k].wait_recv()
        last_y[k].wait_recv()
        send_core(out_ref.at[slot(k, oy, ox, c)], slot(k, oy, ox, c), 4 * k + 3)

    for k in range(4):
        if k:
            z_copies[k - 1].wait_recv()
        spread(k)
        if k:
            relay(k - 1)
            finish(k - 1)
        if k > 1:
            corner(k - 2)
    relay(3)
    finish(3)
    corner(2)
    corner(3)
    own.wait()
    for copy in started:
        copy.wait_send()
    for k in range(4):
        for m, (sy, sx) in enumerate(((y, x), (oy, x), (y, ox), (oy, ox))):
            where = slot(k, sy, sx, c)
            remote(own_ref, out_ref.at[where], c_send.at[4 * k + m], c_recv.at[4 * k + m], c_peer).wait_recv()


def gather_all(shard, collective_id):
    rows, cols = shard.shape
    dma = pltpu.SemaphoreType.DMA
    return pl.pallas_call(
        partial(gather_kernel, rows // 2),
        out_shape=jax.ShapeDtypeStruct((32, rows, cols), shard.dtype),
        in_specs=[pl.BlockSpec(memory_space=pl.ANY)],
        out_specs=pl.BlockSpec(memory_space=pl.ANY),
        scratch_shapes=[dma(()), dma((3,)), dma((3,)), dma((12,)), dma((12,)), dma((12,)), dma((12,)), dma((16,)), dma((16,))],
        compiler_params=pltpu.CompilerParams(collective_id=collective_id, has_side_effects=True),
    )(shard)


def scatter_kernel(half, part_ref, out_ref, acc, got_a, got_b, got_z, c_send, c_recv, x_send, x_recv, y_send, y_recv, z_send, z_recv):
    s, f, z, y, x, c = place()
    oy, ox, oc = 1 - y, 1 - x, 1 - c
    z_peers = [((z + j) % 4 * 2 + y, f) for j in range(1, 4)]
    y_peer, x_peer, c_peer = (z * 2 + oy, f), (s, ox * 2 + c), (s, x * 2 + oc)
    greet(z_peers + [y_peer, x_peer, c_peer])
    rows_a, rows_b = pl.ds(0, half), pl.ds(half, half)
    places = ((0, 0), (0, 1), (1, 0), (1, 1))

    def owner(k, sy, sx, sc):
        return ((z + k + 1) % 4 * 2 + sy) * 4 + sx * 2 + sc

    copies = {}
    for k in range(4):
        for m, (sy, sx) in enumerate(places):
            copy = remote(part_ref.at[owner(k, sy, sx, oc)], acc.at[k, sy, sx], c_send.at[4 * k + m], c_recv.at[4 * k + m], c_peer)
            copy.start()
            copies["c", k, m] = copy

    def first(k):
        for m, (sy, sx) in enumerate(places):
            copies["c", k, m].wait_recv()
            acc[k, sy, sx] = (
                acc[k, sy, sx].astype(jnp.float32) + part_ref[owner(k, sy, sx, c)].astype(jnp.float32)
            ).astype(acc.dtype)
        for sy in range(2):
            copy = remote(acc.at[k, sy, ox, rows_a], got_a.at[k, sy], x_send.at[3 * k + sy], x_recv.at[3 * k + sy], x_peer)
            copy.start()
            copies["a", k, sy] = copy
        for sx in range(2):
            copy = remote(acc.at[k, oy, sx, rows_b], got_b.at[k, sx], y_send.at[3 * k + sx], y_recv.at[3 * k + sx], y_peer)
            copy.start()
            copies["b", k, sx] = copy

    def add(target, extra):
        target[...] = (target[...].astype(jnp.float32) + extra[...].astype(jnp.float32)).astype(target.dtype)

    def second(k):
        for sy in range(2):
            copies["a", k, sy].wait_recv()
            add(acc.at[k, sy, x, rows_a], got_a.at[k, sy])
        copy = remote(acc.at[k, oy, x, rows_a], got_a.at[k, 2], y_send.at[3 * k + 2], y_recv.at[3 * k + 2], y_peer)
        copy.start()
        copies["a", k, 2] = copy
        for sx in range(2):
            copies["b", k, sx].wait_recv()
            add(acc.at[k, y, sx, rows_b], got_b.at[k, sx])
        copy = remote(acc.at[k, y, ox, rows_b], got_b.at[k, 2], x_send.at[3 * k + 2], x_recv.at[3 * k + 2], x_peer)
        copy.start()
        copies["b", k, 2] = copy

    def third(k):
        copies["a", k, 2].wait_recv()
        add(acc.at[k, y, x, rows_a], got_a.at[k, 2])
        copies["b", k, 2].wait_recv()
        add(acc.at[k, y, x, rows_b], got_b.at[k, 2])
        if k < 3:
            copy = remote(acc.at[k, y, x], got_z.at[k], z_send.at[k], z_recv.at[k], z_peers[k])
            copy.start()
            copies["z", k, 0] = copy

    for k in range(6):
        if k < 4:
            first(k)
        if 1 <= k < 5:
            second(k - 1)
        if k >= 2:
            third(k - 2)
    total = acc[3, y, x].astype(jnp.float32)
    for k in range(3):
        copies["z", k, 0].wait_recv()
        total += got_z[k].astype(jnp.float32)
    out_ref[...] = total
    for copy in copies.values():
        copy.wait_send()


def scatter_all(part, collective_id):
    _, rows, cols = part.shape
    dma = pltpu.SemaphoreType.DMA
    half = rows // 2
    return pl.pallas_call(
        partial(scatter_kernel, half),
        out_shape=jax.ShapeDtypeStruct((rows, cols), jnp.float32),
        in_specs=[pl.BlockSpec(memory_space=pltpu.VMEM)],
        out_specs=pl.BlockSpec(memory_space=pltpu.VMEM),
        scratch_shapes=[
            pltpu.VMEM((4, 2, 2, rows, cols), part.dtype),
            pltpu.VMEM((4, 3, half, cols), part.dtype),
            pltpu.VMEM((4, 3, half, cols), part.dtype),
            pltpu.VMEM((3, rows, cols), part.dtype),
            dma((16,)), dma((16,)), dma((12,)), dma((12,)), dma((12,)), dma((12,)), dma((3,)), dma((3,)),
        ],
        compiler_params=pltpu.CompilerParams(
            collective_id=collective_id, has_side_effects=True, vmem_limit_bytes=VMEM_BYTES
        ),
    )(part)
def high(form, left, right):
    return jnp.einsum(form, left, right, precision=HIGHEST)


def product(form, left, right):
    return jnp.einsum(form, left, right, preferred_element_type=f32)


def slot_bounds(lengths):
    ends = jnp.cumsum(lengths)
    starts = ends - lengths
    doc = jnp.arange(SLOTS, dtype=jnp.int32) // NLAND
    seg = jnp.arange(SLOTS, dtype=jnp.int32) % NLAND
    length, start, end = lengths[doc], starts[doc], ends[doc]
    return start, end, start + seg * length // NLAND, start + (seg + 1) * length // NLAND


def newton_forward(a, block):
    eye = jnp.eye(SLOTS, dtype=f32)
    norm = high("ij,jk->ik", block, a * a).sum(axis=1, keepdims=True)
    z = a.T / norm
    kept = []
    p = high("ij,jk->ik", a, z)
    for step in range(NS_ITERS):
        q = high("ij,jk->ik", p, p)
        f = 13.0 * eye - 15.0 * p + 7.0 * q - high("ij,jk->ik", p, q)
        kept.append((z, p, q, f))
        if step < NS_ITERS - 1:
            p = 0.25 * high("ij,jk->ik", p, f)
        z = 0.25 * high("ij,jk->ik", z, f)
    return z, norm, kept


def newton_backward(a, norm, kept, dz, block):
    dp = None
    for step in range(NS_ITERS - 1, -1, -1):
        z, p, q, f = kept[step]
        df = 0.25 * high("ji,jk->ik", z, dz)
        dz = 0.25 * high("ik,jk->ij", dz, f)
        if dp is None:
            dnew = jnp.zeros_like(df)
        else:
            df = df + 0.25 * high("ji,jk->ik", p, dp)
            dnew = 0.25 * high("ik,jk->ij", dp, f)
        dq = 7.0 * df - high("ji,jk->ik", p, df)
        dp = dnew - 15.0 * df - high("ik,jk->ij", df, q) + high("ik,jk->ij", dq, p) + high("ji,jk->ik", p, dq)
    z = kept[0][0]
    da = high("ik,jk->ij", dp, z)
    dz = dz + high("ji,jk->ik", a, dp)
    inner = high("ij,jk->ik", block, dz * z).sum(axis=1, keepdims=True)
    return da + (dz / norm).T - 2.0 * a * inner / norm


def softmax(scores, valid, axis):
    scores = jnp.where(valid, scores, masked_score)
    expo = jnp.exp(scores - jnp.max(scores, axis=axis, keepdims=True))
    return expo / jnp.sum(expo, axis=axis, keepdims=True)


def band(taps):
    rows = jnp.arange(128)[:, None]
    cols = jnp.arange(256)[None, :]
    tap = cols - rows - 64 + REACH
    mat = jnp.zeros((128, 256), f32)
    for o in range(CONV):
        mat = jnp.where(tap == o, taps[o], mat)
    return tap, lax.optimization_barrier(mat)


def attention_forward(tokens, weights, bias_q, bias_v, lengths, taps):
    total = tokens.shape[0]
    width = weights.shape[1] // 3
    heads = width // HD
    start, end, low, top = slot_bounds(lengths)
    place = jnp.arange(total, dtype=jnp.int32)[None, :]
    member = ((place >= low[:, None]) & (place < top[:, None])).astype(f32)
    same = (place >= start[:, None]) & (place < end[:, None])
    count = (top - low).astype(f32)[:, None]
    slot_doc = jnp.arange(SLOTS) // NLAND
    block = (slot_doc[:, None] == slot_doc[None, :])
    ends = jnp.cumsum(lengths)
    doc = jnp.sum((place[0][:, None] >= ends[None, :]).astype(jnp.int32), axis=1)
    doc_wide = jnp.pad(doc, (64, 64), constant_values=-1)
    qkv = product("td,de->te", tokens, weights)
    q = qkv[:, :width] + bias_q
    k = qkv[:, width : 2 * width]
    v = qkv[:, 2 * width :] + bias_v
    ql = high("st,td->sd", member, q) / count
    kl = high("st,td->sd", member, k) / count
    v_wide = jnp.pad(v, ((64, 64), (0, 0)))
    outs, saved = [], []
    for h in range(heads):
        cols = slice(h * HD, (h + 1) * HD)
        qh, kh, vh, qlh, klh = q[:, cols], k[:, cols], v[:, cols], ql[:, cols], kl[:, cols]
        fw = softmax(SCALE * high("td,sd->ts", qh, klh), same.T, 1)
        bw = softmax(SCALE * high("sd,td->st", qlh, kh), same, 1)
        key_mix = high("st,td->sd", bw, vh)
        a = softmax(SCALE * high("sd,rd->sr", qlh, klh), block, 1)
        z, norm, kept = newton_forward(a, block.astype(f32))
        mixing = high("sr,rd->sd", z, key_mix)
        out = high("ts,sd->td", fw, mixing)
        toeplitz = band(taps[:, h])[1]
        conv = []
        for b in range(total // 128):
            rows = slice(128 * b, 128 * b + 128)
            window = slice(128 * b, 128 * b + 256)
            mat = jnp.where(doc[rows][:, None] == doc_wide[window][None, :], toeplitz, 0.0)
            conv.append(high("tu,ud->td", mat, v_wide[window, cols]))
        outs.append((out + jnp.concatenate(conv, axis=0)).astype(bf16))
        saved.append((fw, bw, key_mix, a, z, norm, kept, mixing))
    return jnp.concatenate(outs, axis=1), (q, k, v, ql, kl, member, count, block.astype(f32), doc, doc_wide, saved)


def attention_backward(tokens, weights, taps, d_attn, state):
    q, k, v, ql, kl, member, count, block, doc, doc_wide, saved = state
    total = tokens.shape[0]
    width = q.shape[1]
    heads = width // HD
    d_attn = d_attn.astype(f32)
    d_wide = jnp.pad(d_attn, ((64, 64), (0, 0)))
    v_wide = jnp.pad(v, ((64, 64), (0, 0)))
    grads = [[], [], []]
    kernel_rows = []
    for h in range(heads):
        cols = slice(h * HD, (h + 1) * HD)
        qh, kh, vh, qlh, klh, do = q[:, cols], k[:, cols], v[:, cols], ql[:, cols], kl[:, cols], d_attn[:, cols]
        fw, bw, key_mix, a, z, norm, kept, mixing = saved[h]
        d_mix = high("ts,td->sd", fw, do)
        dfw = high("td,sd->ts", do, mixing)
        dsf = SCALE * fw * (dfw - jnp.sum(fw * dfw, axis=1, keepdims=True))
        dq_f = high("ts,sd->td", dsf, klh)
        dkl = high("ts,td->sd", dsf, qh)
        dz = high("sd,rd->sr", d_mix, key_mix) * block
        d_keymix = high("sr,sd->rd", z, d_mix)
        da = newton_backward(a, norm, kept, dz, block) * block
        dsa = SCALE * a * (da - jnp.sum(a * da, axis=1, keepdims=True))
        dql = high("sr,rd->sd", dsa, klh)
        dkl = dkl + high("sr,sd->rd", dsa, qlh)
        dbw = high("sd,td->st", d_keymix, vh)
        dsb = SCALE * bw * (dbw - jnp.sum(d_keymix * key_mix, axis=1, keepdims=True))
        dql = dql + high("st,td->sd", dsb, kh)
        dk_b = high("st,sd->td", dsb, qlh)
        dv_b = high("st,sd->td", bw, d_keymix)
        tap, toeplitz = band(taps[:, h])
        _, mirror = band(taps[::-1, h])
        dv_conv, spread = [], 0.0
        for b in range(total // 128):
            rows = slice(128 * b, 128 * b + 128)
            window = slice(128 * b, 128 * b + 256)
            near = doc[rows][:, None] == doc_wide[window][None, :]
            dv_conv.append(high("tu,ud->td", jnp.where(near, mirror, 0.0), d_wide[window, cols]))
            spread = spread + jnp.where(near, high("td,ud->tu", do[rows], v_wide[window, cols]), 0.0)
        choose = (tap[None] == jnp.arange(CONV)[:, None, None]).astype(f32)
        kernel_rows.append(jnp.sum(choose * spread[None], axis=(1, 2)))
        grads[0].append((dq_f + high("st,sd->td", member, dql / count)).astype(bf16))
        grads[1].append((dk_b + high("st,sd->td", member, dkl / count)).astype(bf16))
        grads[2].append((dv_b + jnp.concatenate(dv_conv, axis=0)).astype(bf16))
    d_qkv = jnp.concatenate(grads[0] + grads[1] + grads[2], axis=1)
    dw = product("td,te->de", tokens, d_qkv)
    db = jnp.sum(d_qkv.astype(f32), axis=0)
    part = product("te,de->td", d_qkv, weights).astype(bf16)
    return part, dw, db, jnp.stack(kernel_rows, axis=0)


def layer_norm(inputs, gain, shift):
    average = jnp.mean(inputs, axis=-1, keepdims=True)
    centred = inputs - average
    variance = jnp.mean(centred * centred, axis=-1, keepdims=True)
    return centred * lax.rsqrt(variance + epsilon) * gain + shift


def gelu_exact(inputs):
    return jax.nn.gelu(inputs, approximate=False)


def token_part(tokens, cot, attention, w_out, w_up, w_down, b_out, b_up, b_down, g_attn, s_attn, g_mlp, s_mlp):
    out_proj = product("td,de->te", attention, w_out) + b_out
    hidden, norm_one_back = jax.vjp(layer_norm, tokens.astype(f32) + out_proj, g_attn, s_attn)
    hidden_low = hidden.astype(bf16)
    up_pre = product("td,df->tf", hidden_low, w_up) + b_up
    gelu_val, gelu_back = jax.vjp(gelu_exact, up_pre)
    gelu_low = gelu_val.astype(bf16)
    down_pre = product("tf,fd->td", gelu_low, w_down) + b_down
    output, norm_two_back = jax.vjp(layer_norm, hidden + down_pre, g_mlp, s_mlp)
    d_r2, dg_mlp, ds_mlp = norm_two_back(cot.astype(f32))
    d_down = d_r2.astype(bf16)
    db_down = jnp.sum(d_down.astype(f32), axis=0)
    dw_down = product("tf,td->fd", gelu_low, d_down)
    d_gelu = product("td,fd->tf", d_down, w_down)
    d_up = gelu_back(d_gelu)[0].astype(bf16)
    db_up = jnp.sum(d_up.astype(f32), axis=0)
    dw_up = product("td,tf->df", hidden_low, d_up)
    d_hidden = product("tf,df->td", d_up, w_up) + d_r2
    d_r1, dg_attn, ds_attn = norm_one_back(d_hidden)
    d_out = d_r1.astype(bf16)
    db_out = jnp.sum(d_out.astype(f32), axis=0)
    dw_out = product("td,te->de", attention, d_out)
    d_attn = product("te,de->td", d_out, w_out)
    smalls = (db_out, db_up, db_down, dg_attn, ds_attn, dg_mlp, ds_mlp)
    return output.astype(bf16), d_r1, d_attn, dw_out, dw_up, dw_down, smalls
def local(sizes, *args):
    (tokens, cotangent, doc_lengths, w_query, b_query, w_key, w_value, b_value, w_out, b_out, w_up, b_up,
     w_down, b_down, g_attn, s_attn, g_mlp, s_mlp, conv_kernel) = args
    seq, fsdp = sizes
    devices = seq * fsdp
    fast = sizes == (8, 4)
    axes = ("seq", "fsdp")
    rows = D // devices
    hidden_rows = FF // devices
    own_tokens, own_cot, lengths = tokens[0], cotangent[0], doc_lengths[0]
    count = own_tokens.shape[0]
    total = count * seq
    heads = -(-HEADS // seq)
    width = heads * HD
    active = HEADS // heads
    s = lax.axis_index("seq")
    part = s % active

    pack_rows = -(-(rows + 1) // 16) * 16
    bias_row = jnp.zeros((1, 3 * width), bf16)
    bias_row = bias_row.at[0, :rows].set(b_query).at[0, width : width + rows].set(b_value)
    blocks = []
    for b in range(active):
        cols = slice(b * width, (b + 1) * width)
        blocks.append(jnp.concatenate(
            [jnp.concatenate([w_query[:, cols], w_key[:, cols], w_value[:, cols]], axis=1), bias_row,
             jnp.zeros((pack_rows - rows - 1, 3 * width), bf16)], axis=0))
    pack = jnp.stack(blocks)
    if fast:
        all_tokens, all_pack = push(sizes, (("seq", None), ("all", active)), (own_tokens, pack), 0)
    else:
        all_tokens = lax.all_gather(own_tokens, "seq")
        all_pack = lax.all_gather(lax.all_to_all(
            jnp.take(pack, jnp.arange(seq) % active, axis=0), "seq", 0, 0), "fsdp", axis=1).reshape(
                devices, pack_rows, 3 * width)
    all_tokens = all_tokens.reshape(total, D)
    qkv_weights = all_pack[:, :rows].reshape(D, 3 * width)
    bias_q = lax.dynamic_slice_in_dim(all_pack[:, rows, :rows].reshape(D), part * width, width)
    bias_v = lax.dynamic_slice_in_dim(all_pack[:, rows, width : width + rows].reshape(D), part * width, width)

    small = jnp.concatenate([b_out, b_down, g_attn, s_attn, g_mlp, s_mlp, b_up])
    shard_rows = rows + 4 * rows + hidden_rows
    small_rows = -(-(shard_rows + 1) // 16) * 16 - shard_rows
    small = jnp.pad(small, (0, small_rows * D - small.shape[0])).reshape(small_rows, D)
    shard = jnp.concatenate(
        [w_out] + [w_up[:, D * j : D * (j + 1)] for j in range(4)] + [w_down, small], axis=0)
    if fast:
        gathered = gather_all(shard, 1)
    else:
        gathered = lax.all_gather(shard, axes)
    full_out = gathered[:, :rows].reshape(D, D)
    full_up = jnp.concatenate(
        [gathered[:, rows * (1 + j) : rows * (2 + j)].reshape(D, D) for j in range(4)], axis=1)
    full_down = gathered[:, 5 * rows : shard_rows].reshape(FF, D)
    small = gathered[:, shard_rows].astype(f32)
    vectors = [small[:, rows * j : rows * (j + 1)].reshape(D) for j in range(6)]
    f_b_out, f_b_down, f_g_attn, f_s_attn, f_g_mlp, f_s_mlp = vectors
    f_b_up = small[:, 6 * rows : 6 * rows + hidden_rows].reshape(FF)

    taps = lax.dynamic_slice_in_dim(conv_kernel.astype(f32), part * heads, heads, axis=1)
    mixed, state = attention_forward(
        all_tokens, qkv_weights, bias_q.astype(f32), bias_v.astype(f32), lengths, taps)
    mixed = mixed.reshape(seq, count, width)
    if fast:
        (attention,) = push(sizes, (("seq", 0),), (mixed,), 2)
    else:
        attention = lax.all_to_all(mixed, "seq", 0, 0)
    attention = jnp.transpose(attention[:active], (1, 0, 2)).reshape(count, D)

    output, d_r1, d_attn, dw_out, dw_up, dw_down, smalls = token_part(
        own_tokens, own_cot, attention, full_out, full_up, full_down, f_b_out, f_b_up, f_b_down,
        f_g_attn, f_s_attn, f_g_mlp, f_s_mlp)

    d_attn = jnp.transpose(d_attn.astype(bf16).reshape(count, active, width), (1, 0, 2))
    if fast:
        (d_mixed,) = push(sizes, (("seq", active),), (d_attn,), 3)
    else:
        d_mixed = lax.all_to_all(jnp.take(d_attn, jnp.arange(seq) % active, axis=0), "seq", 0, 0)

    db_out, db_up, db_down, dg_attn, ds_attn, dg_mlp, ds_mlp = smalls
    grad_small = jnp.concatenate(
        [entry.reshape(devices, -1) for entry in (db_out, db_down, dg_attn, ds_attn, dg_mlp, ds_mlp, db_up)], axis=1)
    grad_small = jnp.pad(grad_small, ((0, 0), (0, small_rows * D - grad_small.shape[1])))
    parts = jnp.concatenate(
        [dw_out.reshape(devices, rows, D)]
        + [dw_up[:, D * j : D * (j + 1)].reshape(devices, rows, D) for j in range(4)]
        + [dw_down.reshape(devices, hidden_rows, D), grad_small.reshape(devices, small_rows, D)],
        axis=1).astype(bf16)
    if fast:
        summed = scatter_all(parts, 4)
    else:
        summed = lax.psum_scatter(parts.astype(f32), axes, scatter_dimension=0, tiled=False)

    d_part, dw, db, d_taps = attention_backward(
        all_tokens, qkv_weights, taps, d_mixed.reshape(total, width), state)
    extra = jnp.zeros((pack_rows - rows, 3 * width), f32)
    extra = extra.at[0].set(db)
    for h in range(heads):
        extra = extra.at[1 + h, :CONV].set(d_taps[h])
    send = jnp.concatenate(
        [dw.reshape(devices, rows, 3 * width), jnp.broadcast_to(extra[None], (devices, *extra.shape))],
        axis=1).astype(bf16)
    d_part = d_part.reshape(seq, count, D)
    if fast:
        token_parts, grad_parts = push(sizes, (("seq", 0), ("all", 0)), (d_part, send), 5)
    else:
        token_parts = lax.all_to_all(d_part, "seq", 0, 0)
        grad_parts = lax.all_to_all(send, axes, 0, 0)
    d_tokens = (d_r1 + jnp.sum(token_parts[:active].astype(f32), axis=0)).astype(bf16)
    sums = jnp.sum(grad_parts.reshape(seq, fsdp, pack_rows, 3, width)[:active].astype(f32), axis=1)
    dw_query, dw_key, dw_value = (
        jnp.transpose(sums[:, :rows, j], (1, 0, 2)).reshape(rows, D) for j in range(3))
    own = (s * fsdp + lax.axis_index("fsdp")) * rows
    db_query = lax.dynamic_slice_in_dim(sums[:, rows, 0].reshape(D), own, rows)
    db_value = lax.dynamic_slice_in_dim(sums[:, rows, 2].reshape(D), own, rows)
    d_kernel = jnp.transpose(
        sums[:, rows + 1 : rows + 1 + heads].reshape(active * heads, 3 * width)[:, :CONV], (1, 0))

    last = summed[shard_rows:].reshape(-1)
    g = [last[rows * j : rows * (j + 1)] for j in range(6)]
    s_wup = jnp.concatenate([summed[rows * (1 + j) : rows * (2 + j)] for j in range(4)], axis=1)
    return (
        output[None], d_tokens[None], dw_query, db_query, dw_key, dw_value, db_value, summed[:rows], g[0],
        s_wup, last[6 * rows : 6 * rows + hidden_rows], summed[5 * rows : shard_rows], g[1],
        g[2], g[3], g[4], g[5], d_kernel)


def solution(mesh):
    sizes = (mesh.shape["seq"], mesh.shape["fsdp"])
    both = ("seq", "fsdp")
    wide, flat, stream = P(both, None), P(both), P("fsdp", "seq", None)
    in_specs = (stream, stream, P("fsdp", None), wide, flat, wide, wide, flat, wide, flat, wide, flat, wide, flat,
                flat, flat, flat, flat, P())
    out_specs = (stream, stream, wide, flat, wide, wide, flat, wide, flat, wide, flat, wide, flat, flat, flat, flat,
                 flat, P())
    return jax.shard_map(partial(local, sizes), mesh=mesh, in_specs=in_specs, out_specs=out_specs, check_vma=False)
```

```python
from functools import partial
import math

import jax
import jax.numpy as jnp
from jax import lax
from jax.experimental import pallas as pl
from jax.experimental.pallas import tpu as pltpu
from jax.sharding import PartitionSpec as P

D = 768
HEADS = 12
HD = 64
FF = 3072
NLAND = 64
NS_ITERS = 6
CONV = 33
REACH = CONV // 2
DOCS = 4
SLOTS = 256
SCALE = 1.0 / math.sqrt(HD)

HIGHEST = lax.Precision.HIGHEST
epsilon = 1e-05
masked_score = -1e30
f32 = jnp.float32
bf16 = jnp.bfloat16
MESH = pl.DeviceIdType.MESH
VMEM_BYTES = 56 * 1024 * 1024


def greet(peers):
    barrier = pltpu.get_barrier_semaphore()
    for peer in peers:
        pl.semaphore_signal(barrier, inc=1, device_id=peer, device_id_type=MESH)
    pl.semaphore_wait(barrier, len(peers))


def remote(src, dst, send_sem, recv_sem, peer):
    return pltpu.make_async_remote_copy(
        src_ref=src, dst_ref=dst, send_sem=send_sem, recv_sem=recv_sem,
        device_id=peer, device_id_type=MESH,
    )


def push_kernel(sizes, channels, *refs):
    seq, fsdp = sizes
    count = len(channels)
    srcs, dsts = refs[:count], refs[count : 2 * count]
    send_sem, recv_sem, own_sem = refs[2 * count :]
    s, f = lax.axis_index("seq"), lax.axis_index("fsdp")
    whole = any(kind == "all" for kind, _ in channels)
    steps = [(j, i) for j in range(seq) for i in range(fsdp if whole else 1) if (j, i) != (0, 0)]
    greet([((s + j) % seq, (f + i) % fsdp) for j, i in steps])
    copies, n = [], 0
    for c, (kind, period) in enumerate(channels):
        slot = s * fsdp + f if kind == "all" else s
        for j, i in [(0, 0)] + steps:
            if kind != "all" and i:
                continue
            to_s, to_f = (s + j) % seq, (f + i) % fsdp
            if period is None:
                block = srcs[c]
            else:
                index = to_s % period if period else (to_s * fsdp + to_f if kind == "all" else to_s)
                block = srcs[c].at[index]
            if (j, i) == (0, 0):
                copy = pltpu.make_async_copy(block, dsts[c].at[slot], own_sem.at[c])
            else:
                copy = remote(block, dsts[c].at[slot], send_sem.at[n], recv_sem.at[n], (to_s, to_f))
                n += 1
            copy.start()
            copies.append(copy)
    for copy in copies:
        copy.wait()


def push(sizes, channels, arrays, collective_id):
    seq, fsdp = sizes
    shapes, total = [], 0
    for (kind, period), array in zip(channels, arrays):
        slots = seq * fsdp if kind == "all" else seq
        total += slots - 1
        block = array.shape if period is None else array.shape[1:]
        shapes.append(jax.ShapeDtypeStruct((slots, *block), array.dtype))
    return pl.pallas_call(
        partial(push_kernel, sizes, channels),
        out_shape=tuple(shapes),
        in_specs=[pl.BlockSpec(memory_space=pl.ANY)] * len(arrays),
        out_specs=tuple([pl.BlockSpec(memory_space=pl.ANY)] * len(arrays)),
        scratch_shapes=[
            pltpu.SemaphoreType.DMA((total,)),
            pltpu.SemaphoreType.DMA((total,)),
            pltpu.SemaphoreType.DMA((len(arrays),)),
        ],
        compiler_params=pltpu.CompilerParams(collective_id=collective_id, has_side_effects=True),
    )(*arrays)


def place():
    s, f = lax.axis_index("seq"), lax.axis_index("fsdp")
    z, y, x, c = s // 2, s % 2, f // 2, f % 2
    return s, f, z, y, x, c


def gather_kernel(half, own_ref, out_ref, own_sem, z_send, z_recv, y_send, y_recv, x_send, x_recv, c_send, c_recv):
    s, f, z, y, x, c = place()
    oy, ox, oc = 1 - y, 1 - x, 1 - c
    z_peers = [((z + j) % 4 * 2 + y, f) for j in range(1, 4)]
    y_peer, x_peer, c_peer = (z * 2 + oy, f), (s, ox * 2 + c), (s, x * 2 + oc)
    greet(z_peers + [y_peer, x_peer, c_peer])
    rows_a, rows_b = pl.ds(0, half), pl.ds(half, half)

    def slot(k, sy, sx, sc):
        return ((z + 4 - k) % 4 * 2 + sy) * 4 + sx * 2 + sc

    started = []

    def start(copy):
        copy.start()
        started.append(copy)
        return copy

    own = pltpu.make_async_copy(own_ref, out_ref.at[slot(0, y, x, c)], own_sem)
    own.start()
    z_copies = []
    for j in range(1, 4):
        z_copies.append(
            start(remote(own_ref, out_ref.at[slot(0, y, x, c)], z_send.at[j - 1], z_recv.at[j - 1], z_peers[j - 1]))
        )

    def send_half(src, rows, where, sems, n, peer):
        return start(remote(src.at[rows], out_ref.at[where, rows], sems[0].at[n], sems[1].at[n], peer))

    def send_core(src, where, n):
        start(remote(src, out_ref.at[where], c_send.at[n], c_recv.at[n], c_peer))

    ys, xs = (y_send, y_recv), (x_send, x_recv)
    from_y, from_x, last_y, last_x = {}, {}, {}, {}

    def spread(k):
        src = own_ref if k == 0 else out_ref.at[slot(k, y, x, c)]
        where = slot(k, y, x, c)
        from_y[k, 0] = send_half(src, rows_a, where, ys, 3 * k, y_peer)
        from_x[k, 1] = send_half(src, rows_b, where, xs, 3 * k, x_peer)
        from_x[k, 0] = send_half(src, rows_a, where, xs, 3 * k + 1, x_peer)
        from_y[k, 1] = send_half(src, rows_b, where, ys, 3 * k + 1, y_peer)
        send_core(src, where, 4 * k)

    def relay(k):
        from_y[k, 0].wait_recv()
        where = slot(k, oy, x, c)
        last_x[k] = send_half(out_ref.at[where], rows_a, where, xs, 3 * k + 2, x_peer)
        from_x[k, 1].wait_recv()
        where = slot(k, y, ox, c)
        last_y[k] = send_half(out_ref.at[where], rows_b, where, ys, 3 * k + 2, y_peer)

    def finish(k):
        from_y[k, 1].wait_recv()
        send_core(out_ref.at[slot(k, oy, x, c)], slot(k, oy, x, c), 4 * k + 1)
        from_x[k, 0].wait_recv()
        send_core(out_ref.at[slot(k, y, ox, c)], slot(k, y, ox, c), 4 * k + 2)

    def corner(k):
        last_x[k].wait_recv()
        last_y[k].wait_recv()
        send_core(out_ref.at[slot(k, oy, ox, c)], slot(k, oy, ox, c), 4 * k + 3)

    for k in range(4):
        if k:
            z_copies[k - 1].wait_recv()
        spread(k)
        if k:
            relay(k - 1)
            finish(k - 1)
        if k > 1:
            corner(k - 2)
    relay(3)
    finish(3)
    corner(2)
    corner(3)
    own.wait()
    for copy in started:
        copy.wait_send()
    for k in range(4):
        for m, (sy, sx) in enumerate(((y, x), (oy, x), (y, ox), (oy, ox))):
            where = slot(k, sy, sx, c)
            remote(own_ref, out_ref.at[where], c_send.at[4 * k + m], c_recv.at[4 * k + m], c_peer).wait_recv()


def gather_all(shard, collective_id):
    rows, cols = shard.shape
    dma = pltpu.SemaphoreType.DMA
    return pl.pallas_call(
        partial(gather_kernel, rows // 2),
        out_shape=jax.ShapeDtypeStruct((32, rows, cols), shard.dtype),
        in_specs=[pl.BlockSpec(memory_space=pl.ANY)],
        out_specs=pl.BlockSpec(memory_space=pl.ANY),
        scratch_shapes=[dma(()), dma((3,)), dma((3,)), dma((12,)), dma((12,)), dma((12,)), dma((12,)), dma((16,)), dma((16,))],
        compiler_params=pltpu.CompilerParams(collective_id=collective_id, has_side_effects=True),
    )(shard)


def scatter_kernel(half, part_ref, out_ref, acc, got_a, got_b, got_z, c_send, c_recv, x_send, x_recv, y_send, y_recv, z_send, z_recv):
    s, f, z, y, x, c = place()
    oy, ox, oc = 1 - y, 1 - x, 1 - c
    z_peers = [((z + j) % 4 * 2 + y, f) for j in range(1, 4)]
    y_peer, x_peer, c_peer = (z * 2 + oy, f), (s, ox * 2 + c), (s, x * 2 + oc)
    greet(z_peers + [y_peer, x_peer, c_peer])
    rows_a, rows_b = pl.ds(0, half), pl.ds(half, half)
    places = ((0, 0), (0, 1), (1, 0), (1, 1))

    def owner(k, sy, sx, sc):
        return ((z + k + 1) % 4 * 2 + sy) * 4 + sx * 2 + sc

    copies = {}
    for k in range(4):
        for m, (sy, sx) in enumerate(places):
            copy = remote(part_ref.at[owner(k, sy, sx, oc)], acc.at[k, sy, sx], c_send.at[4 * k + m], c_recv.at[4 * k + m], c_peer)
            copy.start()
            copies["c", k, m] = copy

    def first(k):
        for m, (sy, sx) in enumerate(places):
            copies["c", k, m].wait_recv()
            acc[k, sy, sx] = (
                acc[k, sy, sx].astype(jnp.float32) + part_ref[owner(k, sy, sx, c)].astype(jnp.float32)
            ).astype(acc.dtype)
        for sy in range(2):
            copy = remote(acc.at[k, sy, ox, rows_a], got_a.at[k, sy], x_send.at[3 * k + sy], x_recv.at[3 * k + sy], x_peer)
            copy.start()
            copies["a", k, sy] = copy
        for sx in range(2):
            copy = remote(acc.at[k, oy, sx, rows_b], got_b.at[k, sx], y_send.at[3 * k + sx], y_recv.at[3 * k + sx], y_peer)
            copy.start()
            copies["b", k, sx] = copy

    def add(target, extra):
        target[...] = (target[...].astype(jnp.float32) + extra[...].astype(jnp.float32)).astype(target.dtype)

    def second(k):
        for sy in range(2):
            copies["a", k, sy].wait_recv()
            add(acc.at[k, sy, x, rows_a], got_a.at[k, sy])
        copy = remote(acc.at[k, oy, x, rows_a], got_a.at[k, 2], y_send.at[3 * k + 2], y_recv.at[3 * k + 2], y_peer)
        copy.start()
        copies["a", k, 2] = copy
        for sx in range(2):
            copies["b", k, sx].wait_recv()
            add(acc.at[k, y, sx, rows_b], got_b.at[k, sx])
        copy = remote(acc.at[k, y, ox, rows_b], got_b.at[k, 2], x_send.at[3 * k + 2], x_recv.at[3 * k + 2], x_peer)
        copy.start()
        copies["b", k, 2] = copy

    def third(k):
        copies["a", k, 2].wait_recv()
        add(acc.at[k, y, x, rows_a], got_a.at[k, 2])
        copies["b", k, 2].wait_recv()
        add(acc.at[k, y, x, rows_b], got_b.at[k, 2])
        if k < 3:
            copy = remote(acc.at[k, y, x], got_z.at[k], z_send.at[k], z_recv.at[k], z_peers[k])
            copy.start()
            copies["z", k, 0] = copy

    for k in range(6):
        if k < 4:
            first(k)
        if 1 <= k < 5:
            second(k - 1)
        if k >= 2:
            third(k - 2)
    total = acc[3, y, x].astype(jnp.float32)
    for k in range(3):
        copies["z", k, 0].wait_recv()
        total += got_z[k].astype(jnp.float32)
    out_ref[...] = total
    for copy in copies.values():
        copy.wait_send()


def scatter_all(part, collective_id):
    _, rows, cols = part.shape
    dma = pltpu.SemaphoreType.DMA
    half = rows // 2
    return pl.pallas_call(
        partial(scatter_kernel, half),
        out_shape=jax.ShapeDtypeStruct((rows, cols), jnp.float32),
        in_specs=[pl.BlockSpec(memory_space=pltpu.VMEM)],
        out_specs=pl.BlockSpec(memory_space=pltpu.VMEM),
        scratch_shapes=[
            pltpu.VMEM((4, 2, 2, rows, cols), part.dtype),
            pltpu.VMEM((4, 3, half, cols), part.dtype),
            pltpu.VMEM((4, 3, half, cols), part.dtype),
            pltpu.VMEM((3, rows, cols), part.dtype),
            dma((16,)), dma((16,)), dma((12,)), dma((12,)), dma((12,)), dma((12,)), dma((3,)), dma((3,)),
        ],
        compiler_params=pltpu.CompilerParams(
            collective_id=collective_id, has_side_effects=True, vmem_limit_bytes=VMEM_BYTES
        ),
    )(part)
BLOCK = 256
NN = (((1,), (0,)), ((), ()))
NT = (((1,), (1,)), ((), ()))


def dot(left, right, dims=NN):
    return lax.dot_general(left, right, dims, preferred_element_type=f32)


def split(value):
    upper = value.astype(bf16)
    return upper, (value - upper.astype(f32)).astype(bf16)


def dot3(left, right, dims=NN):
    return dot(left[0], right[0], dims) + (dot(left[0], right[1], dims) + dot(left[1], right[0], dims))


def iota(shape, dim):
    return lax.broadcasted_iota(jnp.int32, shape, dim)


def doc_table(lengths_ref):
    ends, start = [], 0
    for d in range(DOCS):
        start = start + lengths_ref[d]
        ends.append(start)
    return ends


def slot_bounds(lengths_ref, shape, dim):
    ends = doc_table(lengths_ref)
    slot = iota(shape, dim)
    doc, seg = slot // NLAND, slot % NLAND
    length, end = jnp.zeros(shape, jnp.int32), jnp.zeros(shape, jnp.int32)
    for d in range(DOCS):
        length = jnp.where(doc == d, lengths_ref[d], length)
        end = jnp.where(doc == d, ends[d], end)
    start = end - length
    return start, end, start + seg * length // NLAND, start + (seg + 1) * length // NLAND


def same_doc(lengths_ref, left, right):
    ends = doc_table(lengths_ref)
    a, b = jnp.zeros(left.shape, jnp.int32), jnp.zeros(right.shape, jnp.int32)
    for d in range(DOCS):
        a = a + (left >= ends[d]).astype(jnp.int32)
        b = b + (right >= ends[d]).astype(jnp.int32)
    return a == b


def head_mask(shape, dim, h):
    return (iota(shape, dim) // HD == h).astype(f32)


def tap_index():
    return iota((128, 256), 1) - iota((128, 256), 0) - 64 + REACH


def toeplitz(taps_ref, head, mirrored):
    tap = tap_index()
    mat = jnp.zeros((128, 256), f32)
    for o in range(CONV):
        mat = jnp.where(tap == o, taps_ref[CONV - 1 - o if mirrored else o, head], mat)
    return mat


def clear_edges(ref, total):
    ref[0:64, :] = jnp.zeros((64, ref.shape[1]), ref.dtype)
    ref[total + 64 : total + 128, :] = jnp.zeros((64, ref.shape[1]), ref.dtype)


def forward_kernel(heads, active, lengths_ref, taps_ref, tokens_ref, weights_ref, bias_ref,
                   mixed_ref, q_ref, k_ref, v_ref, fw_ref, bw_ref, land_ref, mix_ref, a_ref, norm_ref, chain_ref,
                   v_wide, score, chain, sems):
    total = tokens_ref.shape[0]
    width = heads * HD
    part = lax.axis_index("seq") % active
    steps = total // BLOCK
    row_start, row_end, row_low, row_top = slot_bounds(lengths_ref, (1, SLOTS), 1)
    _, _, col_low, col_top = slot_bounds(lengths_ref, (SLOTS, 1), 0)
    count = (col_top - col_low).astype(f32)
    bias = jnp.sum(bias_ref[...].astype(f32), axis=0)[0:1]
    clear_edges(v_wide, total)
    land_ref[...] = jnp.zeros(land_ref.shape, f32)

    def project(i, carry):
        at = pl.ds(pl.multiple_of(i * BLOCK, BLOCK), BLOCK)
        qkv = dot(tokens_ref[at, :], weights_ref[...]) + bias
        q, k, v = (qkv[:, j * width : (j + 1) * width] for j in range(3))
        q_low, k_low = q.astype(bf16), k.astype(bf16)
        q_ref[at, :], k_ref[at, :] = q_low, k_low
        v_ref[at, :] = v
        v_wide[pl.ds(pl.multiple_of(i * BLOCK + 64, 64), BLOCK), :] = v.astype(bf16)
        t = i * BLOCK + iota((1, BLOCK), 1)
        member = ((t >= col_low) & (t < col_top)).astype(f32).astype(bf16)
        land_ref[0] += dot(member, q_low)
        land_ref[1] += dot(member, k_low)
        return carry

    lax.fori_loop(0, steps, project, 0)
    ql, kl = land_ref[0] / count, land_ref[1] / count
    land_ref[0], land_ref[1] = ql, kl
    masks = [head_mask((1, width), 1, h) for h in range(heads)]
    ql_low = [(ql * masks[h]).astype(bf16) for h in range(heads)]
    kl_low = [(kl * masks[h]).astype(bf16) for h in range(heads)]

    def scores(i, tops):
        at = pl.ds(pl.multiple_of(i * BLOCK, BLOCK), BLOCK)
        t = i * BLOCK + iota((BLOCK, 1), 0)
        valid = (t >= row_start) & (t < row_end)
        out = []
        for h in range(heads):
            s = jnp.where(valid, SCALE * dot(q_ref[at, :], kl_low[h], NT), masked_score)
            e = jnp.exp(s - jnp.max(s, axis=1, keepdims=True))
            fw_ref[h, at, :] = (e / jnp.sum(e, axis=1, keepdims=True)).astype(bf16)
            s = jnp.where(valid, SCALE * dot(k_ref[at, :], ql_low[h], NT), masked_score)
            score[h, at, :] = s
            out.append(jnp.maximum(tops[h], jnp.max(s, axis=0, keepdims=True)))
        return tuple(out)

    tops = lax.fori_loop(0, steps, scores, tuple(jnp.full((1, SLOTS), masked_score, f32) for _ in range(heads)))

    def gather(i, carry):
        at = pl.ds(pl.multiple_of(i * BLOCK, BLOCK), BLOCK)
        v_t = split(v_ref[at, :].T)
        out = []
        for h in range(heads):
            e = jnp.exp(score[h, at, :] - tops[h])
            score[h, at, :] = e
            out.append((carry[h][0] + jnp.sum(e, axis=0, keepdims=True), carry[h][1] + dot3(v_t, split(e))))
        return tuple(out)

    sums = lax.fori_loop(0, steps, gather, tuple(
        (jnp.zeros((1, SLOTS), f32), jnp.zeros((width, SLOTS), f32)) for _ in range(heads)))
    scale = [1.0 / sums[h][0] for h in range(heads)]
    tall = [head_mask((width, 1), 0, h) for h in range(heads)]
    key_mix_t = [sums[h][1] * scale[h] * tall[h] for h in range(heads)]

    def normalize(i, carry):
        at = pl.ds(pl.multiple_of(i * BLOCK, BLOCK), BLOCK)
        for h in range(heads):
            bw_ref[h, at, :] = (score[h, at, :] * scale[h]).astype(bf16)
        return carry

    lax.fori_loop(0, steps, normalize, 0)

    block = iota((SLOTS, SLOTS), 0) // NLAND == iota((SLOTS, SLOTS), 1) // NLAND
    diagonal = iota((SLOTS, SLOTS), 0) == iota((SLOTS, SLOTS), 1)
    state = []
    for h in range(heads):
        s = jnp.where(block, SCALE * dot3(split(ql * masks[h]), split(kl), NT), masked_score)
        e = jnp.exp(s - jnp.max(s, axis=1, keepdims=True))
        a = e / jnp.sum(e, axis=1, keepdims=True)
        norm = jnp.sum(jnp.sum((a * a).reshape(DOCS, NLAND, SLOTS), axis=1, keepdims=True), axis=2, keepdims=True)
        norm = jnp.broadcast_to(norm, (DOCS, NLAND, SLOTS)).reshape(SLOTS, SLOTS)
        a_ref[h], norm_ref[h] = a, norm
        u = a / norm
        a_split = split(a)
        state.append((split(u), split(dot3(a_split, split(u), NT))))
    copies = []
    for step in range(NS_ITERS):
        fresh = []
        for h in range(heads):
            u, p = state[h]
            p_full = p[0].astype(f32) + p[1].astype(f32)
            q_full = dot3(p, p)
            q = split(q_full)
            f_full = jnp.where(diagonal, 13.0, 0.0) - 15.0 * p_full + 7.0 * q_full - dot3(p, q)
            f = split(f_full)
            for n, pair in enumerate((u, p, q, f)):
                for half in range(2):
                    chain[step % 2, h, n, half] = pair[half]
            p_next = None if step == NS_ITERS - 1 else split(0.25 * dot3(p, f))
            u_next = split(0.25 * dot3(f, u))
            fresh.append((u_next, p_next))
        if step >= 1:
            copies[step - 1].wait()
        copy = pltpu.make_async_copy(chain.at[step % 2], chain_ref.at[step], sems.at[step])
        copy.start()
        copies.append(copy)
        state = fresh
    mix_t = jnp.zeros((width, SLOTS), f32)
    key_t = jnp.zeros((width, SLOTS), f32)
    for h in range(heads):
        u = state[h][0]
        chain[0, h, 0, 0], chain[0, h, 0, 1] = u
        mix_t = mix_t + dot3(split(key_mix_t[h]), u)
        key_t = key_t + key_mix_t[h]
    last = pltpu.make_async_copy(chain.at[0], chain_ref.at[NS_ITERS], sems.at[NS_ITERS])
    last.start()
    mix_ref[0], mix_ref[1] = mix_t, key_t
    mix_low = [(mix_t * tall[h]).astype(bf16) for h in range(heads)]
    mats = [toeplitz(taps_ref, part * heads + h, False) for h in range(heads)]

    def output(i, carry):
        at = pl.ds(pl.multiple_of(i * 128, 128), 128)
        t = i * 128 + iota((128, 1), 0)
        near = same_doc(lengths_ref, t, i * 128 - 64 + iota((1, 256), 1))
        window = v_wide[pl.ds(pl.multiple_of(i * 128, 128), 256), :]
        out = jnp.zeros((128, width), f32)
        for h in range(heads):
            out = out + dot(fw_ref[h, at, :], mix_low[h], NT)
            conv = dot(jnp.where(near, mats[h], 0.0).astype(bf16), window)
            out = out + conv * masks[h]
        mixed_ref[at, :] = out.astype(bf16)
        return carry

    lax.fori_loop(0, total // 128, output, 0)
    copies[-1].wait()
    last.wait()


def attention_forward(heads, active, tokens, weights, bias, lengths, taps):
    total = tokens.shape[0]
    width = heads * HD
    shape = jax.ShapeDtypeStruct
    vmem, smem, anywhere = (pl.BlockSpec(memory_space=m) for m in (pltpu.VMEM, pltpu.SMEM, pl.ANY))
    chain = (heads, 4, 2, SLOTS, SLOTS)
    return pl.pallas_call(
        partial(forward_kernel, heads, active),
        out_shape=(
            shape((total, width), bf16),
            shape((total, width), bf16),
            shape((total, width), bf16),
            shape((total, width), f32),
            shape((heads, total, SLOTS), bf16),
            shape((heads, total, SLOTS), bf16),
            shape((2, SLOTS, width), f32),
            shape((2, width, SLOTS), f32),
            shape((heads, SLOTS, SLOTS), f32),
            shape((heads, SLOTS, SLOTS), f32),
            shape((NS_ITERS + 1, *chain), bf16),
        ),
        in_specs=[smem, smem, vmem, vmem, vmem],
        out_specs=tuple([vmem] * 10 + [anywhere]),
        scratch_shapes=[
            pltpu.VMEM((total + 128, width), bf16),
            pltpu.VMEM((heads, total, SLOTS), f32),
            pltpu.VMEM((2, *chain), bf16),
            pltpu.SemaphoreType.DMA((NS_ITERS + 1,)),
        ],
        compiler_params=pltpu.CompilerParams(vmem_limit_bytes=VMEM_BYTES),
    )(lengths, taps, tokens, weights, bias)


def backward_kernel(heads, active, lengths_ref, taps_ref, tokens_ref, weights_ref, dout_ref, q_ref, k_ref, v_ref, fw_ref,
                    bw_ref, land_ref, mix_ref, a_ref, norm_ref, chain_ref,
                    part_ref, dw_ref, db_ref, dtaps_ref,
                    chain, v_wide, d_wide, dq_acc, dk_acc, dv_acc, spread, tap_rows, sems):
    total = tokens_ref.shape[0]
    width = heads * HD
    part = lax.axis_index("seq") % active
    steps = total // BLOCK
    order = [NS_ITERS] + list(range(NS_ITERS - 1, -1, -1))
    copies = {}
    for n in order:
        copies[n] = pltpu.make_async_copy(chain_ref.at[n], chain.at[n], sems.at[n])
        copies[n].start()
    _, _, row_low, row_top = slot_bounds(lengths_ref, (1, SLOTS), 1)
    inverse = 1.0 / (row_top - row_low).astype(f32)
    clear_edges(v_wide, total)
    clear_edges(d_wide, total)
    masks = [head_mask((1, width), 1, h) for h in range(heads)]
    tall = [head_mask((width, 1), 0, h) for h in range(heads)]
    ql, kl = land_ref[0], land_ref[1]
    mix_t, key_t = mix_ref[0], mix_ref[1]
    kl_low = [(kl * masks[h]).astype(bf16) for h in range(heads)]
    ql_low = [(ql * masks[h]).astype(bf16) for h in range(heads)]
    mix_low = [(mix_t * tall[h]).astype(bf16) for h in range(heads)]

    def front(i, carry):
        at = pl.ds(pl.multiple_of(i * BLOCK, BLOCK), BLOCK)
        inner = pl.ds(pl.multiple_of(i * BLOCK + 64, 64), BLOCK)
        do = dout_ref[at, :]
        d_wide[inner, :] = do
        v_wide[inner, :] = v_ref[at, :].astype(bf16)
        do_t = do.astype(f32).T.astype(bf16)
        q_t = q_ref[at, :].astype(f32).T.astype(bf16)
        dq = jnp.zeros((BLOCK, width), f32)
        out = []
        for h in range(heads):
            fw = fw_ref[h, at, :]
            wide = fw.astype(f32)
            d_fw = dot(do, mix_low[h])
            ds = (SCALE * wide * (d_fw - jnp.sum(wide * d_fw, axis=1, keepdims=True))).astype(bf16)
            dq = dq + dot(ds, kl_low[h])
            out.append((carry[h][0] + dot(do_t, fw), carry[h][1] + dot(q_t, ds)))
        dq_acc[at, :] = dq
        return tuple(out)

    zeros = jnp.zeros((width, SLOTS), f32)
    sums = lax.fori_loop(0, steps, front, tuple((zeros, zeros) for _ in range(heads)))
    dmix_t = [sums[h][0] * tall[h] for h in range(heads)]
    dkl_t = zeros
    for h in range(heads):
        dkl_t = dkl_t + sums[h][1] * tall[h]
    key = key_t.T
    ql_t = ql.T
    block = iota((SLOTS, SLOTS), 0) // NLAND == iota((SLOTS, SLOTS), 1) // NLAND
    copies[NS_ITERS].wait()
    du, dp, dkey_t = [], [None] * heads, []
    for h in range(heads):
        pair = split(dmix_t[h])
        du.append(jnp.where(block, dot3(split(key), pair), 0.0))
        dkey_t.append(dot3(pair, (chain[NS_ITERS, h, 0, 0], chain[NS_ITERS, h, 0, 1]), NT))
    for step in range(NS_ITERS - 1, -1, -1):
        copies[step].wait()
        for h in range(heads):
            u, p, q, f = ((chain[step, h, n, 0], chain[step, h, n, 1]) for n in range(4))
            du_pair = split(du[h])
            df = 0.25 * dot3(du_pair, u, NT)
            du[h] = 0.25 * dot3(f, du_pair)
            if dp[h] is not None:
                dp_pair = split(dp[h])
                df = df + 0.25 * dot3(p, dp_pair)
                base = 0.25 * dot3(dp_pair, f)
            else:
                base = 0.0
            df_pair = split(df)
            dq = split(7.0 * df - dot3(p, df_pair))
            dp[h] = base - 15.0 * df - dot3(df_pair, q) + (dot3(dq, p) + dot3(p, dq))
    dql = jnp.zeros((SLOTS, width), f32)
    for h in range(heads):
        a, norm = a_ref[h], norm_ref[h]
        u0 = chain[0, h, 0, 0].astype(f32) + chain[0, h, 0, 1].astype(f32)
        p0 = chain[0, h, 1, 0].astype(f32) + chain[0, h, 1, 1].astype(f32)
        a_pair = split(a)
        inner = dp[h] * p0 + du[h] * u0
        inner = jnp.sum(jnp.sum(inner.reshape(DOCS, NLAND, SLOTS), axis=1, keepdims=True), axis=2, keepdims=True)
        inner = jnp.broadcast_to(inner, (DOCS, NLAND, SLOTS)).reshape(SLOTS, SLOTS)
        da = (dot3(split(dp[h] + dp[h].T), a_pair) + du[h] - 2.0 * a * inner) / norm
        dsa = split(SCALE * a * (da - jnp.sum(a * da, axis=1, keepdims=True)))
        dql = dql + dot3(dsa, split(kl * masks[h]))
        dkl_t = dkl_t + dot3(split(ql_t * tall[h]), dsa)
    dkey_low = [x.astype(bf16) for x in dkey_t]
    row_dot = [jnp.sum(dkey_t[h] * key_t, axis=0, keepdims=True) for h in range(heads)]
    dkey = [x.T.astype(bf16) for x in dkey_t]

    def back(i, carry):
        at = pl.ds(pl.multiple_of(i * BLOCK, BLOCK), BLOCK)
        v = v_ref[at, :].astype(bf16)
        k_t = k_ref[at, :].astype(f32).T.astype(bf16)
        dk, dv = jnp.zeros((BLOCK, width), f32), jnp.zeros((BLOCK, width), f32)
        out = []
        for h in range(heads):
            bw = bw_ref[h, at, :]
            ds = (SCALE * bw.astype(f32) * (dot(v, dkey_low[h]) - row_dot[h])).astype(bf16)
            dk = dk + dot(ds, ql_low[h])
            dv = dv + dot(bw, dkey[h])
            out.append(carry[h] + dot(k_t, ds))
        dk_acc[at, :] = dk
        dv_acc[at, :] = dv
        return tuple(out)

    sums = lax.fori_loop(0, steps, back, tuple(zeros for _ in range(heads)))
    dql_t = zeros
    for h in range(heads):
        dql_t = dql_t + sums[h] * tall[h]
    dql_low = ((dql.T + dql_t) * inverse).astype(bf16)
    dkl_low = (dkl_t * inverse).astype(bf16)
    mats = [toeplitz(taps_ref, part * heads + h, True) for h in range(heads)]
    spread[...] = jnp.zeros(spread.shape, f32)

    def convolve(i, carry):
        at = pl.ds(pl.multiple_of(i * 128, 128), 128)
        t = i * 128 + iota((128, 1), 0)
        near = same_doc(lengths_ref, t, i * 128 - 64 + iota((1, 256), 1))
        window = pl.ds(pl.multiple_of(i * 128, 128), 256)
        d_window, v_window = d_wide[window, :], v_wide[window, :]
        do = dout_ref[at, :].astype(f32)
        dv = dv_acc[at, :]
        for h in range(heads):
            dv = dv + dot(jnp.where(near, mats[h], 0.0).astype(bf16), d_window) * masks[h]
            spread[h] += jnp.where(near, dot((do * masks[h]).astype(bf16), v_window, NT), 0.0)
        dv_acc[at, :] = dv
        return carry

    lax.fori_loop(0, total // 128, convolve, 0)
    dw_ref[...] = jnp.zeros(dw_ref.shape, f32)

    def finish(i, carry):
        at = pl.ds(pl.multiple_of(i * BLOCK, BLOCK), BLOCK)
        t = i * BLOCK + iota((BLOCK, 1), 0)
        member = ((t >= row_low) & (t < row_top)).astype(f32).astype(bf16)
        dq = dq_acc[at, :] + dot(member, dql_low, NT)
        dk = dk_acc[at, :] + dot(member, dkl_low, NT)
        d_qkv = jnp.concatenate([dq.astype(bf16), dk.astype(bf16), dv_acc[at, :].astype(bf16)], axis=1)
        part_ref[at, :] = dot(d_qkv, weights_ref[...], NT).astype(bf16)
        wide = d_qkv.astype(f32)
        dw_ref[...] += dot(wide.T.astype(bf16), tokens_ref[at, :])
        return carry + jnp.sum(wide, axis=0, keepdims=True)

    db_ref[...] = lax.fori_loop(0, steps, finish, jnp.zeros((1, 3 * width), f32))
    tap = tap_index()
    tap_rows[...] = jnp.zeros(tap_rows.shape, f32)
    for h in range(heads):
        for o in range(CONV):
            tap_rows[h, o : o + 1, :] = jnp.sum(jnp.where(tap == o, spread[h], 0.0), axis=0, keepdims=True)
        dtaps_ref[h] = jnp.broadcast_to(jnp.sum(tap_rows[h], axis=1, keepdims=True), dtaps_ref.shape[1:])


def attention_backward(heads, active, tokens, weights, dout, lengths, taps, state):
    total = tokens.shape[0]
    width = heads * HD
    shape = jax.ShapeDtypeStruct
    vmem, smem, anywhere = (pl.BlockSpec(memory_space=m) for m in (pltpu.VMEM, pltpu.SMEM, pl.ANY))
    return pl.pallas_call(
        partial(backward_kernel, heads, active),
        out_shape=(
            shape((total, D), bf16),
            shape((3 * width, D), f32),
            shape((1, 3 * width), f32),
            shape((heads, 40, 128), f32),
        ),
        in_specs=[smem, smem] + [vmem] * 12 + [anywhere],
        out_specs=tuple([vmem] * 4),
        scratch_shapes=[
            pltpu.VMEM((NS_ITERS + 1, heads, 4, 2, SLOTS, SLOTS), bf16),
            pltpu.VMEM((total + 128, width), bf16),
            pltpu.VMEM((total + 128, width), bf16),
            pltpu.VMEM((total, width), f32),
            pltpu.VMEM((total, width), f32),
            pltpu.VMEM((total, width), f32),
            pltpu.VMEM((heads, 128, 256), f32),
            pltpu.VMEM((heads, 40, 256), f32),
            pltpu.SemaphoreType.DMA((NS_ITERS + 1,)),
        ],
        compiler_params=pltpu.CompilerParams(vmem_limit_bytes=VMEM_BYTES),
    )(lengths, taps, tokens, weights, dout, *state)
def product(form, left, right):
    return jnp.einsum(form, left, right, preferred_element_type=f32)


def layer_norm(inputs, gain, shift):
    average = jnp.mean(inputs, axis=-1, keepdims=True)
    centred = inputs - average
    variance = jnp.mean(centred * centred, axis=-1, keepdims=True)
    return centred * lax.rsqrt(variance + epsilon) * gain + shift


def gelu_exact(inputs):
    return jax.nn.gelu(inputs, approximate=False)


def token_part(tokens, cot, attention, w_out, w_up, w_down, b_out, b_up, b_down, g_attn, s_attn, g_mlp, s_mlp):
    out_proj = product("td,de->te", attention, w_out) + b_out
    hidden, norm_one_back = jax.vjp(layer_norm, tokens.astype(f32) + out_proj, g_attn, s_attn)
    hidden_low = hidden.astype(bf16)
    up_pre = product("td,df->tf", hidden_low, w_up) + b_up
    gelu_val, gelu_back = jax.vjp(gelu_exact, up_pre)
    gelu_low = gelu_val.astype(bf16)
    down_pre = product("tf,fd->td", gelu_low, w_down) + b_down
    output, norm_two_back = jax.vjp(layer_norm, hidden + down_pre, g_mlp, s_mlp)
    d_r2, dg_mlp, ds_mlp = norm_two_back(cot.astype(f32))
    d_down = d_r2.astype(bf16)
    db_down = jnp.sum(d_down.astype(f32), axis=0)
    dw_down = product("tf,td->fd", gelu_low, d_down)
    d_gelu = product("td,fd->tf", d_down, w_down)
    d_up = gelu_back(d_gelu)[0].astype(bf16)
    db_up = jnp.sum(d_up.astype(f32), axis=0)
    dw_up = product("td,tf->df", hidden_low, d_up)
    d_hidden = product("tf,df->td", d_up, w_up) + d_r2
    d_r1, dg_attn, ds_attn = norm_one_back(d_hidden)
    d_out = d_r1.astype(bf16)
    db_out = jnp.sum(d_out.astype(f32), axis=0)
    dw_out = product("td,te->de", attention, d_out)
    d_attn = product("te,de->td", d_out, w_out)
    smalls = (db_out, db_up, db_down, dg_attn, ds_attn, dg_mlp, ds_mlp)
    return output.astype(bf16), d_r1, d_attn, dw_out, dw_up, dw_down, smalls
def local(sizes, *args):
    (tokens, cotangent, doc_lengths, w_query, b_query, w_key, w_value, b_value, w_out, b_out, w_up, b_up,
     w_down, b_down, g_attn, s_attn, g_mlp, s_mlp, conv_kernel) = args
    seq, fsdp = sizes
    devices = seq * fsdp
    fast = sizes == (8, 4)
    axes = ("seq", "fsdp")
    rows = D // devices
    hidden_rows = FF // devices
    own_tokens, own_cot, lengths = tokens[0], cotangent[0], doc_lengths[0]
    count = own_tokens.shape[0]
    total = count * seq
    heads = -(-HEADS // seq)
    width = heads * HD
    active = HEADS // heads
    s = lax.axis_index("seq")

    pack_rows = -(-(rows + 1) // 16) * 16
    own = (s * fsdp + lax.axis_index("fsdp")) * rows
    bias_rows = [
        lax.dynamic_update_slice(jnp.zeros((D,), bf16), bias, (own,)).reshape(active, 1, width)
        for bias in (b_query, b_value)]
    bias_row = jnp.concatenate([bias_rows[0], jnp.zeros((active, 1, width), bf16), bias_rows[1]], axis=2)
    blocks = []
    for b in range(active):
        cols = slice(b * width, (b + 1) * width)
        blocks.append(jnp.concatenate(
            [jnp.concatenate([w_query[:, cols], w_key[:, cols], w_value[:, cols]], axis=1), bias_row[b],
             jnp.zeros((pack_rows - rows - 1, 3 * width), bf16)], axis=0))
    pack = jnp.stack(blocks)
    if fast:
        all_tokens, all_pack = push(sizes, (("seq", None), ("all", active)), (own_tokens, pack), 0)
    else:
        all_tokens = lax.all_gather(own_tokens, "seq")
        all_pack = lax.all_gather(lax.all_to_all(
            jnp.take(pack, jnp.arange(seq) % active, axis=0), "seq", 0, 0), "fsdp", axis=1).reshape(
                devices, pack_rows, 3 * width)
    all_tokens = all_tokens.reshape(total, D)
    qkv_weights = all_pack[:, :rows].reshape(D, 3 * width)
    bias = all_pack[:, rows:]
    bias = jnp.pad(bias, ((0, 0), (0, -bias.shape[1] % 8), (0, 0)))

    small = jnp.concatenate([b_out, b_down, g_attn, s_attn, g_mlp, s_mlp, b_up])
    shard_rows = rows + 4 * rows + hidden_rows
    small_rows = -(-(shard_rows + 1) // 16) * 16 - shard_rows
    small = jnp.pad(small, (0, small_rows * D - small.shape[0])).reshape(small_rows, D)
    shard = jnp.concatenate(
        [w_out] + [w_up[:, D * j : D * (j + 1)] for j in range(4)] + [w_down, small], axis=0)
    if fast:
        gathered = gather_all(shard, 1)
    else:
        gathered = lax.all_gather(shard, axes)
    full_out = gathered[:, :rows].reshape(D, D)
    full_up = jnp.concatenate(
        [gathered[:, rows * (1 + j) : rows * (2 + j)].reshape(D, D) for j in range(4)], axis=1)
    full_down = gathered[:, 5 * rows : shard_rows].reshape(FF, D)
    small = gathered[:, shard_rows].astype(f32)
    vectors = [small[:, rows * j : rows * (j + 1)].reshape(D) for j in range(6)]
    f_b_out, f_b_down, f_g_attn, f_s_attn, f_g_mlp, f_s_mlp = vectors
    f_b_up = small[:, 6 * rows : 6 * rows + hidden_rows].reshape(FF)

    taps = conv_kernel.astype(f32)
    mixed, *state = attention_forward(heads, active, all_tokens, qkv_weights, bias, lengths, taps)
    mixed = mixed.reshape(seq, count, width)
    if fast:
        (attention,) = push(sizes, (("seq", 0),), (mixed,), 2)
    else:
        attention = lax.all_to_all(mixed, "seq", 0, 0)
    attention = jnp.transpose(attention[:active], (1, 0, 2)).reshape(count, D)

    output, d_r1, d_attn, dw_out, dw_up, dw_down, smalls = token_part(
        own_tokens, own_cot, attention, full_out, full_up, full_down, f_b_out, f_b_up, f_b_down,
        f_g_attn, f_s_attn, f_g_mlp, f_s_mlp)

    d_attn = jnp.transpose(d_attn.astype(bf16).reshape(count, active, width), (1, 0, 2))
    if fast:
        (d_mixed,) = push(sizes, (("seq", active),), (d_attn,), 3)
    else:
        d_mixed = lax.all_to_all(jnp.take(d_attn, jnp.arange(seq) % active, axis=0), "seq", 0, 0)

    db_out, db_up, db_down, dg_attn, ds_attn, dg_mlp, ds_mlp = smalls
    grad_small = jnp.concatenate(
        [entry.reshape(devices, -1) for entry in (db_out, db_down, dg_attn, ds_attn, dg_mlp, ds_mlp, db_up)], axis=1)
    grad_small = jnp.pad(grad_small, ((0, 0), (0, small_rows * D - grad_small.shape[1])))
    parts = jnp.concatenate(
        [dw_out.reshape(devices, rows, D)]
        + [dw_up[:, D * j : D * (j + 1)].reshape(devices, rows, D) for j in range(4)]
        + [dw_down.reshape(devices, hidden_rows, D), grad_small.reshape(devices, small_rows, D)],
        axis=1).astype(bf16)
    if fast:
        summed = scatter_all(parts, 4)
    else:
        summed = lax.psum_scatter(parts.astype(f32), axes, scatter_dimension=0, tiled=False)

    d_part, dw, db, d_taps = attention_backward(
        heads, active, all_tokens, qkv_weights, d_mixed.reshape(total, width), lengths, taps, state)
    d_taps = jnp.pad(d_taps[:, :CONV, 0], ((0, pack_rows - rows - 1 - heads), (0, 3 * width - CONV)))
    extra = jnp.concatenate([db, d_taps], axis=0)
    send = jnp.concatenate(
        [dw.T.reshape(devices, rows, 3 * width), jnp.broadcast_to(extra[None], (devices, *extra.shape))],
        axis=1).astype(bf16)
    d_part = d_part.reshape(seq, count, D)
    if fast:
        token_parts, grad_parts = push(sizes, (("seq", 0), ("all", 0)), (d_part, send), 5)
    else:
        token_parts = lax.all_to_all(d_part, "seq", 0, 0)
        grad_parts = lax.all_to_all(send, axes, 0, 0)
    d_tokens = (d_r1 + jnp.sum(token_parts[:active].astype(f32), axis=0)).astype(bf16)
    sums = jnp.sum(grad_parts.reshape(seq, fsdp, pack_rows, 3, width)[:active].astype(f32), axis=1)
    dw_query, dw_key, dw_value = (
        jnp.transpose(sums[:, :rows, j], (1, 0, 2)).reshape(rows, D) for j in range(3))
    db_query = lax.dynamic_slice_in_dim(sums[:, rows, 0].reshape(D), own, rows)
    db_value = lax.dynamic_slice_in_dim(sums[:, rows, 2].reshape(D), own, rows)
    d_kernel = jnp.transpose(
        sums[:, rows + 1 : rows + 1 + heads].reshape(active * heads, 3 * width)[:, :CONV], (1, 0))

    last = summed[shard_rows:].reshape(-1)
    g = [last[rows * j : rows * (j + 1)] for j in range(6)]
    s_wup = jnp.concatenate([summed[rows * (1 + j) : rows * (2 + j)] for j in range(4)], axis=1)
    return (
        output[None], d_tokens[None], dw_query, db_query, dw_key, dw_value, db_value, summed[:rows], g[0],
        s_wup, last[6 * rows : 6 * rows + hidden_rows], summed[5 * rows : shard_rows], g[1],
        g[2], g[3], g[4], g[5], d_kernel)


def solution(mesh):
    sizes = (mesh.shape["seq"], mesh.shape["fsdp"])
    both = ("seq", "fsdp")
    wide, flat, stream = P(both, None), P(both), P("fsdp", "seq", None)
    in_specs = (stream, stream, P("fsdp", None), wide, flat, wide, wide, flat, wide, flat, wide, flat, wide, flat,
                flat, flat, flat, flat, P())
    out_specs = (stream, stream, wide, flat, wide, wide, flat, wide, flat, wide, flat, wide, flat, flat, flat, flat,
                 flat, P())
    return jax.shard_map(partial(local, sizes), mesh=mesh, in_specs=in_specs, out_specs=out_specs, check_vma=False)
```

```python
from functools import partial
import math

import jax
import jax.numpy as jnp
from jax import lax
from jax.experimental import pallas as pl
from jax.experimental.pallas import tpu as pltpu
from jax.sharding import PartitionSpec as P

D = 768
HEADS = 12
HD = 64
FF = 3072
NLAND = 64
NS_ITERS = 6
CONV = 33
REACH = CONV // 2
DOCS = 4
SLOTS = 256
SCALE = 1.0 / math.sqrt(HD)

HIGHEST = lax.Precision.HIGHEST
epsilon = 1e-05
masked_score = -1e30
f32 = jnp.float32
bf16 = jnp.bfloat16
MESH = pl.DeviceIdType.MESH
VMEM_BYTES = 56 * 1024 * 1024


def greet(peers):
    barrier = pltpu.get_barrier_semaphore()
    for peer in peers:
        pl.semaphore_signal(barrier, inc=1, device_id=peer, device_id_type=MESH)
    pl.semaphore_wait(barrier, len(peers))


def remote(src, dst, send_sem, recv_sem, peer):
    return pltpu.make_async_remote_copy(
        src_ref=src, dst_ref=dst, send_sem=send_sem, recv_sem=recv_sem,
        device_id=peer, device_id_type=MESH,
    )


BLOCK = 256
NN = (((1,), (0,)), ((), ()))
NT = (((1,), (1,)), ((), ()))


def dot(left, right, dims=NN):
    return lax.dot_general(left, right, dims, preferred_element_type=f32)


def split(value):
    upper = value.astype(bf16)
    return upper, (value - upper.astype(f32)).astype(bf16)


def dot3(left, right, dims=NN):
    return dot(left[0], right[0], dims) + (dot(left[0], right[1], dims) + dot(left[1], right[0], dims))


def iota(shape, dim):
    return lax.broadcasted_iota(jnp.int32, shape, dim)


def doc_table(lengths_ref):
    ends, start = [], 0
    for d in range(DOCS):
        start = start + lengths_ref[d]
        ends.append(start)
    return ends


def slot_bounds(lengths_ref, shape, dim):
    ends = doc_table(lengths_ref)
    slot = iota(shape, dim)
    doc, seg = slot // NLAND, slot % NLAND
    length, end = jnp.zeros(shape, jnp.int32), jnp.zeros(shape, jnp.int32)
    for d in range(DOCS):
        length = jnp.where(doc == d, lengths_ref[d], length)
        end = jnp.where(doc == d, ends[d], end)
    start = end - length
    return start, end, start + seg * length // NLAND, start + (seg + 1) * length // NLAND


def same_doc(lengths_ref, left, right):
    ends = doc_table(lengths_ref)
    a, b = jnp.zeros(left.shape, jnp.int32), jnp.zeros(right.shape, jnp.int32)
    for d in range(DOCS):
        a = a + (left >= ends[d]).astype(jnp.int32)
        b = b + (right >= ends[d]).astype(jnp.int32)
    return a == b


def head_mask(shape, dim, h):
    return (iota(shape, dim) // HD == h).astype(f32)


def tap_index():
    return iota((128, 256), 1) - iota((128, 256), 0) - 64 + REACH


def toeplitz(taps_ref, head, mirrored):
    tap = tap_index()
    mat = jnp.zeros((128, 256), f32)
    for o in range(CONV):
        mat = jnp.where(tap == o, taps_ref[CONV - 1 - o if mirrored else o, head], mat)
    return mat


def clear_edges(ref, total):
    ref[0:64, :] = jnp.zeros((64, ref.shape[1]), ref.dtype)
    ref[total + 64 : total + 128, :] = jnp.zeros((64, ref.shape[1]), ref.dtype)


def forward_math(heads, active, lengths_ref, taps_ref, tokens_ref, weights_ref, bias,
                 mixed_ref, q_ref, k_ref, v_ref, fw_ref, bw_ref, land_ref, mix_ref, a_ref, norm_ref, chain_ref,
                 v_wide, score, stage):
    total = tokens_ref.shape[0]
    width = heads * HD
    part = lax.axis_index("seq") % active
    steps = total // BLOCK
    row_start, row_end, row_low, row_top = slot_bounds(lengths_ref, (1, SLOTS), 1)
    _, _, col_low, col_top = slot_bounds(lengths_ref, (SLOTS, 1), 0)
    count = (col_top - col_low).astype(f32)
    clear_edges(v_wide, total)
    land_ref[...] = jnp.zeros(land_ref.shape, f32)

    def project(i, carry):
        at = pl.ds(pl.multiple_of(i * BLOCK, BLOCK), BLOCK)
        qkv = dot(tokens_ref[at, :], weights_ref[...]) + bias
        q, k, v = (qkv[:, j * width : (j + 1) * width] for j in range(3))
        q_low, k_low = q.astype(bf16), k.astype(bf16)
        q_ref[at, :], k_ref[at, :] = q_low, k_low
        v_ref[at, :] = v
        v_wide[pl.ds(pl.multiple_of(i * BLOCK + 64, 64), BLOCK), :] = v.astype(bf16)
        t = i * BLOCK + iota((1, BLOCK), 1)
        member = ((t >= col_low) & (t < col_top)).astype(f32).astype(bf16)
        land_ref[0] += dot(member, q_low)
        land_ref[1] += dot(member, k_low)
        return carry

    lax.fori_loop(0, steps, project, 0)
    stage(1)
    ql, kl = land_ref[0] / count, land_ref[1] / count
    land_ref[0], land_ref[1] = ql, kl
    masks = [head_mask((1, width), 1, h) for h in range(heads)]
    ql_low = [(ql * masks[h]).astype(bf16) for h in range(heads)]
    kl_low = [(kl * masks[h]).astype(bf16) for h in range(heads)]

    def scores(i, tops):
        at = pl.ds(pl.multiple_of(i * BLOCK, BLOCK), BLOCK)
        t = i * BLOCK + iota((BLOCK, 1), 0)
        valid = (t >= row_start) & (t < row_end)
        out = []
        for h in range(heads):
            s = jnp.where(valid, SCALE * dot(q_ref[at, :], kl_low[h], NT), masked_score)
            e = jnp.exp(s - jnp.max(s, axis=1, keepdims=True))
            fw_ref[h, at, :] = (e / jnp.sum(e, axis=1, keepdims=True)).astype(bf16)
            s = jnp.where(valid, SCALE * dot(k_ref[at, :], ql_low[h], NT), masked_score)
            score[h, at, :] = s
            out.append(jnp.maximum(tops[h], jnp.max(s, axis=0, keepdims=True)))
        return tuple(out)

    tops = lax.fori_loop(0, steps, scores, tuple(jnp.full((1, SLOTS), masked_score, f32) for _ in range(heads)))
    stage(2)

    def gather(i, carry):
        at = pl.ds(pl.multiple_of(i * BLOCK, BLOCK), BLOCK)
        v_t = split(v_ref[at, :].T)
        out = []
        for h in range(heads):
            e = jnp.exp(score[h, at, :] - tops[h])
            score[h, at, :] = e
            out.append((carry[h][0] + jnp.sum(e, axis=0, keepdims=True), carry[h][1] + dot3(v_t, split(e))))
        return tuple(out)

    sums = lax.fori_loop(0, steps, gather, tuple(
        (jnp.zeros((1, SLOTS), f32), jnp.zeros((width, SLOTS), f32)) for _ in range(heads)))
    scale = [1.0 / sums[h][0] for h in range(heads)]
    tall = [head_mask((width, 1), 0, h) for h in range(heads)]
    key_mix_t = [sums[h][1] * scale[h] * tall[h] for h in range(heads)]

    def normalize(i, carry):
        at = pl.ds(pl.multiple_of(i * BLOCK, BLOCK), BLOCK)
        for h in range(heads):
            bw_ref[h, at, :] = (score[h, at, :] * scale[h]).astype(bf16)
        return carry

    lax.fori_loop(0, steps, normalize, 0)
    stage(3)

    block = iota((SLOTS, SLOTS), 0) // NLAND == iota((SLOTS, SLOTS), 1) // NLAND
    diagonal = iota((SLOTS, SLOTS), 0) == iota((SLOTS, SLOTS), 1)
    state = []
    for h in range(heads):
        s = jnp.where(block, SCALE * dot3(split(ql * masks[h]), split(kl), NT), masked_score)
        e = jnp.exp(s - jnp.max(s, axis=1, keepdims=True))
        a = e / jnp.sum(e, axis=1, keepdims=True)
        norm = jnp.sum(jnp.sum((a * a).reshape(DOCS, NLAND, SLOTS), axis=1, keepdims=True), axis=2, keepdims=True)
        norm = jnp.broadcast_to(norm, (DOCS, NLAND, SLOTS)).reshape(SLOTS, SLOTS)
        a_ref[h], norm_ref[h] = a, norm
        u = a / norm
        a_split = split(a)
        state.append((split(u), split(dot3(a_split, split(u), NT))))
    for step in range(NS_ITERS):
        fresh = []
        for h in range(heads):
            u, p = state[h]
            p_full = p[0].astype(f32) + p[1].astype(f32)
            q_full = dot3(p, p)
            q = split(q_full)
            f_full = jnp.where(diagonal, 13.0, 0.0) - 15.0 * p_full + 7.0 * q_full - dot3(p, q)
            f = split(f_full)
            for n, pair in enumerate((u, p, q, f)):
                for half in range(2):
                    chain_ref[step, h, n, half] = pair[half]
            p_next = None if step == NS_ITERS - 1 else split(0.25 * dot3(p, f))
            u_next = split(0.25 * dot3(f, u))
            fresh.append((u_next, p_next))
        if step == 2:
            stage(4)
        state = fresh
    mix_t = jnp.zeros((width, SLOTS), f32)
    key_t = jnp.zeros((width, SLOTS), f32)
    for h in range(heads):
        u = state[h][0]
        chain_ref[NS_ITERS, h, 0, 0], chain_ref[NS_ITERS, h, 0, 1] = u
        mix_t = mix_t + dot3(split(key_mix_t[h]), u)
        key_t = key_t + key_mix_t[h]
    mix_ref[0], mix_ref[1] = mix_t, key_t
    stage(5)
    mix_low = [(mix_t * tall[h]).astype(bf16) for h in range(heads)]
    mats = [toeplitz(taps_ref, part * heads + h, False) for h in range(heads)]

    def output(i, carry):
        at = pl.ds(pl.multiple_of(i * 128, 128), 128)
        t = i * 128 + iota((128, 1), 0)
        near = same_doc(lengths_ref, t, i * 128 - 64 + iota((1, 256), 1))
        window = v_wide[pl.ds(pl.multiple_of(i * 128, 128), 256), :]
        out = jnp.zeros((128, width), f32)
        for h in range(heads):
            out = out + dot(fw_ref[h, at, :], mix_low[h], NT)
            conv = dot(jnp.where(near, mats[h], 0.0).astype(bf16), window)
            out = out + conv * masks[h]
        mixed_ref[at, :] = out.astype(bf16)
        return carry

    lax.fori_loop(0, total // 128, output, 0)


def forward_kernel(heads, active, lengths_ref, taps_ref, tokens_ref, weights_ref, bias_ref, *refs):
    bias = jnp.sum(bias_ref[...].astype(f32), axis=0)[0:1]
    forward_math(heads, active, lengths_ref, taps_ref, tokens_ref, weights_ref, bias, *refs, lambda n: None)


def attention_forward(heads, active, tokens, weights, bias, lengths, taps):
    total = tokens.shape[0]
    width = heads * HD
    shape = jax.ShapeDtypeStruct
    vmem, smem = (pl.BlockSpec(memory_space=m) for m in (pltpu.VMEM, pltpu.SMEM))
    chain = (heads, 4, 2, SLOTS, SLOTS)
    return pl.pallas_call(
        partial(forward_kernel, heads, active),
        out_shape=(
            shape((total, width), bf16),
            shape((total, width), bf16),
            shape((total, width), bf16),
            shape((total, width), f32),
            shape((heads, total, SLOTS), bf16),
            shape((heads, total, SLOTS), bf16),
            shape((2, SLOTS, width), f32),
            shape((2, width, SLOTS), f32),
            shape((heads, SLOTS, SLOTS), f32),
            shape((heads, SLOTS, SLOTS), f32),
            shape((NS_ITERS + 1, *chain), bf16),
        ),
        in_specs=[smem, smem, vmem, vmem, vmem],
        out_specs=tuple([vmem] * 11),
        scratch_shapes=[
            pltpu.VMEM((total + 128, width), bf16),
            pltpu.VMEM((heads, total, SLOTS), f32),
        ],
        compiler_params=pltpu.CompilerParams(vmem_limit_bytes=VMEM_BYTES),
    )(lengths, taps, tokens, weights, bias)


def backward_math(heads, active, lengths_ref, taps_ref, tokens_ref, weights_ref, dout_ref, q_ref, k_ref, v_ref, fw_ref,
                  bw_ref, land_ref, mix_ref, a_ref, norm_ref, chain_ref, part_ref, dw_ref, extra_ref,
                  v_wide, d_wide, dq_acc, dk_acc, dv_acc, spread, tap_rows, dqkv, stage, counts, parts_ready):
    total = tokens_ref.shape[0]
    width = heads * HD
    part = lax.axis_index("seq") % active
    steps = total // BLOCK
    _, _, row_low, row_top = slot_bounds(lengths_ref, (1, SLOTS), 1)
    inverse = 1.0 / (row_top - row_low).astype(f32)
    clear_edges(v_wide, total)
    clear_edges(d_wide, total)
    masks = [head_mask((1, width), 1, h) for h in range(heads)]
    tall = [head_mask((width, 1), 0, h) for h in range(heads)]
    ql, kl = land_ref[0], land_ref[1]
    mix_t, key_t = mix_ref[0], mix_ref[1]
    kl_low = [(kl * masks[h]).astype(bf16) for h in range(heads)]
    ql_low = [(ql * masks[h]).astype(bf16) for h in range(heads)]
    mix_low = [(mix_t * tall[h]).astype(bf16) for h in range(heads)]

    def front(i, carry):
        at = pl.ds(pl.multiple_of(i * BLOCK, BLOCK), BLOCK)
        inner = pl.ds(pl.multiple_of(i * BLOCK + 64, 64), BLOCK)
        do = dout_ref[at, :]
        d_wide[inner, :] = do
        v_wide[inner, :] = v_ref[at, :].astype(bf16)
        do_t = do.astype(f32).T.astype(bf16)
        q_t = q_ref[at, :].astype(f32).T.astype(bf16)
        dq = jnp.zeros((BLOCK, width), f32)
        out = []
        for h in range(heads):
            fw = fw_ref[h, at, :]
            wide = fw.astype(f32)
            d_fw = dot(do, mix_low[h])
            ds = (SCALE * wide * (d_fw - jnp.sum(wide * d_fw, axis=1, keepdims=True))).astype(bf16)
            dq = dq + dot(ds, kl_low[h])
            out.append((carry[h][0] + dot(do_t, fw), carry[h][1] + dot(q_t, ds)))
        dq_acc[at, :] = dq
        return tuple(out)

    zeros = jnp.zeros((width, SLOTS), f32)
    sums = lax.fori_loop(0, steps, front, tuple((zeros, zeros) for _ in range(heads)))
    stage(1)
    dmix_t = [sums[h][0] * tall[h] for h in range(heads)]
    dkl_t = zeros
    for h in range(heads):
        dkl_t = dkl_t + sums[h][1] * tall[h]
    key = key_t.T
    ql_t = ql.T
    block = iota((SLOTS, SLOTS), 0) // NLAND == iota((SLOTS, SLOTS), 1) // NLAND
    du, dp, dkey_t = [], [None] * heads, []
    for h in range(heads):
        pair = split(dmix_t[h])
        du.append(jnp.where(block, dot3(split(key), pair), 0.0))
        dkey_t.append(dot3(pair, (chain_ref[NS_ITERS, h, 0, 0], chain_ref[NS_ITERS, h, 0, 1]), NT))
    for step in range(NS_ITERS - 1, -1, -1):
        if step == 3:
            stage(2)
        if step == 1:
            stage(3)
        for h in range(heads):
            u, p, q, f = ((chain_ref[step, h, n, 0], chain_ref[step, h, n, 1]) for n in range(4))
            du_pair = split(du[h])
            df = 0.25 * dot3(du_pair, u, NT)
            du[h] = 0.25 * dot3(f, du_pair)
            if dp[h] is not None:
                dp_pair = split(dp[h])
                df = df + 0.25 * dot3(p, dp_pair)
                base = 0.25 * dot3(dp_pair, f)
            else:
                base = 0.0
            df_pair = split(df)
            dq = split(7.0 * df - dot3(p, df_pair))
            dp[h] = base - 15.0 * df - dot3(df_pair, q) + (dot3(dq, p) + dot3(p, dq))
    dql = jnp.zeros((SLOTS, width), f32)
    for h in range(heads):
        a, norm = a_ref[h], norm_ref[h]
        u0 = chain_ref[0, h, 0, 0].astype(f32) + chain_ref[0, h, 0, 1].astype(f32)
        p0 = chain_ref[0, h, 1, 0].astype(f32) + chain_ref[0, h, 1, 1].astype(f32)
        a_pair = split(a)
        inner = dp[h] * p0 + du[h] * u0
        inner = jnp.sum(jnp.sum(inner.reshape(DOCS, NLAND, SLOTS), axis=1, keepdims=True), axis=2, keepdims=True)
        inner = jnp.broadcast_to(inner, (DOCS, NLAND, SLOTS)).reshape(SLOTS, SLOTS)
        da = (dot3(split(dp[h] + dp[h].T), a_pair) + du[h] - 2.0 * a * inner) / norm
        dsa = split(SCALE * a * (da - jnp.sum(a * da, axis=1, keepdims=True)))
        dql = dql + dot3(dsa, split(kl * masks[h]))
        dkl_t = dkl_t + dot3(split(ql_t * tall[h]), dsa)
    stage(4)
    dkey_low = [x.astype(bf16) for x in dkey_t]
    row_dot = [jnp.sum(dkey_t[h] * key_t, axis=0, keepdims=True) for h in range(heads)]
    dkey = [x.T.astype(bf16) for x in dkey_t]

    def back(i, carry):
        at = pl.ds(pl.multiple_of(i * BLOCK, BLOCK), BLOCK)
        v = v_ref[at, :].astype(bf16)
        k_t = k_ref[at, :].astype(f32).T.astype(bf16)
        dk, dv = jnp.zeros((BLOCK, width), f32), jnp.zeros((BLOCK, width), f32)
        out = []
        for h in range(heads):
            bw = bw_ref[h, at, :]
            ds = (SCALE * bw.astype(f32) * (dot(v, dkey_low[h]) - row_dot[h])).astype(bf16)
            dk = dk + dot(ds, ql_low[h])
            dv = dv + dot(bw, dkey[h])
            out.append(carry[h] + dot(k_t, ds))
        dk_acc[at, :] = dk
        dv_acc[at, :] = dv
        return tuple(out)

    sums = lax.fori_loop(0, steps, back, tuple(zeros for _ in range(heads)))
    stage(5)
    dql_t = zeros
    for h in range(heads):
        dql_t = dql_t + sums[h] * tall[h]
    dql_low = ((dql.T + dql_t) * inverse).astype(bf16)
    dkl_low = (dkl_t * inverse).astype(bf16)
    mats = [toeplitz(taps_ref, part * heads + h, True) for h in range(heads)]
    spread[...] = jnp.zeros(spread.shape, f32)

    def convolve(i, carry):
        at = pl.ds(pl.multiple_of(i * 128, 128), 128)
        t = i * 128 + iota((128, 1), 0)
        near = same_doc(lengths_ref, t, i * 128 - 64 + iota((1, 256), 1))
        window = pl.ds(pl.multiple_of(i * 128, 128), 256)
        d_window, v_window = d_wide[window, :], v_wide[window, :]
        do = dout_ref[at, :].astype(f32)
        dv = dv_acc[at, :]
        for h in range(heads):
            dv = dv + dot(jnp.where(near, mats[h], 0.0).astype(bf16), d_window) * masks[h]
            spread[h] += jnp.where(near, dot((do * masks[h]).astype(bf16), v_window, NT), 0.0)
        dv_acc[at, :] = dv
        return carry

    lax.fori_loop(0, total // 128, convolve, 0)

    def finish(i, carry):
        at = pl.ds(pl.multiple_of(i * BLOCK, BLOCK), BLOCK)
        t = i * BLOCK + iota((BLOCK, 1), 0)
        member = ((t >= row_low) & (t < row_top)).astype(f32).astype(bf16)
        dq = dq_acc[at, :] + dot(member, dql_low, NT)
        dk = dk_acc[at, :] + dot(member, dkl_low, NT)
        grads = jnp.concatenate([dq.astype(bf16), dk.astype(bf16), dv_acc[at, :].astype(bf16)], axis=1)
        dqkv[at, :] = grads
        part_ref[at, :] = jnp.where(counts, dot(grads, weights_ref[...], NT), 0.0).astype(bf16)
        return carry + jnp.sum(grads.astype(f32), axis=0, keepdims=True)

    extra_ref[...] = jnp.zeros(extra_ref.shape, f32)
    extra_ref[0:1, :] = lax.fori_loop(0, steps, finish, jnp.zeros((1, 3 * width), f32))
    parts_ready()
    dw_ref[...] = jnp.zeros(dw_ref.shape, f32)

    def weigh(i, carry):
        at = pl.ds(pl.multiple_of(i * BLOCK, BLOCK), BLOCK)
        for n in range(3):
            grads = dqkv[at, n * width : (n + 1) * width].astype(f32).T.astype(bf16)
            dw_ref[:, n * D : (n + 1) * D] += dot(grads, tokens_ref[at, :])
        return carry

    lax.fori_loop(0, steps, weigh, 0)
    tap = tap_index()
    tap_rows[...] = jnp.zeros(tap_rows.shape, f32)
    for h in range(heads):
        for o in range(CONV):
            tap_rows[o : o + 1, :] = jnp.sum(jnp.where(tap == o, spread[h], 0.0), axis=0, keepdims=True)
        extra_ref[1 + h : 2 + h, 0:128] = jnp.sum(tap_rows[...].T, axis=0, keepdims=True)


def backward_kernel(heads, active, lengths_ref, taps_ref, tokens_ref, weights_ref, *refs):
    backward_math(
        heads, active, lengths_ref, taps_ref, tokens_ref, weights_ref, *refs, lambda n: None,
        lax.axis_index("seq") < active, lambda: None)


def attention_backward(heads, active, tokens, weights, dout, lengths, taps, state):
    total = tokens.shape[0]
    width = heads * HD
    shape = jax.ShapeDtypeStruct
    vmem, smem = (pl.BlockSpec(memory_space=m) for m in (pltpu.VMEM, pltpu.SMEM))
    return pl.pallas_call(
        partial(backward_kernel, heads, active),
        out_shape=(
            shape((total, D), bf16),
            shape((width, 3 * D), f32),
            shape((8, 3 * width), f32),
        ),
        in_specs=[smem, smem] + [vmem] * 13,
        out_specs=tuple([vmem] * 3),
        scratch_shapes=[
            pltpu.VMEM((total + 128, width), bf16),
            pltpu.VMEM((total + 128, width), bf16),
            pltpu.VMEM((total, width), f32),
            pltpu.VMEM((total, width), f32),
            pltpu.VMEM((total, width), f32),
            pltpu.VMEM((heads, 128, 256), f32),
            pltpu.VMEM((128, 256), f32),
            pltpu.VMEM((total, 3 * width), bf16),
        ],
        compiler_params=pltpu.CompilerParams(vmem_limit_bytes=VMEM_BYTES),
    )(lengths, taps, tokens, weights, dout, *state)
def rows_at(index, count):
    return pl.ds(pl.multiple_of(index * count, 8), count)


class Links:
    def __init__(self):
        s, f = lax.axis_index("seq"), lax.axis_index("fsdp")
        self.s, self.f = s, f
        self.z, self.y, self.x, self.c = s // 2, s % 2, f // 2, f % 2
        self.oy, self.ox, self.oc = 1 - self.y, 1 - self.x, 1 - self.c
        self.seq_peers = [((s + j) % 8, f) for j in range(1, 8)]
        self.fsdp_peers = [(s, (f + i) % 4) for i in range(1, 4)]
        self.z_peers = [((self.z + j) % 4 * 2 + self.y, f) for j in range(1, 4)]
        self.above, self.below = self.z_peers[0], self.z_peers[2]
        self.y_peer = (self.z * 2 + self.oy, f)
        self.x_peer = (s, self.ox * 2 + self.c)
        self.c_peer = (s, self.x * 2 + self.oc)
        self.started = []

    def send(self, src, dst, sems, index, peer):
        copy = remote(src, dst, sems[0].at[index], sems[1].at[index], peer)
        copy.start()
        self.started.append(copy)
        return copy

    def drain(self):
        for copy in self.started:
            copy.wait_send()
        self.started = []


def begin(copies):
    for copy in copies:
        copy.start()


def done(copies):
    for copy in copies:
        copy.wait_recv()


def centre(value):
    value = value - jnp.mean(value, axis=1, keepdims=True)
    scale = lax.rsqrt(jnp.mean(value * value, axis=1, keepdims=True) + epsilon)
    return value * scale, scale


def uncentre(grad, normal, scale):
    return scale * (grad - jnp.mean(grad, axis=1, keepdims=True)
                    - normal * jnp.mean(grad * normal, axis=1, keepdims=True))


def column_sum(value):
    return jnp.sum(value, axis=0, keepdims=True)


def token_math(own, cot, attention, up_ref, down_ref, out_ref, vec_ref, gelu_ref, slope_ref, output_ref, dr1_ref, small_ref,
               weights_done):
    vec = vec_ref[...]
    b_out, b_down, g_attn, s_attn, g_mlp, s_mlp = (vec[j : j + 1] for j in range(6))
    normal_one, scale_one = centre(own.astype(f32) + dot(attention, out_ref[...]) + b_out)
    hidden = normal_one * g_attn + s_attn
    hidden_low = hidden.astype(bf16)
    count = hidden.shape[0]

    def upward(i, down):
        cols = pl.ds(pl.multiple_of(i * D, D), D)
        up = dot(hidden_low, up_ref[:, cols]) + vec_ref[pl.ds(6 + i, 1), :]
        share = 0.5 + 0.5 * lax.erf(up * math.sqrt(0.5))
        gelu = (up * share).astype(bf16)
        gelu_ref[:, cols] = gelu
        slope_ref[:, cols] = share + up * (math.sqrt(0.5 / math.pi) * jnp.exp(-0.5 * up * up))
        return down + dot(gelu, down_ref[cols, :])

    down = lax.fori_loop(0, FF // D, upward, jnp.zeros((count, D), f32))
    normal_two, scale_two = centre(hidden + down + b_down)
    output_ref[...] = (normal_two * g_mlp + s_mlp).astype(bf16)
    cot = cot.astype(f32)
    d_r2 = uncentre(cot * g_mlp, normal_two, scale_two)
    d_down = d_r2.astype(bf16)
    small_ref[...] = jnp.zeros(small_ref.shape, f32)
    small_ref[1:2, :] = column_sum(d_down.astype(f32))
    small_ref[4:5, :] = column_sum(cot * normal_two)
    small_ref[5:6, :] = column_sum(cot)
    hidden_t = hidden_low.astype(f32).T.astype(bf16)

    def downward(i, d_hidden):
        cols = pl.ds(pl.multiple_of(i * D, D), D)
        d_gelu = dot(d_down, down_ref[cols, :], NT)
        d_up = (d_gelu * slope_ref[:, cols]).astype(bf16)
        small_ref[pl.ds(6 + i, 1), :] = column_sum(d_up.astype(f32))
        d_hidden = d_hidden + dot(d_up, up_ref[:, cols], NT)
        gelu_t = gelu_ref[:, cols].astype(f32).T.astype(bf16)
        down_ref[cols, :] = dot(gelu_t, d_down).astype(bf16)
        up_ref[:, cols] = dot(hidden_t, d_up).astype(bf16)
        return d_hidden

    d_hidden = lax.fori_loop(0, FF // D, downward, d_r2)
    weights_done()
    d_r1 = uncentre(d_hidden * g_attn, normal_one, scale_one)
    dr1_ref[...] = d_r1
    d_out = d_r1.astype(bf16)
    small_ref[0:1, :] = column_sum(d_out.astype(f32))
    small_ref[2:3, :] = column_sum(d_hidden * normal_one)
    small_ref[3:4, :] = column_sum(d_hidden)
    d_attention = dot(d_out, out_ref[...], NT).astype(bf16)
    out_ref[...] = dot(attention.astype(f32).T.astype(bf16), d_out).astype(bf16)
    return d_attention


def select_lanes(rows, offset, base):
    wide = rows.shape[1]
    choose = (iota((wide, 128), 0) + base == iota((wide, 128), 1) + offset).astype(f32).astype(bf16)
    first = rows.astype(bf16)
    second = (rows - first.astype(f32)).astype(bf16)
    third = (rows - first.astype(f32) - second.astype(f32)).astype(bf16)
    return dot(first, choose) + dot(second, choose) + dot(third, choose)


def layer_kernel(heads, active, names, *refs):
    r = dict(zip(names, refs))
    net = Links()
    s, f, z, y, x, c = net.s, net.f, net.z, net.y, net.x, net.c
    oy, ox, oc = net.oy, net.ox, net.oc
    width = heads * HD
    own_ref, tokens_ref, weights_ref = r["own"], r["tokens"], r["weights"]
    count, rows = own_ref.shape[0], r["wq"].shape[0]
    mine = rows_at(s, count)
    index = s * 4 + f

    loads = [pltpu.make_async_copy(r["in_" + name], r[name], r["load_sems"].at[n])
             for n, name in enumerate(("own", "wq", "wk", "wv", "vectors", "cot"))]
    begin(loads)
    greet(net.seq_peers + net.fsdp_peers)
    for copy in loads:
        copy.wait()

    def pair(name):
        return r[name + "_send"], r[name + "_recv"]

    def token_z(zz, t, up):
        here = tokens_ref.at[rows_at(zz * 2 + y, count)]
        n = 2 * t + (0 if up else 1)
        return remote(own_ref if t == 0 else here, here, r["tz_send"].at[n], r["tz_recv"].at[n], net.above if up else net.below)

    def token_y(zz, own=False):
        here = tokens_ref.at[rows_at(zz * 2 + y, count)]
        return remote(own_ref if own else here, here, r["ty_send"].at[zz], r["ty_recv"].at[zz], net.y_peer)

    pieces = ((r["in_wup"], r["up"], rows), (r["placed"], r["full_small"], 16), (r["in_wout"], r["out"], rows),
              (r["in_wdown"], r["down"], 4 * rows))
    early, late = (0, 1, 2), (3,)

    def slot(zz, sy, sx):
        return (zz * 2 + sy) * 4 + sx * 2 + c

    def weight(m, own, where, send_sem, recv_sem, peer):
        src, full, n = pieces[m]
        here = full.at[rows_at(where, n)]
        return remote(src if own else here, here, send_sem, recv_sem, peer)

    def weight_z(zz, t, up):
        n = 2 * t + (0 if up else 1)
        peer = net.above if up else net.below
        return [weight(m, t == 0, slot(zz, y, x), r["gz_send"].at[n, m], r["gz_recv"].at[n, m], peer) for m in range(4)]

    def to_y(zz, m, own=False):
        return weight(m, own, slot(zz, y, x), r["gy_send"].at[zz, m], r["gy_recv"].at[zz, m], net.y_peer)

    def to_x(zz, m, own=False):
        return weight(m, own, slot(zz, y, x), r["gx_send"].at[zz, m], r["gx_recv"].at[zz, m], net.x_peer)

    def again_x(zz, m):
        return weight(m, False, slot(zz, oy, x), r["gx_send"].at[zz, 4 + m], r["gx_recv"].at[zz, 4 + m], net.x_peer)

    def again_y(zz, m):
        return weight(m, False, slot(zz, y, ox), r["gy_send"].at[zz, 4 + m], r["gy_recv"].at[zz, 4 + m], net.y_peer)

    def to_core(zz, n, m, own=False):
        sy, sx = ((y, x), (oy, x), (y, ox), (oy, ox))[n]
        return weight(m, own, slot(zz, sy, sx), r["gc_send"].at[zz, n, m], r["gc_recv"].at[zz, n, m], net.c_peer)

    def spread(zz):
        begin([to_y(zz, m) for m in early] + [to_x(zz, m) for m in late])
        begin([to_x(zz, m) for m in early] + [to_y(zz, m) for m in late])
        begin([to_core(zz, 0, m) for m in range(4)])

    def onward(zz):
        for m in early:
            done([to_y(zz, m)])
            begin([again_x(zz, m)])
        for m in late:
            done([to_x(zz, m)])
            begin([again_y(zz, m)])
        done([to_y(zz, m) for m in late])
        begin([to_core(zz, 1, m) for m in range(4)])
        done([to_x(zz, m) for m in early])
        begin([to_core(zz, 2, m) for m in range(4)])

    def corner(zz):
        done([again_x(zz, m) for m in early] + [again_y(zz, m) for m in late])
        begin([to_core(zz, 3, m) for m in range(4)])

    def column(t, act):
        for up in (True, False):
            zz = z - 1 - t if up else z + 1 + t

            @pl.when(zz >= 0 if up else zz < 4)
            def _():
                act(zz, up)

    def onto_z(t, act):
        for up in (True, False):
            zz = z - t if up else z + t

            @pl.when((zz >= 0) & (z < 3) if up else (zz < 4) & (z > 0))
            def _():
                act(zz, t, up)

    onto_z(0, lambda zz, t, up: token_z(zz, t, up).start())
    token_y(z, True).start()
    vectors = r["vectors"][...]
    for j in range(16):
        base, row = (96, 6) if 6 <= j < 10 else (24, j)
        lead = (j - 6) * D if 6 <= j < 10 else 0
        if j in (10, 11):
            row = j - 3
        if j >= 12:
            break
        base = 4 * rows if base == 96 else rows
        lane = iota((128, D), 1) + lead - base * index
        choose = ((lane == iota((128, D), 0)) & (lane < base)).astype(f32).astype(bf16)
        value = dot(vectors, choose)[row : row + 1, :]
        r["place"][j : j + 1, :] = value
    r["place"][12:16, :] = jnp.zeros((4, D), f32)
    r["placed"][...] = r["place"][...].astype(bf16)
    pack, landed = r["pack"], r["landed"]
    for b in range(active):
        for n, name in enumerate(("wq", "wk", "wv")):
            pack[b, 0:rows, n * width : (n + 1) * width] = r[name][:, b * width : (b + 1) * width]
        pack[b, rows:, :] = jnp.zeros((pack.shape[1] - rows, 3 * width), bf16)
        for n, j in ((0, 10), (2, 11)):
            bias = jnp.broadcast_to(r["place"][j : j + 1, b * width : (b + 1) * width], (8, width))
            pack[b, rows : rows + 8, n * width : (n + 1) * width] = jnp.where(iota((8, width), 0) == 0, bias, 0.0).astype(bf16)
    from_seq = [
        net.send(pack.at[(s + j + 1) % 8 % active], landed.at[f, s], pair("ps"), j, net.seq_peers[j]) for j in range(7)]
    landed[f, s] = pack[s % active]
    tokens_ref[mine, :] = own_ref[...]
    keep = [pltpu.make_async_copy(src, full.at[rows_at(slot(z, y, x), n)], r["keep_sems"].at[m])
            for m, (src, full, n) in enumerate(pieces)]
    begin(keep)
    for t in range(3):
        def came(zz, up, t=t):
            token_z(zz, t, up).wait_recv()
            token_y(zz).start()

        column(t, came)
        if t < 2:
            onto_z(t + 1, lambda zz, t, up: token_z(zz, t, up).start())
    done(from_seq)
    from_fsdp = [net.send(landed.at[f], landed.at[f], pair("pf"), i, net.fsdp_peers[i]) for i in range(3)]
    onto_z(0, lambda zz, t, up: begin(weight_z(zz, t, up)))
    begin([to_x(z, m, True) for m in (3, 0, 1, 2)] + [to_y(z, m, True) for m in (0, 1, 2, 3)])
    begin([to_core(z, 0, m, True) for m in range(4)])

    def gather_stage(n):
        if n <= 3:
            t = n - 1

            def came(zz, up):
                done(weight_z(zz, t, up))
                spread(zz)

            column(t, came)
            if t < 2:
                onto_z(t + 1, lambda zz, t, up: begin(weight_z(zz, t, up)))
        if n == 1:
            onward(z)
        elif n <= 4:
            column(n - 2, lambda zz, up: onward(zz))
        if n == 2:
            corner(z)
        elif 3 <= n:
            column(n - 3, lambda zz, up: corner(zz))

    for zz in range(4):
        token_y(zz).wait_recv()
    done(from_fsdp)
    bias = jnp.zeros((8, 3 * width), f32)
    for a in range(4):
        for b in range(8):
            weights_ref[rows * (b * 4 + a) : rows * (b * 4 + a + 1), :] = landed[a, b, 0:rows, :]
            bias = bias + landed[a, b, rows : rows + 8, :].astype(f32)

    state = [r[name] for name in ("q", "k", "v", "fw", "bw", "land", "mix", "a", "norm", "chain")]
    lengths_ref, taps_ref, mixed = r["lengths"], r["taps"], r["d_wide"].at[0 : 8 * count, :]
    forward_math(heads, active, lengths_ref, taps_ref, tokens_ref, weights_ref, bias[0:1], mixed, *state,
                 r["v_wide"], r["score"], gather_stage)

    att = r["att"]
    last = [net.send(mixed.at[rows_at((s + j + 1) % 8, count)], att.at[s], pair("at"), j, net.seq_peers[j]) for j in range(7)]
    att[s] = mixed[mine, :]
    for zz in range(4):
        for n in range(4):
            done([to_core(zz, n, m) for m in range(4)])
    for copy in keep:
        copy.wait()

    def sent(zz, t, up):
        token_z(zz, t, up).wait_send()
        for copy in weight_z(zz, t, up):
            copy.wait_send()

    net.drain()
    for t in range(3):
        onto_z(t, sent)
    for zz in range(4):
        token_y(zz).wait_send()
        for m in range(4):
            to_y(zz, m).wait_send()
            to_x(zz, m).wait_send()
            (again_x if m in early else again_y)(zz, m).wait_send()
            for n in range(4):
                to_core(zz, n, m).wait_send()
    vec = jnp.zeros((16, D), f32)
    for n in range(32):
        vec = vec + r["full_small"][16 * n : 16 * n + 16, :].astype(f32)
    r["vec"][...] = vec
    done(last)

    sums = ((r["up"], r["acc_up"], r["got_up"], r["far_up"], rows), (r["out"], r["acc_out"], r["got_out"], r["far_out"], rows),
            (r["down"], r["acc_down"], r["got_down"], r["far_down"], 4 * rows))
    places = ((0, 0), (0, 1), (1, 0), (1, 1))
    moved = {}

    def owner(k, sy, sx, sc):
        return ((z + k + 1) % 4 * 2 + sy) * 4 + sx * 2 + sc

    def to_sibling(pieces_of):
        for k in range(4):
            for m, (sy, sx) in enumerate(places):
                for n in pieces_of:
                    full, acc, _, _, size = sums[n]
                    moved["c", k, m, n] = net.send(
                        full.at[rows_at(owner(k, sy, sx, oc), size)], acc.at[k, sy, sx], pair("rc"), (4 * k + m, n), net.c_peer)

    attention = jnp.concatenate([att[b] for b in range(active)], axis=1)
    d_attention = token_math(
        own_ref[...], r["cot"][...], attention, r["up"], r["down"], r["out"], r["vec"], r["gelu"], r["slope"],
        r["output"], r["dr1"], r["small"], lambda: to_sibling((0, 2)))
    store = [pltpu.make_async_copy(r["output"], r["o_output"], r["store_sems"].at[0])]
    begin(store)
    dattn, dout = r["dattn"], r["dout"]
    for b in range(active):
        dattn[b] = d_attention[:, b * width : (b + 1) * width]
    from_seq = [
        net.send(dattn.at[(s + j + 1) % 8 % active], dout.at[mine], pair("dt"), j, net.seq_peers[j]) for j in range(7)]
    dout[mine, :] = dattn[s % active]
    to_sibling((1,))
    small_put, small_got, small_sum = r["small_put"], r["small_got"], r["small_sum"]
    small_put[...] = r["small"][...].astype(bf16)
    moved["m", 0] = net.send(small_put, small_got.at[0], pair("rm"), 0, net.c_peer)

    def add(target, more, more_index):
        deep, wide = target.shape

        def one(i, carry):
            if wide > D:
                cols = pl.ds(pl.multiple_of(i * D, D), D)
                here, there = (slice(None), cols), (rows_at(more_index, deep), cols)
            else:
                here, there = (rows_at(i, rows), slice(None)), (pl.ds(pl.multiple_of(more_index * deep + i * rows, 8), rows), slice(None))
            target[here] = (target[here].astype(f32) + more[there].astype(f32)).astype(bf16)
            return carry

        lax.fori_loop(0, deep * wide // (rows * D), one, 0)

    def first(k):
        for m, (sy, sx) in enumerate(places):
            for n, (full, acc, _, _, _) in enumerate(sums):
                moved["c", k, m, n].wait_recv()
                add(acc.at[k, sy, sx], full, owner(k, sy, sx, c))
        for i in range(2):
            for n, (_, acc, got, _, _) in enumerate(sums):
                if n < 2:
                    moved["1", k, i, n] = net.send(acc.at[k, i, ox], got.at[k, i], pair("rx"), (3 * k + i, n), net.x_peer)
                else:
                    moved["1", k, i, n] = net.send(acc.at[k, oy, i], got.at[k, i], pair("ry"), (3 * k + i, 0), net.y_peer)

    def second(k):
        for n, (_, acc, got, _, _) in enumerate(sums):
            for i in range(2):
                moved["1", k, i, n].wait_recv()
                add(acc.at[k, i, x] if n < 2 else acc.at[k, y, i], got.at[k, i], 0)
            if n < 2:
                moved["2", k, n] = net.send(acc.at[k, oy, x], got.at[k, 2], pair("ry"), (3 * k + 2, n), net.y_peer)
            else:
                moved["2", k, n] = net.send(acc.at[k, y, ox], got.at[k, 2], pair("rx"), (3 * k + 2, 0), net.x_peer)

    def third(k):
        for n, (_, acc, got, far, _) in enumerate(sums):
            moved["2", k, n].wait_recv()
            add(acc.at[k, y, x], got.at[k, 2], 0)
            if k < 3:
                moved["3", k, n] = net.send(acc.at[k, y, x], far.at[k], pair("rz"), (k, n), net.z_peers[k])

    def small_step(n):
        before = small_put if n == 0 else small_sum.at[n - 1]
        moved["m", n].wait_recv()
        small_sum[n] = (before[...].astype(f32) + small_got[n].astype(f32)).astype(bf16)
        if n < 2:
            moved["m", n + 1] = net.send(
                small_sum.at[n], small_got.at[n + 1], pair("rm"), n + 1, net.x_peer if n == 0 else net.y_peer)
        else:
            for j in range(3):
                moved["m", 3 + j] = net.send(small_sum.at[2], small_got.at[3 + j], pair("rm"), 3 + j, net.z_peers[j])

    def scatter_stage(n):
        if n < 4:
            first(n)
        if 1 <= n < 5:
            second(n - 1)
        if 2 <= n < 6:
            third(n - 2)
        if n < 3:
            small_step(n)

    scatter_stage(0)
    done(from_seq)
    part, y_got, z_got = r["part"], r["y_got"], r["z_got"]
    over_y = []

    def parts_ready():
        for j in range(4):
            there = rows_at((z + j + 1) % 4 * 2 + oy, count)
            over_y.append(net.send(part.at[there], y_got.at[j], pair("dy"), j, net.y_peer))

    score = r["score"]
    accumulators = [score.at[0, :, 0:width], score.at[0, :, width : 2 * width], score.at[1, :, 0:width]]
    dw_t = r["slope"].at[:, 0 : 3 * D]
    backward_math(
        heads, active, lengths_ref, taps_ref, tokens_ref, weights_ref, dout, *state, part, dw_t, r["extra"],
        r["v_wide"], r["d_wide"], *accumulators, r["spread"], r["tap_rows"], r["dqkv"],
        scatter_stage, s < active, parts_ready)

    first_put, first_got, second_put, second_got = landed, r["first_got"], r["second_put"], r["second_got"]
    dw = [dw_t[:, n * D : (n + 1) * D].T.astype(bf16) for n in range(3)]
    tail = r["extra"][...].astype(bf16)
    for a in range(4):
        for b in range(8):
            start = rows * (4 * b + a)
            for n in range(3):
                first_put[a, b, 0:rows, n * width : (n + 1) * width] = dw[n][start : start + rows, :]
            first_put[a, b, rows:, :] = tail
    from_fsdp = [
        net.send(first_put.at[(f + i + 1) % 4], first_got.at[f], pair("wf"), i, net.fsdp_peers[i]) for i in range(3)]
    first_got[f] = first_put[f]
    over_z = []
    for j in range(4):
        done([over_y[j]])
        here = rows_at((z + j + 1) % 4 * 2 + y, count)
        value = part[here, :].astype(f32) + y_got[j].astype(f32)
        if j < 3:
            z_put = r["gelu"].at[:, j * D : (j + 1) * D]
            z_put[...] = value.astype(bf16)
            over_z.append(net.send(z_put, z_got.at[j], pair("dz"), j, net.z_peers[j]))
        else:
            kept = value + r["dr1"][...]
    done(from_fsdp)
    for b in range(8):
        value = first_got[0, b].astype(f32)
        for a in range(1, 4):
            value = value + first_got[a, b].astype(f32)
        second_put[b] = value.astype(bf16)
    from_seq = [
        net.send(second_put.at[(s + j + 1) % 8], second_got.at[s], pair("ws"), j, net.seq_peers[j]) for j in range(7)]
    second_got[s] = second_put[s]

    def put(name, n):
        store.append(pltpu.make_async_copy(r[name], r["o_" + name], r["store_sems"].at[n]))
        begin(store[-1:])

    for n, (name, (_, acc, _, far, _)) in enumerate(zip(("sup", "sout", "sdown"), sums)):
        value = acc[3, y, x].astype(f32)
        for j in range(3):
            done([moved["3", j, n]])
            value = value + far[j].astype(f32)
        r[name][...] = value
        put(name, 1 + n)
    value = small_sum[2].astype(f32)
    for j in range(3):
        done([moved["m", 3 + j]])
        value = value + small_got[3 + j].astype(f32)
    lines = r["lines"]
    lines[...] = jnp.zeros(lines.shape, f32)
    lines[0:8, :] = select_lanes(value, rows * index, 0)[0:8, :]
    b_up = jnp.zeros((16, 128), f32)
    for j in range(4):
        b_up = b_up + jnp.where(iota((16, 128), 0) == 6 + j, select_lanes(value, 4 * rows * index, j * D), 0.0)
    lines[6:7, :] = column_sum(b_up)
    done(over_z)
    for j in range(3):
        kept = kept + z_got[j].astype(f32)
    r["dtok"][...] = kept.astype(bf16)
    put("dtok", 4)
    done(from_seq)
    bias = jnp.zeros((8, 128), f32)
    bias_v = jnp.zeros((8, 128), f32)
    for b in range(active):
        for n, name in enumerate(("dwq", "dwk", "dwv")):
            r[name][:, b * width : (b + 1) * width] = second_got[b, 0:rows, n * width : (n + 1) * width].astype(f32)
        tail = second_got[b, rows:, :].astype(f32)
        bias = bias + select_lanes(tail[:, 0:width], rows * index, b * width)
        bias_v = bias_v + select_lanes(tail[:, 2 * width :], rows * index, b * width)
        lines[16 + b * heads : 16 + (b + 1) * heads, :] = tail[1 : 1 + heads, 0:128]
    lines[7:8, :] = bias[0:1]
    lines[8:9, :] = bias_v[0:1]
    for n, name in enumerate(("dwq", "dwk", "dwv", "lines")):
        put(name, 5 + n)
    net.drain()
    for copy in store:
        copy.wait()


def layer(heads, active, lengths, taps, own, cot, w_query, w_key, w_value, vectors, w_up, w_out, w_down):
    count, rows = own.shape[0], w_query.shape[0]
    total = 8 * count
    width = heads * HD
    shape, buffer, dma = jax.ShapeDtypeStruct, pltpu.VMEM, pltpu.SemaphoreType.DMA
    smem, anywhere = pl.BlockSpec(memory_space=pltpu.SMEM), pl.BlockSpec(memory_space=pl.ANY)
    ins = ["lengths", "taps", "in_own", "in_cot", "in_wq", "in_wk", "in_wv", "in_vectors", "in_wup", "in_wout", "in_wdown"]
    outs = {
        "output": shape((count, D), bf16), "dtok": shape((count, D), bf16),
        "dwq": shape((rows, D), f32), "dwk": shape((rows, D), f32), "dwv": shape((rows, D), f32),
        "sup": shape((rows, FF), f32), "sout": shape((rows, D), f32), "sdown": shape((4 * rows, D), f32),
        "lines": shape((32, 128), f32),
    }
    sizes = {"up": (rows, FF), "out": (rows, D), "down": (4 * rows, D)}
    scratch = {
        "own": buffer((count, D), bf16), "cot": buffer((count, D), bf16),
        "wq": buffer((rows, D), bf16), "wk": buffer((rows, D), bf16), "wv": buffer((rows, D), bf16),
        "vectors": buffer((16, 128), bf16), "place": buffer((16, D), f32), "placed": buffer((16, D), bf16),
        "tokens": buffer((total, D), bf16), "weights": buffer((D, 3 * width), bf16),
        "pack": buffer((active, rows + 8, 3 * width), bf16), "landed": buffer((4, 8, rows + 8, 3 * width), bf16),
        "up": buffer((D, FF), bf16), "full_small": buffer((512, D), bf16), "out": buffer((D, D), bf16),
        "down": buffer((FF, D), bf16), "vec": buffer((16, D), f32),
        "q": buffer((total, width), bf16), "k": buffer((total, width), bf16), "v": buffer((total, width), f32),
        "fw": buffer((heads, total, SLOTS), bf16), "bw": buffer((heads, total, SLOTS), bf16),
        "land": buffer((2, SLOTS, width), f32), "mix": buffer((2, width, SLOTS), f32),
        "a": buffer((heads, SLOTS, SLOTS), f32), "norm": buffer((heads, SLOTS, SLOTS), f32),
        "chain": buffer((NS_ITERS + 1, heads, 4, 2, SLOTS, SLOTS), bf16),
        "v_wide": buffer((total + 128, width), bf16),
        "score": buffer((heads, total, SLOTS), f32), "att": buffer((8, count, width), bf16),
        "gelu": buffer((count, FF), bf16), "slope": buffer((count, FF), f32), "dr1": buffer((count, D), f32),
        "small": buffer((16, D), f32), "small_put": buffer((16, D), bf16), "small_got": buffer((6, 16, D), bf16),
        "small_sum": buffer((3, 16, D), bf16),
        "dattn": buffer((active, count, width), bf16), "dout": buffer((total, width), bf16),
        "d_wide": buffer((total + 128, width), bf16),
        "spread": buffer((heads, 128, 256), f32), "tap_rows": buffer((128, 256), f32),
        "dqkv": buffer((total, 3 * width), bf16), "part": buffer((total, D), bf16),
        "extra": buffer((8, 3 * width), f32),
        "y_got": buffer((4, count, D), bf16), "z_got": buffer((3, count, D), bf16),
        "first_got": buffer((4, 8, rows + 8, 3 * width), bf16),
        "second_put": buffer((8, rows + 8, 3 * width), bf16), "second_got": buffer((8, rows + 8, 3 * width), bf16),
    }
    for name, size in sizes.items():
        scratch["acc_" + name] = buffer((4, 2, 2, *size), bf16)
        scratch["got_" + name] = buffer((4, 3, *size), bf16)
        scratch["far_" + name] = buffer((3, *size), bf16)
    for name, value in outs.items():
        scratch[name] = buffer(value.shape, value.dtype)
    pairs = {
        "tz": (6,), "ty": (4,), "ps": (7,), "pf": (3,), "at": (7,), "gz": (6, 4), "gy": (4, 8), "gx": (4, 8), "gc": (4, 4, 4),
        "rc": (16, 3), "rx": (12, 2), "ry": (12, 2), "rz": (3, 3), "rm": (6,), "dt": (7,), "dy": (4,), "dz": (3,),
        "wf": (3,), "ws": (7,),
    }
    for name, size in pairs.items():
        scratch[name + "_send"] = dma(size)
        scratch[name + "_recv"] = dma(size)
    scratch["load_sems"], scratch["keep_sems"], scratch["store_sems"] = dma((6,)), dma((4,)), dma((9,))
    names = ins + ["o_" + name for name in outs] + list(scratch)
    return pl.pallas_call(
        partial(layer_kernel, heads, active, names),
        out_shape=tuple(outs.values()),
        in_specs=[smem, smem] + [anywhere] * 9,
        out_specs=tuple([anywhere] * len(outs)),
        scratch_shapes=list(scratch.values()),
        compiler_params=pltpu.CompilerParams(collective_id=0, has_side_effects=True, vmem_limit_bytes=63_000_000),
    )(lengths, taps, own, cot, w_query, w_key, w_value, vectors, w_up, w_out, w_down)


def product(form, left, right):
    return jnp.einsum(form, left, right, preferred_element_type=f32)


def layer_norm(inputs, gain, shift):
    average = jnp.mean(inputs, axis=-1, keepdims=True)
    centred = inputs - average
    variance = jnp.mean(centred * centred, axis=-1, keepdims=True)
    return centred * lax.rsqrt(variance + epsilon) * gain + shift


def gelu_exact(inputs):
    return jax.nn.gelu(inputs, approximate=False)


def token_part(tokens, cot, attention, w_out, w_up, w_down, b_out, b_up, b_down, g_attn, s_attn, g_mlp, s_mlp):
    out_proj = product("td,de->te", attention, w_out) + b_out
    hidden, norm_one_back = jax.vjp(layer_norm, tokens.astype(f32) + out_proj, g_attn, s_attn)
    hidden_low = hidden.astype(bf16)
    up_pre = product("td,df->tf", hidden_low, w_up) + b_up
    gelu_val, gelu_back = jax.vjp(gelu_exact, up_pre)
    gelu_low = gelu_val.astype(bf16)
    down_pre = product("tf,fd->td", gelu_low, w_down) + b_down
    output, norm_two_back = jax.vjp(layer_norm, hidden + down_pre, g_mlp, s_mlp)
    d_r2, dg_mlp, ds_mlp = norm_two_back(cot.astype(f32))
    d_down = d_r2.astype(bf16)
    db_down = jnp.sum(d_down.astype(f32), axis=0)
    dw_down = product("tf,td->fd", gelu_low, d_down)
    d_gelu = product("td,fd->tf", d_down, w_down)
    d_up = gelu_back(d_gelu)[0].astype(bf16)
    db_up = jnp.sum(d_up.astype(f32), axis=0)
    dw_up = product("td,tf->df", hidden_low, d_up)
    d_hidden = product("tf,df->td", d_up, w_up) + d_r2
    d_r1, dg_attn, ds_attn = norm_one_back(d_hidden)
    d_out = d_r1.astype(bf16)
    db_out = jnp.sum(d_out.astype(f32), axis=0)
    dw_out = product("td,te->de", attention, d_out)
    d_attn = product("te,de->td", d_out, w_out)
    smalls = (db_out, db_up, db_down, dg_attn, ds_attn, dg_mlp, ds_mlp)
    return output.astype(bf16), d_r1, d_attn, dw_out, dw_up, dw_down, smalls
def local(sizes, *args):
    (tokens, cotangent, doc_lengths, w_query, b_query, w_key, w_value, b_value, w_out, b_out, w_up, b_up,
     w_down, b_down, g_attn, s_attn, g_mlp, s_mlp, conv_kernel) = args
    seq, fsdp = sizes
    devices = seq * fsdp
    fast = sizes == (8, 4)
    axes = ("seq", "fsdp")
    rows = D // devices
    hidden_rows = FF // devices
    own_tokens, own_cot, lengths = tokens[0], cotangent[0], doc_lengths[0]
    count = own_tokens.shape[0]
    total = count * seq
    heads = -(-HEADS // seq)
    width = heads * HD
    active = HEADS // heads
    s = lax.axis_index("seq")

    taps = conv_kernel.astype(f32)
    if fast:
        vectors = [jnp.pad(v, (0, 128 - v.shape[0])) for v in (
            b_out, b_down, g_attn, s_attn, g_mlp, s_mlp, b_up, b_query, b_value)]
        vectors = jnp.pad(jnp.stack(vectors), ((0, 7), (0, 0)))
        output, d_tokens, dw_query, dw_key, dw_value, s_up, s_out, s_down, lines = layer(
            heads, active, lengths, taps, own_tokens, own_cot, w_query, w_key, w_value, vectors, w_up, w_out, w_down)
        g = [lines[j, :rows] for j in range(6)]
        s_b_up, db_query, db_value = lines[6, :hidden_rows], lines[7, :rows], lines[8, :rows]
        d_kernel = jnp.transpose(lines[16 : 16 + HEADS, :CONV], (1, 0))
        return (
            output[None], d_tokens[None], dw_query, db_query, dw_key, dw_value, db_value, s_out, g[0],
            s_up, s_b_up, s_down, g[1], g[2], g[3], g[4], g[5], d_kernel)

    own = (s * fsdp + lax.axis_index("fsdp")) * rows
    pack_rows = -(-rows // 8) * 8 + 8
    lead = pack_rows - 8

    def placed(vector, at, size):
        return lax.dynamic_update_slice(jnp.zeros((size,), bf16), vector, (at,))

    bias_q, bias_v = (placed(b, own, D).reshape(active, 1, width) for b in (b_query, b_value))
    bias = jnp.concatenate([bias_q, jnp.zeros((active, 1, width), bf16), bias_v], axis=2)
    bias = jnp.pad(bias, ((0, 0), (0, 7), (0, 0)))
    small = [placed(v, own, D) for v in (b_out, b_down, g_attn, s_attn, g_mlp, s_mlp)]
    small = jnp.concatenate(small + [placed(b_up, own * 4, FF), jnp.zeros((6 * D,), bf16)]).reshape(16, D)
    blocks = []
    for b in range(active):
        cols = slice(b * width, (b + 1) * width)
        blocks.append(jnp.concatenate([w_query[:, cols], w_key[:, cols], w_value[:, cols]], axis=1))
    pack = jnp.concatenate([jnp.pad(jnp.stack(blocks), ((0, 0), (0, lead - rows), (0, 0))), bias], axis=1)
    all_tokens = lax.all_gather(own_tokens, "seq").reshape(total, D)
    all_pack = lax.all_gather(lax.all_to_all(
        jnp.take(pack, jnp.arange(seq) % active, axis=0), "seq", 0, 0), "fsdp", axis=1).reshape(
            devices, pack_rows, 3 * width)
    qkv_weights = all_pack[:, :rows].reshape(D, 3 * width)
    full_up, full_small, full_down, full_out = (
        lax.all_gather(w, axes, tiled=True) for w in (w_up, small, w_down, w_out))
    mixed, *state = attention_forward(heads, active, all_tokens, qkv_weights, all_pack[:, lead:], lengths, taps)
    attention = lax.all_to_all(mixed.reshape(seq, count, width), "seq", 0, 0)
    vectors = jnp.sum(full_small.reshape(devices, 16, D).astype(f32), axis=0)
    attention = jnp.transpose(attention[:active], (1, 0, 2)).reshape(count, D)
    output, d_r1, d_attn, dw_out, dw_up, dw_down, smalls = token_part(
        own_tokens, own_cot, attention, full_out, full_up, full_down, vectors[0], vectors[6:10].reshape(FF),
        *(vectors[j] for j in range(1, 6)))
    d_attn = jnp.transpose(d_attn.astype(bf16).reshape(count, active, width), (1, 0, 2))
    d_mixed = lax.all_to_all(jnp.take(d_attn, jnp.arange(seq) % active, axis=0), "seq", 0, 0)
    s_up, s_out, s_down = (
        lax.psum_scatter(w, axes, scatter_dimension=0, tiled=True) for w in (dw_up, dw_out, dw_down))
    small = [lax.psum_scatter(v, axes, scatter_dimension=0, tiled=True) for v in smalls]
    part, dw, extra = attention_backward(
        heads, active, all_tokens, qkv_weights, d_mixed.reshape(total, width), lengths, taps, state)
    token_parts = lax.all_to_all(part.reshape(seq, count, D), "seq", 0, 0)
    d_tokens = (d_r1 + jnp.sum(token_parts.astype(f32), axis=0)).astype(bf16)
    extra = lax.psum(lax.all_gather(extra, "seq")[:active], "fsdp")
    dw = jnp.transpose(dw.reshape(width, 3, devices, rows), (2, 3, 1, 0)).reshape(devices, rows, 3 * width)
    dw = lax.all_to_all(dw, axes, 0, 0)
    dw = jnp.sum(dw.reshape(seq, fsdp, rows, 3, width)[:active], axis=1)
    dw_query, dw_key, dw_value = (jnp.transpose(dw[:, :, j], (1, 0, 2)).reshape(rows, D) for j in range(3))
    db_query = lax.dynamic_slice_in_dim(extra[:, 0, :width].reshape(D), own, rows)
    db_value = lax.dynamic_slice_in_dim(extra[:, 0, 2 * width :].reshape(D), own, rows)
    d_kernel = jnp.transpose(extra[:, 1 : 1 + heads, :CONV].reshape(active * heads, CONV), (1, 0))
    s_b_out, s_b_up, s_b_down, s_g_attn, s_s_attn, s_g_mlp, s_s_mlp = small
    return (
        output[None], d_tokens[None], dw_query, db_query, dw_key, dw_value, db_value, s_out, s_b_out,
        s_up, s_b_up, s_down, s_b_down, s_g_attn, s_s_attn, s_g_mlp, s_s_mlp, d_kernel)


def solution(mesh):
    sizes = (mesh.shape["seq"], mesh.shape["fsdp"])
    both = ("seq", "fsdp")
    wide, flat, stream = P(both, None), P(both), P("fsdp", "seq", None)
    in_specs = (stream, stream, P("fsdp", None), wide, flat, wide, wide, flat, wide, flat, wide, flat, wide, flat,
                flat, flat, flat, flat, P())
    out_specs = (stream, stream, wide, flat, wide, wide, flat, wide, flat, wide, flat, wide, flat, flat, flat, flat,
                 flat, P())
    return jax.shard_map(partial(local, sizes), mesh=mesh, in_specs=in_specs, out_specs=out_specs, check_vma=False)
```

```python
from functools import partial
import math

import jax
import jax.numpy as jnp
from jax import lax
from jax.experimental import pallas as pl
from jax.experimental.pallas import tpu as pltpu
from jax.sharding import PartitionSpec as P

D = 768
HEADS = 12
HD = 64
FF = 3072
NLAND = 64
NS_ITERS = 6
CONV = 33
REACH = CONV // 2
DOCS = 4
SLOTS = 256
SCALE = 1.0 / math.sqrt(HD)

HIGHEST = lax.Precision.HIGHEST
epsilon = 1e-05
masked_score = -1e30
f32 = jnp.float32
bf16 = jnp.bfloat16
MESH = pl.DeviceIdType.MESH
VMEM_BYTES = 56 * 1024 * 1024


def greet(peers):
    barrier = pltpu.get_barrier_semaphore()
    for peer in peers:
        pl.semaphore_signal(barrier, inc=1, device_id=peer, device_id_type=MESH)
    pl.semaphore_wait(barrier, len(peers))


def remote(src, dst, send_sem, recv_sem, peer):
    return pltpu.make_async_remote_copy(
        src_ref=src, dst_ref=dst, send_sem=send_sem, recv_sem=recv_sem,
        device_id=peer, device_id_type=MESH,
    )


BLOCK = 256
NN = (((1,), (0,)), ((), ()))
NT = (((1,), (1,)), ((), ()))


def dot(left, right, dims=NN):
    return lax.dot_general(left, right, dims, preferred_element_type=f32)


def split(value):
    upper = value.astype(bf16)
    return upper, (value - upper.astype(f32)).astype(bf16)


def dot3(left, right, dims=NN):
    return dot(left[0], right[0], dims) + (dot(left[0], right[1], dims) + dot(left[1], right[0], dims))


def iota(shape, dim):
    return lax.broadcasted_iota(jnp.int32, shape, dim)


def doc_table(lengths_ref):
    ends, start = [], 0
    for d in range(DOCS):
        start = start + lengths_ref[d]
        ends.append(start)
    return ends


def slot_bounds(lengths_ref, shape, dim):
    ends = doc_table(lengths_ref)
    slot = iota(shape, dim)
    doc, seg = slot // NLAND, slot % NLAND
    length, end = jnp.zeros(shape, jnp.int32), jnp.zeros(shape, jnp.int32)
    for d in range(DOCS):
        length = jnp.where(doc == d, lengths_ref[d], length)
        end = jnp.where(doc == d, ends[d], end)
    start = end - length
    return start, end, start + seg * length // NLAND, start + (seg + 1) * length // NLAND


def same_doc(lengths_ref, left, right):
    ends = doc_table(lengths_ref)
    a, b = jnp.zeros(left.shape, jnp.int32), jnp.zeros(right.shape, jnp.int32)
    for d in range(DOCS):
        a = a + (left >= ends[d]).astype(jnp.int32)
        b = b + (right >= ends[d]).astype(jnp.int32)
    return a == b


def head_mask(shape, dim, h):
    return (iota(shape, dim) // HD == h).astype(f32)


def tap_index():
    return iota((128, 256), 1) - iota((128, 256), 0) - 64 + REACH


def toeplitz(taps_ref, head, mirrored):
    tap = tap_index()
    mat = jnp.zeros((128, 256), f32)
    for o in range(CONV):
        mat = jnp.where(tap == o, taps_ref[CONV - 1 - o if mirrored else o, head], mat)
    return mat


def clear_edges(ref, total):
    ref[0:64, :] = jnp.zeros((64, ref.shape[1]), ref.dtype)
    ref[total + 64 : total + 128, :] = jnp.zeros((64, ref.shape[1]), ref.dtype)


def forward_math(heads, active, lengths_ref, taps_ref, tokens_ref, weights_ref, bias,
                 mixed_ref, q_ref, k_ref, v_ref, fw_ref, bw_ref, land_ref, mix_ref, a_ref, norm_ref, chain_ref,
                 v_wide, score, stage):
    total = tokens_ref.shape[0]
    width = heads * HD
    part = lax.axis_index("seq") % active
    steps = total // BLOCK
    row_start, row_end, row_low, row_top = slot_bounds(lengths_ref, (1, SLOTS), 1)
    _, _, col_low, col_top = slot_bounds(lengths_ref, (SLOTS, 1), 0)
    count = (col_top - col_low).astype(f32)
    clear_edges(v_wide, total)
    land_ref[...] = jnp.zeros(land_ref.shape, f32)

    def project(i, carry):
        at = pl.ds(pl.multiple_of(i * BLOCK, BLOCK), BLOCK)
        qkv = dot(tokens_ref[at, :], weights_ref[...]) + bias
        q, k, v = (qkv[:, j * width : (j + 1) * width] for j in range(3))
        q_low, k_low = q.astype(bf16), k.astype(bf16)
        q_ref[at, :], k_ref[at, :] = q_low, k_low
        v_ref[at, :] = v
        v_wide[pl.ds(pl.multiple_of(i * BLOCK + 64, 64), BLOCK), :] = v.astype(bf16)
        t = i * BLOCK + iota((1, BLOCK), 1)
        member = ((t >= col_low) & (t < col_top)).astype(f32).astype(bf16)
        land_ref[0] += dot(member, q_low)
        land_ref[1] += dot(member, k_low)
        return carry

    lax.fori_loop(0, steps, project, 0)
    stage("proj")
    ql, kl = land_ref[0] / count, land_ref[1] / count
    land_ref[0], land_ref[1] = ql, kl
    masks = [head_mask((1, width), 1, h) for h in range(heads)]
    ql_low = [(ql * masks[h]).astype(bf16) for h in range(heads)]
    kl_low = [(kl * masks[h]).astype(bf16) for h in range(heads)]

    def scores(i, tops):
        at = pl.ds(pl.multiple_of(i * BLOCK, BLOCK), BLOCK)
        t = i * BLOCK + iota((BLOCK, 1), 0)
        valid = (t >= row_start) & (t < row_end)
        out = []
        for h in range(heads):
            s = jnp.where(valid, SCALE * dot(q_ref[at, :], kl_low[h], NT), masked_score)
            e = jnp.exp(s - jnp.max(s, axis=1, keepdims=True))
            fw_ref[h, at, :] = (e / jnp.sum(e, axis=1, keepdims=True)).astype(bf16)
            s = jnp.where(valid, SCALE * dot(k_ref[at, :], ql_low[h], NT), masked_score)
            score[h, at, :] = s
            out.append(jnp.maximum(tops[h], jnp.max(s, axis=0, keepdims=True)))
        return tuple(out)

    tops = lax.fori_loop(0, steps, scores, tuple(jnp.full((1, SLOTS), masked_score, f32) for _ in range(heads)))
    stage("scores")

    def gather(i, carry):
        at = pl.ds(pl.multiple_of(i * BLOCK, BLOCK), BLOCK)
        v_t = split(v_ref[at, :].T)
        out = []
        for h in range(heads):
            e = jnp.exp(score[h, at, :] - tops[h])
            score[h, at, :] = e
            out.append((carry[h][0] + jnp.sum(e, axis=0, keepdims=True), carry[h][1] + dot3(v_t, split(e))))
        return tuple(out)

    sums = lax.fori_loop(0, steps, gather, tuple(
        (jnp.zeros((1, SLOTS), f32), jnp.zeros((width, SLOTS), f32)) for _ in range(heads)))
    scale = [1.0 / sums[h][0] for h in range(heads)]
    tall = [head_mask((width, 1), 0, h) for h in range(heads)]
    key_mix_t = [sums[h][1] * scale[h] * tall[h] for h in range(heads)]

    def normalize(i, carry):
        at = pl.ds(pl.multiple_of(i * BLOCK, BLOCK), BLOCK)
        for h in range(heads):
            bw_ref[h, at, :] = (score[h, at, :] * scale[h]).astype(bf16)
        return carry

    lax.fori_loop(0, steps, normalize, 0)
    stage("key_mix")

    block = iota((SLOTS, SLOTS), 0) // NLAND == iota((SLOTS, SLOTS), 1) // NLAND
    diagonal = iota((SLOTS, SLOTS), 0) == iota((SLOTS, SLOTS), 1)
    state = []
    for h in range(heads):
        s = jnp.where(block, SCALE * dot3(split(ql * masks[h]), split(kl), NT), masked_score)
        e = jnp.exp(s - jnp.max(s, axis=1, keepdims=True))
        a = e / jnp.sum(e, axis=1, keepdims=True)
        norm = jnp.sum(jnp.sum((a * a).reshape(DOCS, NLAND, SLOTS), axis=1, keepdims=True), axis=2, keepdims=True)
        norm = jnp.broadcast_to(norm, (DOCS, NLAND, SLOTS)).reshape(SLOTS, SLOTS)
        a_ref[h], norm_ref[h] = a, norm
        u = a / norm
        a_split = split(a)
        state.append((split(u), split(dot3(a_split, split(u), NT))))
    for step in range(NS_ITERS):
        fresh = []
        for h in range(heads):
            u, p = state[h]
            p_full = p[0].astype(f32) + p[1].astype(f32)
            q_full = dot3(p, p)
            q = split(q_full)
            f_full = jnp.where(diagonal, 13.0, 0.0) - 15.0 * p_full + 7.0 * q_full - dot3(p, q)
            f = split(f_full)
            for n, pair in enumerate((u, p, q, f)):
                for half in range(2):
                    chain_ref[step, h, n, half] = pair[half]
            p_next = None if step == NS_ITERS - 1 else split(0.25 * dot3(p, f))
            u_next = split(0.25 * dot3(f, u))
            fresh.append((u_next, p_next))
        stage("newton" + str(step))
        state = fresh
    mix_t = jnp.zeros((width, SLOTS), f32)
    key_t = jnp.zeros((width, SLOTS), f32)
    for h in range(heads):
        u = state[h][0]
        chain_ref[NS_ITERS, h, 0, 0], chain_ref[NS_ITERS, h, 0, 1] = u
        mix_t = mix_t + dot3(split(key_mix_t[h]), u)
        key_t = key_t + key_mix_t[h]
    mix_ref[0], mix_ref[1] = mix_t, key_t
    stage("mix")
    mix_low = [(mix_t * tall[h]).astype(bf16) for h in range(heads)]
    mats = [toeplitz(taps_ref, part * heads + h, False) for h in range(heads)]

    def output(i, carry):
        at = pl.ds(pl.multiple_of(i * 128, 128), 128)
        t = i * 128 + iota((128, 1), 0)
        near = same_doc(lengths_ref, t, i * 128 - 64 + iota((1, 256), 1))
        window = v_wide[pl.ds(pl.multiple_of(i * 128, 128), 256), :]
        out = jnp.zeros((128, width), f32)
        for h in range(heads):
            out = out + dot(fw_ref[h, at, :], mix_low[h], NT)
            conv = dot(jnp.where(near, mats[h], 0.0).astype(bf16), window)
            out = out + conv * masks[h]
        mixed_ref[at, :] = out.astype(bf16)
        return carry

    lax.fori_loop(0, total // 128, output, 0)


def forward_kernel(heads, active, lengths_ref, taps_ref, tokens_ref, weights_ref, bias_ref, *refs):
    bias = jnp.sum(bias_ref[...].astype(f32), axis=0)[0:1]
    forward_math(heads, active, lengths_ref, taps_ref, tokens_ref, weights_ref, bias, *refs, lambda n: None)


def attention_forward(heads, active, tokens, weights, bias, lengths, taps):
    total = tokens.shape[0]
    width = heads * HD
    shape = jax.ShapeDtypeStruct
    vmem, smem = (pl.BlockSpec(memory_space=m) for m in (pltpu.VMEM, pltpu.SMEM))
    chain = (heads, 4, 2, SLOTS, SLOTS)
    return pl.pallas_call(
        partial(forward_kernel, heads, active),
        out_shape=(
            shape((total, width), bf16),
            shape((total, width), bf16),
            shape((total, width), bf16),
            shape((total, width), f32),
            shape((heads, total, SLOTS), bf16),
            shape((heads, total, SLOTS), bf16),
            shape((2, SLOTS, width), f32),
            shape((2, width, SLOTS), f32),
            shape((heads, SLOTS, SLOTS), f32),
            shape((heads, SLOTS, SLOTS), f32),
            shape((NS_ITERS + 1, *chain), bf16),
        ),
        in_specs=[smem, smem, vmem, vmem, vmem],
        out_specs=tuple([vmem] * 11),
        scratch_shapes=[
            pltpu.VMEM((total + 128, width), bf16),
            pltpu.VMEM((heads, total, SLOTS), f32),
        ],
        compiler_params=pltpu.CompilerParams(vmem_limit_bytes=VMEM_BYTES),
    )(lengths, taps, tokens, weights, bias)


def backward_math(heads, active, lengths_ref, taps_ref, tokens_ref, weights_ref, dout_ref, q_ref, k_ref, v_ref, fw_ref,
                  bw_ref, land_ref, mix_ref, a_ref, norm_ref, chain_ref, dw_ref, extra_ref,
                  v_wide, d_wide, dq_acc, dk_acc, dv_acc, spread, tap_rows, dqkv, stage):
    total = tokens_ref.shape[0]
    width = heads * HD
    part = lax.axis_index("seq") % active
    steps = total // BLOCK
    _, _, row_low, row_top = slot_bounds(lengths_ref, (1, SLOTS), 1)
    inverse = 1.0 / (row_top - row_low).astype(f32)
    clear_edges(v_wide, total)
    clear_edges(d_wide, total)
    masks = [head_mask((1, width), 1, h) for h in range(heads)]
    tall = [head_mask((width, 1), 0, h) for h in range(heads)]
    ql, kl = land_ref[0], land_ref[1]
    mix_t, key_t = mix_ref[0], mix_ref[1]
    kl_low = [(kl * masks[h]).astype(bf16) for h in range(heads)]
    ql_low = [(ql * masks[h]).astype(bf16) for h in range(heads)]
    mix_low = [(mix_t * tall[h]).astype(bf16) for h in range(heads)]

    def front(i, carry):
        at = pl.ds(pl.multiple_of(i * BLOCK, BLOCK), BLOCK)
        inner = pl.ds(pl.multiple_of(i * BLOCK + 64, 64), BLOCK)
        do = dout_ref[at, :]
        d_wide[inner, :] = do
        v_wide[inner, :] = v_ref[at, :].astype(bf16)
        do_t = do.astype(f32).T.astype(bf16)
        q_t = q_ref[at, :].astype(f32).T.astype(bf16)
        dq = jnp.zeros((BLOCK, width), f32)
        out = []
        for h in range(heads):
            fw = fw_ref[h, at, :]
            wide = fw.astype(f32)
            d_fw = dot(do, mix_low[h])
            ds = (SCALE * wide * (d_fw - jnp.sum(wide * d_fw, axis=1, keepdims=True))).astype(bf16)
            dq = dq + dot(ds, kl_low[h])
            out.append((carry[h][0] + dot(do_t, fw), carry[h][1] + dot(q_t, ds)))
        dq_acc[at, :] = dq
        return tuple(out)

    zeros = jnp.zeros((width, SLOTS), f32)
    sums = lax.fori_loop(0, steps, front, tuple((zeros, zeros) for _ in range(heads)))
    stage("front")
    dmix_t = [sums[h][0] * tall[h] for h in range(heads)]
    dkl_t = zeros
    for h in range(heads):
        dkl_t = dkl_t + sums[h][1] * tall[h]
    key = key_t.T
    ql_t = ql.T
    block = iota((SLOTS, SLOTS), 0) // NLAND == iota((SLOTS, SLOTS), 1) // NLAND
    du, dp, dkey_t = [], [None] * heads, []
    for h in range(heads):
        pair = split(dmix_t[h])
        du.append(jnp.where(block, dot3(split(key), pair), 0.0))
        dkey_t.append(dot3(pair, (chain_ref[NS_ITERS, h, 0, 0], chain_ref[NS_ITERS, h, 0, 1]), NT))
    for step in range(NS_ITERS - 1, -1, -1):
        stage("newton" + str(step))
        for h in range(heads):
            u, p, q, f = ((chain_ref[step, h, n, 0], chain_ref[step, h, n, 1]) for n in range(4))
            du_pair = split(du[h])
            df = 0.25 * dot3(du_pair, u, NT)
            du[h] = 0.25 * dot3(f, du_pair)
            if dp[h] is not None:
                dp_pair = split(dp[h])
                df = df + 0.25 * dot3(p, dp_pair)
                base = 0.25 * dot3(dp_pair, f)
            else:
                base = 0.0
            df_pair = split(df)
            dq = split(7.0 * df - dot3(p, df_pair))
            dp[h] = base - 15.0 * df - dot3(df_pair, q) + (dot3(dq, p) + dot3(p, dq))
    dql = jnp.zeros((SLOTS, width), f32)
    for h in range(heads):
        a, norm = a_ref[h], norm_ref[h]
        u0 = chain_ref[0, h, 0, 0].astype(f32) + chain_ref[0, h, 0, 1].astype(f32)
        p0 = chain_ref[0, h, 1, 0].astype(f32) + chain_ref[0, h, 1, 1].astype(f32)
        a_pair = split(a)
        inner = dp[h] * p0 + du[h] * u0
        inner = jnp.sum(jnp.sum(inner.reshape(DOCS, NLAND, SLOTS), axis=1, keepdims=True), axis=2, keepdims=True)
        inner = jnp.broadcast_to(inner, (DOCS, NLAND, SLOTS)).reshape(SLOTS, SLOTS)
        da = (dot3(split(dp[h] + dp[h].T), a_pair) + du[h] - 2.0 * a * inner) / norm
        dsa = split(SCALE * a * (da - jnp.sum(a * da, axis=1, keepdims=True)))
        dql = dql + dot3(dsa, split(kl * masks[h]))
        dkl_t = dkl_t + dot3(split(ql_t * tall[h]), dsa)
    stage("core")
    dkey_low = [x.astype(bf16) for x in dkey_t]
    row_dot = [jnp.sum(dkey_t[h] * key_t, axis=0, keepdims=True) for h in range(heads)]
    dkey = [x.T.astype(bf16) for x in dkey_t]

    def back(i, carry):
        at = pl.ds(pl.multiple_of(i * BLOCK, BLOCK), BLOCK)
        v = v_ref[at, :].astype(bf16)
        k_t = k_ref[at, :].astype(f32).T.astype(bf16)
        dk, dv = jnp.zeros((BLOCK, width), f32), jnp.zeros((BLOCK, width), f32)
        out = []
        for h in range(heads):
            bw = bw_ref[h, at, :]
            ds = (SCALE * bw.astype(f32) * (dot(v, dkey_low[h]) - row_dot[h])).astype(bf16)
            dk = dk + dot(ds, ql_low[h])
            dv = dv + dot(bw, dkey[h])
            out.append(carry[h] + dot(k_t, ds))
        dk_acc[at, :] = dk
        dv_acc[at, :] = dv
        return tuple(out)

    sums = lax.fori_loop(0, steps, back, tuple(zeros for _ in range(heads)))
    stage("back")
    dql_t = zeros
    for h in range(heads):
        dql_t = dql_t + sums[h] * tall[h]
    dql_low = ((dql.T + dql_t) * inverse).astype(bf16)
    dkl_low = (dkl_t * inverse).astype(bf16)
    mats = [toeplitz(taps_ref, part * heads + h, True) for h in range(heads)]
    spread[...] = jnp.zeros(spread.shape, f32)

    def convolve(i, carry):
        at = pl.ds(pl.multiple_of(i * 128, 128), 128)
        t = i * 128 + iota((128, 1), 0)
        near = same_doc(lengths_ref, t, i * 128 - 64 + iota((1, 256), 1))
        window = pl.ds(pl.multiple_of(i * 128, 128), 256)
        d_window, v_window = d_wide[window, :], v_wide[window, :]
        do = dout_ref[at, :].astype(f32)
        dv = dv_acc[at, :]
        for h in range(heads):
            dv = dv + dot(jnp.where(near, mats[h], 0.0).astype(bf16), d_window) * masks[h]
            spread[h] += jnp.where(near, dot((do * masks[h]).astype(bf16), v_window, NT), 0.0)
        dv_acc[at, :] = dv
        return carry

    lax.fori_loop(0, total // 128, convolve, 0)
    stage("conv")

    def finish(i, carry):
        at = pl.ds(pl.multiple_of(i * BLOCK, BLOCK), BLOCK)
        t = i * BLOCK + iota((BLOCK, 1), 0)
        member = ((t >= row_low) & (t < row_top)).astype(f32).astype(bf16)
        dq = dq_acc[at, :] + dot(member, dql_low, NT)
        dk = dk_acc[at, :] + dot(member, dkl_low, NT)
        grads = jnp.concatenate([dq.astype(bf16), dk.astype(bf16), dv_acc[at, :].astype(bf16)], axis=1)
        dqkv[at, :] = grads
        return carry + jnp.sum(grads.astype(f32), axis=0, keepdims=True)

    extra_ref[...] = jnp.zeros(extra_ref.shape, f32)
    extra_ref[0:1, :] = lax.fori_loop(0, steps, finish, jnp.zeros((1, 3 * width), f32))
    stage("parts")
    dw_ref[...] = jnp.zeros(dw_ref.shape, f32)

    def weigh(i, carry):
        at = pl.ds(pl.multiple_of(i * BLOCK, BLOCK), BLOCK)
        for n in range(3):
            grads = dqkv[at, n * width : (n + 1) * width].astype(f32).T.astype(bf16)
            dw_ref[:, n * D : (n + 1) * D] += dot(grads, tokens_ref[at, :])
        return carry

    lax.fori_loop(0, steps, weigh, 0)
    tap = tap_index()
    tap_rows[...] = jnp.zeros(tap_rows.shape, f32)
    for h in range(heads):
        for o in range(CONV):
            tap_rows[o : o + 1, :] = jnp.sum(jnp.where(tap == o, spread[h], 0.0), axis=0, keepdims=True)
        extra_ref[1 + h : 2 + h, 0:128] = jnp.sum(tap_rows[...].T, axis=0, keepdims=True)


def backward_kernel(heads, active, lengths_ref, taps_ref, tokens_ref, weights_ref, *refs):
    inputs, part_ref, outputs, dqkv = refs[:11], refs[11], refs[12:-1], refs[-1]
    backward_math(heads, active, lengths_ref, taps_ref, tokens_ref, weights_ref, *inputs, *outputs, dqkv, lambda point: None)

    def project(i, carry):
        at = pl.ds(pl.multiple_of(i * BLOCK, BLOCK), BLOCK)
        part = dot(dqkv[at, :], weights_ref[...], NT)
        part_ref[at, :] = jnp.where(lax.axis_index("seq") < active, part, 0.0).astype(bf16)
        return carry

    lax.fori_loop(0, tokens_ref.shape[0] // BLOCK, project, 0)


def attention_backward(heads, active, tokens, weights, dout, lengths, taps, state):
    total = tokens.shape[0]
    width = heads * HD
    shape = jax.ShapeDtypeStruct
    vmem, smem = (pl.BlockSpec(memory_space=m) for m in (pltpu.VMEM, pltpu.SMEM))
    return pl.pallas_call(
        partial(backward_kernel, heads, active),
        out_shape=(
            shape((total, D), bf16),
            shape((width, 3 * D), f32),
            shape((8, 3 * width), f32),
        ),
        in_specs=[smem, smem] + [vmem] * 13,
        out_specs=tuple([vmem] * 3),
        scratch_shapes=[
            pltpu.VMEM((total + 128, width), bf16),
            pltpu.VMEM((total + 128, width), bf16),
            pltpu.VMEM((total, width), f32),
            pltpu.VMEM((total, width), f32),
            pltpu.VMEM((total, width), f32),
            pltpu.VMEM((heads, 128, 256), f32),
            pltpu.VMEM((128, 256), f32),
            pltpu.VMEM((total, 3 * width), bf16),
        ],
        compiler_params=pltpu.CompilerParams(vmem_limit_bytes=VMEM_BYTES),
    )(lengths, taps, tokens, weights, dout, *state)
def rows_at(index, count):
    return pl.ds(pl.multiple_of(index * count, 8), count)


class Links:
    def __init__(self):
        s, f = lax.axis_index("seq"), lax.axis_index("fsdp")
        self.s, self.f = s, f
        self.z, self.y, self.x, self.c = s // 2, s % 2, f // 2, f % 2
        self.oy, self.ox, self.oc = 1 - self.y, 1 - self.x, 1 - self.c
        self.seq_peers = [((s + j) % 8, f) for j in range(1, 8)]
        self.fsdp_peers = [(s, (f + i) % 4) for i in range(1, 4)]
        self.z_peers = [((self.z + j) % 4 * 2 + self.y, f) for j in range(1, 4)]
        self.above, self.below = self.z_peers[0], self.z_peers[2]
        self.y_peer = (self.z * 2 + self.oy, f)
        self.x_peer = (s, self.ox * 2 + self.c)
        self.c_peer = (s, self.x * 2 + self.oc)
        self.started = []

    def send(self, src, dst, sems, index, peer):
        copy = remote(src, dst, sems[0].at[index], sems[1].at[index], peer)
        copy.start()
        self.started.append(copy)
        return copy

    def drain(self):
        for copy in self.started:
            copy.wait_send()
        self.started = []


def begin(copies):
    for copy in copies:
        copy.start()


def done(copies):
    for copy in copies:
        copy.wait_recv()


def centre(value):
    value = value - jnp.mean(value, axis=1, keepdims=True)
    scale = lax.rsqrt(jnp.mean(value * value, axis=1, keepdims=True) + epsilon)
    return value * scale, scale


def uncentre(grad, normal, scale):
    return scale * (grad - jnp.mean(grad, axis=1, keepdims=True)
                    - normal * jnp.mean(grad * normal, axis=1, keepdims=True))


def column_sum(value):
    return jnp.sum(value, axis=0, keepdims=True)


def token_math(own, cot, attention, up_ref, down_ref, out_ref, vec_ref, gelu_ref, slope_ref, output_ref, dr1_ref, small_ref,
               weights_done):
    vec = vec_ref[...]
    b_out, b_down, g_attn, s_attn, g_mlp, s_mlp = (vec[j : j + 1] for j in range(6))
    normal_one, scale_one = centre(own.astype(f32) + dot(attention, out_ref[...]) + b_out)
    hidden = normal_one * g_attn + s_attn
    hidden_low = hidden.astype(bf16)
    count = hidden.shape[0]

    def upward(i, down):
        cols = pl.ds(pl.multiple_of(i * D, D), D)
        up = dot(hidden_low, up_ref[:, cols]) + vec_ref[pl.ds(6 + i, 1), :]
        share = 0.5 + 0.5 * lax.erf(up * math.sqrt(0.5))
        gelu = (up * share).astype(bf16)
        gelu_ref[:, cols] = gelu
        slope_ref[:, cols] = share + up * (math.sqrt(0.5 / math.pi) * jnp.exp(-0.5 * up * up))
        return down + dot(gelu, down_ref[cols, :])

    down = lax.fori_loop(0, FF // D, upward, jnp.zeros((count, D), f32))
    normal_two, scale_two = centre(hidden + down + b_down)
    output_ref[...] = (normal_two * g_mlp + s_mlp).astype(bf16)
    cot = cot.astype(f32)
    d_r2 = uncentre(cot * g_mlp, normal_two, scale_two)
    d_down = d_r2.astype(bf16)
    small_ref[...] = jnp.zeros(small_ref.shape, f32)
    small_ref[1:2, :] = column_sum(d_down.astype(f32))
    small_ref[4:5, :] = column_sum(cot * normal_two)
    small_ref[5:6, :] = column_sum(cot)
    hidden_t = hidden_low.astype(f32).T.astype(bf16)

    def downward(i, d_hidden):
        cols = pl.ds(pl.multiple_of(i * D, D), D)
        d_gelu = dot(d_down, down_ref[cols, :], NT)
        d_up = (d_gelu * slope_ref[:, cols]).astype(bf16)
        small_ref[pl.ds(6 + i, 1), :] = column_sum(d_up.astype(f32))
        d_hidden = d_hidden + dot(d_up, up_ref[:, cols], NT)
        gelu_t = gelu_ref[:, cols].astype(f32).T.astype(bf16)
        down_ref[cols, :] = dot(gelu_t, d_down).astype(bf16)
        up_ref[:, cols] = dot(hidden_t, d_up).astype(bf16)
        return d_hidden

    d_hidden = lax.fori_loop(0, FF // D, downward, d_r2)
    weights_done()
    d_r1 = uncentre(d_hidden * g_attn, normal_one, scale_one)
    dr1_ref[...] = d_r1
    d_out = d_r1.astype(bf16)
    small_ref[0:1, :] = column_sum(d_out.astype(f32))
    small_ref[2:3, :] = column_sum(d_hidden * normal_one)
    small_ref[3:4, :] = column_sum(d_hidden)
    d_attention = dot(d_out, out_ref[...], NT).astype(bf16)
    out_ref[...] = dot(attention.astype(f32).T.astype(bf16), d_out).astype(bf16)
    return d_attention


def select_lanes(rows, offset, base):
    wide = rows.shape[1]
    choose = (iota((wide, 128), 0) + base == iota((wide, 128), 1) + offset).astype(f32).astype(bf16)
    first = rows.astype(bf16)
    second = (rows - first.astype(f32)).astype(bf16)
    third = (rows - first.astype(f32) - second.astype(f32)).astype(bf16)
    return dot(first, choose) + dot(second, choose) + dot(third, choose)


GATHER = {"proj": "w1", "scores": "w2", "key_mix": "o0", "mix": "o1 c0", "end": "o2 c1 c2"}
PLAN = {
    "start": "f0 f1 m0", "newton3": "s0 f2 m1", "core": "s1 t0 f3 m2", "parts": "y0 s2 t1",
    "end": "z0 s3 t2 z1 w0 z2 z3 t3",
}


def layer_kernel(heads, active, names, *refs):
    r = dict(zip(names, refs))
    net = Links()
    s, f, z, y, x, c = net.s, net.f, net.z, net.y, net.x, net.c
    oy, ox, oc = net.oy, net.ox, net.oc
    width = heads * HD
    own_ref, tokens_ref, weights_ref = r["own"], r["tokens"], r["weights"]
    count, rows = own_ref.shape[0], r["wq"].shape[0]
    mine = rows_at(s, count)
    index = s * 4 + f

    loads = [pltpu.make_async_copy(r["in_" + name], r[name], r["load_sems"].at[n])
             for n, name in enumerate(("own", "wq", "wk", "wv", "vectors", "cot"))]
    begin(loads)
    greet(net.seq_peers + net.fsdp_peers)
    for copy in loads:
        copy.wait()

    def pair(name):
        return r[name + "_send"], r[name + "_recv"]

    def token_z(zz, t, up):
        here = tokens_ref.at[rows_at(zz * 2 + y, count)]
        n = 2 * t + (0 if up else 1)
        return remote(own_ref if t == 0 else here, here, r["tz_send"].at[n], r["tz_recv"].at[n], net.above if up else net.below)

    def token_y(zz, own=False):
        here = tokens_ref.at[rows_at(zz * 2 + y, count)]
        return remote(own_ref if own else here, here, r["ty_send"].at[zz], r["ty_recv"].at[zz], net.y_peer)

    pieces = ((r["in_wup"], r["up"], rows), (r["placed"], r["full_small"], 16), (r["in_wout"], r["out"], rows),
              (r["in_wdown"], r["down"], 4 * rows))
    early, late = (0, 1, 2), (3,)

    def slot(zz, sy, sx):
        return (zz * 2 + sy) * 4 + sx * 2 + c

    def weight(m, own, where, send_sem, recv_sem, peer):
        src, full, n = pieces[m]
        here = full.at[rows_at(where, n)]
        return remote(src if own else here, here, send_sem, recv_sem, peer)

    def weight_z(zz, t, up):
        n = 2 * t + (0 if up else 1)
        peer = net.above if up else net.below
        return [weight(m, t == 0, slot(zz, y, x), r["gz_send"].at[n, m], r["gz_recv"].at[n, m], peer) for m in range(4)]

    def to_y(zz, m, own=False):
        return weight(m, own, slot(zz, y, x), r["gy_send"].at[zz, m], r["gy_recv"].at[zz, m], net.y_peer)

    def to_x(zz, m, own=False):
        return weight(m, own, slot(zz, y, x), r["gx_send"].at[zz, m], r["gx_recv"].at[zz, m], net.x_peer)

    def again_x(zz, m):
        return weight(m, False, slot(zz, oy, x), r["gx_send"].at[zz, 4 + m], r["gx_recv"].at[zz, 4 + m], net.x_peer)

    def again_y(zz, m):
        return weight(m, False, slot(zz, y, ox), r["gy_send"].at[zz, 4 + m], r["gy_recv"].at[zz, 4 + m], net.y_peer)

    def to_core(zz, n, m, own=False):
        sy, sx = ((y, x), (oy, x), (y, ox), (oy, ox))[n]
        return weight(m, own, slot(zz, sy, sx), r["gc_send"].at[zz, n, m], r["gc_recv"].at[zz, n, m], net.c_peer)

    def spread(zz):
        begin([to_y(zz, m) for m in early] + [to_x(zz, m) for m in late])
        begin([to_x(zz, m) for m in early] + [to_y(zz, m) for m in late])
        begin([to_core(zz, 0, m) for m in range(4)])

    def onward(zz):
        for m in early:
            done([to_y(zz, m)])
            begin([again_x(zz, m)])
        for m in late:
            done([to_x(zz, m)])
            begin([again_y(zz, m)])
        done([to_y(zz, m) for m in late])
        begin([to_core(zz, 1, m) for m in range(4)])
        done([to_x(zz, m) for m in early])
        begin([to_core(zz, 2, m) for m in range(4)])

    def corner(zz):
        done([again_x(zz, m) for m in early] + [again_y(zz, m) for m in late])
        begin([to_core(zz, 3, m) for m in range(4)])

    def column(t, act):
        for up in (True, False):
            zz = z - 1 - t if up else z + 1 + t

            @pl.when(zz >= 0 if up else zz < 4)
            def _():
                act(zz, up)

    def onto_z(t, act):
        for up in (True, False):
            zz = z - t if up else z + t

            @pl.when((zz >= 0) & (z < 3) if up else (zz < 4) & (z > 0))
            def _():
                act(zz, t, up)

    onto_z(0, lambda zz, t, up: token_z(zz, t, up).start())
    token_y(z, True).start()
    begin([to_x(z, m, True) for m in (3, 0, 2)] + [to_y(z, m, True) for m in (0, 2, 3)])
    vectors = r["vectors"][...]
    for j in range(16):
        base, row = (96, 6) if 6 <= j < 10 else (24, j)
        lead = (j - 6) * D if 6 <= j < 10 else 0
        if j in (10, 11):
            row = j - 3
        if j >= 12:
            break
        base = 4 * rows if base == 96 else rows
        lane = iota((128, D), 1) + lead - base * index
        choose = ((lane == iota((128, D), 0)) & (lane < base)).astype(f32).astype(bf16)
        value = dot(vectors, choose)[row : row + 1, :]
        r["place"][j : j + 1, :] = value
    r["place"][12:16, :] = jnp.zeros((4, D), f32)
    r["placed"][...] = r["place"][...].astype(bf16)
    pack, landed = r["pack"], r["landed"]
    for b in range(active):
        for n, name in enumerate(("wq", "wk", "wv")):
            pack[b, 0:rows, n * width : (n + 1) * width] = r[name][:, b * width : (b + 1) * width]
        pack[b, rows:, :] = jnp.zeros((pack.shape[1] - rows, 3 * width), bf16)
        for n, j in ((0, 10), (2, 11)):
            bias = jnp.broadcast_to(r["place"][j : j + 1, b * width : (b + 1) * width], (8, width))
            pack[b, rows : rows + 8, n * width : (n + 1) * width] = jnp.where(iota((8, width), 0) == 0, bias, 0.0).astype(bf16)
    from_seq = [
        net.send(pack.at[(s + j + 1) % 8 % active], landed.at[f, s], pair("ps"), j, net.seq_peers[j]) for j in range(7)]
    begin([to_x(z, 1, True), to_y(z, 1, True)] + [to_core(z, 0, m, True) for m in range(4)])
    landed[f, s] = pack[s % active]
    tokens_ref[mine, :] = own_ref[...]
    keep = [pltpu.make_async_copy(src, full.at[rows_at(slot(z, y, x), n)], r["keep_sems"].at[m])
            for m, (src, full, n) in enumerate(pieces)]
    begin(keep)

    def weights_on(t):
        def came(zz, up):
            done(weight_z(zz, t, up))
            spread(zz)

        column(t, came)
        if t < 2:
            onto_z(t + 1, lambda zz, t, up: begin(weight_z(zz, t, up)))

    def tokens_on(t):
        def came(zz, up):
            token_z(zz, t, up).wait_recv()
            token_y(zz).start()

        column(t, came)
        if t < 2:
            onto_z(t + 1, lambda zz, t, up: token_z(zz, t, up).start())

    tokens_on(0)
    onto_z(0, lambda zz, t, up: begin(weight_z(zz, t, up)))
    tokens_on(1)
    onward(z)
    done(from_seq)
    from_fsdp = [net.send(landed.at[f], landed.at[f], pair("pf"), i, net.fsdp_peers[i]) for i in range(3)]
    tokens_on(2)
    weights_on(0)
    corner(z)

    gather_steps = {
        "w": weights_on, "o": lambda t: column(t, lambda zz, up: onward(zz)), "c": lambda t: column(t, lambda zz, up: corner(zz))}

    def gather_stage(point):
        for step in GATHER.get(point, "").split():
            gather_steps[step[0]](int(step[1]))

    for zz in range(4):
        token_y(zz).wait_recv()
    done(from_fsdp)
    bias = jnp.zeros((8, 3 * width), f32)
    for a in range(4):
        for b in range(8):
            weights_ref[rows * (b * 4 + a) : rows * (b * 4 + a + 1), :] = landed[a, b, 0:rows, :]
            bias = bias + landed[a, b, rows : rows + 8, :].astype(f32)

    state = [r[name] for name in ("q", "k", "v", "fw", "bw", "land", "mix", "a", "norm", "chain")]
    lengths_ref, taps_ref, mixed = r["lengths"], r["taps"], r["d_wide"].at[0 : 8 * count, :]
    forward_math(heads, active, lengths_ref, taps_ref, tokens_ref, weights_ref, bias[0:1], mixed, *state,
                 r["v_wide"], r["score"], gather_stage)

    att = r["att"]
    last = [net.send(mixed.at[rows_at((s + j + 1) % 8, count)], att.at[s], pair("at"), j, net.seq_peers[j]) for j in range(7)]
    att[s] = mixed[mine, :]
    gather_stage("end")
    for zz in range(4):
        for n in range(4):
            done([to_core(zz, n, m) for m in range(4)])
    for copy in keep:
        copy.wait()

    def sent(zz, t, up):
        token_z(zz, t, up).wait_send()
        for copy in weight_z(zz, t, up):
            copy.wait_send()

    net.drain()
    for t in range(3):
        onto_z(t, sent)
    for zz in range(4):
        token_y(zz).wait_send()
        for m in range(4):
            to_y(zz, m).wait_send()
            to_x(zz, m).wait_send()
            (again_x if m in early else again_y)(zz, m).wait_send()
            for n in range(4):
                to_core(zz, n, m).wait_send()
    vec = jnp.zeros((16, D), f32)
    for n in range(32):
        vec = vec + r["full_small"][16 * n : 16 * n + 16, :].astype(f32)
    r["vec"][...] = vec
    done(last)
    peer_weights = net.send(weights_ref, r["peer_weights"], pair("wp"), 0, net.y_peer)

    sums = ((r["up"], r["acc_up"], r["got_up"], r["far_up"], rows), (r["out"], r["acc_out"], r["got_out"], r["far_out"], rows),
            (r["down"], r["acc_down"], r["got_down"], r["far_down"], 4 * rows))
    places = ((0, 0), (0, 1), (1, 0), (1, 1))
    moved = {}

    def owner(k, sy, sx, sc):
        return ((z + k + 1) % 4 * 2 + sy) * 4 + sx * 2 + sc

    def to_sibling(pieces_of):
        for k in range(4):
            for m, (sy, sx) in enumerate(places):
                for n in pieces_of:
                    full, acc, _, _, size = sums[n]
                    moved["c", k, m, n] = net.send(
                        full.at[rows_at(owner(k, sy, sx, oc), size)], acc.at[k, sy, sx], pair("rc"), (4 * k + m, n), net.c_peer)

    attention = jnp.concatenate([att[b] for b in range(active)], axis=1)
    d_attention = token_math(
        own_ref[...], r["cot"][...], attention, r["up"], r["down"], r["out"], r["vec"], r["gelu"], r["slope"],
        r["output"], r["dr1"], r["small"], lambda: to_sibling((0, 2)))
    store = [pltpu.make_async_copy(r["output"], r["o_output"], r["store_sems"].at[0])]
    begin(store)
    dattn, dout = r["dattn"], r["dout"]
    for b in range(active):
        dattn[b] = d_attention[:, b * width : (b + 1) * width]
    from_seq = [
        net.send(dattn.at[(s + j + 1) % 8 % active], dout.at[mine], pair("dt"), j, net.seq_peers[j]) for j in range(7)]
    dout[mine, :] = dattn[s % active]
    to_sibling((1,))
    small_put, small_got, small_sum = r["small_put"], r["small_got"], r["small_sum"]
    small_put[...] = r["small"][...].astype(bf16)
    moved["m", 0] = net.send(small_put, small_got.at[0], pair("rm"), 0, net.c_peer)

    def add(target, more, more_index):
        deep, wide = target.shape

        def one(i, carry):
            if wide > D:
                cols = pl.ds(pl.multiple_of(i * D, D), D)
                here, there = (slice(None), cols), (rows_at(more_index, deep), cols)
            else:
                here, there = (rows_at(i, rows), slice(None)), (pl.ds(pl.multiple_of(more_index * deep + i * rows, 8), rows), slice(None))
            target[here] = (target[here].astype(f32) + more[there].astype(f32)).astype(bf16)
            return carry

        lax.fori_loop(0, deep * wide // (rows * D), one, 0)

    def first(k):
        for m, (sy, sx) in enumerate(places):
            for n, (full, acc, _, _, _) in enumerate(sums):
                moved["c", k, m, n].wait_recv()
                add(acc.at[k, sy, sx], full, owner(k, sy, sx, c))
        for i in range(2):
            for n, (_, acc, got, _, _) in enumerate(sums):
                if n < 2:
                    moved["1", k, i, n] = net.send(acc.at[k, i, ox], got.at[k, i], pair("rx"), (3 * k + i, n), net.x_peer)
                else:
                    moved["1", k, i, n] = net.send(acc.at[k, oy, i], got.at[k, i], pair("ry"), (3 * k + i, 0), net.y_peer)

    def second(k):
        for n, (_, acc, got, _, _) in enumerate(sums):
            for i in range(2):
                moved["1", k, i, n].wait_recv()
                add(acc.at[k, i, x] if n < 2 else acc.at[k, y, i], got.at[k, i], 0)
            if n < 2:
                moved["2", k, n] = net.send(acc.at[k, oy, x], got.at[k, 2], pair("ry"), (3 * k + 2, n), net.y_peer)
            else:
                moved["2", k, n] = net.send(acc.at[k, y, ox], got.at[k, 2], pair("rx"), (3 * k + 2, 0), net.x_peer)

    def third(k):
        for n, (_, acc, got, far, _) in enumerate(sums):
            moved["2", k, n].wait_recv()
            add(acc.at[k, y, x], got.at[k, 2], 0)
            if k < 3:
                moved["3", k, n] = net.send(acc.at[k, y, x], far.at[k], pair("rz"), (k, n), net.z_peers[k])

    def small_step(n):
        before = small_put if n == 0 else small_sum.at[n - 1]
        moved["m", n].wait_recv()
        small_sum[n] = (before[...].astype(f32) + small_got[n].astype(f32)).astype(bf16)
        if n < 2:
            moved["m", n + 1] = net.send(
                small_sum.at[n], small_got.at[n + 1], pair("rm"), n + 1, net.x_peer if n == 0 else net.y_peer)
        else:
            for j in range(3):
                moved["m", 3 + j] = net.send(small_sum.at[2], small_got.at[3 + j], pair("rm"), 3 + j, net.z_peers[j])

    steps = {"f": first, "s": second, "t": third, "m": small_step}

    def scatter_stage(point):
        for step in PLAN.get(point, "").split():
            steps[step[0]](int(step[1]))

    scatter_stage("start")
    done(from_seq)
    dqkv, y_got, z_got = r["dqkv"], r["y_got"], r["z_got"]
    over_y = []

    def send_gradients(_):
        for j in range(4):
            there = rows_at((z + j + 1) % 4 * 2 + oy, count)
            over_y.append(net.send(dqkv.at[there], y_got.at[j], pair("dy"), j, net.y_peer))

    steps["y"] = send_gradients
    score = r["score"]
    accumulators = [score.at[0, :, 0:width], score.at[0, :, width : 2 * width], score.at[1, :, 0:width]]
    dw_t = r["slope"].at[:, 0 : 3 * D]
    backward_math(
        heads, active, lengths_ref, taps_ref, tokens_ref, weights_ref, dout, *state, dw_t, r["extra"],
        r["v_wide"], r["d_wide"], *accumulators, r["spread"], r["tap_rows"], r["dqkv"],
        scatter_stage)

    first_put, first_got, second_put, second_got = landed, r["first_got"], r["second_put"], r["second_got"]
    dw = [dw_t[:, n * D : (n + 1) * D].T.astype(bf16) for n in range(3)]
    tail = r["extra"][...].astype(bf16)
    for a in range(4):
        for b in range(8):
            start = rows * (4 * b + a)
            for n in range(3):
                first_put[a, b, 0:rows, n * width : (n + 1) * width] = dw[n][start : start + rows, :]
            first_put[a, b, rows:, :] = tail
    from_fsdp = [
        net.send(first_put.at[(f + i + 1) % 4], first_got.at[f], pair("wf"), i, net.fsdp_peers[i]) for i in range(3)]
    first_got[f] = first_put[f]
    over_z, held = [], {}

    def token_parts(j):
        done([over_y[j]])
        here = rows_at((z + j + 1) % 4 * 2 + y, count)
        value = jnp.where(s < active, dot(dqkv[here, :], weights_ref[...], NT), 0.0)
        value = value + jnp.where(z * 2 + oy < active, dot(y_got[j], r["peer_weights"][...], NT), 0.0)
        if j < 3:
            z_put = r["gelu"].at[:, j * D : (j + 1) * D]
            z_put[...] = value.astype(bf16)
            over_z.append(net.send(z_put, z_got.at[j], pair("dz"), j, net.z_peers[j]))
        else:
            held["kept"] = value + r["dr1"][...]

    def weight_parts(_):
        done(from_fsdp)
        for b in range(8):
            value = first_got[0, b].astype(f32)
            for a in range(1, 4):
                value = value + first_got[a, b].astype(f32)
            second_put[b] = value.astype(bf16)
        held["seq"] = [
            net.send(second_put.at[(s + j + 1) % 8], second_got.at[s], pair("ws"), j, net.seq_peers[j]) for j in range(7)]
        second_got[s] = second_put[s]

    steps.update(z=token_parts, w=weight_parts)
    done([peer_weights])
    scatter_stage("end")
    kept, from_seq = held["kept"], held["seq"]

    def put(name, n):
        store.append(pltpu.make_async_copy(r[name], r["o_" + name], r["store_sems"].at[n]))
        begin(store[-1:])

    for n, (name, (_, acc, _, far, _)) in enumerate(zip(("sup", "sout", "sdown"), sums)):
        value = acc[3, y, x].astype(f32)
        for j in range(3):
            done([moved["3", j, n]])
            value = value + far[j].astype(f32)
        r[name][...] = value
        put(name, 1 + n)
    value = small_sum[2].astype(f32)
    for j in range(3):
        done([moved["m", 3 + j]])
        value = value + small_got[3 + j].astype(f32)
    lines = r["lines"]
    lines[...] = jnp.zeros(lines.shape, f32)
    lines[0:8, :] = select_lanes(value, rows * index, 0)[0:8, :]
    b_up = jnp.zeros((16, 128), f32)
    for j in range(4):
        b_up = b_up + jnp.where(iota((16, 128), 0) == 6 + j, select_lanes(value, 4 * rows * index, j * D), 0.0)
    lines[6:7, :] = column_sum(b_up)
    done(over_z)
    for j in range(3):
        kept = kept + z_got[j].astype(f32)
    r["dtok"][...] = kept.astype(bf16)
    put("dtok", 4)
    done(from_seq)
    bias = jnp.zeros((8, 128), f32)
    bias_v = jnp.zeros((8, 128), f32)
    for b in range(active):
        for n, name in enumerate(("dwq", "dwk", "dwv")):
            r[name][:, b * width : (b + 1) * width] = second_got[b, 0:rows, n * width : (n + 1) * width].astype(f32)
        tail = second_got[b, rows:, :].astype(f32)
        bias = bias + select_lanes(tail[:, 0:width], rows * index, b * width)
        bias_v = bias_v + select_lanes(tail[:, 2 * width :], rows * index, b * width)
        lines[16 + b * heads : 16 + (b + 1) * heads, :] = tail[1 : 1 + heads, 0:128]
    lines[7:8, :] = bias[0:1]
    lines[8:9, :] = bias_v[0:1]
    for n, name in enumerate(("dwq", "dwk", "dwv", "lines")):
        put(name, 5 + n)
    net.drain()
    for copy in store:
        copy.wait()


def layer(heads, active, lengths, taps, own, cot, w_query, w_key, w_value, vectors, w_up, w_out, w_down):
    count, rows = own.shape[0], w_query.shape[0]
    total = 8 * count
    width = heads * HD
    shape, buffer, dma = jax.ShapeDtypeStruct, pltpu.VMEM, pltpu.SemaphoreType.DMA
    smem, anywhere = pl.BlockSpec(memory_space=pltpu.SMEM), pl.BlockSpec(memory_space=pl.ANY)
    ins = ["lengths", "taps", "in_own", "in_cot", "in_wq", "in_wk", "in_wv", "in_vectors", "in_wup", "in_wout", "in_wdown"]
    outs = {
        "output": shape((count, D), bf16), "dtok": shape((count, D), bf16),
        "dwq": shape((rows, D), f32), "dwk": shape((rows, D), f32), "dwv": shape((rows, D), f32),
        "sup": shape((rows, FF), f32), "sout": shape((rows, D), f32), "sdown": shape((4 * rows, D), f32),
        "lines": shape((32, 128), f32),
    }
    sizes = {"up": (rows, FF), "out": (rows, D), "down": (4 * rows, D)}
    scratch = {
        "own": buffer((count, D), bf16), "cot": buffer((count, D), bf16),
        "wq": buffer((rows, D), bf16), "wk": buffer((rows, D), bf16), "wv": buffer((rows, D), bf16),
        "vectors": buffer((16, 128), bf16), "place": buffer((16, D), f32), "placed": buffer((16, D), bf16),
        "tokens": buffer((total, D), bf16), "weights": buffer((D, 3 * width), bf16),
        "pack": buffer((active, rows + 8, 3 * width), bf16), "landed": buffer((4, 8, rows + 8, 3 * width), bf16),
        "up": buffer((D, FF), bf16), "full_small": buffer((512, D), bf16), "out": buffer((D, D), bf16),
        "down": buffer((FF, D), bf16), "vec": buffer((16, D), f32),
        "q": buffer((total, width), bf16), "k": buffer((total, width), bf16), "v": buffer((total, width), f32),
        "fw": buffer((heads, total, SLOTS), bf16), "bw": buffer((heads, total, SLOTS), bf16),
        "land": buffer((2, SLOTS, width), f32), "mix": buffer((2, width, SLOTS), f32),
        "a": buffer((heads, SLOTS, SLOTS), f32), "norm": buffer((heads, SLOTS, SLOTS), f32),
        "chain": buffer((NS_ITERS + 1, heads, 4, 2, SLOTS, SLOTS), bf16),
        "v_wide": buffer((total + 128, width), bf16),
        "score": buffer((heads, total, SLOTS), f32), "att": buffer((8, count, width), bf16),
        "gelu": buffer((count, FF), bf16), "slope": buffer((count, FF), f32), "dr1": buffer((count, D), f32),
        "small": buffer((16, D), f32), "small_put": buffer((16, D), bf16), "small_got": buffer((6, 16, D), bf16),
        "small_sum": buffer((3, 16, D), bf16),
        "dattn": buffer((active, count, width), bf16), "dout": buffer((total, width), bf16),
        "d_wide": buffer((total + 128, width), bf16),
        "spread": buffer((heads, 128, 256), f32), "tap_rows": buffer((128, 256), f32),
        "dqkv": buffer((total, 3 * width), bf16), "peer_weights": buffer((D, 3 * width), bf16),
        "extra": buffer((8, 3 * width), f32),
        "y_got": buffer((4, count, 3 * width), bf16), "z_got": buffer((3, count, D), bf16),
        "first_got": buffer((4, 8, rows + 8, 3 * width), bf16),
        "second_put": buffer((8, rows + 8, 3 * width), bf16), "second_got": buffer((8, rows + 8, 3 * width), bf16),
    }
    for name, size in sizes.items():
        scratch["acc_" + name] = buffer((4, 2, 2, *size), bf16)
        scratch["got_" + name] = buffer((4, 3, *size), bf16)
        scratch["far_" + name] = buffer((3, *size), bf16)
    for name, value in outs.items():
        scratch[name] = buffer(value.shape, value.dtype)
    pairs = {
        "tz": (6,), "ty": (4,), "ps": (7,), "pf": (3,), "at": (7,), "gz": (6, 4), "gy": (4, 8), "gx": (4, 8), "gc": (4, 4, 4),
        "rc": (16, 3), "rx": (12, 2), "ry": (12, 2), "rz": (3, 3), "rm": (6,), "dt": (7,), "dy": (4,), "dz": (3,),
        "wf": (3,), "ws": (7,), "wp": (1,),
    }
    for name, size in pairs.items():
        scratch[name + "_send"] = dma(size)
        scratch[name + "_recv"] = dma(size)
    scratch["load_sems"], scratch["keep_sems"], scratch["store_sems"] = dma((6,)), dma((4,)), dma((9,))
    names = ins + ["o_" + name for name in outs] + list(scratch)
    return pl.pallas_call(
        partial(layer_kernel, heads, active, names),
        out_shape=tuple(outs.values()),
        in_specs=[smem, smem] + [anywhere] * 9,
        out_specs=tuple([anywhere] * len(outs)),
        scratch_shapes=list(scratch.values()),
        compiler_params=pltpu.CompilerParams(collective_id=0, has_side_effects=True, vmem_limit_bytes=63_000_000),
    )(lengths, taps, own, cot, w_query, w_key, w_value, vectors, w_up, w_out, w_down)


def product(form, left, right):
    return jnp.einsum(form, left, right, preferred_element_type=f32)


def layer_norm(inputs, gain, shift):
    average = jnp.mean(inputs, axis=-1, keepdims=True)
    centred = inputs - average
    variance = jnp.mean(centred * centred, axis=-1, keepdims=True)
    return centred * lax.rsqrt(variance + epsilon) * gain + shift


def gelu_exact(inputs):
    return jax.nn.gelu(inputs, approximate=False)


def token_part(tokens, cot, attention, w_out, w_up, w_down, b_out, b_up, b_down, g_attn, s_attn, g_mlp, s_mlp):
    out_proj = product("td,de->te", attention, w_out) + b_out
    hidden, norm_one_back = jax.vjp(layer_norm, tokens.astype(f32) + out_proj, g_attn, s_attn)
    hidden_low = hidden.astype(bf16)
    up_pre = product("td,df->tf", hidden_low, w_up) + b_up
    gelu_val, gelu_back = jax.vjp(gelu_exact, up_pre)
    gelu_low = gelu_val.astype(bf16)
    down_pre = product("tf,fd->td", gelu_low, w_down) + b_down
    output, norm_two_back = jax.vjp(layer_norm, hidden + down_pre, g_mlp, s_mlp)
    d_r2, dg_mlp, ds_mlp = norm_two_back(cot.astype(f32))
    d_down = d_r2.astype(bf16)
    db_down = jnp.sum(d_down.astype(f32), axis=0)
    dw_down = product("tf,td->fd", gelu_low, d_down)
    d_gelu = product("td,fd->tf", d_down, w_down)
    d_up = gelu_back(d_gelu)[0].astype(bf16)
    db_up = jnp.sum(d_up.astype(f32), axis=0)
    dw_up = product("td,tf->df", hidden_low, d_up)
    d_hidden = product("tf,df->td", d_up, w_up) + d_r2
    d_r1, dg_attn, ds_attn = norm_one_back(d_hidden)
    d_out = d_r1.astype(bf16)
    db_out = jnp.sum(d_out.astype(f32), axis=0)
    dw_out = product("td,te->de", attention, d_out)
    d_attn = product("te,de->td", d_out, w_out)
    smalls = (db_out, db_up, db_down, dg_attn, ds_attn, dg_mlp, ds_mlp)
    return output.astype(bf16), d_r1, d_attn, dw_out, dw_up, dw_down, smalls
def local(sizes, *args):
    (tokens, cotangent, doc_lengths, w_query, b_query, w_key, w_value, b_value, w_out, b_out, w_up, b_up,
     w_down, b_down, g_attn, s_attn, g_mlp, s_mlp, conv_kernel) = args
    seq, fsdp = sizes
    devices = seq * fsdp
    fast = sizes == (8, 4)
    axes = ("seq", "fsdp")
    rows = D // devices
    hidden_rows = FF // devices
    own_tokens, own_cot, lengths = tokens[0], cotangent[0], doc_lengths[0]
    count = own_tokens.shape[0]
    total = count * seq
    heads = -(-HEADS // seq)
    width = heads * HD
    active = HEADS // heads
    s = lax.axis_index("seq")

    taps = conv_kernel.astype(f32)
    if fast:
        vectors = [jnp.pad(v, (0, 128 - v.shape[0])) for v in (
            b_out, b_down, g_attn, s_attn, g_mlp, s_mlp, b_up, b_query, b_value)]
        vectors = jnp.pad(jnp.stack(vectors), ((0, 7), (0, 0)))
        output, d_tokens, dw_query, dw_key, dw_value, s_up, s_out, s_down, lines = layer(
            heads, active, lengths, taps, own_tokens, own_cot, w_query, w_key, w_value, vectors, w_up, w_out, w_down)
        g = [lines[j, :rows] for j in range(6)]
        s_b_up, db_query, db_value = lines[6, :hidden_rows], lines[7, :rows], lines[8, :rows]
        d_kernel = jnp.transpose(lines[16 : 16 + HEADS, :CONV], (1, 0))
        return (
            output[None], d_tokens[None], dw_query, db_query, dw_key, dw_value, db_value, s_out, g[0],
            s_up, s_b_up, s_down, g[1], g[2], g[3], g[4], g[5], d_kernel)

    own = (s * fsdp + lax.axis_index("fsdp")) * rows
    pack_rows = -(-rows // 8) * 8 + 8
    lead = pack_rows - 8

    def placed(vector, at, size):
        return lax.dynamic_update_slice(jnp.zeros((size,), bf16), vector, (at,))

    bias_q, bias_v = (placed(b, own, D).reshape(active, 1, width) for b in (b_query, b_value))
    bias = jnp.concatenate([bias_q, jnp.zeros((active, 1, width), bf16), bias_v], axis=2)
    bias = jnp.pad(bias, ((0, 0), (0, 7), (0, 0)))
    small = [placed(v, own, D) for v in (b_out, b_down, g_attn, s_attn, g_mlp, s_mlp)]
    small = jnp.concatenate(small + [placed(b_up, own * 4, FF), jnp.zeros((6 * D,), bf16)]).reshape(16, D)
    blocks = []
    for b in range(active):
        cols = slice(b * width, (b + 1) * width)
        blocks.append(jnp.concatenate([w_query[:, cols], w_key[:, cols], w_value[:, cols]], axis=1))
    pack = jnp.concatenate([jnp.pad(jnp.stack(blocks), ((0, 0), (0, lead - rows), (0, 0))), bias], axis=1)
    all_tokens = lax.all_gather(own_tokens, "seq").reshape(total, D)
    all_pack = lax.all_gather(lax.all_to_all(
        jnp.take(pack, jnp.arange(seq) % active, axis=0), "seq", 0, 0), "fsdp", axis=1).reshape(
            devices, pack_rows, 3 * width)
    qkv_weights = all_pack[:, :rows].reshape(D, 3 * width)
    full_up, full_small, full_down, full_out = (
        lax.all_gather(w, axes, tiled=True) for w in (w_up, small, w_down, w_out))
    mixed, *state = attention_forward(heads, active, all_tokens, qkv_weights, all_pack[:, lead:], lengths, taps)
    attention = lax.all_to_all(mixed.reshape(seq, count, width), "seq", 0, 0)
    vectors = jnp.sum(full_small.reshape(devices, 16, D).astype(f32), axis=0)
    attention = jnp.transpose(attention[:active], (1, 0, 2)).reshape(count, D)
    output, d_r1, d_attn, dw_out, dw_up, dw_down, smalls = token_part(
        own_tokens, own_cot, attention, full_out, full_up, full_down, vectors[0], vectors[6:10].reshape(FF),
        *(vectors[j] for j in range(1, 6)))
    d_attn = jnp.transpose(d_attn.astype(bf16).reshape(count, active, width), (1, 0, 2))
    d_mixed = lax.all_to_all(jnp.take(d_attn, jnp.arange(seq) % active, axis=0), "seq", 0, 0)
    s_up, s_out, s_down = (
        lax.psum_scatter(w, axes, scatter_dimension=0, tiled=True) for w in (dw_up, dw_out, dw_down))
    small = [lax.psum_scatter(v, axes, scatter_dimension=0, tiled=True) for v in smalls]
    part, dw, extra = attention_backward(
        heads, active, all_tokens, qkv_weights, d_mixed.reshape(total, width), lengths, taps, state)
    token_parts = lax.all_to_all(part.reshape(seq, count, D), "seq", 0, 0)
    d_tokens = (d_r1 + jnp.sum(token_parts.astype(f32), axis=0)).astype(bf16)
    extra = lax.psum(lax.all_gather(extra, "seq")[:active], "fsdp")
    dw = jnp.transpose(dw.reshape(width, 3, devices, rows), (2, 3, 1, 0)).reshape(devices, rows, 3 * width)
    dw = lax.all_to_all(dw, axes, 0, 0)
    dw = jnp.sum(dw.reshape(seq, fsdp, rows, 3, width)[:active], axis=1)
    dw_query, dw_key, dw_value = (jnp.transpose(dw[:, :, j], (1, 0, 2)).reshape(rows, D) for j in range(3))
    db_query = lax.dynamic_slice_in_dim(extra[:, 0, :width].reshape(D), own, rows)
    db_value = lax.dynamic_slice_in_dim(extra[:, 0, 2 * width :].reshape(D), own, rows)
    d_kernel = jnp.transpose(extra[:, 1 : 1 + heads, :CONV].reshape(active * heads, CONV), (1, 0))
    s_b_out, s_b_up, s_b_down, s_g_attn, s_s_attn, s_g_mlp, s_s_mlp = small
    return (
        output[None], d_tokens[None], dw_query, db_query, dw_key, dw_value, db_value, s_out, s_b_out,
        s_up, s_b_up, s_down, s_b_down, s_g_attn, s_s_attn, s_g_mlp, s_s_mlp, d_kernel)


def solution(mesh):
    sizes = (mesh.shape["seq"], mesh.shape["fsdp"])
    both = ("seq", "fsdp")
    wide, flat, stream = P(both, None), P(both), P("fsdp", "seq", None)
    in_specs = (stream, stream, P("fsdp", None), wide, flat, wide, wide, flat, wide, flat, wide, flat, wide, flat,
                flat, flat, flat, flat, P())
    out_specs = (stream, stream, wide, flat, wide, wide, flat, wide, flat, wide, flat, wide, flat, flat, flat, flat,
                 flat, P())
    return jax.shard_map(partial(local, sizes), mesh=mesh, in_specs=in_specs, out_specs=out_specs, check_vma=False)
```

```python
from functools import partial
import math

import jax
import jax.numpy as jnp
from jax import lax
from jax.experimental import pallas as pl
from jax.experimental.pallas import tpu as pltpu
from jax.sharding import PartitionSpec as P

D = 768
HEADS = 12
HD = 64
FF = 3072
NLAND = 64
NS_ITERS = 6
CONV = 33
REACH = CONV // 2
DOCS = 4
SLOTS = 256
SCALE = 1.0 / math.sqrt(HD)

HIGHEST = lax.Precision.HIGHEST
epsilon = 1e-05
masked_score = -1e30
f32 = jnp.float32
bf16 = jnp.bfloat16
MESH = pl.DeviceIdType.MESH
VMEM_BYTES = 56 * 1024 * 1024


def greet(peers):
    barrier = pltpu.get_barrier_semaphore()
    for peer in peers:
        pl.semaphore_signal(barrier, inc=1, device_id=peer, device_id_type=MESH)
    pl.semaphore_wait(barrier, len(peers))


def remote(src, dst, send_sem, recv_sem, peer):
    return pltpu.make_async_remote_copy(
        src_ref=src, dst_ref=dst, send_sem=send_sem, recv_sem=recv_sem,
        device_id=peer, device_id_type=MESH,
    )


BLOCK = 256
NN = (((1,), (0,)), ((), ()))
NT = (((1,), (1,)), ((), ()))


def dot(left, right, dims=NN):
    return lax.dot_general(left, right, dims, preferred_element_type=f32)


def split(value):
    upper = value.astype(bf16)
    return upper, (value - upper.astype(f32)).astype(bf16)


def dot3(left, right, dims=NN):
    return dot(left[0], right[0], dims) + (dot(left[0], right[1], dims) + dot(left[1], right[0], dims))


def iota(shape, dim):
    return lax.broadcasted_iota(jnp.int32, shape, dim)


def doc_table(lengths_ref):
    ends, start = [], 0
    for d in range(DOCS):
        start = start + lengths_ref[d]
        ends.append(start)
    return ends


def slot_bounds(lengths_ref, shape, dim):
    ends = doc_table(lengths_ref)
    slot = iota(shape, dim)
    doc, seg = slot // NLAND, slot % NLAND
    length, end = jnp.zeros(shape, jnp.int32), jnp.zeros(shape, jnp.int32)
    for d in range(DOCS):
        length = jnp.where(doc == d, lengths_ref[d], length)
        end = jnp.where(doc == d, ends[d], end)
    start = end - length
    return start, end, start + seg * length // NLAND, start + (seg + 1) * length // NLAND


def same_doc(lengths_ref, left, right):
    ends = doc_table(lengths_ref)
    a, b = jnp.zeros(left.shape, jnp.int32), jnp.zeros(right.shape, jnp.int32)
    for d in range(DOCS):
        a = a + (left >= ends[d]).astype(jnp.int32)
        b = b + (right >= ends[d]).astype(jnp.int32)
    return a == b


def head_mask(shape, dim, h):
    return (iota(shape, dim) // HD == h).astype(f32)


def tap_index():
    return iota((128, 256), 1) - iota((128, 256), 0) - 64 + REACH


def toeplitz(taps_ref, head, mirrored):
    taps = taps_ref[...].astype(f32)
    taps = jnp.sum(jnp.where(iota(taps.shape, 0) == head, taps, 0.0), axis=0, keepdims=True)
    tap = tap_index()
    mat = jnp.zeros((128, 256), f32)
    for o in range(CONV):
        n = CONV - 1 - o if mirrored else o
        mat = jnp.where(tap == o, taps[:, n : n + 1], mat)
    return mat


def clear_edges(ref, total):
    ref[0:64, :] = jnp.zeros((64, ref.shape[1]), ref.dtype)
    ref[total + 64 : total + 128, :] = jnp.zeros((64, ref.shape[1]), ref.dtype)


def forward_math(heads, active, lengths_ref, taps_ref, tokens_ref, weights_ref, bias,
                 mixed_ref, q_ref, k_ref, v_ref, fw_ref, bw_ref, land_ref, mix_ref, a_ref, norm_ref, chain_ref,
                 v_wide, score, stage):
    total = tokens_ref.shape[0]
    width = heads * HD
    part = lax.axis_index("seq") % active
    steps = total // BLOCK
    row_start, row_end, row_low, row_top = slot_bounds(lengths_ref, (1, SLOTS), 1)
    _, _, col_low, col_top = slot_bounds(lengths_ref, (SLOTS, 1), 0)
    count = (col_top - col_low).astype(f32)
    clear_edges(v_wide, total)
    land_ref[...] = jnp.zeros(land_ref.shape, f32)

    def project(i, carry):
        at = pl.ds(pl.multiple_of(i * BLOCK, BLOCK), BLOCK)
        qkv = dot(tokens_ref[at, :], weights_ref[...]) + bias
        q, k, v = (qkv[:, j * width : (j + 1) * width] for j in range(3))
        q_low, k_low = q.astype(bf16), k.astype(bf16)
        q_ref[at, :], k_ref[at, :] = q_low, k_low
        v_ref[at, :] = v
        v_wide[pl.ds(pl.multiple_of(i * BLOCK + 64, 64), BLOCK), :] = v.astype(bf16)
        t = i * BLOCK + iota((1, BLOCK), 1)
        member = ((t >= col_low) & (t < col_top)).astype(f32).astype(bf16)
        land_ref[0] += dot(member, q_low)
        land_ref[1] += dot(member, k_low)
        return carry

    lax.fori_loop(0, steps, project, 0)
    stage("proj")
    ql, kl = land_ref[0] / count, land_ref[1] / count
    land_ref[0], land_ref[1] = ql, kl
    masks = [head_mask((1, width), 1, h) for h in range(heads)]
    ql_low = [(ql * masks[h]).astype(bf16) for h in range(heads)]
    kl_low = [(kl * masks[h]).astype(bf16) for h in range(heads)]

    def scores(i, tops):
        at = pl.ds(pl.multiple_of(i * BLOCK, BLOCK), BLOCK)
        t = i * BLOCK + iota((BLOCK, 1), 0)
        valid = (t >= row_start) & (t < row_end)
        out = []
        for h in range(heads):
            s = jnp.where(valid, SCALE * dot(q_ref[at, :], kl_low[h], NT), masked_score)
            e = jnp.exp(s - jnp.max(s, axis=1, keepdims=True))
            fw_ref[h, at, :] = (e / jnp.sum(e, axis=1, keepdims=True)).astype(bf16)
            s = jnp.where(valid, SCALE * dot(k_ref[at, :], ql_low[h], NT), masked_score)
            score[h, at, :] = s
            out.append(jnp.maximum(tops[h], jnp.max(s, axis=0, keepdims=True)))
        return tuple(out)

    tops = lax.fori_loop(0, steps, scores, tuple(jnp.full((1, SLOTS), masked_score, f32) for _ in range(heads)))
    stage("scores")

    def gather(i, carry):
        at = pl.ds(pl.multiple_of(i * BLOCK, BLOCK), BLOCK)
        v_t = split(v_ref[at, :].T)
        out = []
        for h in range(heads):
            e = jnp.exp(score[h, at, :] - tops[h])
            score[h, at, :] = e
            out.append((carry[h][0] + jnp.sum(e, axis=0, keepdims=True), carry[h][1] + dot3(v_t, split(e))))
        return tuple(out)

    sums = lax.fori_loop(0, steps, gather, tuple(
        (jnp.zeros((1, SLOTS), f32), jnp.zeros((width, SLOTS), f32)) for _ in range(heads)))
    scale = [1.0 / sums[h][0] for h in range(heads)]
    tall = [head_mask((width, 1), 0, h) for h in range(heads)]
    key_mix_t = [sums[h][1] * scale[h] * tall[h] for h in range(heads)]

    def normalize(i, carry):
        at = pl.ds(pl.multiple_of(i * BLOCK, BLOCK), BLOCK)
        for h in range(heads):
            bw_ref[h, at, :] = (score[h, at, :] * scale[h]).astype(bf16)
        return carry

    lax.fori_loop(0, steps, normalize, 0)
    stage("key_mix")

    block = iota((SLOTS, SLOTS), 0) // NLAND == iota((SLOTS, SLOTS), 1) // NLAND
    diagonal = iota((SLOTS, SLOTS), 0) == iota((SLOTS, SLOTS), 1)
    state = []
    for h in range(heads):
        s = jnp.where(block, SCALE * dot3(split(ql * masks[h]), split(kl), NT), masked_score)
        e = jnp.exp(s - jnp.max(s, axis=1, keepdims=True))
        a = e / jnp.sum(e, axis=1, keepdims=True)
        norm = jnp.sum(jnp.sum((a * a).reshape(DOCS, NLAND, SLOTS), axis=1, keepdims=True), axis=2, keepdims=True)
        norm = jnp.broadcast_to(norm, (DOCS, NLAND, SLOTS)).reshape(SLOTS, SLOTS)
        a_ref[h], norm_ref[h] = a, norm
        u = a / norm
        a_split = split(a)
        state.append((split(u), split(dot3(a_split, split(u), NT))))
    for step in range(NS_ITERS):
        fresh = []
        for h in range(heads):
            u, p = state[h]
            p_full = p[0].astype(f32) + p[1].astype(f32)
            q_full = dot3(p, p)
            q = split(q_full)
            f_full = jnp.where(diagonal, 13.0, 0.0) - 15.0 * p_full + 7.0 * q_full - dot3(p, q)
            f = split(f_full)
            for n, pair in enumerate((u, p, q, f)):
                for half in range(2):
                    chain_ref[step, h, n, half] = pair[half]
            p_next = None if step == NS_ITERS - 1 else split(0.25 * dot3(p, f))
            u_next = split(0.25 * dot3(f, u))
            fresh.append((u_next, p_next))
        stage("newton" + str(step))
        state = fresh
    mix_t = jnp.zeros((width, SLOTS), f32)
    key_t = jnp.zeros((width, SLOTS), f32)
    for h in range(heads):
        u = state[h][0]
        chain_ref[NS_ITERS, h, 0, 0], chain_ref[NS_ITERS, h, 0, 1] = u
        mix_t = mix_t + dot3(split(key_mix_t[h]), u)
        key_t = key_t + key_mix_t[h]
    mix_ref[0], mix_ref[1] = mix_t, key_t
    stage("mix")
    mix_low = [(mix_t * tall[h]).astype(bf16) for h in range(heads)]
    mats = [toeplitz(taps_ref, part * heads + h, False) for h in range(heads)]

    def output(i, carry):
        at = pl.ds(pl.multiple_of(i * 128, 128), 128)
        t = i * 128 + iota((128, 1), 0)
        near = same_doc(lengths_ref, t, i * 128 - 64 + iota((1, 256), 1))
        window = v_wide[pl.ds(pl.multiple_of(i * 128, 128), 256), :]
        out = jnp.zeros((128, width), f32)
        for h in range(heads):
            out = out + dot(fw_ref[h, at, :], mix_low[h], NT)
            conv = dot(jnp.where(near, mats[h], 0.0).astype(bf16), window)
            out = out + conv * masks[h]
        mixed_ref[at, :] = out.astype(bf16)
        return carry

    lax.fori_loop(0, total // 128, output, 0)


def forward_kernel(heads, active, lengths_ref, taps_ref, tokens_ref, weights_ref, bias_ref, *refs):
    bias = jnp.sum(bias_ref[...].astype(f32), axis=0)[0:1]
    forward_math(heads, active, lengths_ref, taps_ref, tokens_ref, weights_ref, bias, *refs, lambda n: None)


def attention_forward(heads, active, tokens, weights, bias, lengths, taps):
    total = tokens.shape[0]
    width = heads * HD
    shape = jax.ShapeDtypeStruct
    vmem, smem = (pl.BlockSpec(memory_space=m) for m in (pltpu.VMEM, pltpu.SMEM))
    chain = (heads, 4, 2, SLOTS, SLOTS)
    return pl.pallas_call(
        partial(forward_kernel, heads, active),
        out_shape=(
            shape((total, width), bf16),
            shape((total, width), bf16),
            shape((total, width), bf16),
            shape((total, width), f32),
            shape((heads, total, SLOTS), bf16),
            shape((heads, total, SLOTS), bf16),
            shape((2, SLOTS, width), f32),
            shape((2, width, SLOTS), f32),
            shape((heads, SLOTS, SLOTS), f32),
            shape((heads, SLOTS, SLOTS), f32),
            shape((NS_ITERS + 1, *chain), bf16),
        ),
        in_specs=[smem, vmem, vmem, vmem, vmem],
        out_specs=tuple([vmem] * 11),
        scratch_shapes=[
            pltpu.VMEM((total + 128, width), bf16),
            pltpu.VMEM((heads, total, SLOTS), f32),
        ],
        compiler_params=pltpu.CompilerParams(vmem_limit_bytes=VMEM_BYTES),
    )(lengths, taps, tokens, weights, bias)


def backward_math(heads, active, lengths_ref, taps_ref, tokens_ref, weights_ref, dout_ref, q_ref, k_ref, v_ref, fw_ref,
                  bw_ref, land_ref, mix_ref, a_ref, norm_ref, chain_ref, dw_ref, extra_ref,
                  v_wide, d_wide, dq_acc, dk_acc, dv_acc, spread, tap_rows, dqkv, stage):
    total = tokens_ref.shape[0]
    width = heads * HD
    part = lax.axis_index("seq") % active
    steps = total // BLOCK
    _, _, row_low, row_top = slot_bounds(lengths_ref, (1, SLOTS), 1)
    inverse = 1.0 / (row_top - row_low).astype(f32)
    clear_edges(v_wide, total)
    clear_edges(d_wide, total)
    masks = [head_mask((1, width), 1, h) for h in range(heads)]
    tall = [head_mask((width, 1), 0, h) for h in range(heads)]
    ql, kl = land_ref[0], land_ref[1]
    mix_t, key_t = mix_ref[0], mix_ref[1]
    kl_low = [(kl * masks[h]).astype(bf16) for h in range(heads)]
    ql_low = [(ql * masks[h]).astype(bf16) for h in range(heads)]
    mix_low = [(mix_t * tall[h]).astype(bf16) for h in range(heads)]

    def front(i, carry):
        at = pl.ds(pl.multiple_of(i * BLOCK, BLOCK), BLOCK)
        inner = pl.ds(pl.multiple_of(i * BLOCK + 64, 64), BLOCK)
        do = dout_ref[at, :]
        d_wide[inner, :] = do
        v_wide[inner, :] = v_ref[at, :].astype(bf16)
        do_t = do.astype(f32).T.astype(bf16)
        q_t = q_ref[at, :].astype(f32).T.astype(bf16)
        dq = jnp.zeros((BLOCK, width), f32)
        out = []
        for h in range(heads):
            fw = fw_ref[h, at, :]
            wide = fw.astype(f32)
            d_fw = dot(do, mix_low[h])
            ds = (SCALE * wide * (d_fw - jnp.sum(wide * d_fw, axis=1, keepdims=True))).astype(bf16)
            dq = dq + dot(ds, kl_low[h])
            out.append((carry[h][0] + dot(do_t, fw), carry[h][1] + dot(q_t, ds)))
        dq_acc[at, :] = dq
        return tuple(out)

    zeros = jnp.zeros((width, SLOTS), f32)
    sums = lax.fori_loop(0, steps, front, tuple((zeros, zeros) for _ in range(heads)))
    stage("front")
    dmix_t = [sums[h][0] * tall[h] for h in range(heads)]
    dkl_t = zeros
    for h in range(heads):
        dkl_t = dkl_t + sums[h][1] * tall[h]
    key = key_t.T
    ql_t = ql.T
    block = iota((SLOTS, SLOTS), 0) // NLAND == iota((SLOTS, SLOTS), 1) // NLAND
    du, dp, dkey_t = [], [None] * heads, []
    for h in range(heads):
        pair = split(dmix_t[h])
        du.append(jnp.where(block, dot3(split(key), pair), 0.0))
        dkey_t.append(dot3(pair, (chain_ref[NS_ITERS, h, 0, 0], chain_ref[NS_ITERS, h, 0, 1]), NT))
    for step in range(NS_ITERS - 1, -1, -1):
        stage("newton" + str(step))
        for h in range(heads):
            u, p, q, f = ((chain_ref[step, h, n, 0], chain_ref[step, h, n, 1]) for n in range(4))
            du_pair = split(du[h])
            df = 0.25 * dot3(du_pair, u, NT)
            du[h] = 0.25 * dot3(f, du_pair)
            if dp[h] is not None:
                dp_pair = split(dp[h])
                df = df + 0.25 * dot3(p, dp_pair)
                base = 0.25 * dot3(dp_pair, f)
            else:
                base = 0.0
            df_pair = split(df)
            dq = split(7.0 * df - dot3(p, df_pair))
            dp[h] = base - 15.0 * df - dot3(df_pair, q) + (dot3(dq, p) + dot3(p, dq))
    dql = jnp.zeros((SLOTS, width), f32)
    for h in range(heads):
        a, norm = a_ref[h], norm_ref[h]
        u0 = chain_ref[0, h, 0, 0].astype(f32) + chain_ref[0, h, 0, 1].astype(f32)
        p0 = chain_ref[0, h, 1, 0].astype(f32) + chain_ref[0, h, 1, 1].astype(f32)
        a_pair = split(a)
        inner = dp[h] * p0 + du[h] * u0
        inner = jnp.sum(jnp.sum(inner.reshape(DOCS, NLAND, SLOTS), axis=1, keepdims=True), axis=2, keepdims=True)
        inner = jnp.broadcast_to(inner, (DOCS, NLAND, SLOTS)).reshape(SLOTS, SLOTS)
        da = (dot3(split(dp[h] + dp[h].T), a_pair) + du[h] - 2.0 * a * inner) / norm
        dsa = split(SCALE * a * (da - jnp.sum(a * da, axis=1, keepdims=True)))
        dql = dql + dot3(dsa, split(kl * masks[h]))
        dkl_t = dkl_t + dot3(split(ql_t * tall[h]), dsa)
    stage("core")
    dkey_low = [x.astype(bf16) for x in dkey_t]
    row_dot = [jnp.sum(dkey_t[h] * key_t, axis=0, keepdims=True) for h in range(heads)]
    dkey = [x.T.astype(bf16) for x in dkey_t]

    def back(i, carry):
        at = pl.ds(pl.multiple_of(i * BLOCK, BLOCK), BLOCK)
        v = v_ref[at, :].astype(bf16)
        k_t = k_ref[at, :].astype(f32).T.astype(bf16)
        dk, dv = jnp.zeros((BLOCK, width), f32), jnp.zeros((BLOCK, width), f32)
        out = []
        for h in range(heads):
            bw = bw_ref[h, at, :]
            ds = (SCALE * bw.astype(f32) * (dot(v, dkey_low[h]) - row_dot[h])).astype(bf16)
            dk = dk + dot(ds, ql_low[h])
            dv = dv + dot(bw, dkey[h])
            out.append(carry[h] + dot(k_t, ds))
        dk_acc[at, :] = dk
        dv_acc[at, :] = dv
        return tuple(out)

    sums = lax.fori_loop(0, steps, back, tuple(zeros for _ in range(heads)))
    stage("back")
    dql_t = zeros
    for h in range(heads):
        dql_t = dql_t + sums[h] * tall[h]
    dql_low = ((dql.T + dql_t) * inverse).astype(bf16)
    dkl_low = (dkl_t * inverse).astype(bf16)
    mats = [toeplitz(taps_ref, part * heads + h, True) for h in range(heads)]
    spread[...] = jnp.zeros(spread.shape, f32)

    def convolve(i, carry):
        at = pl.ds(pl.multiple_of(i * 128, 128), 128)
        t = i * 128 + iota((128, 1), 0)
        near = same_doc(lengths_ref, t, i * 128 - 64 + iota((1, 256), 1))
        window = pl.ds(pl.multiple_of(i * 128, 128), 256)
        d_window, v_window = d_wide[window, :], v_wide[window, :]
        do = dout_ref[at, :].astype(f32)
        dv = dv_acc[at, :]
        for h in range(heads):
            dv = dv + dot(jnp.where(near, mats[h], 0.0).astype(bf16), d_window) * masks[h]
            spread[h] += jnp.where(near, dot((do * masks[h]).astype(bf16), v_window, NT), 0.0)
        dv_acc[at, :] = dv
        return carry

    lax.fori_loop(0, total // 128, convolve, 0)
    stage("conv")

    def finish(i, carry):
        at = pl.ds(pl.multiple_of(i * BLOCK, BLOCK), BLOCK)
        t = i * BLOCK + iota((BLOCK, 1), 0)
        member = ((t >= row_low) & (t < row_top)).astype(f32).astype(bf16)
        dq = dq_acc[at, :] + dot(member, dql_low, NT)
        dk = dk_acc[at, :] + dot(member, dkl_low, NT)
        grads = jnp.concatenate([dq.astype(bf16), dk.astype(bf16), dv_acc[at, :].astype(bf16)], axis=1)
        dqkv[at, :] = grads
        return carry + jnp.sum(grads.astype(f32), axis=0, keepdims=True)

    extra_ref[...] = jnp.zeros(extra_ref.shape, f32)
    extra_ref[0:1, :] = lax.fori_loop(0, steps, finish, jnp.zeros((1, 3 * width), f32))
    stage("parts")
    dw_ref[...] = jnp.zeros(dw_ref.shape, f32)

    def weigh(i, carry):
        at = pl.ds(pl.multiple_of(i * BLOCK, BLOCK), BLOCK)
        for n in range(3):
            grads = dqkv[at, n * width : (n + 1) * width].astype(f32).T.astype(bf16)
            dw_ref[:, n * D : (n + 1) * D] += dot(grads, tokens_ref[at, :])
        return carry

    lax.fori_loop(0, steps, weigh, 0)
    tap = tap_index()
    tap_rows[...] = jnp.zeros(tap_rows.shape, f32)
    for h in range(heads):
        for o in range(CONV):
            tap_rows[o : o + 1, :] = jnp.sum(jnp.where(tap == o, spread[h], 0.0), axis=0, keepdims=True)
        extra_ref[1 + h : 2 + h, 0:128] = jnp.sum(tap_rows[...].T, axis=0, keepdims=True)


def backward_kernel(heads, active, lengths_ref, taps_ref, tokens_ref, weights_ref, *refs):
    inputs, part_ref, outputs, dqkv = refs[:11], refs[11], refs[12:-1], refs[-1]
    backward_math(heads, active, lengths_ref, taps_ref, tokens_ref, weights_ref, *inputs, *outputs, dqkv, lambda point: None)

    def project(i, carry):
        at = pl.ds(pl.multiple_of(i * BLOCK, BLOCK), BLOCK)
        part = dot(dqkv[at, :], weights_ref[...], NT)
        part_ref[at, :] = jnp.where(lax.axis_index("seq") < active, part, 0.0).astype(bf16)
        return carry

    lax.fori_loop(0, tokens_ref.shape[0] // BLOCK, project, 0)


def attention_backward(heads, active, tokens, weights, dout, lengths, taps, state):
    total = tokens.shape[0]
    width = heads * HD
    shape = jax.ShapeDtypeStruct
    vmem, smem = (pl.BlockSpec(memory_space=m) for m in (pltpu.VMEM, pltpu.SMEM))
    return pl.pallas_call(
        partial(backward_kernel, heads, active),
        out_shape=(
            shape((total, D), bf16),
            shape((width, 3 * D), f32),
            shape((8, 3 * width), f32),
        ),
        in_specs=[smem] + [vmem] * 14,
        out_specs=tuple([vmem] * 3),
        scratch_shapes=[
            pltpu.VMEM((total + 128, width), bf16),
            pltpu.VMEM((total + 128, width), bf16),
            pltpu.VMEM((total, width), f32),
            pltpu.VMEM((total, width), f32),
            pltpu.VMEM((total, width), f32),
            pltpu.VMEM((heads, 128, 256), f32),
            pltpu.VMEM((128, 256), f32),
            pltpu.VMEM((total, 3 * width), bf16),
        ],
        compiler_params=pltpu.CompilerParams(vmem_limit_bytes=VMEM_BYTES),
    )(lengths, taps, tokens, weights, dout, *state)
def rows_at(index, count):
    return pl.ds(pl.multiple_of(index * count, 8), count)


class Links:
    def __init__(self):
        s, f = lax.axis_index("seq"), lax.axis_index("fsdp")
        self.s, self.f = s, f
        self.z, self.y, self.x, self.c = s // 2, s % 2, f // 2, f % 2
        self.oy, self.ox, self.oc = 1 - self.y, 1 - self.x, 1 - self.c
        self.seq_peers = [((s + j) % 8, f) for j in range(1, 8)]
        self.fsdp_peers = [(s, (f + i) % 4) for i in range(1, 4)]
        self.z_peers = [((self.z + j) % 4 * 2 + self.y, f) for j in range(1, 4)]
        self.above, self.below = self.z_peers[0], self.z_peers[2]
        self.y_peer = (self.z * 2 + self.oy, f)
        self.x_peer = (s, self.ox * 2 + self.c)
        self.c_peer = (s, self.x * 2 + self.oc)
        self.started = []

    def send(self, src, dst, sems, index, peer):
        copy = remote(src, dst, sems[0].at[index], sems[1].at[index], peer)
        copy.start()
        self.started.append(copy)
        return copy

    def drain(self):
        for copy in self.started:
            copy.wait_send()
        self.started = []


def begin(copies):
    for copy in copies:
        copy.start()


def done(copies):
    for copy in copies:
        copy.wait_recv()


def centre(value):
    value = value - jnp.mean(value, axis=1, keepdims=True)
    scale = lax.rsqrt(jnp.mean(value * value, axis=1, keepdims=True) + epsilon)
    return value * scale, scale


def uncentre(grad, normal, scale):
    return scale * (grad - jnp.mean(grad, axis=1, keepdims=True)
                    - normal * jnp.mean(grad * normal, axis=1, keepdims=True))


def column_sum(value):
    return jnp.sum(value, axis=0, keepdims=True)


def token_math(own, cot, attention, up_ref, down_ref, out_ref, vec_ref, gelu_ref, slope_ref, output_ref, dr1_ref, small_ref,
               weights_done):
    vec = vec_ref[...]
    b_out, b_down, g_attn, s_attn, g_mlp, s_mlp = (vec[j : j + 1] for j in range(6))
    normal_one, scale_one = centre(own.astype(f32) + dot(attention, out_ref[...]) + b_out)
    hidden = normal_one * g_attn + s_attn
    hidden_low = hidden.astype(bf16)
    count = hidden.shape[0]

    def upward(i, down):
        cols = pl.ds(pl.multiple_of(i * D, D), D)
        up = dot(hidden_low, up_ref[:, cols]) + vec_ref[pl.ds(6 + i, 1), :]
        share = 0.5 + 0.5 * lax.erf(up * math.sqrt(0.5))
        gelu = (up * share).astype(bf16)
        gelu_ref[:, cols] = gelu
        slope_ref[:, cols] = share + up * (math.sqrt(0.5 / math.pi) * jnp.exp(-0.5 * up * up))
        return down + dot(gelu, down_ref[cols, :])

    down = lax.fori_loop(0, FF // D, upward, jnp.zeros((count, D), f32))
    normal_two, scale_two = centre(hidden + down + b_down)
    output_ref[...] = (normal_two * g_mlp + s_mlp).astype(bf16)
    cot = cot.astype(f32)
    d_r2 = uncentre(cot * g_mlp, normal_two, scale_two)
    d_down = d_r2.astype(bf16)
    small_ref[...] = jnp.zeros(small_ref.shape, f32)
    small_ref[1:2, :] = column_sum(d_down.astype(f32))
    small_ref[4:5, :] = column_sum(cot * normal_two)
    small_ref[5:6, :] = column_sum(cot)
    hidden_t = hidden_low.astype(f32).T.astype(bf16)

    def downward(i, d_hidden):
        cols = pl.ds(pl.multiple_of(i * D, D), D)
        d_gelu = dot(d_down, down_ref[cols, :], NT)
        d_up = (d_gelu * slope_ref[:, cols]).astype(bf16)
        small_ref[pl.ds(6 + i, 1), :] = column_sum(d_up.astype(f32))
        d_hidden = d_hidden + dot(d_up, up_ref[:, cols], NT)
        gelu_t = gelu_ref[:, cols].astype(f32).T.astype(bf16)
        down_ref[cols, :] = dot(gelu_t, d_down).astype(bf16)
        up_ref[:, cols] = dot(hidden_t, d_up).astype(bf16)
        return d_hidden

    d_hidden = lax.fori_loop(0, FF // D, downward, d_r2)
    weights_done()
    d_r1 = uncentre(d_hidden * g_attn, normal_one, scale_one)
    dr1_ref[...] = d_r1
    d_out = d_r1.astype(bf16)
    small_ref[0:1, :] = column_sum(d_out.astype(f32))
    small_ref[2:3, :] = column_sum(d_hidden * normal_one)
    small_ref[3:4, :] = column_sum(d_hidden)
    d_attention = dot(d_out, out_ref[...], NT).astype(bf16)
    out_ref[...] = dot(attention.astype(f32).T.astype(bf16), d_out).astype(bf16)
    return d_attention


def select_lanes(rows, offset, base):
    wide = rows.shape[1]
    choose = (iota((wide, 128), 0) + base == iota((wide, 128), 1) + offset).astype(f32).astype(bf16)
    first = rows.astype(bf16)
    second = (rows - first.astype(f32)).astype(bf16)
    third = (rows - first.astype(f32) - second.astype(f32)).astype(bf16)
    return dot(first, choose) + dot(second, choose) + dot(third, choose)


GATHER = {"proj": "w1", "scores": "w2", "key_mix": "o0", "mix": "o1 c0", "end": "o2 c1 c2"}
PLAN = {
    "start": "f0 m0", "front": "f1", "newton3": "s0 f2 m1", "core": "s1 t0 f3 m2", "parts": "y0 s2 t1",
    "end": "s3 z0 t2 z1 z2 w0 z3 t3",
}


VECTORS = ("b_out", "b_down", "g_attn", "s_attn", "g_mlp", "s_mlp", "b_up", "b_query", "b_value")


def layer_kernel(heads, active, names, *refs):
    r = dict(zip(names, refs))
    net = Links()
    s, f, z, y, x, c = net.s, net.f, net.z, net.y, net.x, net.c
    oy, ox, oc = net.oy, net.ox, net.oc
    width = heads * HD
    own_ref, tokens_ref, weights_ref = r["own"], r["tokens"], r["weights"]
    count, rows = own_ref.shape[0], r["wq"].shape[0]
    mine = rows_at(s, count)
    index = s * 4 + f

    loads = [pltpu.make_async_copy(r["in_" + name], r[name], r["load_sems"].at[n])
             for n, name in enumerate(("own", "wq", "wk", "wv", "cot", "taps") + VECTORS)]
    begin(loads)
    greet(net.seq_peers + net.fsdp_peers)
    for copy in loads:
        copy.wait()

    def pair(name):
        return r[name + "_send"], r[name + "_recv"]

    def token_z(zz, t, up):
        here = tokens_ref.at[rows_at(zz * 2 + y, count)]
        n = 2 * t + (0 if up else 1)
        return remote(own_ref if t == 0 else here, here, r["tz_send"].at[n], r["tz_recv"].at[n], net.above if up else net.below)

    def token_y(zz, own=False):
        here = tokens_ref.at[rows_at(zz * 2 + y, count)]
        return remote(own_ref if own else here, here, r["ty_send"].at[zz], r["ty_recv"].at[zz], net.y_peer)

    pieces = ((r["in_wup"], r["up"], rows), (r["placed"], r["full_small"], 16), (r["in_wout"], r["out"], rows),
              (r["in_wdown"], r["down"], 4 * rows))
    early, late = (0, 1, 2), (3,)

    def slot(zz, sy, sx):
        return (zz * 2 + sy) * 4 + sx * 2 + c

    def weight(m, own, where, send_sem, recv_sem, peer):
        src, full, n = pieces[m]
        here = full.at[rows_at(where, n)]
        return remote(src if own else here, here, send_sem, recv_sem, peer)

    def weight_z(zz, t, up):
        n = 2 * t + (0 if up else 1)
        peer = net.above if up else net.below
        return [weight(m, t == 0, slot(zz, y, x), r["gz_send"].at[n, m], r["gz_recv"].at[n, m], peer) for m in range(4)]

    def to_y(zz, m, own=False):
        return weight(m, own, slot(zz, y, x), r["gy_send"].at[zz, m], r["gy_recv"].at[zz, m], net.y_peer)

    def to_x(zz, m, own=False):
        return weight(m, own, slot(zz, y, x), r["gx_send"].at[zz, m], r["gx_recv"].at[zz, m], net.x_peer)

    def again_x(zz, m):
        return weight(m, False, slot(zz, oy, x), r["gx_send"].at[zz, 4 + m], r["gx_recv"].at[zz, 4 + m], net.x_peer)

    def again_y(zz, m):
        return weight(m, False, slot(zz, y, ox), r["gy_send"].at[zz, 4 + m], r["gy_recv"].at[zz, 4 + m], net.y_peer)

    def to_core(zz, n, m, own=False):
        sy, sx = ((y, x), (oy, x), (y, ox), (oy, ox))[n]
        return weight(m, own, slot(zz, sy, sx), r["gc_send"].at[zz, n, m], r["gc_recv"].at[zz, n, m], net.c_peer)

    def spread(zz):
        begin([to_y(zz, m) for m in early] + [to_x(zz, m) for m in late])
        begin([to_x(zz, m) for m in early] + [to_y(zz, m) for m in late])
        begin([to_core(zz, 0, m) for m in range(4)])

    def onward(zz):
        for m in early:
            done([to_y(zz, m)])
            begin([again_x(zz, m)])
        for m in late:
            done([to_x(zz, m)])
            begin([again_y(zz, m)])
        done([to_y(zz, m) for m in late])
        begin([to_core(zz, 1, m) for m in range(4)])
        done([to_x(zz, m) for m in early])
        begin([to_core(zz, 2, m) for m in range(4)])

    def corner(zz):
        done([again_x(zz, m) for m in early] + [again_y(zz, m) for m in late])
        begin([to_core(zz, 3, m) for m in range(4)])

    def column(t, act):
        for up in (True, False):
            zz = z - 1 - t if up else z + 1 + t

            @pl.when(zz >= 0 if up else zz < 4)
            def _():
                act(zz, up)

    def onto_z(t, act):
        for up in (True, False):
            zz = z - t if up else z + t

            @pl.when((zz >= 0) & (z < 3) if up else (zz < 4) & (z > 0))
            def _():
                act(zz, t, up)

    onto_z(0, lambda zz, t, up: token_z(zz, t, up).start())
    token_y(z, True).start()
    begin([to_x(z, m, True) for m in (3, 0, 2)] + [to_y(z, m, True) for m in (0, 2, 3)])
    vectors = r["vectors"]
    vectors[...] = jnp.zeros(vectors.shape, f32)
    for n, name in enumerate(VECTORS):
        vector = r[name][...].astype(f32)
        vectors[n : n + 1, 0 : vector.shape[0]] = vector.reshape(1, vector.shape[0])
    vectors = vectors[...].astype(bf16)
    for j in range(16):
        base, row = (96, 6) if 6 <= j < 10 else (24, j)
        lead = (j - 6) * D if 6 <= j < 10 else 0
        if j in (10, 11):
            row = j - 3
        if j >= 12:
            break
        base = 4 * rows if base == 96 else rows
        lane = iota((128, D), 1) + lead - base * index
        choose = ((lane == iota((128, D), 0)) & (lane < base)).astype(f32).astype(bf16)
        value = dot(vectors, choose)[row : row + 1, :]
        r["place"][j : j + 1, :] = value
    r["place"][12:16, :] = jnp.zeros((4, D), f32)
    r["placed"][...] = r["place"][...].astype(bf16)
    pack, landed = r["pack"], r["landed"]
    for b in range(active):
        for n, name in enumerate(("wq", "wk", "wv")):
            pack[b, 0:rows, n * width : (n + 1) * width] = r[name][:, b * width : (b + 1) * width]
        pack[b, rows:, :] = jnp.zeros((pack.shape[1] - rows, 3 * width), bf16)
        for n, j in ((0, 10), (2, 11)):
            bias = jnp.broadcast_to(r["place"][j : j + 1, b * width : (b + 1) * width], (8, width))
            pack[b, rows : rows + 8, n * width : (n + 1) * width] = jnp.where(iota((8, width), 0) == 0, bias, 0.0).astype(bf16)
    from_seq = [
        net.send(pack.at[(s + j + 1) % 8 % active], landed.at[f, s], pair("ps"), j, net.seq_peers[j]) for j in range(7)]
    begin([to_x(z, 1, True), to_y(z, 1, True)] + [to_core(z, 0, m, True) for m in range(4)])
    landed[f, s] = pack[s % active]
    tokens_ref[mine, :] = own_ref[...]
    keep = [pltpu.make_async_copy(src, full.at[rows_at(slot(z, y, x), n)], r["keep_sems"].at[m])
            for m, (src, full, n) in enumerate(pieces)]
    begin(keep)

    def weights_on(t):
        def came(zz, up):
            done(weight_z(zz, t, up))
            spread(zz)

        column(t, came)
        if t < 2:
            onto_z(t + 1, lambda zz, t, up: begin(weight_z(zz, t, up)))

    def tokens_on(t):
        def came(zz, up):
            token_z(zz, t, up).wait_recv()
            token_y(zz).start()

        column(t, came)
        if t < 2:
            onto_z(t + 1, lambda zz, t, up: token_z(zz, t, up).start())

    tokens_on(0)
    onto_z(0, lambda zz, t, up: begin(weight_z(zz, t, up)))
    tokens_on(1)
    onward(z)
    done(from_seq)
    from_fsdp = [net.send(landed.at[f], landed.at[f], pair("pf"), i, net.fsdp_peers[i]) for i in range(3)]
    tokens_on(2)
    weights_on(0)
    corner(z)

    gather_steps = {
        "w": weights_on, "o": lambda t: column(t, lambda zz, up: onward(zz)), "c": lambda t: column(t, lambda zz, up: corner(zz))}

    def gather_stage(point):
        for step in GATHER.get(point, "").split():
            gather_steps[step[0]](int(step[1]))

    for zz in range(4):
        token_y(zz).wait_recv()
    done(from_fsdp)
    bias = jnp.zeros((8, 3 * width), f32)
    for a in range(4):
        for b in range(8):
            weights_ref[rows * (b * 4 + a) : rows * (b * 4 + a + 1), :] = landed[a, b, 0:rows, :]
            bias = bias + landed[a, b, rows : rows + 8, :].astype(f32)

    state = [r[name] for name in ("q", "k", "v", "fw", "bw", "land", "mix", "a", "norm", "chain")]
    lengths_ref, taps_ref, mixed = r["lengths"], r["taps"], r["d_wide"].at[0 : 8 * count, :]
    forward_math(heads, active, lengths_ref, taps_ref, tokens_ref, weights_ref, bias[0:1], mixed, *state,
                 r["v_wide"], r["score"], gather_stage)

    att = r["att"]
    last = [net.send(mixed.at[rows_at((s + j + 1) % 8, count)], att.at[s], pair("at"), j, net.seq_peers[j]) for j in range(7)]
    att[s] = mixed[mine, :]
    gather_stage("end")
    for zz in range(4):
        for n in range(4):
            done([to_core(zz, n, m) for m in range(4)])
    for copy in keep:
        copy.wait()

    def sent(zz, t, up):
        token_z(zz, t, up).wait_send()
        for copy in weight_z(zz, t, up):
            copy.wait_send()

    net.drain()
    for t in range(3):
        onto_z(t, sent)
    for zz in range(4):
        token_y(zz).wait_send()
        for m in range(4):
            to_y(zz, m).wait_send()
            to_x(zz, m).wait_send()
            (again_x if m in early else again_y)(zz, m).wait_send()
            for n in range(4):
                to_core(zz, n, m).wait_send()
    vec = jnp.zeros((16, D), f32)
    for n in range(32):
        vec = vec + r["full_small"][16 * n : 16 * n + 16, :].astype(f32)
    r["vec"][...] = vec
    done(last)
    peer_weights = net.send(weights_ref, r["peer_weights"], pair("wp"), 0, net.y_peer)

    sums = ((r["up"], r["acc_up"], r["got_up"], r["far_up"], rows), (r["out"], r["acc_out"], r["got_out"], r["far_out"], rows),
            (r["down"], r["acc_down"], r["got_down"], r["far_down"], 4 * rows))
    places = ((0, 0), (0, 1), (1, 0), (1, 1))
    moved = {}

    def owner(k, sy, sx, sc):
        return ((z + k + 1) % 4 * 2 + sy) * 4 + sx * 2 + sc

    def to_sibling(pieces_of):
        for k in range(4):
            for m, (sy, sx) in enumerate(places):
                for n in pieces_of:
                    full, acc, _, _, size = sums[n]
                    moved["c", k, m, n] = net.send(
                        full.at[rows_at(owner(k, sy, sx, oc), size)], acc.at[k, sy, sx], pair("rc"), (4 * k + m, n), net.c_peer)

    attention = jnp.concatenate([att[b] for b in range(active)], axis=1)
    d_attention = token_math(
        own_ref[...], r["cot"][...], attention, r["up"], r["down"], r["out"], r["vec"], r["gelu"], r["slope"],
        r["output"], r["dr1"], r["small"], lambda: to_sibling((0, 2)))
    store = [pltpu.make_async_copy(r["output"], r["o_output"], r["store_sems"].at[0])]
    begin(store)
    dattn, dout = r["dattn"], r["dout"]
    for b in range(active):
        dattn[b] = d_attention[:, b * width : (b + 1) * width]
    from_seq = [
        net.send(dattn.at[(s + j + 1) % 8 % active], dout.at[mine], pair("dt"), j, net.seq_peers[j]) for j in range(7)]
    dout[mine, :] = dattn[s % active]
    to_sibling((1,))
    small_put, small_got, small_sum = r["small_put"], r["small_got"], r["small_sum"]
    small_put[...] = r["small"][...].astype(bf16)
    moved["m", 0] = net.send(small_put, small_got.at[0], pair("rm"), 0, net.c_peer)

    def add(target, more, more_index):
        deep, wide = target.shape

        def one(i, carry):
            if wide > D:
                cols = pl.ds(pl.multiple_of(i * D, D), D)
                here, there = (slice(None), cols), (rows_at(more_index, deep), cols)
            else:
                here, there = (rows_at(i, rows), slice(None)), (pl.ds(pl.multiple_of(more_index * deep + i * rows, 8), rows), slice(None))
            target[here] = (target[here].astype(f32) + more[there].astype(f32)).astype(bf16)
            return carry

        lax.fori_loop(0, deep * wide // (rows * D), one, 0)

    def first(k):
        for m, (sy, sx) in enumerate(places):
            for n, (full, acc, _, _, _) in enumerate(sums):
                moved["c", k, m, n].wait_recv()
                add(acc.at[k, sy, sx], full, owner(k, sy, sx, c))
        for i in range(2):
            for n, (_, acc, got, _, _) in enumerate(sums):
                if n < 2:
                    moved["1", k, i, n] = net.send(acc.at[k, i, ox], got.at[k, i], pair("rx"), (3 * k + i, n), net.x_peer)
                else:
                    moved["1", k, i, n] = net.send(acc.at[k, oy, i], got.at[k, i], pair("ry"), (3 * k + i, 0), net.y_peer)

    def second(k):
        for n, (_, acc, got, _, _) in enumerate(sums):
            for i in range(2):
                moved["1", k, i, n].wait_recv()
                add(acc.at[k, i, x] if n < 2 else acc.at[k, y, i], got.at[k, i], 0)
            if n < 2:
                moved["2", k, n] = net.send(acc.at[k, oy, x], got.at[k, 2], pair("ry"), (3 * k + 2, n), net.y_peer)
            else:
                moved["2", k, n] = net.send(acc.at[k, y, ox], got.at[k, 2], pair("rx"), (3 * k + 2, 0), net.x_peer)

    def third(k):
        for n, (_, acc, got, far, _) in enumerate(sums):
            moved["2", k, n].wait_recv()
            add(acc.at[k, y, x], got.at[k, 2], 0)
            if k < 3:
                moved["3", k, n] = net.send(acc.at[k, y, x], far.at[k], pair("rz"), (k, n), net.z_peers[k])

    def small_step(n):
        before = small_put if n == 0 else small_sum.at[n - 1]
        moved["m", n].wait_recv()
        small_sum[n] = (before[...].astype(f32) + small_got[n].astype(f32)).astype(bf16)
        if n < 2:
            moved["m", n + 1] = net.send(
                small_sum.at[n], small_got.at[n + 1], pair("rm"), n + 1, net.x_peer if n == 0 else net.y_peer)
        else:
            for j in range(3):
                moved["m", 3 + j] = net.send(small_sum.at[2], small_got.at[3 + j], pair("rm"), 3 + j, net.z_peers[j])

    steps = {"f": first, "s": second, "t": third, "m": small_step}

    def scatter_stage(point):
        for step in PLAN.get(point, "").split():
            steps[step[0]](int(step[1]))

    scatter_stage("start")
    done(from_seq)
    dqkv, y_got, z_got = r["dqkv"], r["y_got"], r["z_got"]
    over_y = []

    def send_gradients(_):
        for j in range(4):
            there = rows_at((z + j + 1) % 4 * 2 + oy, count)
            over_y.append(net.send(dqkv.at[there], y_got.at[j], pair("dy"), j, net.y_peer))

    steps["y"] = send_gradients
    score = r["score"]
    accumulators = [score.at[0, :, 0:width], score.at[0, :, width : 2 * width], score.at[1, :, 0:width]]
    dw_t = r["slope"].at[:, 0 : 3 * D]
    backward_math(
        heads, active, lengths_ref, taps_ref, tokens_ref, weights_ref, dout, *state, dw_t, r["extra"],
        r["v_wide"], r["d_wide"], *accumulators, r["spread"], r["tap_rows"], r["dqkv"],
        scatter_stage)

    first_put, first_got, second_put, second_got = landed, r["first_got"], r["second_put"], r["second_got"]
    dw = [dw_t[:, n * D : (n + 1) * D].T.astype(bf16) for n in range(3)]
    tail = r["extra"][...].astype(bf16)
    for a in range(4):
        for b in range(8):
            start = rows * (4 * b + a)
            for n in range(3):
                first_put[a, b, 0:rows, n * width : (n + 1) * width] = dw[n][start : start + rows, :]
            first_put[a, b, rows:, :] = tail
    from_fsdp = [
        net.send(first_put.at[(f + i + 1) % 4], first_got.at[f], pair("wf"), i, net.fsdp_peers[i]) for i in range(3)]
    first_got[f] = first_put[f]
    over_z, held = [], {}

    def token_parts(j):
        done([over_y[j]])
        here = rows_at((z + j + 1) % 4 * 2 + y, count)
        value = jnp.where(s < active, dot(dqkv[here, :], weights_ref[...], NT), 0.0)
        value = value + jnp.where(z * 2 + oy < active, dot(y_got[j], r["peer_weights"][...], NT), 0.0)
        if j < 3:
            z_put = r["gelu"].at[:, j * D : (j + 1) * D]
            z_put[...] = value.astype(bf16)
            over_z.append(net.send(z_put, z_got.at[j], pair("dz"), j, net.z_peers[j]))
        else:
            held["kept"] = value + r["dr1"][...]

    def weight_parts(_):
        done(from_fsdp)
        for b in range(8):
            value = first_got[0, b].astype(f32)
            for a in range(1, 4):
                value = value + first_got[a, b].astype(f32)
            second_put[b] = value.astype(bf16)
        held["seq"] = [
            net.send(second_put.at[(s + j + 1) % 8], second_got.at[s], pair("ws"), j, net.seq_peers[j]) for j in range(7)]
        second_got[s] = second_put[s]

    steps.update(z=token_parts, w=weight_parts)
    done([peer_weights])
    scatter_stage("end")
    kept, from_seq = held["kept"], held["seq"]

    def put(name, n):
        store.append(pltpu.make_async_copy(r[name], r["o_" + name], r["store_sems"].at[n]))
        begin(store[-1:])

    for n, (name, (_, acc, _, far, _)) in enumerate(zip(("sup", "sout", "sdown"), sums)):
        value = acc[3, y, x].astype(f32)
        for j in range(3):
            done([moved["3", j, n]])
            value = value + far[j].astype(f32)
        r[name][...] = value
        put(name, 1 + n)
    value = small_sum[2].astype(f32)
    for j in range(3):
        done([moved["m", 3 + j]])
        value = value + small_got[3 + j].astype(f32)
    lines = r["lines"]
    lines[...] = jnp.zeros(lines.shape, f32)
    lines[0:8, :] = select_lanes(value, rows * index, 0)[0:8, :]
    b_up = jnp.zeros((16, 128), f32)
    for j in range(4):
        b_up = b_up + jnp.where(iota((16, 128), 0) == 6 + j, select_lanes(value, 4 * rows * index, j * D), 0.0)
    lines[6:7, :] = column_sum(b_up)
    done(over_z)
    for j in range(3):
        kept = kept + z_got[j].astype(f32)
    r["dtok"][...] = kept.astype(bf16)
    put("dtok", 4)
    done(from_seq)
    bias = jnp.zeros((8, 128), f32)
    bias_v = jnp.zeros((8, 128), f32)
    for b in range(active):
        for n, name in enumerate(("dwq", "dwk", "dwv")):
            r[name][:, b * width : (b + 1) * width] = second_got[b, 0:rows, n * width : (n + 1) * width].astype(f32)
        tail = second_got[b, rows:, :].astype(f32)
        bias = bias + select_lanes(tail[:, 0:width], rows * index, b * width)
        bias_v = bias_v + select_lanes(tail[:, 2 * width :], rows * index, b * width)
        lines[16 + b * heads : 16 + (b + 1) * heads, :] = tail[1 : 1 + heads, 0:128]
    lines[7:8, :] = bias[0:1]
    lines[8:9, :] = bias_v[0:1]
    for n, name in enumerate(("dwq", "dwk", "dwv", "lines")):
        put(name, 5 + n)
    net.drain()
    for copy in store:
        copy.wait()


def layer(heads, active, lengths, taps, own, cot, w_query, w_key, w_value, vectors, w_up, w_out, w_down):
    count, rows = own.shape[0], w_query.shape[0]
    total = 8 * count
    width = heads * HD
    shape, buffer, dma = jax.ShapeDtypeStruct, pltpu.VMEM, pltpu.SemaphoreType.DMA
    smem, anywhere = pl.BlockSpec(memory_space=pltpu.SMEM), pl.BlockSpec(memory_space=pl.ANY)
    ins = ["lengths", "in_taps", "in_own", "in_cot", "in_wq", "in_wk", "in_wv", "in_wup", "in_wout", "in_wdown"]
    ins += ["in_" + name for name in VECTORS]
    outs = {
        "output": shape((count, D), bf16), "dtok": shape((count, D), bf16),
        "dwq": shape((rows, D), f32), "dwk": shape((rows, D), f32), "dwv": shape((rows, D), f32),
        "sup": shape((rows, FF), f32), "sout": shape((rows, D), f32), "sdown": shape((4 * rows, D), f32),
        "lines": shape((32, 128), f32),
    }
    sizes = {"up": (rows, FF), "out": (rows, D), "down": (4 * rows, D)}
    scratch = {
        "own": buffer((count, D), bf16), "cot": buffer((count, D), bf16),
        "wq": buffer((rows, D), bf16), "wk": buffer((rows, D), bf16), "wv": buffer((rows, D), bf16),
        "vectors": buffer((16, 128), f32), "taps": buffer((HEADS, CONV), bf16), "place": buffer((16, D), f32), "placed": buffer((16, D), bf16),
        "tokens": buffer((total, D), bf16), "weights": buffer((D, 3 * width), bf16),
        "pack": buffer((active, rows + 8, 3 * width), bf16), "landed": buffer((4, 8, rows + 8, 3 * width), bf16),
        "up": buffer((D, FF), bf16), "full_small": buffer((512, D), bf16), "out": buffer((D, D), bf16),
        "down": buffer((FF, D), bf16), "vec": buffer((16, D), f32),
        "q": buffer((total, width), bf16), "k": buffer((total, width), bf16), "v": buffer((total, width), f32),
        "fw": buffer((heads, total, SLOTS), bf16), "bw": buffer((heads, total, SLOTS), bf16),
        "land": buffer((2, SLOTS, width), f32), "mix": buffer((2, width, SLOTS), f32),
        "a": buffer((heads, SLOTS, SLOTS), f32), "norm": buffer((heads, SLOTS, SLOTS), f32),
        "chain": buffer((NS_ITERS + 1, heads, 4, 2, SLOTS, SLOTS), bf16),
        "v_wide": buffer((total + 128, width), bf16),
        "score": buffer((heads, total, SLOTS), f32), "att": buffer((8, count, width), bf16),
        "gelu": buffer((count, FF), bf16), "slope": buffer((count, FF), f32), "dr1": buffer((count, D), f32),
        "small": buffer((16, D), f32), "small_put": buffer((16, D), bf16), "small_got": buffer((6, 16, D), bf16),
        "small_sum": buffer((3, 16, D), bf16),
        "dattn": buffer((active, count, width), bf16), "dout": buffer((total, width), bf16),
        "d_wide": buffer((total + 128, width), bf16),
        "spread": buffer((heads, 128, 256), f32), "tap_rows": buffer((128, 256), f32),
        "dqkv": buffer((total, 3 * width), bf16), "peer_weights": buffer((D, 3 * width), bf16),
        "extra": buffer((8, 3 * width), f32),
        "y_got": buffer((4, count, 3 * width), bf16), "z_got": buffer((3, count, D), bf16),
        "first_got": buffer((4, 8, rows + 8, 3 * width), bf16),
        "second_put": buffer((8, rows + 8, 3 * width), bf16), "second_got": buffer((8, rows + 8, 3 * width), bf16),
    }
    for name, size in sizes.items():
        scratch["acc_" + name] = buffer((4, 2, 2, *size), bf16)
        scratch["got_" + name] = buffer((4, 3, *size), bf16)
        scratch["far_" + name] = buffer((3, *size), bf16)
    for name, vector in zip(VECTORS, vectors):
        scratch[name] = buffer(vector.shape, bf16)
    for name, value in outs.items():
        scratch[name] = buffer(value.shape, value.dtype)
    pairs = {
        "tz": (6,), "ty": (4,), "ps": (7,), "pf": (3,), "at": (7,), "gz": (6, 4), "gy": (4, 8), "gx": (4, 8), "gc": (4, 4, 4),
        "rc": (16, 3), "rx": (12, 2), "ry": (12, 2), "rz": (3, 3), "rm": (6,), "dt": (7,), "dy": (4,), "dz": (3,),
        "wf": (3,), "ws": (7,), "wp": (1,),
    }
    for name, size in pairs.items():
        scratch[name + "_send"] = dma(size)
        scratch[name + "_recv"] = dma(size)
    scratch["load_sems"], scratch["keep_sems"], scratch["store_sems"] = dma((15,)), dma((4,)), dma((9,))
    names = ins + ["o_" + name for name in outs] + list(scratch)
    return pl.pallas_call(
        partial(layer_kernel, heads, active, names),
        out_shape=tuple(outs.values()),
        in_specs=[smem] + [anywhere] * (len(ins) - 1),
        out_specs=tuple([anywhere] * len(outs)),
        scratch_shapes=list(scratch.values()),
        compiler_params=pltpu.CompilerParams(collective_id=0, has_side_effects=True, vmem_limit_bytes=63_000_000),
    )(lengths, taps, own, cot, w_query, w_key, w_value, w_up, w_out, w_down, *vectors)


def finish_kernel(rows, hidden_rows, *refs):
    big, lines, outs, small, taps, held, sems = refs[:8], refs[8], refs[9:17], refs[17:26], refs[26], refs[27:35], refs[35]
    loads = [pltpu.make_async_copy(src, dst, sems.at[0, n]) for n, (src, dst) in enumerate(zip(big, held))]
    copies = [pltpu.make_async_copy(src, dst, sems.at[1, n]) for n, (src, dst) in enumerate(zip(held, outs))]
    begin(loads)
    for j, ref in enumerate(small):
        ref[...] = lines[j, 0 : ref.shape[0]]
    taps[...] = lines[16 : 16 + HEADS, 0:CONV]
    for load, copy in zip(loads, copies):
        load.wait()
        copy.start()
    for copy in copies:
        copy.wait()


def finish(results, hidden_rows):
    *big, lines = results
    rows = big[2].shape[0]
    shape = jax.ShapeDtypeStruct
    vmem, anywhere = pl.BlockSpec(memory_space=pltpu.VMEM), pl.BlockSpec(memory_space=pl.ANY)
    small = [shape((hidden_rows if j == 6 else rows,), f32) for j in range(9)]
    return pl.pallas_call(
        partial(finish_kernel, rows, hidden_rows),
        out_shape=tuple([shape(value.shape, value.dtype) for value in big] + small + [shape((HEADS, CONV), f32)]),
        in_specs=[anywhere] * 8 + [vmem],
        out_specs=tuple([anywhere] * 8 + [vmem] * 10),
        scratch_shapes=[pltpu.VMEM(value.shape, value.dtype) for value in big] + [pltpu.SemaphoreType.DMA((2, 8))],
    )(*big, lines)


def product(form, left, right):
    return jnp.einsum(form, left, right, preferred_element_type=f32)


def layer_norm(inputs, gain, shift):
    average = jnp.mean(inputs, axis=-1, keepdims=True)
    centred = inputs - average
    variance = jnp.mean(centred * centred, axis=-1, keepdims=True)
    return centred * lax.rsqrt(variance + epsilon) * gain + shift


def gelu_exact(inputs):
    return jax.nn.gelu(inputs, approximate=False)


def token_part(tokens, cot, attention, w_out, w_up, w_down, b_out, b_up, b_down, g_attn, s_attn, g_mlp, s_mlp):
    out_proj = product("td,de->te", attention, w_out) + b_out
    hidden, norm_one_back = jax.vjp(layer_norm, tokens.astype(f32) + out_proj, g_attn, s_attn)
    hidden_low = hidden.astype(bf16)
    up_pre = product("td,df->tf", hidden_low, w_up) + b_up
    gelu_val, gelu_back = jax.vjp(gelu_exact, up_pre)
    gelu_low = gelu_val.astype(bf16)
    down_pre = product("tf,fd->td", gelu_low, w_down) + b_down
    output, norm_two_back = jax.vjp(layer_norm, hidden + down_pre, g_mlp, s_mlp)
    d_r2, dg_mlp, ds_mlp = norm_two_back(cot.astype(f32))
    d_down = d_r2.astype(bf16)
    db_down = jnp.sum(d_down.astype(f32), axis=0)
    dw_down = product("tf,td->fd", gelu_low, d_down)
    d_gelu = product("td,fd->tf", d_down, w_down)
    d_up = gelu_back(d_gelu)[0].astype(bf16)
    db_up = jnp.sum(d_up.astype(f32), axis=0)
    dw_up = product("td,tf->df", hidden_low, d_up)
    d_hidden = product("tf,df->td", d_up, w_up) + d_r2
    d_r1, dg_attn, ds_attn = norm_one_back(d_hidden)
    d_out = d_r1.astype(bf16)
    db_out = jnp.sum(d_out.astype(f32), axis=0)
    dw_out = product("td,te->de", attention, d_out)
    d_attn = product("te,de->td", d_out, w_out)
    smalls = (db_out, db_up, db_down, dg_attn, ds_attn, dg_mlp, ds_mlp)
    return output.astype(bf16), d_r1, d_attn, dw_out, dw_up, dw_down, smalls
def local(sizes, *args):
    (tokens, cotangent, doc_lengths, w_query, b_query, w_key, w_value, b_value, w_out, b_out, w_up, b_up,
     w_down, b_down, g_attn, s_attn, g_mlp, s_mlp, conv_kernel) = args
    seq, fsdp = sizes
    devices = seq * fsdp
    fast = sizes == (8, 4)
    axes = ("seq", "fsdp")
    rows = D // devices
    hidden_rows = FF // devices
    own_tokens, own_cot, lengths = tokens[0], cotangent[0], doc_lengths[0]
    count = own_tokens.shape[0]
    total = count * seq
    heads = -(-HEADS // seq)
    width = heads * HD
    active = HEADS // heads
    s = lax.axis_index("seq")

    taps = conv_kernel.T
    if fast:
        vectors = (b_out, b_down, g_attn, s_attn, g_mlp, s_mlp, b_up, b_query, b_value)
        results = layer(
            heads, active, lengths, taps, own_tokens, own_cot, w_query, w_key, w_value, vectors, w_up, w_out, w_down)
        output, d_tokens, dw_query, dw_key, dw_value, s_up, s_out, s_down, *g, d_kernel = finish(results, hidden_rows)
        return (
            output[None], d_tokens[None], dw_query, g[7], dw_key, dw_value, g[8], s_out, g[0],
            s_up, g[6], s_down, g[1], g[2], g[3], g[4], g[5], d_kernel.T)

    own = (s * fsdp + lax.axis_index("fsdp")) * rows
    pack_rows = -(-rows // 8) * 8 + 8
    lead = pack_rows - 8

    def placed(vector, at, size):
        return lax.dynamic_update_slice(jnp.zeros((size,), bf16), vector, (at,))

    bias_q, bias_v = (placed(b, own, D).reshape(active, 1, width) for b in (b_query, b_value))
    bias = jnp.concatenate([bias_q, jnp.zeros((active, 1, width), bf16), bias_v], axis=2)
    bias = jnp.pad(bias, ((0, 0), (0, 7), (0, 0)))
    small = [placed(v, own, D) for v in (b_out, b_down, g_attn, s_attn, g_mlp, s_mlp)]
    small = jnp.concatenate(small + [placed(b_up, own * 4, FF), jnp.zeros((6 * D,), bf16)]).reshape(16, D)
    blocks = []
    for b in range(active):
        cols = slice(b * width, (b + 1) * width)
        blocks.append(jnp.concatenate([w_query[:, cols], w_key[:, cols], w_value[:, cols]], axis=1))
    pack = jnp.concatenate([jnp.pad(jnp.stack(blocks), ((0, 0), (0, lead - rows), (0, 0))), bias], axis=1)
    all_tokens = lax.all_gather(own_tokens, "seq").reshape(total, D)
    all_pack = lax.all_gather(lax.all_to_all(
        jnp.take(pack, jnp.arange(seq) % active, axis=0), "seq", 0, 0), "fsdp", axis=1).reshape(
            devices, pack_rows, 3 * width)
    qkv_weights = all_pack[:, :rows].reshape(D, 3 * width)
    full_up, full_small, full_down, full_out = (
        lax.all_gather(w, axes, tiled=True) for w in (w_up, small, w_down, w_out))
    mixed, *state = attention_forward(heads, active, all_tokens, qkv_weights, all_pack[:, lead:], lengths, taps)
    attention = lax.all_to_all(mixed.reshape(seq, count, width), "seq", 0, 0)
    vectors = jnp.sum(full_small.reshape(devices, 16, D).astype(f32), axis=0)
    attention = jnp.transpose(attention[:active], (1, 0, 2)).reshape(count, D)
    output, d_r1, d_attn, dw_out, dw_up, dw_down, smalls = token_part(
        own_tokens, own_cot, attention, full_out, full_up, full_down, vectors[0], vectors[6:10].reshape(FF),
        *(vectors[j] for j in range(1, 6)))
    d_attn = jnp.transpose(d_attn.astype(bf16).reshape(count, active, width), (1, 0, 2))
    d_mixed = lax.all_to_all(jnp.take(d_attn, jnp.arange(seq) % active, axis=0), "seq", 0, 0)
    s_up, s_out, s_down = (
        lax.psum_scatter(w, axes, scatter_dimension=0, tiled=True) for w in (dw_up, dw_out, dw_down))
    small = [lax.psum_scatter(v, axes, scatter_dimension=0, tiled=True) for v in smalls]
    part, dw, extra = attention_backward(
        heads, active, all_tokens, qkv_weights, d_mixed.reshape(total, width), lengths, taps, state)
    token_parts = lax.all_to_all(part.reshape(seq, count, D), "seq", 0, 0)
    d_tokens = (d_r1 + jnp.sum(token_parts.astype(f32), axis=0)).astype(bf16)
    extra = lax.psum(lax.all_gather(extra, "seq")[:active], "fsdp")
    dw = jnp.transpose(dw.reshape(width, 3, devices, rows), (2, 3, 1, 0)).reshape(devices, rows, 3 * width)
    dw = lax.all_to_all(dw, axes, 0, 0)
    dw = jnp.sum(dw.reshape(seq, fsdp, rows, 3, width)[:active], axis=1)
    dw_query, dw_key, dw_value = (jnp.transpose(dw[:, :, j], (1, 0, 2)).reshape(rows, D) for j in range(3))
    db_query = lax.dynamic_slice_in_dim(extra[:, 0, :width].reshape(D), own, rows)
    db_value = lax.dynamic_slice_in_dim(extra[:, 0, 2 * width :].reshape(D), own, rows)
    d_kernel = jnp.transpose(extra[:, 1 : 1 + heads, :CONV].reshape(active * heads, CONV), (1, 0))
    s_b_out, s_b_up, s_b_down, s_g_attn, s_s_attn, s_g_mlp, s_s_mlp = small
    return (
        output[None], d_tokens[None], dw_query, db_query, dw_key, dw_value, db_value, s_out, s_b_out,
        s_up, s_b_up, s_down, s_b_down, s_g_attn, s_s_attn, s_g_mlp, s_s_mlp, d_kernel)


def solution(mesh):
    sizes = (mesh.shape["seq"], mesh.shape["fsdp"])
    both = ("seq", "fsdp")
    wide, flat, stream = P(both, None), P(both), P("fsdp", "seq", None)
    in_specs = (stream, stream, P("fsdp", None), wide, flat, wide, wide, flat, wide, flat, wide, flat, wide, flat,
                flat, flat, flat, flat, P())
    out_specs = (stream, stream, wide, flat, wide, wide, flat, wide, flat, wide, flat, wide, flat, flat, flat, flat,
                 flat, P())
    return jax.shard_map(partial(local, sizes), mesh=mesh, in_specs=in_specs, out_specs=out_specs, check_vma=False)
```

```python
from functools import partial
import math

import jax
import jax.numpy as jnp
from jax import lax
from jax.experimental import pallas as pl
from jax.experimental.pallas import tpu as pltpu
from jax.sharding import PartitionSpec as P

D = 768
HEADS = 12
HD = 64
FF = 3072
NLAND = 64
NS_ITERS = 6
CONV = 33
REACH = CONV // 2
DOCS = 4
SLOTS = 256
SCALE = 1.0 / math.sqrt(HD)

HIGHEST = lax.Precision.HIGHEST
epsilon = 1e-05
masked_score = -1e30
f32 = jnp.float32
bf16 = jnp.bfloat16
MESH = pl.DeviceIdType.MESH
VMEM_BYTES = 56 * 1024 * 1024


def greet(peers):
    barrier = pltpu.get_barrier_semaphore()
    for peer in peers:
        pl.semaphore_signal(barrier, inc=1, device_id=peer, device_id_type=MESH)
    pl.semaphore_wait(barrier, len(peers))


def remote(src, dst, send_sem, recv_sem, peer):
    return pltpu.make_async_remote_copy(
        src_ref=src, dst_ref=dst, send_sem=send_sem, recv_sem=recv_sem,
        device_id=peer, device_id_type=MESH,
    )


BLOCK = 256
NN = (((1,), (0,)), ((), ()))
NT = (((1,), (1,)), ((), ()))


def dot(left, right, dims=NN):
    return lax.dot_general(left, right, dims, preferred_element_type=f32)


def split(value):
    upper = value.astype(bf16)
    return upper, (value - upper.astype(f32)).astype(bf16)


def dot3(left, right, dims=NN):
    return dot(left[0], right[0], dims) + (dot(left[0], right[1], dims) + dot(left[1], right[0], dims))


def iota(shape, dim):
    return lax.broadcasted_iota(jnp.int32, shape, dim)


def doc_table(lengths_ref):
    ends, start = [], 0
    for d in range(DOCS):
        start = start + lengths_ref[d]
        ends.append(start)
    return ends


def slot_bounds(lengths_ref, shape, dim):
    ends = doc_table(lengths_ref)
    slot = iota(shape, dim)
    doc, seg = slot // NLAND, slot % NLAND
    length, end = jnp.zeros(shape, jnp.int32), jnp.zeros(shape, jnp.int32)
    for d in range(DOCS):
        length = jnp.where(doc == d, lengths_ref[d], length)
        end = jnp.where(doc == d, ends[d], end)
    start = end - length
    return start, end, start + seg * length // NLAND, start + (seg + 1) * length // NLAND


def same_doc(lengths_ref, left, right):
    ends = doc_table(lengths_ref)
    a, b = jnp.zeros(left.shape, jnp.int32), jnp.zeros(right.shape, jnp.int32)
    for d in range(DOCS):
        a = a + (left >= ends[d]).astype(jnp.int32)
        b = b + (right >= ends[d]).astype(jnp.int32)
    return a == b


def head_mask(shape, dim, h):
    return (iota(shape, dim) // HD == h).astype(f32)


def tap_index():
    return iota((128, 256), 1) - iota((128, 256), 0) - 64 + REACH


def toeplitz(taps_ref, head, mirrored):
    taps = taps_ref[...].astype(f32)
    taps = jnp.sum(jnp.where(iota(taps.shape, 0) == head, taps, 0.0), axis=0, keepdims=True)
    tap = tap_index()
    mat = jnp.zeros((128, 256), f32)
    for o in range(CONV):
        n = CONV - 1 - o if mirrored else o
        mat = jnp.where(tap == o, taps[:, n : n + 1], mat)
    return mat


def clear_edges(ref, total):
    ref[0:64, :] = jnp.zeros((64, ref.shape[1]), ref.dtype)
    ref[total + 64 : total + 128, :] = jnp.zeros((64, ref.shape[1]), ref.dtype)


def forward_math(heads, active, lengths_ref, taps_ref, tokens_ref, weights_ref, bias,
                 mixed_ref, q_ref, k_ref, v_ref, fw_ref, bw_ref, land_ref, mix_ref, a_ref, norm_ref, chain_ref,
                 v_wide, score, stage):
    total = tokens_ref.shape[0]
    width = heads * HD
    part = lax.axis_index("seq") % active
    steps = total // BLOCK
    row_start, row_end, row_low, row_top = slot_bounds(lengths_ref, (1, SLOTS), 1)
    _, _, col_low, col_top = slot_bounds(lengths_ref, (SLOTS, 1), 0)
    count = (col_top - col_low).astype(f32)
    clear_edges(v_wide, total)
    land_ref[...] = jnp.zeros(land_ref.shape, f32)

    def project(i, carry):
        at = pl.ds(pl.multiple_of(i * BLOCK, BLOCK), BLOCK)
        qkv = dot(tokens_ref[at, :], weights_ref[...]) + bias
        q, k, v = (qkv[:, j * width : (j + 1) * width] for j in range(3))
        q_low, k_low = q.astype(bf16), k.astype(bf16)
        q_ref[at, :], k_ref[at, :] = q_low, k_low
        v_ref[at, :] = v
        v_wide[pl.ds(pl.multiple_of(i * BLOCK + 64, 64), BLOCK), :] = v.astype(bf16)
        t = i * BLOCK + iota((1, BLOCK), 1)
        member = ((t >= col_low) & (t < col_top)).astype(f32).astype(bf16)
        land_ref[0] += dot(member, q_low)
        land_ref[1] += dot(member, k_low)
        return carry

    lax.fori_loop(0, steps, project, 0)
    stage("proj")
    ql, kl = land_ref[0] / count, land_ref[1] / count
    land_ref[0], land_ref[1] = ql, kl
    masks = [head_mask((1, width), 1, h) for h in range(heads)]
    ql_low = [(ql * masks[h]).astype(bf16) for h in range(heads)]
    kl_low = [(kl * masks[h]).astype(bf16) for h in range(heads)]

    def scores(i, tops):
        at = pl.ds(pl.multiple_of(i * BLOCK, BLOCK), BLOCK)
        t = i * BLOCK + iota((BLOCK, 1), 0)
        valid = (t >= row_start) & (t < row_end)
        out = []
        for h in range(heads):
            s = jnp.where(valid, SCALE * dot(q_ref[at, :], kl_low[h], NT), masked_score)
            e = jnp.exp(s - jnp.max(s, axis=1, keepdims=True))
            fw_ref[h, at, :] = (e / jnp.sum(e, axis=1, keepdims=True)).astype(bf16)
            s = jnp.where(valid, SCALE * dot(k_ref[at, :], ql_low[h], NT), masked_score)
            score[h, at, :] = s
            out.append(jnp.maximum(tops[h], jnp.max(s, axis=0, keepdims=True)))
        return tuple(out)

    tops = lax.fori_loop(0, steps, scores, tuple(jnp.full((1, SLOTS), masked_score, f32) for _ in range(heads)))
    stage("scores")

    def gather(i, carry):
        at = pl.ds(pl.multiple_of(i * BLOCK, BLOCK), BLOCK)
        v_t = split(v_ref[at, :].T)
        out = []
        for h in range(heads):
            e = jnp.exp(score[h, at, :] - tops[h])
            score[h, at, :] = e
            out.append((carry[h][0] + jnp.sum(e, axis=0, keepdims=True), carry[h][1] + dot3(v_t, split(e))))
        return tuple(out)

    sums = lax.fori_loop(0, steps, gather, tuple(
        (jnp.zeros((1, SLOTS), f32), jnp.zeros((width, SLOTS), f32)) for _ in range(heads)))
    scale = [1.0 / sums[h][0] for h in range(heads)]
    tall = [head_mask((width, 1), 0, h) for h in range(heads)]
    key_mix_t = [sums[h][1] * scale[h] * tall[h] for h in range(heads)]

    def normalize(i, carry):
        at = pl.ds(pl.multiple_of(i * BLOCK, BLOCK), BLOCK)
        for h in range(heads):
            bw_ref[h, at, :] = (score[h, at, :] * scale[h]).astype(bf16)
        return carry

    lax.fori_loop(0, steps, normalize, 0)
    stage("key_mix")

    block = iota((SLOTS, SLOTS), 0) // NLAND == iota((SLOTS, SLOTS), 1) // NLAND
    diagonal = iota((SLOTS, SLOTS), 0) == iota((SLOTS, SLOTS), 1)
    state = []
    for h in range(heads):
        s = jnp.where(block, SCALE * dot3(split(ql * masks[h]), split(kl), NT), masked_score)
        e = jnp.exp(s - jnp.max(s, axis=1, keepdims=True))
        a = e / jnp.sum(e, axis=1, keepdims=True)
        norm = jnp.sum(jnp.sum((a * a).reshape(DOCS, NLAND, SLOTS), axis=1, keepdims=True), axis=2, keepdims=True)
        norm = jnp.broadcast_to(norm, (DOCS, NLAND, SLOTS)).reshape(SLOTS, SLOTS)
        a_ref[h], norm_ref[h] = a, norm
        u = a / norm
        a_split = split(a)
        state.append((split(u), split(dot3(a_split, split(u), NT))))
    for step in range(NS_ITERS):
        fresh = []
        for h in range(heads):
            u, p = state[h]
            p_full = p[0].astype(f32) + p[1].astype(f32)
            q_full = dot3(p, p)
            q = split(q_full)
            f_full = jnp.where(diagonal, 13.0, 0.0) - 15.0 * p_full + 7.0 * q_full - dot3(p, q)
            f = split(f_full)
            for n, pair in enumerate((u, p, q, f)):
                for half in range(2):
                    chain_ref[step, h, n, half] = pair[half]
            p_next = None if step == NS_ITERS - 1 else split(0.25 * dot3(p, f))
            u_next = split(0.25 * dot3(f, u))
            fresh.append((u_next, p_next))
        stage("newton" + str(step))
        state = fresh
    mix_t = jnp.zeros((width, SLOTS), f32)
    key_t = jnp.zeros((width, SLOTS), f32)
    for h in range(heads):
        u = state[h][0]
        chain_ref[NS_ITERS, h, 0, 0], chain_ref[NS_ITERS, h, 0, 1] = u
        mix_t = mix_t + dot3(split(key_mix_t[h]), u)
        key_t = key_t + key_mix_t[h]
    mix_ref[0], mix_ref[1] = mix_t, key_t
    stage("mix")
    mix_low = [(mix_t * tall[h]).astype(bf16) for h in range(heads)]
    mats = [toeplitz(taps_ref, part * heads + h, False) for h in range(heads)]

    def output(i, carry):
        at = pl.ds(pl.multiple_of(i * 128, 128), 128)
        t = i * 128 + iota((128, 1), 0)
        near = same_doc(lengths_ref, t, i * 128 - 64 + iota((1, 256), 1))
        window = v_wide[pl.ds(pl.multiple_of(i * 128, 128), 256), :]
        out = jnp.zeros((128, width), f32)
        for h in range(heads):
            out = out + dot(fw_ref[h, at, :], mix_low[h], NT)
            conv = dot(jnp.where(near, mats[h], 0.0).astype(bf16), window)
            out = out + conv * masks[h]
        mixed_ref[at, :] = out.astype(bf16)
        return carry

    lax.fori_loop(0, total // 128, output, 0)


def forward_kernel(heads, active, lengths_ref, taps_ref, tokens_ref, weights_ref, bias_ref, *refs):
    bias = jnp.sum(bias_ref[...].astype(f32), axis=0)[0:1]
    forward_math(heads, active, lengths_ref, taps_ref, tokens_ref, weights_ref, bias, *refs, lambda n: None)


def attention_forward(heads, active, tokens, weights, bias, lengths, taps):
    total = tokens.shape[0]
    width = heads * HD
    shape = jax.ShapeDtypeStruct
    vmem, smem = (pl.BlockSpec(memory_space=m) for m in (pltpu.VMEM, pltpu.SMEM))
    chain = (heads, 4, 2, SLOTS, SLOTS)
    return pl.pallas_call(
        partial(forward_kernel, heads, active),
        out_shape=(
            shape((total, width), bf16),
            shape((total, width), bf16),
            shape((total, width), bf16),
            shape((total, width), f32),
            shape((heads, total, SLOTS), bf16),
            shape((heads, total, SLOTS), bf16),
            shape((2, SLOTS, width), f32),
            shape((2, width, SLOTS), f32),
            shape((heads, SLOTS, SLOTS), f32),
            shape((heads, SLOTS, SLOTS), f32),
            shape((NS_ITERS + 1, *chain), bf16),
        ),
        in_specs=[smem, vmem, vmem, vmem, vmem],
        out_specs=tuple([vmem] * 11),
        scratch_shapes=[
            pltpu.VMEM((total + 128, width), bf16),
            pltpu.VMEM((heads, total, SLOTS), f32),
        ],
        compiler_params=pltpu.CompilerParams(vmem_limit_bytes=VMEM_BYTES),
    )(lengths, taps, tokens, weights, bias)


def backward_math(heads, active, lengths_ref, taps_ref, tokens_ref, weights_ref, dout_ref, q_ref, k_ref, v_ref, fw_ref,
                  bw_ref, land_ref, mix_ref, a_ref, norm_ref, chain_ref, dw_ref, extra_ref,
                  v_wide, d_wide, dq_acc, dk_acc, dv_acc, spread, tap_rows, dqkv, stage):
    total = tokens_ref.shape[0]
    width = heads * HD
    part = lax.axis_index("seq") % active
    steps = total // BLOCK
    _, _, row_low, row_top = slot_bounds(lengths_ref, (1, SLOTS), 1)
    inverse = 1.0 / (row_top - row_low).astype(f32)
    clear_edges(v_wide, total)
    clear_edges(d_wide, total)
    masks = [head_mask((1, width), 1, h) for h in range(heads)]
    tall = [head_mask((width, 1), 0, h) for h in range(heads)]
    ql, kl = land_ref[0], land_ref[1]
    mix_t, key_t = mix_ref[0], mix_ref[1]
    kl_low = [(kl * masks[h]).astype(bf16) for h in range(heads)]
    ql_low = [(ql * masks[h]).astype(bf16) for h in range(heads)]
    mix_low = [(mix_t * tall[h]).astype(bf16) for h in range(heads)]

    def front(i, carry):
        at = pl.ds(pl.multiple_of(i * BLOCK, BLOCK), BLOCK)
        inner = pl.ds(pl.multiple_of(i * BLOCK + 64, 64), BLOCK)
        do = dout_ref[at, :]
        d_wide[inner, :] = do
        v_wide[inner, :] = v_ref[at, :].astype(bf16)
        do_t = do.astype(f32).T.astype(bf16)
        q_t = q_ref[at, :].astype(f32).T.astype(bf16)
        dq = jnp.zeros((BLOCK, width), f32)
        out = []
        for h in range(heads):
            fw = fw_ref[h, at, :]
            wide = fw.astype(f32)
            d_fw = dot(do, mix_low[h])
            ds = (SCALE * wide * (d_fw - jnp.sum(wide * d_fw, axis=1, keepdims=True))).astype(bf16)
            dq = dq + dot(ds, kl_low[h])
            out.append((carry[h][0] + dot(do_t, fw), carry[h][1] + dot(q_t, ds)))
        dq_acc[at, :] = dq
        return tuple(out)

    zeros = jnp.zeros((width, SLOTS), f32)
    sums = lax.fori_loop(0, steps, front, tuple((zeros, zeros) for _ in range(heads)))
    stage("front")
    dmix_t = [sums[h][0] * tall[h] for h in range(heads)]
    dkl_t = zeros
    for h in range(heads):
        dkl_t = dkl_t + sums[h][1] * tall[h]
    key = key_t.T
    ql_t = ql.T
    block = iota((SLOTS, SLOTS), 0) // NLAND == iota((SLOTS, SLOTS), 1) // NLAND
    du, dp, dkey_t = [], [None] * heads, []
    for h in range(heads):
        pair = split(dmix_t[h])
        du.append(jnp.where(block, dot3(split(key), pair), 0.0))
        dkey_t.append(dot3(pair, (chain_ref[NS_ITERS, h, 0, 0], chain_ref[NS_ITERS, h, 0, 1]), NT))
    for step in range(NS_ITERS - 1, -1, -1):
        stage("newton" + str(step))
        for h in range(heads):
            u, p, q, f = ((chain_ref[step, h, n, 0], chain_ref[step, h, n, 1]) for n in range(4))
            du_pair = split(du[h])
            df = 0.25 * dot3(du_pair, u, NT)
            du[h] = 0.25 * dot3(f, du_pair)
            if dp[h] is not None:
                dp_pair = split(dp[h])
                df = df + 0.25 * dot3(p, dp_pair)
                base = 0.25 * dot3(dp_pair, f)
            else:
                base = 0.0
            df_pair = split(df)
            dq = split(7.0 * df - dot3(p, df_pair))
            dp[h] = base - 15.0 * df - dot3(df_pair, q) + (dot3(dq, p) + dot3(p, dq))
    dql = jnp.zeros((SLOTS, width), f32)
    for h in range(heads):
        a, norm = a_ref[h], norm_ref[h]
        u0 = chain_ref[0, h, 0, 0].astype(f32) + chain_ref[0, h, 0, 1].astype(f32)
        p0 = chain_ref[0, h, 1, 0].astype(f32) + chain_ref[0, h, 1, 1].astype(f32)
        a_pair = split(a)
        inner = dp[h] * p0 + du[h] * u0
        inner = jnp.sum(jnp.sum(inner.reshape(DOCS, NLAND, SLOTS), axis=1, keepdims=True), axis=2, keepdims=True)
        inner = jnp.broadcast_to(inner, (DOCS, NLAND, SLOTS)).reshape(SLOTS, SLOTS)
        da = (dot3(split(dp[h] + dp[h].T), a_pair) + du[h] - 2.0 * a * inner) / norm
        dsa = split(SCALE * a * (da - jnp.sum(a * da, axis=1, keepdims=True)))
        dql = dql + dot3(dsa, split(kl * masks[h]))
        dkl_t = dkl_t + dot3(split(ql_t * tall[h]), dsa)
    stage("core")
    dkey_low = [x.astype(bf16) for x in dkey_t]
    row_dot = [jnp.sum(dkey_t[h] * key_t, axis=0, keepdims=True) for h in range(heads)]
    dkey = [x.T.astype(bf16) for x in dkey_t]

    def back(i, carry):
        at = pl.ds(pl.multiple_of(i * BLOCK, BLOCK), BLOCK)
        v = v_ref[at, :].astype(bf16)
        k_t = k_ref[at, :].astype(f32).T.astype(bf16)
        dk, dv = jnp.zeros((BLOCK, width), f32), jnp.zeros((BLOCK, width), f32)
        out = []
        for h in range(heads):
            bw = bw_ref[h, at, :]
            ds = (SCALE * bw.astype(f32) * (dot(v, dkey_low[h]) - row_dot[h])).astype(bf16)
            dk = dk + dot(ds, ql_low[h])
            dv = dv + dot(bw, dkey[h])
            out.append(carry[h] + dot(k_t, ds))
        dk_acc[at, :] = dk
        dv_acc[at, :] = dv
        return tuple(out)

    sums = lax.fori_loop(0, steps, back, tuple(zeros for _ in range(heads)))
    stage("back")
    dql_t = zeros
    for h in range(heads):
        dql_t = dql_t + sums[h] * tall[h]
    dql_low = ((dql.T + dql_t) * inverse).astype(bf16)
    dkl_low = (dkl_t * inverse).astype(bf16)
    mats = [toeplitz(taps_ref, part * heads + h, True) for h in range(heads)]
    spread[...] = jnp.zeros(spread.shape, f32)

    def convolve(i, carry):
        at = pl.ds(pl.multiple_of(i * 128, 128), 128)
        t = i * 128 + iota((128, 1), 0)
        near = same_doc(lengths_ref, t, i * 128 - 64 + iota((1, 256), 1))
        window = pl.ds(pl.multiple_of(i * 128, 128), 256)
        d_window, v_window = d_wide[window, :], v_wide[window, :]
        do = dout_ref[at, :].astype(f32)
        dv = dv_acc[at, :]
        for h in range(heads):
            dv = dv + dot(jnp.where(near, mats[h], 0.0).astype(bf16), d_window) * masks[h]
            spread[h] += jnp.where(near, dot((do * masks[h]).astype(bf16), v_window, NT), 0.0)
        dv_acc[at, :] = dv
        return carry

    lax.fori_loop(0, total // 128, convolve, 0)
    stage("conv")

    def finish(i, carry):
        at = pl.ds(pl.multiple_of(i * BLOCK, BLOCK), BLOCK)
        t = i * BLOCK + iota((BLOCK, 1), 0)
        member = ((t >= row_low) & (t < row_top)).astype(f32).astype(bf16)
        dq = dq_acc[at, :] + dot(member, dql_low, NT)
        dk = dk_acc[at, :] + dot(member, dkl_low, NT)
        grads = jnp.concatenate([dq.astype(bf16), dk.astype(bf16), dv_acc[at, :].astype(bf16)], axis=1)
        dqkv[at, :] = grads
        return carry + jnp.sum(grads.astype(f32), axis=0, keepdims=True)

    extra_ref[...] = jnp.zeros(extra_ref.shape, f32)
    extra_ref[0:1, :] = lax.fori_loop(0, steps, finish, jnp.zeros((1, 3 * width), f32))
    stage("parts")
    dw_ref[...] = jnp.zeros(dw_ref.shape, f32)

    def weigh(i, carry):
        at = pl.ds(pl.multiple_of(i * BLOCK, BLOCK), BLOCK)
        for n in range(3):
            grads = dqkv[at, n * width : (n + 1) * width].astype(f32).T.astype(bf16)
            dw_ref[:, n * D : (n + 1) * D] += dot(grads, tokens_ref[at, :])
        return carry

    lax.fori_loop(0, steps, weigh, 0)
    tap = tap_index()
    tap_rows[...] = jnp.zeros(tap_rows.shape, f32)
    for h in range(heads):
        for o in range(CONV):
            tap_rows[o : o + 1, :] = jnp.sum(jnp.where(tap == o, spread[h], 0.0), axis=0, keepdims=True)
        extra_ref[1 + h : 2 + h, 0:128] = jnp.sum(tap_rows[...].T, axis=0, keepdims=True)


def backward_kernel(heads, active, lengths_ref, taps_ref, tokens_ref, weights_ref, *refs):
    inputs, part_ref, outputs, dqkv = refs[:11], refs[11], refs[12:-1], refs[-1]
    backward_math(heads, active, lengths_ref, taps_ref, tokens_ref, weights_ref, *inputs, *outputs, dqkv, lambda point: None)

    def project(i, carry):
        at = pl.ds(pl.multiple_of(i * BLOCK, BLOCK), BLOCK)
        part = dot(dqkv[at, :], weights_ref[...], NT)
        part_ref[at, :] = jnp.where(lax.axis_index("seq") < active, part, 0.0).astype(bf16)
        return carry

    lax.fori_loop(0, tokens_ref.shape[0] // BLOCK, project, 0)


def attention_backward(heads, active, tokens, weights, dout, lengths, taps, state):
    total = tokens.shape[0]
    width = heads * HD
    shape = jax.ShapeDtypeStruct
    vmem, smem = (pl.BlockSpec(memory_space=m) for m in (pltpu.VMEM, pltpu.SMEM))
    return pl.pallas_call(
        partial(backward_kernel, heads, active),
        out_shape=(
            shape((total, D), bf16),
            shape((width, 3 * D), f32),
            shape((8, 3 * width), f32),
        ),
        in_specs=[smem] + [vmem] * 14,
        out_specs=tuple([vmem] * 3),
        scratch_shapes=[
            pltpu.VMEM((total + 128, width), bf16),
            pltpu.VMEM((total + 128, width), bf16),
            pltpu.VMEM((total, width), f32),
            pltpu.VMEM((total, width), f32),
            pltpu.VMEM((total, width), f32),
            pltpu.VMEM((heads, 128, 256), f32),
            pltpu.VMEM((128, 256), f32),
            pltpu.VMEM((total, 3 * width), bf16),
        ],
        compiler_params=pltpu.CompilerParams(vmem_limit_bytes=VMEM_BYTES),
    )(lengths, taps, tokens, weights, dout, *state)
def rows_at(index, count):
    return pl.ds(pl.multiple_of(index * count, 8), count)


class Links:
    def __init__(self):
        s, f = lax.axis_index("seq"), lax.axis_index("fsdp")
        self.s, self.f = s, f
        self.z, self.y, self.x, self.c = s // 2, s % 2, f // 2, f % 2
        self.oy, self.ox, self.oc = 1 - self.y, 1 - self.x, 1 - self.c
        self.seq_peers = [((s + j) % 8, f) for j in range(1, 8)]
        self.fsdp_peers = [(s, (f + i) % 4) for i in range(1, 4)]
        self.z_peers = [((self.z + j) % 4 * 2 + self.y, f) for j in range(1, 4)]
        self.above, self.below = self.z_peers[0], self.z_peers[2]
        self.y_peer = (self.z * 2 + self.oy, f)
        self.x_peer = (s, self.ox * 2 + self.c)
        self.c_peer = (s, self.x * 2 + self.oc)
        self.started = []

    def send(self, src, dst, sems, index, peer):
        copy = remote(src, dst, sems[0].at[index], sems[1].at[index], peer)
        copy.start()
        self.started.append(copy)
        return copy

    def drain(self):
        for copy in self.started:
            copy.wait_send()
        self.started = []


def begin(copies):
    for copy in copies:
        copy.start()


def done(copies):
    for copy in copies:
        copy.wait_recv()


def centre(value):
    value = value - jnp.mean(value, axis=1, keepdims=True)
    scale = lax.rsqrt(jnp.mean(value * value, axis=1, keepdims=True) + epsilon)
    return value * scale, scale


def uncentre(grad, normal, scale):
    return scale * (grad - jnp.mean(grad, axis=1, keepdims=True)
                    - normal * jnp.mean(grad * normal, axis=1, keepdims=True))


def column_sum(value):
    return jnp.sum(value, axis=0, keepdims=True)


def token_math(own, cot, attention, up_ref, down_ref, out_ref, vec_ref, gelu_ref, slope_ref, output_ref, dr1_ref, small_ref,
               weights_done):
    vec = vec_ref[...]
    b_out, b_down, g_attn, s_attn, g_mlp, s_mlp = (vec[j : j + 1] for j in range(6))
    normal_one, scale_one = centre(own.astype(f32) + dot(attention, out_ref[...]) + b_out)
    hidden = normal_one * g_attn + s_attn
    hidden_low = hidden.astype(bf16)
    count = hidden.shape[0]

    def upward(i, down):
        cols = pl.ds(pl.multiple_of(i * D, D), D)
        up = dot(hidden_low, up_ref[:, cols]) + vec_ref[pl.ds(6 + i, 1), :]
        share = 0.5 + 0.5 * lax.erf(up * math.sqrt(0.5))
        gelu = (up * share).astype(bf16)
        gelu_ref[:, cols] = gelu
        slope_ref[:, cols] = share + up * (math.sqrt(0.5 / math.pi) * jnp.exp(-0.5 * up * up))
        return down + dot(gelu, down_ref[cols, :])

    down = lax.fori_loop(0, FF // D, upward, jnp.zeros((count, D), f32))
    normal_two, scale_two = centre(hidden + down + b_down)
    output_ref[...] = (normal_two * g_mlp + s_mlp).astype(bf16)
    cot = cot.astype(f32)
    d_r2 = uncentre(cot * g_mlp, normal_two, scale_two)
    d_down = d_r2.astype(bf16)
    small_ref[...] = jnp.zeros(small_ref.shape, f32)
    small_ref[1:2, :] = column_sum(d_down.astype(f32))
    small_ref[4:5, :] = column_sum(cot * normal_two)
    small_ref[5:6, :] = column_sum(cot)
    hidden_t = hidden_low.astype(f32).T.astype(bf16)

    def downward(i, d_hidden):
        cols = pl.ds(pl.multiple_of(i * D, D), D)
        d_gelu = dot(d_down, down_ref[cols, :], NT)
        d_up = (d_gelu * slope_ref[:, cols]).astype(bf16)
        small_ref[pl.ds(6 + i, 1), :] = column_sum(d_up.astype(f32))
        d_hidden = d_hidden + dot(d_up, up_ref[:, cols], NT)
        gelu_t = gelu_ref[:, cols].astype(f32).T.astype(bf16)
        down_ref[cols, :] = dot(gelu_t, d_down).astype(bf16)
        up_ref[:, cols] = dot(hidden_t, d_up).astype(bf16)
        return d_hidden

    d_hidden = lax.fori_loop(0, FF // D, downward, d_r2)
    weights_done()
    d_r1 = uncentre(d_hidden * g_attn, normal_one, scale_one)
    dr1_ref[...] = d_r1
    d_out = d_r1.astype(bf16)
    small_ref[0:1, :] = column_sum(d_out.astype(f32))
    small_ref[2:3, :] = column_sum(d_hidden * normal_one)
    small_ref[3:4, :] = column_sum(d_hidden)
    d_attention = dot(d_out, out_ref[...], NT).astype(bf16)
    out_ref[...] = dot(attention.astype(f32).T.astype(bf16), d_out).astype(bf16)
    return d_attention


def select_lanes(rows, offset, base):
    wide = rows.shape[1]
    choose = (iota((wide, 128), 0) + base == iota((wide, 128), 1) + offset).astype(f32).astype(bf16)
    first = rows.astype(bf16)
    second = (rows - first.astype(f32)).astype(bf16)
    third = (rows - first.astype(f32) - second.astype(f32)).astype(bf16)
    return dot(first, choose) + dot(second, choose) + dot(third, choose)


GATHER = {
    "proj": "w1", "scores": "w2", "key_mix": "o0 q2", "newton2": "q3", "newton4": "o1", "mix": "q4 c0", "end": "o2 c1 c2",
}
PLAN = {
    "start": "f0 m0", "front": "f1", "newton4": "s0 f2 m1", "newton1": "s1 t0 f3", "core": "m2 l0", "conv": "s2 t1",
    "parts": "y0 l1", "end": "s3 z0 t2 z1 z2 w0 z3 l2 t3",
}


VECTORS = ("b_out", "b_down", "g_attn", "s_attn", "g_mlp", "s_mlp", "b_up", "b_query", "b_value")


def layer_kernel(heads, active, names, *refs):
    r = dict(zip(names, refs))
    net = Links()
    s, f, z, y, x, c = net.s, net.f, net.z, net.y, net.x, net.c
    oy, ox, oc = net.oy, net.ox, net.oc
    width = heads * HD
    own_ref, tokens_ref, weights_ref = r["own"], r["tokens"], r["weights"]
    count, rows = own_ref.shape[0], r["wq"].shape[0]
    mine = rows_at(s, count)
    index = s * 4 + f

    loads = [pltpu.make_async_copy(r["in_" + name], r[name], r["load_sems"].at[n])
             for n, name in enumerate(("own", "wq", "wk", "wv", "cot", "taps") + VECTORS)]
    begin(loads)
    greet(net.seq_peers + net.fsdp_peers)
    for copy in loads:
        copy.wait()

    def pair(name):
        return r[name + "_send"], r[name + "_recv"]

    def token_z(zz, t, up):
        here = tokens_ref.at[rows_at(zz * 2 + y, count)]
        n = 2 * t + (0 if up else 1)
        return remote(own_ref if t == 0 else here, here, r["tz_send"].at[n], r["tz_recv"].at[n], net.above if up else net.below)

    def token_y(zz, own=False):
        here = tokens_ref.at[rows_at(zz * 2 + y, count)]
        return remote(own_ref if own else here, here, r["ty_send"].at[zz], r["ty_recv"].at[zz], net.y_peer)

    pieces = ((r["in_wup"], r["up"], rows, 0, rows), (r["placed"], r["full_small"], 16, 0, 16),
              (r["in_wout"], r["out"], rows, 0, rows), (r["in_wdown"].at[0 : 3 * rows], r["down"], 4 * rows, 0, 3 * rows),
              (r["in_wdown"].at[3 * rows : 4 * rows], r["down"], 4 * rows, 3 * rows, rows))
    early, late = (0, 1, 2), (3,)

    def slot(zz, sy, sx):
        return (zz * 2 + sy) * 4 + sx * 2 + c

    def weight(m, own, where, send_sem, recv_sem, peer):
        src, full, stride, lead, n = pieces[m]
        here = full.at[pl.ds(pl.multiple_of(where * stride + lead, 8), n)]
        return remote(src if own else here, here, send_sem, recv_sem, peer)

    quad = ((y, x), (oy, x), (y, ox), (oy, ox))

    def quad_x():
        return weight(4, True, slot(z, y, x), r["qx_send"].at[0], r["qx_recv"].at[0], net.x_peer)

    def quad_y(n):
        return weight(4, n == 0, slot(z, y, (x, ox)[n]), r["qy_send"].at[n], r["qy_recv"].at[n], net.y_peer)

    def quad_z(zz, t, up):
        n = 2 * t + (0 if up else 1)
        peer = net.above if up else net.below
        return [weight(4, False, slot(zz, *quad[q]), r["qz_send"].at[n, q], r["qz_recv"].at[n, q], peer) for q in range(4)]

    def quad_core(zz):
        return [weight(4, False, slot(zz, *quad[q]), r["qc_send"].at[zz, q], r["qc_recv"].at[zz, q], net.c_peer)
                for q in range(4)]

    def quad_step(n):
        if n == 0:
            quad_x().wait_recv()
            quad_y(1).start()
        elif n == 1:
            keep[4].wait()
            done([quad_y(0), quad_y(1)])
            onto_z(0, lambda zz, t, up: begin(quad_z(zz, t, up)))
            begin(quad_core(z))
        else:
            t = n - 2

            def came(zz, up):
                done(quad_z(zz, t, up))
                begin(quad_core(zz))

            column(t, came)
            if t < 2:
                onto_z(t + 1, lambda zz, t, up: begin(quad_z(zz, t, up)))

    def weight_z(zz, t, up):
        n = 2 * t + (0 if up else 1)
        peer = net.above if up else net.below
        return [weight(m, t == 0, slot(zz, y, x), r["gz_send"].at[n, m], r["gz_recv"].at[n, m], peer) for m in range(4)]

    def to_y(zz, m, own=False):
        return weight(m, own, slot(zz, y, x), r["gy_send"].at[zz, m], r["gy_recv"].at[zz, m], net.y_peer)

    def to_x(zz, m, own=False):
        return weight(m, own, slot(zz, y, x), r["gx_send"].at[zz, m], r["gx_recv"].at[zz, m], net.x_peer)

    def again_x(zz, m):
        return weight(m, False, slot(zz, oy, x), r["gx_send"].at[zz, 4 + m], r["gx_recv"].at[zz, 4 + m], net.x_peer)

    def again_y(zz, m):
        return weight(m, False, slot(zz, y, ox), r["gy_send"].at[zz, 4 + m], r["gy_recv"].at[zz, 4 + m], net.y_peer)

    def to_core(zz, n, m, own=False):
        sy, sx = ((y, x), (oy, x), (y, ox), (oy, ox))[n]
        return weight(m, own, slot(zz, sy, sx), r["gc_send"].at[zz, n, m], r["gc_recv"].at[zz, n, m], net.c_peer)

    def spread(zz):
        begin([to_y(zz, m) for m in early] + [to_x(zz, m) for m in late])
        begin([to_x(zz, m) for m in early] + [to_y(zz, m) for m in late])
        begin([to_core(zz, 0, m) for m in range(4)])

    def onward(zz):
        for m in early:
            done([to_y(zz, m)])
            begin([again_x(zz, m)])
        for m in late:
            done([to_x(zz, m)])
            begin([again_y(zz, m)])
        done([to_y(zz, m) for m in late])
        begin([to_core(zz, 1, m) for m in range(4)])
        done([to_x(zz, m) for m in early])
        begin([to_core(zz, 2, m) for m in range(4)])

    def corner(zz):
        done([again_x(zz, m) for m in early] + [again_y(zz, m) for m in late])
        begin([to_core(zz, 3, m) for m in range(4)])

    def column(t, act):
        for up in (True, False):
            zz = z - 1 - t if up else z + 1 + t

            @pl.when(zz >= 0 if up else zz < 4)
            def _():
                act(zz, up)

    def onto_z(t, act):
        for up in (True, False):
            zz = z - t if up else z + t

            @pl.when((zz >= 0) & (z < 3) if up else (zz < 4) & (z > 0))
            def _():
                act(zz, t, up)

    onto_z(0, lambda zz, t, up: token_z(zz, t, up).start())
    token_y(z, True).start()
    begin([quad_x(), quad_y(0)])
    begin([to_x(z, m, True) for m in (3, 0, 2)] + [to_y(z, m, True) for m in (0, 2, 3)])
    vectors = r["vectors"]
    vectors[...] = jnp.zeros(vectors.shape, f32)
    for n, name in enumerate(VECTORS):
        vector = r[name][...].astype(f32)
        vectors[n : n + 1, 0 : vector.shape[0]] = vector.reshape(1, vector.shape[0])
    vectors = vectors[...].astype(bf16)
    for j in range(16):
        base, row = (96, 6) if 6 <= j < 10 else (24, j)
        lead = (j - 6) * D if 6 <= j < 10 else 0
        if j in (10, 11):
            row = j - 3
        if j >= 12:
            break
        base = 4 * rows if base == 96 else rows
        lane = iota((128, D), 1) + lead - base * index
        choose = ((lane == iota((128, D), 0)) & (lane < base)).astype(f32).astype(bf16)
        value = dot(vectors, choose)[row : row + 1, :]
        r["place"][j : j + 1, :] = value
    r["place"][12:16, :] = jnp.zeros((4, D), f32)
    r["placed"][...] = r["place"][...].astype(bf16)
    pack, landed = r["pack"], r["landed"]
    for b in range(active):
        for n, name in enumerate(("wq", "wk", "wv")):
            pack[b, 0:rows, n * width : (n + 1) * width] = r[name][:, b * width : (b + 1) * width]
        pack[b, rows:, :] = jnp.zeros((pack.shape[1] - rows, 3 * width), bf16)
        for n, j in ((0, 10), (2, 11)):
            bias = jnp.broadcast_to(r["place"][j : j + 1, b * width : (b + 1) * width], (8, width))
            pack[b, rows : rows + 8, n * width : (n + 1) * width] = jnp.where(iota((8, width), 0) == 0, bias, 0.0).astype(bf16)
    from_seq = [
        net.send(pack.at[(s + j + 1) % 8 % active], landed.at[f, s], pair("ps"), j, net.seq_peers[j]) for j in range(7)]
    begin([to_x(z, 1, True), to_y(z, 1, True)] + [to_core(z, 0, m, True) for m in range(4)])
    landed[f, s] = pack[s % active]
    tokens_ref[mine, :] = own_ref[...]
    keep = [pltpu.make_async_copy(
        src, full.at[pl.ds(pl.multiple_of(slot(z, y, x) * stride + lead, 8), n)], r["keep_sems"].at[m])
        for m, (src, full, stride, lead, n) in enumerate(pieces)]
    begin(keep)

    def weights_on(t):
        def came(zz, up):
            done(weight_z(zz, t, up))
            spread(zz)

        column(t, came)
        if t < 2:
            onto_z(t + 1, lambda zz, t, up: begin(weight_z(zz, t, up)))

    def tokens_on(t):
        def came(zz, up):
            token_z(zz, t, up).wait_recv()
            token_y(zz).start()

        column(t, came)
        if t < 2:
            onto_z(t + 1, lambda zz, t, up: token_z(zz, t, up).start())

    tokens_on(0)
    onto_z(0, lambda zz, t, up: begin(weight_z(zz, t, up)))
    tokens_on(1)
    quad_step(0)
    onward(z)
    done(from_seq)
    from_fsdp = [net.send(landed.at[f], landed.at[f], pair("pf"), i, net.fsdp_peers[i]) for i in range(3)]
    tokens_on(2)
    weights_on(0)
    quad_step(1)
    corner(z)

    gather_steps = {
        "w": weights_on, "o": lambda t: column(t, lambda zz, up: onward(zz)), "c": lambda t: column(t, lambda zz, up: corner(zz)),
        "q": quad_step}

    def gather_stage(point):
        for step in GATHER.get(point, "").split():
            gather_steps[step[0]](int(step[1]))

    for zz in range(4):
        token_y(zz).wait_recv()
    done(from_fsdp)
    bias = jnp.zeros((8, 3 * width), f32)
    for a in range(4):
        for b in range(8):
            weights_ref[rows * (b * 4 + a) : rows * (b * 4 + a + 1), :] = landed[a, b, 0:rows, :]
            bias = bias + landed[a, b, rows : rows + 8, :].astype(f32)

    state = [r[name] for name in ("q", "k", "v", "fw", "bw", "land", "mix", "a", "norm", "chain")]
    lengths_ref, taps_ref, mixed = r["lengths"], r["taps"], r["d_wide"].at[0 : 8 * count, :]
    forward_math(heads, active, lengths_ref, taps_ref, tokens_ref, weights_ref, bias[0:1], mixed, *state,
                 r["v_wide"], r["score"], gather_stage)

    att = r["att"]
    last = [net.send(mixed.at[rows_at((s + j + 1) % 8, count)], att.at[s], pair("at"), j, net.seq_peers[j]) for j in range(7)]
    att[s] = mixed[mine, :]
    gather_stage("end")
    for zz in range(4):
        for n in range(4):
            done([to_core(zz, n, m) for m in range(4)])
        done(quad_core(zz))
    for copy in keep[:4]:
        copy.wait()

    def sent(zz, t, up):
        token_z(zz, t, up).wait_send()
        for copy in weight_z(zz, t, up) + quad_z(zz, t, up):
            copy.wait_send()

    net.drain()
    for t in range(3):
        onto_z(t, sent)
    for copy in (quad_x(), quad_y(0), quad_y(1)):
        copy.wait_send()
    for zz in range(4):
        for copy in quad_core(zz):
            copy.wait_send()
        token_y(zz).wait_send()
        for m in range(4):
            to_y(zz, m).wait_send()
            to_x(zz, m).wait_send()
            (again_x if m in early else again_y)(zz, m).wait_send()
            for n in range(4):
                to_core(zz, n, m).wait_send()
    vec = jnp.zeros((16, D), f32)
    for n in range(32):
        vec = vec + r["full_small"][16 * n : 16 * n + 16, :].astype(f32)
    r["vec"][...] = vec
    done(last)
    peer_weights = net.send(weights_ref, r["peer_weights"], pair("wp"), 0, net.y_peer)

    sums = ((r["up"], r["acc_up"], r["got_up"], r["far_up"], rows, 0), (r["out"], r["acc_out"], r["got_out"], r["far_out"], rows, 0),
            (r["down"], r["acc_down"], r["got_down"], r["far_down"], 4 * rows, 0),
            (r["down"], r["acc_last"], None, None, 4 * rows, 3 * rows))
    places = ((0, 0), (0, 1), (1, 0), (1, 1))
    moved = {}

    def owner(k, sy, sx, sc):
        return ((z + k + 1) % 4 * 2 + sy) * 4 + sx * 2 + sc

    def to_sibling(pieces_of, distances):
        for k in distances:
            for m, (sy, sx) in enumerate(places):
                for n in pieces_of:
                    full, acc, _, _, stride, lead = sums[n]
                    there = pl.ds(pl.multiple_of(owner(k, sy, sx, oc) * stride + lead, 8), acc.shape[3])
                    moved["c", k, m, n] = net.send(
                        full.at[there], acc.at[k, sy, sx], pair("rc"), (4 * k + m, n), net.c_peer)

    attention = jnp.concatenate([att[b] for b in range(active)], axis=1)
    d_attention = token_math(
        own_ref[...], r["cot"][...], attention, r["up"], r["down"], r["out"], r["vec"], r["gelu"], r["slope"],
        r["output"], r["dr1"], r["small"], lambda: to_sibling((0, 2, 3), (0,)))
    store = [pltpu.make_async_copy(r["output"], r["o_output"], r["store_sems"].at[0])]
    begin(store)
    dattn, dout = r["dattn"], r["dout"]
    for b in range(active):
        dattn[b] = d_attention[:, b * width : (b + 1) * width]
    from_seq = [
        net.send(dattn.at[(s + j + 1) % 8 % active], dout.at[mine], pair("dt"), j, net.seq_peers[j]) for j in range(7)]
    dout[mine, :] = dattn[s % active]
    to_sibling((1,), (0,))
    to_sibling((0, 1, 2, 3), (1, 2, 3))
    small_put, small_got, small_sum = r["small_put"], r["small_got"], r["small_sum"]
    small_put[...] = r["small"][...].astype(bf16)
    moved["m", 0] = net.send(small_put, small_got.at[0], pair("rm"), 0, net.c_peer)

    def add(target, more, base):
        deep, wide = target.shape

        def one(i, carry):
            if wide > D:
                cols = pl.ds(pl.multiple_of(i * D, D), D)
                here, there = (slice(None), cols), (pl.ds(pl.multiple_of(base, 8), deep), cols)
            else:
                here, there = (rows_at(i, rows), slice(None)), (pl.ds(pl.multiple_of(base + i * rows, 8), rows), slice(None))
            target[here] = (target[here].astype(f32) + more[there].astype(f32)).astype(bf16)
            return carry

        lax.fori_loop(0, deep * wide // (rows * D), one, 0)

    def first(k):
        for n in range(4):
            done([moved["c", k, m, n] for m in range(4)])

        def own(n, sy, sx):
            full, acc, _, _, stride, lead = sums[n]
            add(acc.at[k, sy, sx], full, owner(k, sy, sx, c) * stride + lead)

        for i in range(2):
            for n in range(3):
                _, acc, got, _, _, _ = sums[n]
                if n < 2:
                    own(n, i, ox)
                    moved["1", k, i, n] = net.send(acc.at[k, i, ox], got.at[k, i], pair("rx"), (3 * k + i, n), net.x_peer)
                else:
                    own(n, oy, i)
                    moved["1", k, i, n] = net.send(acc.at[k, oy, i], got.at[k, i], pair("ry"), (3 * k + i, 0), net.y_peer)
        for sy, sx in places:
            own(3, sy, sx)
        if k < 3:
            moved["l", k] = net.send(r["acc_last"].at[k], r["last_z"].at[k], pair("lz"), k, net.z_peers[k])
        for i in range(2):
            for n in range(3):
                if n < 2:
                    own(n, i, x)
                else:
                    own(n, y, i)

    def second(k):
        for n, (_, acc, got, _, _, _) in enumerate(sums[:3]):
            for i in range(2):
                moved["1", k, i, n].wait_recv()
                add(acc.at[k, i, x] if n < 2 else acc.at[k, y, i], got.at[k, i], 0)
            if n < 2:
                moved["2", k, n] = net.send(acc.at[k, oy, x], got.at[k, 2], pair("ry"), (3 * k + 2, n), net.y_peer)
            else:
                moved["2", k, n] = net.send(acc.at[k, y, ox], got.at[k, 2], pair("rx"), (3 * k + 2, 0), net.x_peer)

    def third(k):
        for n, (_, acc, got, far, _, _) in enumerate(sums[:3]):
            moved["2", k, n].wait_recv()
            add(acc.at[k, y, x], got.at[k, 2], 0)
            if k < 3:
                moved["3", k, n] = net.send(acc.at[k, y, x], far.at[k], pair("rz"), (k, n), net.z_peers[k])

    def small_step(n):
        before = small_put if n == 0 else small_sum.at[n - 1]
        moved["m", n].wait_recv()
        small_sum[n] = (before[...].astype(f32) + small_got[n].astype(f32)).astype(bf16)
        if n < 2:
            moved["m", n + 1] = net.send(
                small_sum.at[n], small_got.at[n + 1], pair("rm"), n + 1, net.x_peer if n == 0 else net.y_peer)
        else:
            for j in range(3):
                moved["m", 3 + j] = net.send(small_sum.at[2], small_got.at[3 + j], pair("rm"), 3 + j, net.z_peers[j])

    def last_step(n):
        mine_last = r["acc_last"].at[3]
        if n == 0:
            done([moved["l", k] for k in range(3)])
            for sy, sx in places:
                for k in range(3):
                    add(mine_last.at[sy, sx], r["last_z"].at[k, sy, sx], 0)
            moved["l", 3] = net.send(mine_last.at[oy], r["last_y"], pair("lz"), 3, net.y_peer)
        elif n == 1:
            done([moved["l", 3]])
            for sx in range(2):
                add(mine_last.at[y, sx], r["last_y"].at[sx], 0)
            moved["l", 4] = net.send(mine_last.at[y, ox], r["last_x"], pair("lz"), 4, net.x_peer)
        else:
            done([moved["l", 4]])
            r["sdown"][3 * rows : 4 * rows, :] = mine_last[y, x].astype(f32) + r["last_x"][...].astype(f32)

    steps = {"f": first, "s": second, "t": third, "m": small_step, "l": last_step}

    def scatter_stage(point):
        for step in PLAN.get(point, "").split():
            steps[step[0]](int(step[1]))

    scatter_stage("start")
    done(from_seq)
    dqkv, y_got, z_got = r["dqkv"], r["y_got"], r["z_got"]
    over_y = []

    def send_gradients(_):
        for j in range(4):
            there = rows_at((z + j + 1) % 4 * 2 + oy, count)
            over_y.append(net.send(dqkv.at[there], y_got.at[j], pair("dy"), j, net.y_peer))

    steps["y"] = send_gradients
    score = r["score"]
    accumulators = [score.at[0, :, 0:width], score.at[0, :, width : 2 * width], score.at[1, :, 0:width]]
    dw_t = r["slope"].at[:, 0 : 3 * D]
    backward_math(
        heads, active, lengths_ref, taps_ref, tokens_ref, weights_ref, dout, *state, dw_t, r["extra"],
        r["v_wide"], r["d_wide"], *accumulators, r["spread"], r["tap_rows"], r["dqkv"],
        scatter_stage)

    first_put, first_got, second_put, second_got = landed, r["first_got"], r["second_put"], r["second_got"]
    dw = [dw_t[:, n * D : (n + 1) * D].T.astype(bf16) for n in range(3)]
    tail = r["extra"][...].astype(bf16)
    for a in range(4):
        for b in range(8):
            start = rows * (4 * b + a)
            for n in range(3):
                first_put[a, b, 0:rows, n * width : (n + 1) * width] = dw[n][start : start + rows, :]
            first_put[a, b, rows:, :] = tail
    from_fsdp = [
        net.send(first_put.at[(f + i + 1) % 4], first_got.at[f], pair("wf"), i, net.fsdp_peers[i]) for i in range(3)]
    first_got[f] = first_put[f]
    over_z, held = [], {}

    def token_parts(j):
        done([over_y[j]])
        here = rows_at((z + j + 1) % 4 * 2 + y, count)
        value = jnp.where(s < active, dot(dqkv[here, :], weights_ref[...], NT), 0.0)
        value = value + jnp.where(z * 2 + oy < active, dot(y_got[j], r["peer_weights"][...], NT), 0.0)
        if j < 3:
            z_put = r["gelu"].at[:, j * D : (j + 1) * D]
            z_put[...] = value.astype(bf16)
            over_z.append(net.send(z_put, z_got.at[j], pair("dz"), j, net.z_peers[j]))
        else:
            held["kept"] = value + r["dr1"][...]

    def weight_parts(_):
        done(from_fsdp)
        for b in range(8):
            value = first_got[0, b].astype(f32)
            for a in range(1, 4):
                value = value + first_got[a, b].astype(f32)
            second_put[b] = value.astype(bf16)
        held["seq"] = [
            net.send(second_put.at[(s + j + 1) % 8], second_got.at[s], pair("ws"), j, net.seq_peers[j]) for j in range(7)]
        second_got[s] = second_put[s]

    steps.update(z=token_parts, w=weight_parts)
    done([peer_weights])
    scatter_stage("end")
    kept, from_seq = held["kept"], held["seq"]

    def put(name, n):
        store.append(pltpu.make_async_copy(r[name], r["o_" + name], r["store_sems"].at[n]))
        begin(store[-1:])

    for n, (name, (_, acc, _, far, _, _)) in enumerate(zip(("sup", "sout", "sdown"), sums)):
        value = acc[3, y, x].astype(f32)
        for j in range(3):
            done([moved["3", j, n]])
            value = value + far[j].astype(f32)
        r[name][0 : value.shape[0], :] = value
        put(name, 1 + n)
    value = small_sum[2].astype(f32)
    for j in range(3):
        done([moved["m", 3 + j]])
        value = value + small_got[3 + j].astype(f32)
    lines = r["lines"]
    lines[...] = jnp.zeros(lines.shape, f32)
    lines[0:8, :] = select_lanes(value, rows * index, 0)[0:8, :]
    b_up = jnp.zeros((16, 128), f32)
    for j in range(4):
        b_up = b_up + jnp.where(iota((16, 128), 0) == 6 + j, select_lanes(value, 4 * rows * index, j * D), 0.0)
    lines[6:7, :] = column_sum(b_up)
    done(over_z)
    for j in range(3):
        kept = kept + z_got[j].astype(f32)
    r["dtok"][...] = kept.astype(bf16)
    put("dtok", 4)
    done(from_seq)
    bias = jnp.zeros((8, 128), f32)
    bias_v = jnp.zeros((8, 128), f32)
    for b in range(active):
        for n, name in enumerate(("dwq", "dwk", "dwv")):
            r[name][:, b * width : (b + 1) * width] = second_got[b, 0:rows, n * width : (n + 1) * width].astype(f32)
        tail = second_got[b, rows:, :].astype(f32)
        bias = bias + select_lanes(tail[:, 0:width], rows * index, b * width)
        bias_v = bias_v + select_lanes(tail[:, 2 * width :], rows * index, b * width)
        lines[16 + b * heads : 16 + (b + 1) * heads, :] = tail[1 : 1 + heads, 0:128]
    lines[7:8, :] = bias[0:1]
    lines[8:9, :] = bias_v[0:1]
    for n, name in enumerate(("dwq", "dwk", "dwv", "lines")):
        put(name, 5 + n)
    net.drain()
    for copy in store:
        copy.wait()


def layer(heads, active, lengths, taps, own, cot, w_query, w_key, w_value, vectors, w_up, w_out, w_down):
    count, rows = own.shape[0], w_query.shape[0]
    total = 8 * count
    width = heads * HD
    shape, buffer, dma = jax.ShapeDtypeStruct, pltpu.VMEM, pltpu.SemaphoreType.DMA
    smem, anywhere = pl.BlockSpec(memory_space=pltpu.SMEM), pl.BlockSpec(memory_space=pl.ANY)
    ins = ["lengths", "in_taps", "in_own", "in_cot", "in_wq", "in_wk", "in_wv", "in_wup", "in_wout", "in_wdown"]
    ins += ["in_" + name for name in VECTORS]
    outs = {
        "output": shape((count, D), bf16), "dtok": shape((count, D), bf16),
        "dwq": shape((rows, D), f32), "dwk": shape((rows, D), f32), "dwv": shape((rows, D), f32),
        "sup": shape((rows, FF), f32), "sout": shape((rows, D), f32), "sdown": shape((4 * rows, D), f32),
        "lines": shape((32, 128), f32),
    }
    sizes = {"up": (rows, FF), "out": (rows, D), "down": (3 * rows, D)}
    scratch = {
        "own": buffer((count, D), bf16), "cot": buffer((count, D), bf16),
        "wq": buffer((rows, D), bf16), "wk": buffer((rows, D), bf16), "wv": buffer((rows, D), bf16),
        "vectors": buffer((16, 128), f32), "taps": buffer((HEADS, CONV), bf16), "place": buffer((16, D), f32), "placed": buffer((16, D), bf16),
        "tokens": buffer((total, D), bf16), "weights": buffer((D, 3 * width), bf16),
        "pack": buffer((active, rows + 8, 3 * width), bf16), "landed": buffer((4, 8, rows + 8, 3 * width), bf16),
        "up": buffer((D, FF), bf16), "full_small": buffer((512, D), bf16), "out": buffer((D, D), bf16),
        "down": buffer((FF, D), bf16), "vec": buffer((16, D), f32),
        "q": buffer((total, width), bf16), "k": buffer((total, width), bf16), "v": buffer((total, width), f32),
        "fw": buffer((heads, total, SLOTS), bf16), "bw": buffer((heads, total, SLOTS), bf16),
        "land": buffer((2, SLOTS, width), f32), "mix": buffer((2, width, SLOTS), f32),
        "a": buffer((heads, SLOTS, SLOTS), f32), "norm": buffer((heads, SLOTS, SLOTS), f32),
        "chain": buffer((NS_ITERS + 1, heads, 4, 2, SLOTS, SLOTS), bf16),
        "v_wide": buffer((total + 128, width), bf16),
        "score": buffer((heads, total, SLOTS), f32), "att": buffer((8, count, width), bf16),
        "gelu": buffer((count, FF), bf16), "slope": buffer((count, FF), f32), "dr1": buffer((count, D), f32),
        "small": buffer((16, D), f32), "small_put": buffer((16, D), bf16), "small_got": buffer((6, 16, D), bf16),
        "small_sum": buffer((3, 16, D), bf16),
        "dattn": buffer((active, count, width), bf16), "dout": buffer((total, width), bf16),
        "d_wide": buffer((total + 128, width), bf16),
        "spread": buffer((heads, 128, 256), f32), "tap_rows": buffer((128, 256), f32),
        "dqkv": buffer((total, 3 * width), bf16), "peer_weights": buffer((D, 3 * width), bf16),
        "extra": buffer((8, 3 * width), f32),
        "y_got": buffer((4, count, 3 * width), bf16), "z_got": buffer((3, count, D), bf16),
        "first_got": buffer((4, 8, rows + 8, 3 * width), bf16),
        "second_put": buffer((8, rows + 8, 3 * width), bf16), "second_got": buffer((8, rows + 8, 3 * width), bf16),
    }
    for name, size in sizes.items():
        scratch["acc_" + name] = buffer((4, 2, 2, *size), bf16)
        scratch["got_" + name] = buffer((4, 3, *size), bf16)
        scratch["far_" + name] = buffer((3, *size), bf16)
    scratch["acc_last"], scratch["last_z"] = buffer((4, 2, 2, rows, D), bf16), buffer((3, 2, 2, rows, D), bf16)
    scratch["last_y"], scratch["last_x"] = buffer((2, rows, D), bf16), buffer((rows, D), bf16)
    for name, vector in zip(VECTORS, vectors):
        scratch[name] = buffer(vector.shape, bf16)
    for name, value in outs.items():
        scratch[name] = buffer(value.shape, value.dtype)
    pairs = {
        "tz": (6,), "ty": (4,), "ps": (7,), "pf": (3,), "at": (7,), "gz": (6, 4), "gy": (4, 8), "gx": (4, 8), "gc": (4, 4, 4),
        "rc": (16, 4), "rx": (12, 2), "ry": (12, 2), "rz": (3, 3), "rm": (6,), "dt": (7,), "dy": (4,), "dz": (3,),
        "wf": (3,), "ws": (7,), "wp": (1,),
        "qx": (1,), "qy": (2,), "qz": (6, 4), "qc": (4, 4), "lz": (5,),
    }
    for name, size in pairs.items():
        scratch[name + "_send"] = dma(size)
        scratch[name + "_recv"] = dma(size)
    scratch["load_sems"], scratch["keep_sems"], scratch["store_sems"] = dma((15,)), dma((5,)), dma((9,))
    names = ins + ["o_" + name for name in outs] + list(scratch)
    return pl.pallas_call(
        partial(layer_kernel, heads, active, names),
        out_shape=tuple(outs.values()),
        in_specs=[smem] + [anywhere] * (len(ins) - 1),
        out_specs=tuple([anywhere] * len(outs)),
        scratch_shapes=list(scratch.values()),
        compiler_params=pltpu.CompilerParams(collective_id=0, has_side_effects=True, vmem_limit_bytes=63_000_000),
    )(lengths, taps, own, cot, w_query, w_key, w_value, w_up, w_out, w_down, *vectors)


def finish_kernel(rows, hidden_rows, *refs):
    big, lines, outs, small, taps, held, sems = refs[:8], refs[8], refs[9:17], refs[17:26], refs[26], refs[27:35], refs[35]
    loads = [pltpu.make_async_copy(src, dst, sems.at[0, n]) for n, (src, dst) in enumerate(zip(big, held))]
    copies = [pltpu.make_async_copy(src, dst, sems.at[1, n]) for n, (src, dst) in enumerate(zip(held, outs))]
    begin(loads)
    for j, ref in enumerate(small):
        ref[...] = lines[j, 0 : ref.shape[0]]
    taps[...] = lines[16 : 16 + HEADS, 0:CONV]
    for load, copy in zip(loads, copies):
        load.wait()
        copy.start()
    for copy in copies:
        copy.wait()


def finish(results, hidden_rows):
    *big, lines = results
    rows = big[2].shape[0]
    shape = jax.ShapeDtypeStruct
    vmem, anywhere = pl.BlockSpec(memory_space=pltpu.VMEM), pl.BlockSpec(memory_space=pl.ANY)
    small = [shape((hidden_rows if j == 6 else rows,), f32) for j in range(9)]
    return pl.pallas_call(
        partial(finish_kernel, rows, hidden_rows),
        out_shape=tuple([shape(value.shape, value.dtype) for value in big] + small + [shape((HEADS, CONV), f32)]),
        in_specs=[anywhere] * 8 + [vmem],
        out_specs=tuple([anywhere] * 8 + [vmem] * 10),
        scratch_shapes=[pltpu.VMEM(value.shape, value.dtype) for value in big] + [pltpu.SemaphoreType.DMA((2, 8))],
    )(*big, lines)


def product(form, left, right):
    return jnp.einsum(form, left, right, preferred_element_type=f32)


def layer_norm(inputs, gain, shift):
    average = jnp.mean(inputs, axis=-1, keepdims=True)
    centred = inputs - average
    variance = jnp.mean(centred * centred, axis=-1, keepdims=True)
    return centred * lax.rsqrt(variance + epsilon) * gain + shift


def gelu_exact(inputs):
    return jax.nn.gelu(inputs, approximate=False)


def token_part(tokens, cot, attention, w_out, w_up, w_down, b_out, b_up, b_down, g_attn, s_attn, g_mlp, s_mlp):
    out_proj = product("td,de->te", attention, w_out) + b_out
    hidden, norm_one_back = jax.vjp(layer_norm, tokens.astype(f32) + out_proj, g_attn, s_attn)
    hidden_low = hidden.astype(bf16)
    up_pre = product("td,df->tf", hidden_low, w_up) + b_up
    gelu_val, gelu_back = jax.vjp(gelu_exact, up_pre)
    gelu_low = gelu_val.astype(bf16)
    down_pre = product("tf,fd->td", gelu_low, w_down) + b_down
    output, norm_two_back = jax.vjp(layer_norm, hidden + down_pre, g_mlp, s_mlp)
    d_r2, dg_mlp, ds_mlp = norm_two_back(cot.astype(f32))
    d_down = d_r2.astype(bf16)
    db_down = jnp.sum(d_down.astype(f32), axis=0)
    dw_down = product("tf,td->fd", gelu_low, d_down)
    d_gelu = product("td,fd->tf", d_down, w_down)
    d_up = gelu_back(d_gelu)[0].astype(bf16)
    db_up = jnp.sum(d_up.astype(f32), axis=0)
    dw_up = product("td,tf->df", hidden_low, d_up)
    d_hidden = product("tf,df->td", d_up, w_up) + d_r2
    d_r1, dg_attn, ds_attn = norm_one_back(d_hidden)
    d_out = d_r1.astype(bf16)
    db_out = jnp.sum(d_out.astype(f32), axis=0)
    dw_out = product("td,te->de", attention, d_out)
    d_attn = product("te,de->td", d_out, w_out)
    smalls = (db_out, db_up, db_down, dg_attn, ds_attn, dg_mlp, ds_mlp)
    return output.astype(bf16), d_r1, d_attn, dw_out, dw_up, dw_down, smalls
def local(sizes, *args):
    (tokens, cotangent, doc_lengths, w_query, b_query, w_key, w_value, b_value, w_out, b_out, w_up, b_up,
     w_down, b_down, g_attn, s_attn, g_mlp, s_mlp, conv_kernel) = args
    seq, fsdp = sizes
    devices = seq * fsdp
    fast = sizes == (8, 4)
    axes = ("seq", "fsdp")
    rows = D // devices
    hidden_rows = FF // devices
    own_tokens, own_cot, lengths = tokens[0], cotangent[0], doc_lengths[0]
    count = own_tokens.shape[0]
    total = count * seq
    heads = -(-HEADS // seq)
    width = heads * HD
    active = HEADS // heads
    s = lax.axis_index("seq")

    taps = conv_kernel.T
    if fast:
        vectors = (b_out, b_down, g_attn, s_attn, g_mlp, s_mlp, b_up, b_query, b_value)
        results = layer(
            heads, active, lengths, taps, own_tokens, own_cot, w_query, w_key, w_value, vectors, w_up, w_out, w_down)
        output, d_tokens, dw_query, dw_key, dw_value, s_up, s_out, s_down, *g, d_kernel = finish(results, hidden_rows)
        return (
            output[None], d_tokens[None], dw_query, g[7], dw_key, dw_value, g[8], s_out, g[0],
            s_up, g[6], s_down, g[1], g[2], g[3], g[4], g[5], d_kernel.T)

    own = (s * fsdp + lax.axis_index("fsdp")) * rows
    pack_rows = -(-rows // 8) * 8 + 8
    lead = pack_rows - 8

    def placed(vector, at, size):
        return lax.dynamic_update_slice(jnp.zeros((size,), bf16), vector, (at,))

    bias_q, bias_v = (placed(b, own, D).reshape(active, 1, width) for b in (b_query, b_value))
    bias = jnp.concatenate([bias_q, jnp.zeros((active, 1, width), bf16), bias_v], axis=2)
    bias = jnp.pad(bias, ((0, 0), (0, 7), (0, 0)))
    small = [placed(v, own, D) for v in (b_out, b_down, g_attn, s_attn, g_mlp, s_mlp)]
    small = jnp.concatenate(small + [placed(b_up, own * 4, FF), jnp.zeros((6 * D,), bf16)]).reshape(16, D)
    blocks = []
    for b in range(active):
        cols = slice(b * width, (b + 1) * width)
        blocks.append(jnp.concatenate([w_query[:, cols], w_key[:, cols], w_value[:, cols]], axis=1))
    pack = jnp.concatenate([jnp.pad(jnp.stack(blocks), ((0, 0), (0, lead - rows), (0, 0))), bias], axis=1)
    all_tokens = lax.all_gather(own_tokens, "seq").reshape(total, D)
    all_pack = lax.all_gather(lax.all_to_all(
        jnp.take(pack, jnp.arange(seq) % active, axis=0), "seq", 0, 0), "fsdp", axis=1).reshape(
            devices, pack_rows, 3 * width)
    qkv_weights = all_pack[:, :rows].reshape(D, 3 * width)
    full_up, full_small, full_down, full_out = (
        lax.all_gather(w, axes, tiled=True) for w in (w_up, small, w_down, w_out))
    mixed, *state = attention_forward(heads, active, all_tokens, qkv_weights, all_pack[:, lead:], lengths, taps)
    attention = lax.all_to_all(mixed.reshape(seq, count, width), "seq", 0, 0)
    vectors = jnp.sum(full_small.reshape(devices, 16, D).astype(f32), axis=0)
    attention = jnp.transpose(attention[:active], (1, 0, 2)).reshape(count, D)
    output, d_r1, d_attn, dw_out, dw_up, dw_down, smalls = token_part(
        own_tokens, own_cot, attention, full_out, full_up, full_down, vectors[0], vectors[6:10].reshape(FF),
        *(vectors[j] for j in range(1, 6)))
    d_attn = jnp.transpose(d_attn.astype(bf16).reshape(count, active, width), (1, 0, 2))
    d_mixed = lax.all_to_all(jnp.take(d_attn, jnp.arange(seq) % active, axis=0), "seq", 0, 0)
    s_up, s_out, s_down = (
        lax.psum_scatter(w, axes, scatter_dimension=0, tiled=True) for w in (dw_up, dw_out, dw_down))
    small = [lax.psum_scatter(v, axes, scatter_dimension=0, tiled=True) for v in smalls]
    part, dw, extra = attention_backward(
        heads, active, all_tokens, qkv_weights, d_mixed.reshape(total, width), lengths, taps, state)
    token_parts = lax.all_to_all(part.reshape(seq, count, D), "seq", 0, 0)
    d_tokens = (d_r1 + jnp.sum(token_parts.astype(f32), axis=0)).astype(bf16)
    extra = lax.psum(lax.all_gather(extra, "seq")[:active], "fsdp")
    dw = jnp.transpose(dw.reshape(width, 3, devices, rows), (2, 3, 1, 0)).reshape(devices, rows, 3 * width)
    dw = lax.all_to_all(dw, axes, 0, 0)
    dw = jnp.sum(dw.reshape(seq, fsdp, rows, 3, width)[:active], axis=1)
    dw_query, dw_key, dw_value = (jnp.transpose(dw[:, :, j], (1, 0, 2)).reshape(rows, D) for j in range(3))
    db_query = lax.dynamic_slice_in_dim(extra[:, 0, :width].reshape(D), own, rows)
    db_value = lax.dynamic_slice_in_dim(extra[:, 0, 2 * width :].reshape(D), own, rows)
    d_kernel = jnp.transpose(extra[:, 1 : 1 + heads, :CONV].reshape(active * heads, CONV), (1, 0))
    s_b_out, s_b_up, s_b_down, s_g_attn, s_s_attn, s_g_mlp, s_s_mlp = small
    return (
        output[None], d_tokens[None], dw_query, db_query, dw_key, dw_value, db_value, s_out, s_b_out,
        s_up, s_b_up, s_down, s_b_down, s_g_attn, s_s_attn, s_g_mlp, s_s_mlp, d_kernel)


def solution(mesh):
    sizes = (mesh.shape["seq"], mesh.shape["fsdp"])
    both = ("seq", "fsdp")
    wide, flat, stream = P(both, None), P(both), P("fsdp", "seq", None)
    in_specs = (stream, stream, P("fsdp", None), wide, flat, wide, wide, flat, wide, flat, wide, flat, wide, flat,
                flat, flat, flat, flat, P())
    out_specs = (stream, stream, wide, flat, wide, wide, flat, wide, flat, wide, flat, wide, flat, flat, flat, flat,
                 flat, P())
    return jax.shard_map(partial(local, sizes), mesh=mesh, in_specs=in_specs, out_specs=out_specs, check_vma=False)
```

```python
from functools import partial
import math

import jax
import jax.numpy as jnp
from jax import lax
from jax.experimental import pallas as pl
from jax.experimental.pallas import tpu as pltpu
from jax.sharding import PartitionSpec as P

D = 768
HEADS = 12
HD = 64
FF = 3072
NLAND = 64
NS_ITERS = 6
CONV = 33
REACH = CONV // 2
DOCS = 4
SLOTS = 256
SCALE = 1.0 / math.sqrt(HD)

HIGHEST = lax.Precision.HIGHEST
epsilon = 1e-05
masked_score = -1e30
f32 = jnp.float32
bf16 = jnp.bfloat16
MESH = pl.DeviceIdType.MESH
VMEM_BYTES = 56 * 1024 * 1024


def greet(peers):
    barrier = pltpu.get_barrier_semaphore()
    for peer in peers:
        pl.semaphore_signal(barrier, inc=1, device_id=peer, device_id_type=MESH)
    pl.semaphore_wait(barrier, len(peers))


def remote(src, dst, send_sem, recv_sem, peer):
    return pltpu.make_async_remote_copy(
        src_ref=src, dst_ref=dst, send_sem=send_sem, recv_sem=recv_sem,
        device_id=peer, device_id_type=MESH,
    )


BLOCK = 256
NN = (((1,), (0,)), ((), ()))
NT = (((1,), (1,)), ((), ()))


def dot(left, right, dims=NN):
    return lax.dot_general(left, right, dims, preferred_element_type=f32)


def split(value):
    upper = value.astype(bf16)
    return upper, (value - upper.astype(f32)).astype(bf16)


def dot3(left, right, dims=NN):
    return dot(left[0], right[0], dims) + (dot(left[0], right[1], dims) + dot(left[1], right[0], dims))


def iota(shape, dim):
    return lax.broadcasted_iota(jnp.int32, shape, dim)


def doc_table(lengths_ref):
    ends, start = [], 0
    for d in range(DOCS):
        start = start + lengths_ref[d]
        ends.append(start)
    return ends


def slot_bounds(lengths_ref, shape, dim):
    ends = doc_table(lengths_ref)
    slot = iota(shape, dim)
    doc, seg = slot // NLAND, slot % NLAND
    length, end = jnp.zeros(shape, jnp.int32), jnp.zeros(shape, jnp.int32)
    for d in range(DOCS):
        length = jnp.where(doc == d, lengths_ref[d], length)
        end = jnp.where(doc == d, ends[d], end)
    start = end - length
    return start, end, start + seg * length // NLAND, start + (seg + 1) * length // NLAND


def same_doc(lengths_ref, left, right):
    ends = doc_table(lengths_ref)
    a, b = jnp.zeros(left.shape, jnp.int32), jnp.zeros(right.shape, jnp.int32)
    for d in range(DOCS):
        a = a + (left >= ends[d]).astype(jnp.int32)
        b = b + (right >= ends[d]).astype(jnp.int32)
    return a == b


def head_mask(shape, dim, h):
    return (iota(shape, dim) // HD == h).astype(f32)


def tap_index():
    return iota((128, 256), 1) - iota((128, 256), 0) - 64 + REACH


def toeplitz(taps_ref, head, mirrored):
    taps = taps_ref[...].astype(f32)
    taps = jnp.sum(jnp.where(iota(taps.shape, 0) == head, taps, 0.0), axis=0, keepdims=True)
    tap = tap_index()
    mat = jnp.zeros((128, 256), f32)
    for o in range(CONV):
        n = CONV - 1 - o if mirrored else o
        mat = jnp.where(tap == o, taps[:, n : n + 1], mat)
    return mat


def clear_edges(ref, total):
    ref[0:64, :] = jnp.zeros((64, ref.shape[1]), ref.dtype)
    ref[total + 64 : total + 128, :] = jnp.zeros((64, ref.shape[1]), ref.dtype)


def forward_math(heads, active, lengths_ref, taps_ref, tokens_ref, weights_ref, bias,
                 mixed_ref, q_ref, k_ref, v_ref, fw_ref, bw_ref, land_ref, mix_ref, a_ref, norm_ref, chain_ref,
                 v_wide, score, stage):
    total = tokens_ref.shape[0]
    width = heads * HD
    part = lax.axis_index("seq") % active
    steps = total // BLOCK
    row_start, row_end, row_low, row_top = slot_bounds(lengths_ref, (1, SLOTS), 1)
    _, _, col_low, col_top = slot_bounds(lengths_ref, (SLOTS, 1), 0)
    count = (col_top - col_low).astype(f32)
    clear_edges(v_wide, total)
    land_ref[...] = jnp.zeros(land_ref.shape, f32)

    def project(i, carry):
        at = pl.ds(pl.multiple_of(i * BLOCK, BLOCK), BLOCK)
        qkv = dot(tokens_ref[at, :], weights_ref[...]) + bias
        q, k, v = (qkv[:, j * width : (j + 1) * width] for j in range(3))
        q_low, k_low = q.astype(bf16), k.astype(bf16)
        q_ref[at, :], k_ref[at, :] = q_low, k_low
        v_ref[at, :] = v
        v_wide[pl.ds(pl.multiple_of(i * BLOCK + 64, 64), BLOCK), :] = v.astype(bf16)
        t = i * BLOCK + iota((1, BLOCK), 1)
        member = ((t >= col_low) & (t < col_top)).astype(f32).astype(bf16)
        land_ref[0] += dot(member, q_low)
        land_ref[1] += dot(member, k_low)
        return carry

    lax.fori_loop(0, steps, project, 0)
    stage("proj")
    ql, kl = land_ref[0] / count, land_ref[1] / count
    land_ref[0], land_ref[1] = ql, kl
    masks = [head_mask((1, width), 1, h) for h in range(heads)]
    ql_low = [(ql * masks[h]).astype(bf16) for h in range(heads)]
    kl_low = [(kl * masks[h]).astype(bf16) for h in range(heads)]

    def scores(i, tops):
        at = pl.ds(pl.multiple_of(i * BLOCK, BLOCK), BLOCK)
        t = i * BLOCK + iota((BLOCK, 1), 0)
        valid = (t >= row_start) & (t < row_end)
        out = []
        for h in range(heads):
            s = jnp.where(valid, SCALE * dot(q_ref[at, :], kl_low[h], NT), masked_score)
            e = jnp.exp(s - jnp.max(s, axis=1, keepdims=True))
            fw_ref[h, at, :] = (e / jnp.sum(e, axis=1, keepdims=True)).astype(bf16)
            s = jnp.where(valid, SCALE * dot(k_ref[at, :], ql_low[h], NT), masked_score)
            score[h, at, :] = s
            out.append(jnp.maximum(tops[h], jnp.max(s, axis=0, keepdims=True)))
        return tuple(out)

    tops = lax.fori_loop(0, steps, scores, tuple(jnp.full((1, SLOTS), masked_score, f32) for _ in range(heads)))
    stage("scores")

    def gather(i, carry):
        at = pl.ds(pl.multiple_of(i * BLOCK, BLOCK), BLOCK)
        v_t = split(v_ref[at, :].T)
        out = []
        for h in range(heads):
            e = jnp.exp(score[h, at, :] - tops[h])
            score[h, at, :] = e
            out.append((carry[h][0] + jnp.sum(e, axis=0, keepdims=True), carry[h][1] + dot3(v_t, split(e))))
        return tuple(out)

    sums = lax.fori_loop(0, steps, gather, tuple(
        (jnp.zeros((1, SLOTS), f32), jnp.zeros((width, SLOTS), f32)) for _ in range(heads)))
    scale = [1.0 / sums[h][0] for h in range(heads)]
    tall = [head_mask((width, 1), 0, h) for h in range(heads)]
    key_mix_t = [sums[h][1] * scale[h] * tall[h] for h in range(heads)]

    def normalize(i, carry):
        at = pl.ds(pl.multiple_of(i * BLOCK, BLOCK), BLOCK)
        for h in range(heads):
            bw_ref[h, at, :] = (score[h, at, :] * scale[h]).astype(bf16)
        return carry

    lax.fori_loop(0, steps, normalize, 0)
    stage("key_mix")

    block = iota((SLOTS, SLOTS), 0) // NLAND == iota((SLOTS, SLOTS), 1) // NLAND
    diagonal = iota((SLOTS, SLOTS), 0) == iota((SLOTS, SLOTS), 1)
    state = []
    for h in range(heads):
        s = jnp.where(block, SCALE * dot3(split(ql * masks[h]), split(kl), NT), masked_score)
        e = jnp.exp(s - jnp.max(s, axis=1, keepdims=True))
        a = e / jnp.sum(e, axis=1, keepdims=True)
        norm = jnp.sum(jnp.sum((a * a).reshape(DOCS, NLAND, SLOTS), axis=1, keepdims=True), axis=2, keepdims=True)
        norm = jnp.broadcast_to(norm, (DOCS, NLAND, SLOTS)).reshape(SLOTS, SLOTS)
        a_ref[h], norm_ref[h] = a, norm
        u = a / norm
        a_split = split(a)
        state.append((split(u), split(dot3(a_split, split(u), NT))))
    for step in range(NS_ITERS):
        fresh = []
        for h in range(heads):
            u, p = state[h]
            p_full = p[0].astype(f32) + p[1].astype(f32)
            q_full = dot3(p, p)
            q = split(q_full)
            f_full = jnp.where(diagonal, 13.0, 0.0) - 15.0 * p_full + 7.0 * q_full - dot3(p, q)
            f = split(f_full)
            for n, pair in enumerate((u, p, q, f)):
                for half in range(2):
                    chain_ref[step, h, n, half] = pair[half]
            p_next = None if step == NS_ITERS - 1 else split(0.25 * dot3(p, f))
            u_next = split(0.25 * dot3(f, u))
            fresh.append((u_next, p_next))
        stage("newton" + str(step))
        state = fresh
    mix_t = jnp.zeros((width, SLOTS), f32)
    key_t = jnp.zeros((width, SLOTS), f32)
    for h in range(heads):
        u = state[h][0]
        chain_ref[NS_ITERS, h, 0, 0], chain_ref[NS_ITERS, h, 0, 1] = u
        mix_t = mix_t + dot3(split(key_mix_t[h]), u)
        key_t = key_t + key_mix_t[h]
    mix_ref[0], mix_ref[1] = mix_t, key_t
    stage("mix")
    mix_low = [(mix_t * tall[h]).astype(bf16) for h in range(heads)]
    mats = [toeplitz(taps_ref, part * heads + h, False) for h in range(heads)]

    def output(i, carry):
        at = pl.ds(pl.multiple_of(i * 128, 128), 128)
        t = i * 128 + iota((128, 1), 0)
        near = same_doc(lengths_ref, t, i * 128 - 64 + iota((1, 256), 1))
        window = v_wide[pl.ds(pl.multiple_of(i * 128, 128), 256), :]
        out = jnp.zeros((128, width), f32)
        for h in range(heads):
            out = out + dot(fw_ref[h, at, :], mix_low[h], NT)
            conv = dot(jnp.where(near, mats[h], 0.0).astype(bf16), window)
            out = out + conv * masks[h]
        mixed_ref[at, :] = out.astype(bf16)
        return carry

    lax.fori_loop(0, total // 128, output, 0)


def forward_kernel(heads, active, lengths_ref, taps_ref, tokens_ref, weights_ref, bias_ref, *refs):
    bias = jnp.sum(bias_ref[...].astype(f32), axis=0)[0:1]
    forward_math(heads, active, lengths_ref, taps_ref, tokens_ref, weights_ref, bias, *refs, lambda n: None)


def attention_forward(heads, active, tokens, weights, bias, lengths, taps):
    total = tokens.shape[0]
    width = heads * HD
    shape = jax.ShapeDtypeStruct
    vmem, smem = (pl.BlockSpec(memory_space=m) for m in (pltpu.VMEM, pltpu.SMEM))
    chain = (heads, 4, 2, SLOTS, SLOTS)
    return pl.pallas_call(
        partial(forward_kernel, heads, active),
        out_shape=(
            shape((total, width), bf16),
            shape((total, width), bf16),
            shape((total, width), bf16),
            shape((total, width), f32),
            shape((heads, total, SLOTS), bf16),
            shape((heads, total, SLOTS), bf16),
            shape((2, SLOTS, width), f32),
            shape((2, width, SLOTS), f32),
            shape((heads, SLOTS, SLOTS), f32),
            shape((heads, SLOTS, SLOTS), f32),
            shape((NS_ITERS + 1, *chain), bf16),
        ),
        in_specs=[smem, vmem, vmem, vmem, vmem],
        out_specs=tuple([vmem] * 11),
        scratch_shapes=[
            pltpu.VMEM((total + 128, width), bf16),
            pltpu.VMEM((heads, total, SLOTS), f32),
        ],
        compiler_params=pltpu.CompilerParams(vmem_limit_bytes=VMEM_BYTES),
    )(lengths, taps, tokens, weights, bias)


def backward_math(heads, active, lengths_ref, taps_ref, tokens_ref, weights_ref, dout_ref, q_ref, k_ref, v_ref, fw_ref,
                  bw_ref, land_ref, mix_ref, a_ref, norm_ref, chain_ref, dw_ref, extra_ref,
                  v_wide, d_wide, dq_acc, dk_acc, dv_acc, spread, tap_rows, dqkv, stage):
    total = tokens_ref.shape[0]
    width = heads * HD
    part = lax.axis_index("seq") % active
    steps = total // BLOCK
    _, _, row_low, row_top = slot_bounds(lengths_ref, (1, SLOTS), 1)
    inverse = 1.0 / (row_top - row_low).astype(f32)
    clear_edges(v_wide, total)
    clear_edges(d_wide, total)
    masks = [head_mask((1, width), 1, h) for h in range(heads)]
    tall = [head_mask((width, 1), 0, h) for h in range(heads)]
    ql, kl = land_ref[0], land_ref[1]
    mix_t, key_t = mix_ref[0], mix_ref[1]
    kl_low = [(kl * masks[h]).astype(bf16) for h in range(heads)]
    ql_low = [(ql * masks[h]).astype(bf16) for h in range(heads)]
    mix_low = [(mix_t * tall[h]).astype(bf16) for h in range(heads)]

    def front(i, carry):
        at = pl.ds(pl.multiple_of(i * BLOCK, BLOCK), BLOCK)
        inner = pl.ds(pl.multiple_of(i * BLOCK + 64, 64), BLOCK)
        do = dout_ref[at, :]
        d_wide[inner, :] = do
        v_wide[inner, :] = v_ref[at, :].astype(bf16)
        do_t = do.astype(f32).T.astype(bf16)
        q_t = q_ref[at, :].astype(f32).T.astype(bf16)
        dq = jnp.zeros((BLOCK, width), f32)
        out = []
        for h in range(heads):
            fw = fw_ref[h, at, :]
            wide = fw.astype(f32)
            d_fw = dot(do, mix_low[h])
            ds = (SCALE * wide * (d_fw - jnp.sum(wide * d_fw, axis=1, keepdims=True))).astype(bf16)
            dq = dq + dot(ds, kl_low[h])
            out.append((carry[h][0] + dot(do_t, fw), carry[h][1] + dot(q_t, ds)))
        dq_acc[at, :] = dq
        return tuple(out)

    zeros = jnp.zeros((width, SLOTS), f32)
    sums = lax.fori_loop(0, steps, front, tuple((zeros, zeros) for _ in range(heads)))
    stage("front")
    dmix_t = [sums[h][0] * tall[h] for h in range(heads)]
    dkl_t = zeros
    for h in range(heads):
        dkl_t = dkl_t + sums[h][1] * tall[h]
    key = key_t.T
    ql_t = ql.T
    block = iota((SLOTS, SLOTS), 0) // NLAND == iota((SLOTS, SLOTS), 1) // NLAND
    du, dp, dkey_t = [], [None] * heads, []
    for h in range(heads):
        pair = split(dmix_t[h])
        du.append(jnp.where(block, dot3(split(key), pair), 0.0))
        dkey_t.append(dot3(pair, (chain_ref[NS_ITERS, h, 0, 0], chain_ref[NS_ITERS, h, 0, 1]), NT))

    def unwind(step, du, dp):
        du, dp = list(du), list(dp)
        for h in range(heads):
            u, p, q, f = ((chain_ref[step, h, n, 0], chain_ref[step, h, n, 1]) for n in range(4))
            du_pair = split(du[h])
            df = 0.25 * dot3(du_pair, u, NT)
            du[h] = 0.25 * dot3(f, du_pair)
            if dp[h] is not None:
                dp_pair = split(dp[h])
                df = df + 0.25 * dot3(p, dp_pair)
                base = 0.25 * dot3(dp_pair, f)
            else:
                base = 0.0
            df_pair = split(df)
            dq = split(7.0 * df - dot3(p, df_pair))
            dp[h] = base - 15.0 * df - dot3(df_pair, q) + (dot3(dq, p) + dot3(p, dq))
        return tuple(du), tuple(dp)

    du, dp = unwind(NS_ITERS - 1, du, dp)
    stage("newton4")
    du, dp = lax.fori_loop(0, NS_ITERS - 3, lambda n, carry: unwind(NS_ITERS - 2 - n, *carry), (du, dp))
    stage("newton1")
    du, dp = lax.fori_loop(0, 2, lambda n, carry: unwind(1 - n, *carry), (du, dp))
    dql = jnp.zeros((SLOTS, width), f32)
    for h in range(heads):
        a, norm = a_ref[h], norm_ref[h]
        u0 = chain_ref[0, h, 0, 0].astype(f32) + chain_ref[0, h, 0, 1].astype(f32)
        p0 = chain_ref[0, h, 1, 0].astype(f32) + chain_ref[0, h, 1, 1].astype(f32)
        a_pair = split(a)
        inner = dp[h] * p0 + du[h] * u0
        inner = jnp.sum(jnp.sum(inner.reshape(DOCS, NLAND, SLOTS), axis=1, keepdims=True), axis=2, keepdims=True)
        inner = jnp.broadcast_to(inner, (DOCS, NLAND, SLOTS)).reshape(SLOTS, SLOTS)
        da = (dot3(split(dp[h] + dp[h].T), a_pair) + du[h] - 2.0 * a * inner) / norm
        dsa = split(SCALE * a * (da - jnp.sum(a * da, axis=1, keepdims=True)))
        dql = dql + dot3(dsa, split(kl * masks[h]))
        dkl_t = dkl_t + dot3(split(ql_t * tall[h]), dsa)
    stage("core")
    dkey_low = [x.astype(bf16) for x in dkey_t]
    row_dot = [jnp.sum(dkey_t[h] * key_t, axis=0, keepdims=True) for h in range(heads)]
    dkey = [x.T.astype(bf16) for x in dkey_t]

    def back(i, carry):
        at = pl.ds(pl.multiple_of(i * BLOCK, BLOCK), BLOCK)
        v = v_ref[at, :].astype(bf16)
        k_t = k_ref[at, :].astype(f32).T.astype(bf16)
        dk, dv = jnp.zeros((BLOCK, width), f32), jnp.zeros((BLOCK, width), f32)
        out = []
        for h in range(heads):
            bw = bw_ref[h, at, :]
            ds = (SCALE * bw.astype(f32) * (dot(v, dkey_low[h]) - row_dot[h])).astype(bf16)
            dk = dk + dot(ds, ql_low[h])
            dv = dv + dot(bw, dkey[h])
            out.append(carry[h] + dot(k_t, ds))
        dk_acc[at, :] = dk
        dv_acc[at, :] = dv
        return tuple(out)

    sums = lax.fori_loop(0, steps, back, tuple(zeros for _ in range(heads)))
    stage("back")
    dql_t = zeros
    for h in range(heads):
        dql_t = dql_t + sums[h] * tall[h]
    dql_low = ((dql.T + dql_t) * inverse).astype(bf16)
    dkl_low = (dkl_t * inverse).astype(bf16)
    mats = [toeplitz(taps_ref, part * heads + h, True) for h in range(heads)]
    spread[...] = jnp.zeros(spread.shape, f32)

    def convolve(i, carry):
        at = pl.ds(pl.multiple_of(i * 128, 128), 128)
        t = i * 128 + iota((128, 1), 0)
        near = same_doc(lengths_ref, t, i * 128 - 64 + iota((1, 256), 1))
        window = pl.ds(pl.multiple_of(i * 128, 128), 256)
        d_window, v_window = d_wide[window, :], v_wide[window, :]
        do = dout_ref[at, :].astype(f32)
        dv = dv_acc[at, :]
        for h in range(heads):
            dv = dv + dot(jnp.where(near, mats[h], 0.0).astype(bf16), d_window) * masks[h]
            spread[h] += jnp.where(near, dot((do * masks[h]).astype(bf16), v_window, NT), 0.0)
        dv_acc[at, :] = dv
        return carry

    lax.fori_loop(0, total // 128, convolve, 0)
    stage("conv")

    def finish(i, carry):
        at = pl.ds(pl.multiple_of(i * BLOCK, BLOCK), BLOCK)
        t = i * BLOCK + iota((BLOCK, 1), 0)
        member = ((t >= row_low) & (t < row_top)).astype(f32).astype(bf16)
        dq = dq_acc[at, :] + dot(member, dql_low, NT)
        dk = dk_acc[at, :] + dot(member, dkl_low, NT)
        grads = jnp.concatenate([dq.astype(bf16), dk.astype(bf16), dv_acc[at, :].astype(bf16)], axis=1)
        dqkv[at, :] = grads
        return carry + jnp.sum(grads.astype(f32), axis=0, keepdims=True)

    extra_ref[...] = jnp.zeros(extra_ref.shape, f32)
    extra_ref[0:1, :] = lax.fori_loop(0, steps, finish, jnp.zeros((1, 3 * width), f32))
    stage("parts")
    dw_ref[...] = jnp.zeros(dw_ref.shape, f32)

    def weigh(i, carry):
        at = pl.ds(pl.multiple_of(i * BLOCK, BLOCK), BLOCK)
        for n in range(3):
            grads = dqkv[at, n * width : (n + 1) * width].astype(f32).T.astype(bf16)
            dw_ref[:, n * D : (n + 1) * D] += dot(grads, tokens_ref[at, :])
        return carry

    lax.fori_loop(0, steps, weigh, 0)
    tap = tap_index()
    tap_rows[...] = jnp.zeros(tap_rows.shape, f32)
    for h in range(heads):
        for o in range(CONV):
            tap_rows[o : o + 1, :] = jnp.sum(jnp.where(tap == o, spread[h], 0.0), axis=0, keepdims=True)
        extra_ref[1 + h : 2 + h, 0:128] = jnp.sum(tap_rows[...].T, axis=0, keepdims=True)


def backward_kernel(heads, active, lengths_ref, taps_ref, tokens_ref, weights_ref, *refs):
    inputs, part_ref, outputs, dqkv = refs[:11], refs[11], refs[12:-1], refs[-1]
    backward_math(heads, active, lengths_ref, taps_ref, tokens_ref, weights_ref, *inputs, *outputs, dqkv, lambda point: None)

    def project(i, carry):
        at = pl.ds(pl.multiple_of(i * BLOCK, BLOCK), BLOCK)
        part = dot(dqkv[at, :], weights_ref[...], NT)
        part_ref[at, :] = jnp.where(lax.axis_index("seq") < active, part, 0.0).astype(bf16)
        return carry

    lax.fori_loop(0, tokens_ref.shape[0] // BLOCK, project, 0)


def attention_backward(heads, active, tokens, weights, dout, lengths, taps, state):
    total = tokens.shape[0]
    width = heads * HD
    shape = jax.ShapeDtypeStruct
    vmem, smem = (pl.BlockSpec(memory_space=m) for m in (pltpu.VMEM, pltpu.SMEM))
    return pl.pallas_call(
        partial(backward_kernel, heads, active),
        out_shape=(
            shape((total, D), bf16),
            shape((width, 3 * D), f32),
            shape((8, 3 * width), f32),
        ),
        in_specs=[smem] + [vmem] * 14,
        out_specs=tuple([vmem] * 3),
        scratch_shapes=[
            pltpu.VMEM((total + 128, width), bf16),
            pltpu.VMEM((total + 128, width), bf16),
            pltpu.VMEM((total, width), f32),
            pltpu.VMEM((total, width), f32),
            pltpu.VMEM((total, width), f32),
            pltpu.VMEM((heads, 128, 256), f32),
            pltpu.VMEM((128, 256), f32),
            pltpu.VMEM((total, 3 * width), bf16),
        ],
        compiler_params=pltpu.CompilerParams(vmem_limit_bytes=VMEM_BYTES),
    )(lengths, taps, tokens, weights, dout, *state)
def rows_at(index, count):
    return pl.ds(pl.multiple_of(index * count, 8), count)


class Links:
    def __init__(self):
        s, f = lax.axis_index("seq"), lax.axis_index("fsdp")
        self.s, self.f = s, f
        self.z, self.y, self.x, self.c = s // 2, s % 2, f // 2, f % 2
        self.oy, self.ox, self.oc = 1 - self.y, 1 - self.x, 1 - self.c
        self.seq_peers = [((s + j) % 8, f) for j in range(1, 8)]
        self.fsdp_peers = [(s, (f + i) % 4) for i in range(1, 4)]
        self.z_peers = [((self.z + j) % 4 * 2 + self.y, f) for j in range(1, 4)]
        self.above, self.below = self.z_peers[0], self.z_peers[2]
        self.y_peer = (self.z * 2 + self.oy, f)
        self.x_peer = (s, self.ox * 2 + self.c)
        self.c_peer = (s, self.x * 2 + self.oc)
        self.started = []

    def send(self, src, dst, sems, index, peer):
        copy = remote(src, dst, sems[0].at[index], sems[1].at[index], peer)
        copy.start()
        self.started.append(copy)
        return copy

    def drain(self):
        for copy in self.started:
            copy.wait_send()
        self.started = []


def begin(copies):
    for copy in copies:
        copy.start()


def done(copies):
    for copy in copies:
        copy.wait_recv()


def centre(value):
    value = value - jnp.mean(value, axis=1, keepdims=True)
    scale = lax.rsqrt(jnp.mean(value * value, axis=1, keepdims=True) + epsilon)
    return value * scale, scale


def uncentre(grad, normal, scale):
    return scale * (grad - jnp.mean(grad, axis=1, keepdims=True)
                    - normal * jnp.mean(grad * normal, axis=1, keepdims=True))


def column_sum(value):
    return jnp.sum(value, axis=0, keepdims=True)


def token_math(own, cot, attention, up_ref, down_ref, out_ref, vec_ref, gelu_ref, slope_ref, output_ref, dr1_ref, small_ref,
               weights_done):
    vec = vec_ref[...]
    b_out, b_down, g_attn, s_attn, g_mlp, s_mlp = (vec[j : j + 1] for j in range(6))
    normal_one, scale_one = centre(own.astype(f32) + dot(attention, out_ref[...]) + b_out)
    hidden = normal_one * g_attn + s_attn
    hidden_low = hidden.astype(bf16)
    count = hidden.shape[0]

    def upward(i, down):
        cols = pl.ds(pl.multiple_of(i * D, D), D)
        up = dot(hidden_low, up_ref[:, cols]) + vec_ref[pl.ds(6 + i, 1), :]
        share = 0.5 + 0.5 * lax.erf(up * math.sqrt(0.5))
        gelu = (up * share).astype(bf16)
        gelu_ref[:, cols] = gelu
        slope_ref[:, cols] = share + up * (math.sqrt(0.5 / math.pi) * jnp.exp(-0.5 * up * up))
        return down + dot(gelu, down_ref[cols, :])

    down = lax.fori_loop(0, FF // D, upward, jnp.zeros((count, D), f32))
    normal_two, scale_two = centre(hidden + down + b_down)
    output_ref[...] = (normal_two * g_mlp + s_mlp).astype(bf16)
    cot = cot.astype(f32)
    d_r2 = uncentre(cot * g_mlp, normal_two, scale_two)
    d_down = d_r2.astype(bf16)
    small_ref[...] = jnp.zeros(small_ref.shape, f32)
    small_ref[1:2, :] = column_sum(d_down.astype(f32))
    small_ref[4:5, :] = column_sum(cot * normal_two)
    small_ref[5:6, :] = column_sum(cot)
    hidden_t = hidden_low.astype(f32).T.astype(bf16)

    def downward(i, carry):
        cols = pl.ds(pl.multiple_of(i * D, D), D)
        d_gelu = dot(d_down, down_ref[cols, :], NT)
        d_up = (d_gelu * slope_ref[:, cols]).astype(bf16)
        small_ref[pl.ds(6 + i, 1), :] = column_sum(d_up.astype(f32))
        gelu_t = gelu_ref[:, cols].astype(f32).T.astype(bf16)
        gelu_ref[:, cols] = d_up
        down_ref[cols, :] = dot(gelu_t, d_down).astype(bf16)
        return carry

    def back_up(i, d_hidden):
        cols = pl.ds(pl.multiple_of(i * D, D), D)
        d_up = gelu_ref[:, cols]
        d_hidden = d_hidden + dot(d_up, up_ref[:, cols], NT)
        up_ref[:, cols] = dot(hidden_t, d_up).astype(bf16)
        return d_hidden

    lax.fori_loop(0, FF // D, downward, 0)
    weights_done(True)
    d_hidden = lax.fori_loop(0, FF // D, back_up, d_r2)
    weights_done(False)
    d_r1 = uncentre(d_hidden * g_attn, normal_one, scale_one)
    dr1_ref[...] = d_r1
    d_out = d_r1.astype(bf16)
    small_ref[0:1, :] = column_sum(d_out.astype(f32))
    small_ref[2:3, :] = column_sum(d_hidden * normal_one)
    small_ref[3:4, :] = column_sum(d_hidden)
    d_attention = dot(d_out, out_ref[...], NT).astype(bf16)
    out_ref[...] = dot(attention.astype(f32).T.astype(bf16), d_out).astype(bf16)
    return d_attention


def select_lanes(rows, offset, base):
    wide = rows.shape[1]
    choose = (iota((wide, 128), 0) + base == iota((wide, 128), 1) + offset).astype(f32).astype(bf16)
    first = rows.astype(bf16)
    second = (rows - first.astype(f32)).astype(bf16)
    third = (rows - first.astype(f32) - second.astype(f32)).astype(bf16)
    return dot(first, choose) + dot(second, choose) + dot(third, choose)


GATHER = {
    "proj": "w1", "scores": "w2", "key_mix": "o0 q2", "newton2": "q3", "newton4": "o1", "mix": "q4 c0", "end": "o2 c1 c2",
}
PLAN = {
    "start": "f0 m0", "front": "f1", "newton4": "s0 f2 m1", "newton1": "s1 t0 f3", "core": "m2 l0", "conv": "s2 t1",
    "parts": "y0 l1", "end": "s3 z0 t2 z1 z2 w0 z3 l2 t3",
}


VECTORS = ("b_out", "b_down", "g_attn", "s_attn", "g_mlp", "s_mlp", "b_up", "b_query", "b_value")


def layer_kernel(heads, active, names, *refs):
    r = dict(zip(names, refs))
    net = Links()
    s, f, z, y, x, c = net.s, net.f, net.z, net.y, net.x, net.c
    oy, ox, oc = net.oy, net.ox, net.oc
    width = heads * HD
    own_ref, tokens_ref, weights_ref = r["own"], r["tokens"], r["weights"]
    count, rows = own_ref.shape[0], r["wq"].shape[0]
    mine = rows_at(s, count)
    index = s * 4 + f

    loads = [pltpu.make_async_copy(r["in_" + name], r[name], r["load_sems"].at[n])
             for n, name in enumerate(("own", "wq", "wk", "wv", "cot", "taps") + VECTORS)]
    begin(loads)
    greet(net.seq_peers + net.fsdp_peers)
    for copy in loads:
        copy.wait()

    def pair(name):
        return r[name + "_send"], r[name + "_recv"]

    def token_z(zz, t, up):
        here = tokens_ref.at[rows_at(zz * 2 + y, count)]
        n = 2 * t + (0 if up else 1)
        return remote(own_ref if t == 0 else here, here, r["tz_send"].at[n], r["tz_recv"].at[n], net.above if up else net.below)

    def token_y(zz, own=False):
        here = tokens_ref.at[rows_at(zz * 2 + y, count)]
        return remote(own_ref if own else here, here, r["ty_send"].at[zz], r["ty_recv"].at[zz], net.y_peer)

    pieces = ((r["in_wup"], r["up"], rows, 0, rows), (r["placed"], r["full_small"], 16, 0, 16),
              (r["in_wout"], r["out"], rows, 0, rows), (r["in_wdown"].at[0 : 3 * rows], r["down"], 4 * rows, 0, 3 * rows),
              (r["in_wdown"].at[3 * rows : 4 * rows], r["down"], 4 * rows, 3 * rows, rows))
    early, late = (0, 1, 2), (3,)

    def slot(zz, sy, sx):
        return (zz * 2 + sy) * 4 + sx * 2 + c

    def weight(m, own, where, send_sem, recv_sem, peer):
        src, full, stride, lead, n = pieces[m]
        here = full.at[pl.ds(pl.multiple_of(where * stride + lead, 8), n)]
        return remote(src if own else here, here, send_sem, recv_sem, peer)

    quad = ((y, x), (oy, x), (y, ox), (oy, ox))

    def quad_x():
        return weight(4, True, slot(z, y, x), r["qx_send"].at[0], r["qx_recv"].at[0], net.x_peer)

    def quad_y(n):
        return weight(4, n == 0, slot(z, y, (x, ox)[n]), r["qy_send"].at[n], r["qy_recv"].at[n], net.y_peer)

    def quad_z(zz, t, up):
        n = 2 * t + (0 if up else 1)
        peer = net.above if up else net.below
        return [weight(4, False, slot(zz, *quad[q]), r["qz_send"].at[n, q], r["qz_recv"].at[n, q], peer) for q in range(4)]

    def quad_core(zz):
        return [weight(4, False, slot(zz, *quad[q]), r["qc_send"].at[zz, q], r["qc_recv"].at[zz, q], net.c_peer)
                for q in range(4)]

    def quad_step(n):
        if n == 0:
            quad_x().wait_recv()
            quad_y(1).start()
        elif n == 1:
            keep[4].wait()
            done([quad_y(0), quad_y(1)])
            onto_z(0, lambda zz, t, up: begin(quad_z(zz, t, up)))
            begin(quad_core(z))
        else:
            t = n - 2

            def came(zz, up):
                done(quad_z(zz, t, up))
                begin(quad_core(zz))

            column(t, came)
            if t < 2:
                onto_z(t + 1, lambda zz, t, up: begin(quad_z(zz, t, up)))

    def weight_z(zz, t, up):
        n = 2 * t + (0 if up else 1)
        peer = net.above if up else net.below
        return [weight(m, t == 0, slot(zz, y, x), r["gz_send"].at[n, m], r["gz_recv"].at[n, m], peer) for m in range(4)]

    def to_y(zz, m, own=False):
        return weight(m, own, slot(zz, y, x), r["gy_send"].at[zz, m], r["gy_recv"].at[zz, m], net.y_peer)

    def to_x(zz, m, own=False):
        return weight(m, own, slot(zz, y, x), r["gx_send"].at[zz, m], r["gx_recv"].at[zz, m], net.x_peer)

    def again_x(zz, m):
        return weight(m, False, slot(zz, oy, x), r["gx_send"].at[zz, 4 + m], r["gx_recv"].at[zz, 4 + m], net.x_peer)

    def again_y(zz, m):
        return weight(m, False, slot(zz, y, ox), r["gy_send"].at[zz, 4 + m], r["gy_recv"].at[zz, 4 + m], net.y_peer)

    def to_core(zz, n, m, own=False):
        sy, sx = ((y, x), (oy, x), (y, ox), (oy, ox))[n]
        return weight(m, own, slot(zz, sy, sx), r["gc_send"].at[zz, n, m], r["gc_recv"].at[zz, n, m], net.c_peer)

    def spread(zz):
        begin([to_y(zz, m) for m in early] + [to_x(zz, m) for m in late])
        begin([to_x(zz, m) for m in early] + [to_y(zz, m) for m in late])
        begin([to_core(zz, 0, m) for m in range(4)])

    def onward(zz):
        for m in early:
            done([to_y(zz, m)])
            begin([again_x(zz, m)])
        for m in late:
            done([to_x(zz, m)])
            begin([again_y(zz, m)])
        done([to_y(zz, m) for m in late])
        begin([to_core(zz, 1, m) for m in range(4)])
        done([to_x(zz, m) for m in early])
        begin([to_core(zz, 2, m) for m in range(4)])

    def corner(zz):
        done([again_x(zz, m) for m in early] + [again_y(zz, m) for m in late])
        begin([to_core(zz, 3, m) for m in range(4)])

    def column(t, act):
        for up in (True, False):
            zz = z - 1 - t if up else z + 1 + t

            @pl.when(zz >= 0 if up else zz < 4)
            def _():
                act(zz, up)

    def onto_z(t, act):
        for up in (True, False):
            zz = z - t if up else z + t

            @pl.when((zz >= 0) & (z < 3) if up else (zz < 4) & (z > 0))
            def _():
                act(zz, t, up)

    onto_z(0, lambda zz, t, up: token_z(zz, t, up).start())
    token_y(z, True).start()
    begin([quad_x(), quad_y(0)])
    begin([to_x(z, m, True) for m in (3, 0, 2)] + [to_y(z, m, True) for m in (0, 2, 3)])
    vectors = r["vectors"]
    vectors[...] = jnp.zeros(vectors.shape, f32)
    for n, name in enumerate(VECTORS):
        vector = r[name][...].astype(f32)
        vectors[n : n + 1, 0 : vector.shape[0]] = vector.reshape(1, vector.shape[0])
    vectors = vectors[...].astype(bf16)
    for j in range(16):
        base, row = (96, 6) if 6 <= j < 10 else (24, j)
        lead = (j - 6) * D if 6 <= j < 10 else 0
        if j in (10, 11):
            row = j - 3
        if j >= 12:
            break
        base = 4 * rows if base == 96 else rows
        lane = iota((128, D), 1) + lead - base * index
        choose = ((lane == iota((128, D), 0)) & (lane < base)).astype(f32).astype(bf16)
        value = dot(vectors, choose)[row : row + 1, :]
        r["place"][j : j + 1, :] = value
    r["place"][12:16, :] = jnp.zeros((4, D), f32)
    r["placed"][...] = r["place"][...].astype(bf16)
    pack, landed = r["pack"], r["landed"]
    for b in range(active):
        for n, name in enumerate(("wq", "wk", "wv")):
            pack[b, 0:rows, n * width : (n + 1) * width] = r[name][:, b * width : (b + 1) * width]
        pack[b, rows:, :] = jnp.zeros((pack.shape[1] - rows, 3 * width), bf16)
        for n, j in ((0, 10), (2, 11)):
            bias = jnp.broadcast_to(r["place"][j : j + 1, b * width : (b + 1) * width], (8, width))
            pack[b, rows : rows + 8, n * width : (n + 1) * width] = jnp.where(iota((8, width), 0) == 0, bias, 0.0).astype(bf16)
    from_seq = [
        net.send(pack.at[(s + j + 1) % 8 % active], landed.at[f, s], pair("ps"), j, net.seq_peers[j]) for j in range(7)]
    begin([to_x(z, 1, True), to_y(z, 1, True)] + [to_core(z, 0, m, True) for m in range(4)])
    landed[f, s] = pack[s % active]
    tokens_ref[mine, :] = own_ref[...]
    keep = [pltpu.make_async_copy(
        src, full.at[pl.ds(pl.multiple_of(slot(z, y, x) * stride + lead, 8), n)], r["keep_sems"].at[m])
        for m, (src, full, stride, lead, n) in enumerate(pieces)]
    begin(keep)

    def weights_on(t):
        def came(zz, up):
            done(weight_z(zz, t, up))
            spread(zz)

        column(t, came)
        if t < 2:
            onto_z(t + 1, lambda zz, t, up: begin(weight_z(zz, t, up)))

    def tokens_on(t):
        def came(zz, up):
            token_z(zz, t, up).wait_recv()
            token_y(zz).start()

        column(t, came)
        if t < 2:
            onto_z(t + 1, lambda zz, t, up: token_z(zz, t, up).start())

    tokens_on(0)
    onto_z(0, lambda zz, t, up: begin(weight_z(zz, t, up)))
    tokens_on(1)
    quad_step(0)
    onward(z)
    done(from_seq)
    from_fsdp = [net.send(landed.at[f], landed.at[f], pair("pf"), i, net.fsdp_peers[i]) for i in range(3)]
    tokens_on(2)
    weights_on(0)
    quad_step(1)
    corner(z)

    gather_steps = {
        "w": weights_on, "o": lambda t: column(t, lambda zz, up: onward(zz)), "c": lambda t: column(t, lambda zz, up: corner(zz)),
        "q": quad_step}

    def gather_stage(point):
        for step in GATHER.get(point, "").split():
            gather_steps[step[0]](int(step[1]))

    for zz in range(4):
        token_y(zz).wait_recv()
    done(from_fsdp)
    bias = jnp.zeros((8, 3 * width), f32)
    for a in range(4):
        for b in range(8):
            weights_ref[rows * (b * 4 + a) : rows * (b * 4 + a + 1), :] = landed[a, b, 0:rows, :]
            bias = bias + landed[a, b, rows : rows + 8, :].astype(f32)

    state = [r[name] for name in ("q", "k", "v", "fw", "bw", "land", "mix", "a", "norm", "chain")]
    lengths_ref, taps_ref, mixed = r["lengths"], r["taps"], r["d_wide"].at[0 : 8 * count, :]
    forward_math(heads, active, lengths_ref, taps_ref, tokens_ref, weights_ref, bias[0:1], mixed, *state,
                 r["v_wide"], r["score"], gather_stage)

    att = r["att"]
    last = [net.send(mixed.at[rows_at((s + j + 1) % 8, count)], att.at[s], pair("at"), j, net.seq_peers[j]) for j in range(7)]
    att[s] = mixed[mine, :]
    gather_stage("end")
    for zz in range(4):
        for n in range(4):
            done([to_core(zz, n, m) for m in range(4)])
        done(quad_core(zz))
    for copy in keep[:4]:
        copy.wait()

    def sent(zz, t, up):
        token_z(zz, t, up).wait_send()
        for copy in weight_z(zz, t, up) + quad_z(zz, t, up):
            copy.wait_send()

    net.drain()
    for t in range(3):
        onto_z(t, sent)
    for copy in (quad_x(), quad_y(0), quad_y(1)):
        copy.wait_send()
    for zz in range(4):
        for copy in quad_core(zz):
            copy.wait_send()
        token_y(zz).wait_send()
        for m in range(4):
            to_y(zz, m).wait_send()
            to_x(zz, m).wait_send()
            (again_x if m in early else again_y)(zz, m).wait_send()
            for n in range(4):
                to_core(zz, n, m).wait_send()
    vec = jnp.zeros((16, D), f32)
    for n in range(32):
        vec = vec + r["full_small"][16 * n : 16 * n + 16, :].astype(f32)
    r["vec"][...] = vec
    done(last)
    peer_weights = net.send(weights_ref, r["peer_weights"], pair("wp"), 0, net.y_peer)

    sums = ((r["up"], r["acc_up"], r["got_up"], r["far_up"], rows, 0), (r["out"], r["acc_out"], r["got_out"], r["far_out"], rows, 0),
            (r["down"], r["acc_down"], r["got_down"], r["far_down"], 4 * rows, 0),
            (r["down"], r["acc_last"], None, None, 4 * rows, 3 * rows))
    places = ((0, 0), (0, 1), (1, 0), (1, 1))
    moved = {}

    def owner(k, sy, sx, sc):
        return ((z + k + 1) % 4 * 2 + sy) * 4 + sx * 2 + sc

    def to_sibling(pieces_of, distances):
        for k in distances:
            for m, (sy, sx) in enumerate(places):
                for n in pieces_of:
                    full, acc, _, _, stride, lead = sums[n]
                    there = pl.ds(pl.multiple_of(owner(k, sy, sx, oc) * stride + lead, 8), acc.shape[3])
                    moved["c", k, m, n] = net.send(
                        full.at[there], acc.at[k, sy, sx], pair("rc"), (4 * k + m, n), net.c_peer)

    attention = jnp.concatenate([att[b] for b in range(active)], axis=1)
    d_attention = token_math(
        own_ref[...], r["cot"][...], attention, r["up"], r["down"], r["out"], r["vec"], r["gelu"], r["slope"],
        r["output"], r["dr1"], r["small"], lambda down: to_sibling((2, 3) if down else (0,), (0,)))
    store = [pltpu.make_async_copy(r["output"], r["o_output"], r["store_sems"].at[0])]
    begin(store)
    dattn, dout = r["dattn"], r["dout"]
    for b in range(active):
        dattn[b] = d_attention[:, b * width : (b + 1) * width]
    from_seq = [
        net.send(dattn.at[(s + j + 1) % 8 % active], dout.at[mine], pair("dt"), j, net.seq_peers[j]) for j in range(7)]
    dout[mine, :] = dattn[s % active]
    to_sibling((1,), (0,))
    to_sibling((0, 1, 2, 3), (1, 2, 3))
    small_put, small_got, small_sum = r["small_put"], r["small_got"], r["small_sum"]
    small_put[...] = r["small"][...].astype(bf16)
    moved["m", 0] = net.send(small_put, small_got.at[0], pair("rm"), 0, net.c_peer)

    def add(target, more, base):
        deep, wide = target.shape

        def one(i, carry):
            if wide > D:
                cols = pl.ds(pl.multiple_of(i * D, D), D)
                here, there = (slice(None), cols), (pl.ds(pl.multiple_of(base, 8), deep), cols)
            else:
                here, there = (rows_at(i, rows), slice(None)), (pl.ds(pl.multiple_of(base + i * rows, 8), rows), slice(None))
            target[here] = (target[here].astype(f32) + more[there].astype(f32)).astype(bf16)
            return carry

        lax.fori_loop(0, deep * wide // (rows * D), one, 0)

    def first(k):
        for n in range(4):
            done([moved["c", k, m, n] for m in range(4)])

        def own(n, sy, sx):
            full, acc, _, _, stride, lead = sums[n]
            add(acc.at[k, sy, sx], full, owner(k, sy, sx, c) * stride + lead)

        for i in range(2):
            for n in range(3):
                _, acc, got, _, _, _ = sums[n]
                if n < 2:
                    own(n, i, ox)
                    moved["1", k, i, n] = net.send(acc.at[k, i, ox], got.at[k, i], pair("rx"), (3 * k + i, n), net.x_peer)
                else:
                    own(n, oy, i)
                    moved["1", k, i, n] = net.send(acc.at[k, oy, i], got.at[k, i], pair("ry"), (3 * k + i, 0), net.y_peer)

        def last_rows(i, carry):
            own(3, i // 2, i % 2)
            return carry

        lax.fori_loop(0, 4, last_rows, 0)
        if k < 3:
            moved["l", k] = net.send(r["acc_last"].at[k], r["last_z"].at[k], pair("lz"), k, net.z_peers[k])

        def stays(i, carry):
            own(0, i, x)
            own(1, i, x)
            own(2, y, i)
            return carry

        lax.fori_loop(0, 2, stays, 0)

    def second(k):
        for n, (_, acc, got, _, _, _) in enumerate(sums[:3]):
            for i in range(2):
                moved["1", k, i, n].wait_recv()
                add(acc.at[k, i, x] if n < 2 else acc.at[k, y, i], got.at[k, i], 0)
            if n < 2:
                moved["2", k, n] = net.send(acc.at[k, oy, x], got.at[k, 2], pair("ry"), (3 * k + 2, n), net.y_peer)
            else:
                moved["2", k, n] = net.send(acc.at[k, y, ox], got.at[k, 2], pair("rx"), (3 * k + 2, 0), net.x_peer)

    def third(k):
        for n, (_, acc, got, far, _, _) in enumerate(sums[:3]):
            moved["2", k, n].wait_recv()
            add(acc.at[k, y, x], got.at[k, 2], 0)
            if k < 3:
                moved["3", k, n] = net.send(acc.at[k, y, x], far.at[k], pair("rz"), (k, n), net.z_peers[k])

    def small_step(n):
        before = small_put if n == 0 else small_sum.at[n - 1]
        moved["m", n].wait_recv()
        small_sum[n] = (before[...].astype(f32) + small_got[n].astype(f32)).astype(bf16)
        if n < 2:
            moved["m", n + 1] = net.send(
                small_sum.at[n], small_got.at[n + 1], pair("rm"), n + 1, net.x_peer if n == 0 else net.y_peer)
        else:
            for j in range(3):
                moved["m", 3 + j] = net.send(small_sum.at[2], small_got.at[3 + j], pair("rm"), 3 + j, net.z_peers[j])

    def last_step(n):
        mine_last = r["acc_last"].at[3]
        if n == 0:
            done([moved["l", k] for k in range(3)])

            def collect(i, carry):
                add(mine_last.at[i // 3 // 2, i // 3 % 2], r["last_z"].at[i % 3, i // 3 // 2, i // 3 % 2], 0)
                return carry

            lax.fori_loop(0, 12, collect, 0)
            moved["l", 3] = net.send(mine_last.at[oy], r["last_y"], pair("lz"), 3, net.y_peer)
        elif n == 1:
            done([moved["l", 3]])
            for sx in range(2):
                add(mine_last.at[y, sx], r["last_y"].at[sx], 0)
            moved["l", 4] = net.send(mine_last.at[y, ox], r["last_x"], pair("lz"), 4, net.x_peer)
        else:
            done([moved["l", 4]])
            r["sdown"][3 * rows : 4 * rows, :] = mine_last[y, x].astype(f32) + r["last_x"][...].astype(f32)

    steps = {"f": first, "s": second, "t": third, "m": small_step, "l": last_step}

    def scatter_stage(point):
        for step in PLAN.get(point, "").split():
            steps[step[0]](int(step[1]))

    scatter_stage("start")
    done(from_seq)
    dqkv, y_got, z_got = r["dqkv"], r["y_got"], r["z_got"]
    over_y = []

    def send_gradients(_):
        for j in range(4):
            there = rows_at((z + j + 1) % 4 * 2 + oy, count)
            over_y.append(net.send(dqkv.at[there], y_got.at[j], pair("dy"), j, net.y_peer))

    steps["y"] = send_gradients
    score = r["score"]
    accumulators = [score.at[0, :, 0:width], score.at[0, :, width : 2 * width], score.at[1, :, 0:width]]
    dw_t = r["slope"].at[:, 0 : 3 * D]
    backward_math(
        heads, active, lengths_ref, taps_ref, tokens_ref, weights_ref, dout, *state, dw_t, r["extra"],
        r["v_wide"], r["d_wide"], *accumulators, r["spread"], r["tap_rows"], r["dqkv"],
        scatter_stage)

    first_put, first_got, second_put, second_got = landed, r["first_got"], r["second_put"], r["second_got"]
    dw = [dw_t[:, n * D : (n + 1) * D].T.astype(bf16) for n in range(3)]
    tail = r["extra"][...].astype(bf16)
    for a in range(4):
        for b in range(8):
            start = rows * (4 * b + a)
            for n in range(3):
                first_put[a, b, 0:rows, n * width : (n + 1) * width] = dw[n][start : start + rows, :]
            first_put[a, b, rows:, :] = tail
    from_fsdp = [
        net.send(first_put.at[(f + i + 1) % 4], first_got.at[f], pair("wf"), i, net.fsdp_peers[i]) for i in range(3)]
    first_got[f] = first_put[f]
    over_z, held = [], {}

    def token_parts(j):
        done([over_y[j]])
        here = rows_at((z + j + 1) % 4 * 2 + y, count)
        value = jnp.where(s < active, dot(dqkv[here, :], weights_ref[...], NT), 0.0)
        value = value + jnp.where(z * 2 + oy < active, dot(y_got[j], r["peer_weights"][...], NT), 0.0)
        if j < 3:
            z_put = r["gelu"].at[:, j * D : (j + 1) * D]
            z_put[...] = value.astype(bf16)
            over_z.append(net.send(z_put, z_got.at[j], pair("dz"), j, net.z_peers[j]))
        else:
            held["kept"] = value + r["dr1"][...]

    def weight_parts(_):
        done(from_fsdp)
        for b in range(8):
            value = first_got[0, b].astype(f32)
            for a in range(1, 4):
                value = value + first_got[a, b].astype(f32)
            second_put[b] = value.astype(bf16)
        held["seq"] = [
            net.send(second_put.at[(s + j + 1) % 8], second_got.at[s], pair("ws"), j, net.seq_peers[j]) for j in range(7)]
        second_got[s] = second_put[s]

    steps.update(z=token_parts, w=weight_parts)
    done([peer_weights])
    scatter_stage("end")
    kept, from_seq = held["kept"], held["seq"]

    def put(name, n):
        store.append(pltpu.make_async_copy(r[name], r["o_" + name], r["store_sems"].at[n]))
        begin(store[-1:])

    for n, (name, (_, acc, _, far, _, _)) in enumerate(zip(("sup", "sout", "sdown"), sums)):
        value = acc[3, y, x].astype(f32)
        for j in range(3):
            done([moved["3", j, n]])
            value = value + far[j].astype(f32)
        r[name][0 : value.shape[0], :] = value
        put(name, 1 + n)
    value = small_sum[2].astype(f32)
    for j in range(3):
        done([moved["m", 3 + j]])
        value = value + small_got[3 + j].astype(f32)
    lines = r["lines"]
    lines[...] = jnp.zeros(lines.shape, f32)
    lines[0:8, :] = select_lanes(value, rows * index, 0)[0:8, :]
    b_up = jnp.zeros((16, 128), f32)
    for j in range(4):
        b_up = b_up + jnp.where(iota((16, 128), 0) == 6 + j, select_lanes(value, 4 * rows * index, j * D), 0.0)
    lines[6:7, :] = column_sum(b_up)
    done(over_z)
    for j in range(3):
        kept = kept + z_got[j].astype(f32)
    r["dtok"][...] = kept.astype(bf16)
    put("dtok", 4)
    done(from_seq)
    bias = jnp.zeros((8, 128), f32)
    bias_v = jnp.zeros((8, 128), f32)
    for b in range(active):
        for n, name in enumerate(("dwq", "dwk", "dwv")):
            r[name][:, b * width : (b + 1) * width] = second_got[b, 0:rows, n * width : (n + 1) * width].astype(f32)
        tail = second_got[b, rows:, :].astype(f32)
        bias = bias + select_lanes(tail[:, 0:width], rows * index, b * width)
        bias_v = bias_v + select_lanes(tail[:, 2 * width :], rows * index, b * width)
        lines[16 + b * heads : 16 + (b + 1) * heads, :] = tail[1 : 1 + heads, 0:128]
    lines[7:8, :] = bias[0:1]
    lines[8:9, :] = bias_v[0:1]
    for n, name in enumerate(("dwq", "dwk", "dwv", "lines")):
        put(name, 5 + n)
    net.drain()
    for copy in store:
        copy.wait()


def layer(heads, active, lengths, taps, own, cot, w_query, w_key, w_value, vectors, w_up, w_out, w_down):
    count, rows = own.shape[0], w_query.shape[0]
    total = 8 * count
    width = heads * HD
    shape, buffer, dma = jax.ShapeDtypeStruct, pltpu.VMEM, pltpu.SemaphoreType.DMA
    smem, anywhere = pl.BlockSpec(memory_space=pltpu.SMEM), pl.BlockSpec(memory_space=pl.ANY)
    ins = ["lengths", "in_taps", "in_own", "in_cot", "in_wq", "in_wk", "in_wv", "in_wup", "in_wout", "in_wdown"]
    ins += ["in_" + name for name in VECTORS]
    outs = {
        "output": shape((count, D), bf16), "dtok": shape((count, D), bf16),
        "dwq": shape((rows, D), f32), "dwk": shape((rows, D), f32), "dwv": shape((rows, D), f32),
        "sup": shape((rows, FF), f32), "sout": shape((rows, D), f32), "sdown": shape((4 * rows, D), f32),
        "lines": shape((32, 128), f32),
    }
    sizes = {"up": (rows, FF), "out": (rows, D), "down": (3 * rows, D)}
    scratch = {
        "own": buffer((count, D), bf16), "cot": buffer((count, D), bf16),
        "wq": buffer((rows, D), bf16), "wk": buffer((rows, D), bf16), "wv": buffer((rows, D), bf16),
        "vectors": buffer((16, 128), f32), "taps": buffer((HEADS, CONV), bf16), "place": buffer((16, D), f32), "placed": buffer((16, D), bf16),
        "tokens": buffer((total, D), bf16), "weights": buffer((D, 3 * width), bf16),
        "pack": buffer((active, rows + 8, 3 * width), bf16), "landed": buffer((4, 8, rows + 8, 3 * width), bf16),
        "up": buffer((D, FF), bf16), "full_small": buffer((512, D), bf16), "out": buffer((D, D), bf16),
        "down": buffer((FF, D), bf16), "vec": buffer((16, D), f32),
        "q": buffer((total, width), bf16), "k": buffer((total, width), bf16), "v": buffer((total, width), f32),
        "fw": buffer((heads, total, SLOTS), bf16), "bw": buffer((heads, total, SLOTS), bf16),
        "land": buffer((2, SLOTS, width), f32), "mix": buffer((2, width, SLOTS), f32),
        "a": buffer((heads, SLOTS, SLOTS), f32), "norm": buffer((heads, SLOTS, SLOTS), f32),
        "chain": buffer((NS_ITERS + 1, heads, 4, 2, SLOTS, SLOTS), bf16),
        "v_wide": buffer((total + 128, width), bf16),
        "score": buffer((heads, total, SLOTS), f32), "att": buffer((8, count, width), bf16),
        "gelu": buffer((count, FF), bf16), "slope": buffer((count, FF), f32), "dr1": buffer((count, D), f32),
        "small": buffer((16, D), f32), "small_put": buffer((16, D), bf16), "small_got": buffer((6, 16, D), bf16),
        "small_sum": buffer((3, 16, D), bf16),
        "dattn": buffer((active, count, width), bf16), "dout": buffer((total, width), bf16),
        "d_wide": buffer((total + 128, width), bf16),
        "spread": buffer((heads, 128, 256), f32), "tap_rows": buffer((128, 256), f32),
        "dqkv": buffer((total, 3 * width), bf16), "peer_weights": buffer((D, 3 * width), bf16),
        "extra": buffer((8, 3 * width), f32),
        "y_got": buffer((4, count, 3 * width), bf16), "z_got": buffer((3, count, D), bf16),
        "first_got": buffer((4, 8, rows + 8, 3 * width), bf16),
        "second_put": buffer((8, rows + 8, 3 * width), bf16), "second_got": buffer((8, rows + 8, 3 * width), bf16),
    }
    for name, size in sizes.items():
        scratch["acc_" + name] = buffer((4, 2, 2, *size), bf16)
        scratch["got_" + name] = buffer((4, 3, *size), bf16)
        scratch["far_" + name] = buffer((3, *size), bf16)
    scratch["acc_last"], scratch["last_z"] = buffer((4, 2, 2, rows, D), bf16), buffer((3, 2, 2, rows, D), bf16)
    scratch["last_y"], scratch["last_x"] = buffer((2, rows, D), bf16), buffer((rows, D), bf16)
    for name, vector in zip(VECTORS, vectors):
        scratch[name] = buffer(vector.shape, bf16)
    for name, value in outs.items():
        scratch[name] = buffer(value.shape, value.dtype)
    pairs = {
        "tz": (6,), "ty": (4,), "ps": (7,), "pf": (3,), "at": (7,), "gz": (6, 4), "gy": (4, 8), "gx": (4, 8), "gc": (4, 4, 4),
        "rc": (16, 4), "rx": (12, 2), "ry": (12, 2), "rz": (3, 3), "rm": (6,), "dt": (7,), "dy": (4,), "dz": (3,),
        "wf": (3,), "ws": (7,), "wp": (1,),
        "qx": (1,), "qy": (2,), "qz": (6, 4), "qc": (4, 4), "lz": (5,),
    }
    for name, size in pairs.items():
        scratch[name + "_send"] = dma(size)
        scratch[name + "_recv"] = dma(size)
    scratch["load_sems"], scratch["keep_sems"], scratch["store_sems"] = dma((15,)), dma((5,)), dma((9,))
    names = ins + ["o_" + name for name in outs] + list(scratch)
    return pl.pallas_call(
        partial(layer_kernel, heads, active, names),
        out_shape=tuple(outs.values()),
        in_specs=[smem] + [anywhere] * (len(ins) - 1),
        out_specs=tuple([anywhere] * len(outs)),
        scratch_shapes=list(scratch.values()),
        compiler_params=pltpu.CompilerParams(collective_id=0, has_side_effects=True, vmem_limit_bytes=63_000_000),
    )(lengths, taps, own, cot, w_query, w_key, w_value, w_up, w_out, w_down, *vectors)


def finish_kernel(rows, hidden_rows, *refs):
    big, lines, outs, small, taps, held, sems = refs[:8], refs[8], refs[9:17], refs[17:26], refs[26], refs[27:35], refs[35]
    loads = [pltpu.make_async_copy(src, dst, sems.at[0, n]) for n, (src, dst) in enumerate(zip(big, held))]
    copies = [pltpu.make_async_copy(src, dst, sems.at[1, n]) for n, (src, dst) in enumerate(zip(held, outs))]
    begin(loads)
    for j, ref in enumerate(small):
        ref[...] = lines[j, 0 : ref.shape[0]]
    taps[...] = lines[16 : 16 + HEADS, 0:CONV]
    for load, copy in zip(loads, copies):
        load.wait()
        copy.start()
    for copy in copies:
        copy.wait()


def finish(results, hidden_rows):
    *big, lines = results
    rows = big[2].shape[0]
    shape = jax.ShapeDtypeStruct
    vmem, anywhere = pl.BlockSpec(memory_space=pltpu.VMEM), pl.BlockSpec(memory_space=pl.ANY)
    small = [shape((hidden_rows if j == 6 else rows,), f32) for j in range(9)]
    return pl.pallas_call(
        partial(finish_kernel, rows, hidden_rows),
        out_shape=tuple([shape(value.shape, value.dtype) for value in big] + small + [shape((HEADS, CONV), f32)]),
        in_specs=[anywhere] * 8 + [vmem],
        out_specs=tuple([anywhere] * 8 + [vmem] * 10),
        scratch_shapes=[pltpu.VMEM(value.shape, value.dtype) for value in big] + [pltpu.SemaphoreType.DMA((2, 8))],
    )(*big, lines)


def product(form, left, right):
    return jnp.einsum(form, left, right, preferred_element_type=f32)


def layer_norm(inputs, gain, shift):
    average = jnp.mean(inputs, axis=-1, keepdims=True)
    centred = inputs - average
    variance = jnp.mean(centred * centred, axis=-1, keepdims=True)
    return centred * lax.rsqrt(variance + epsilon) * gain + shift


def gelu_exact(inputs):
    return jax.nn.gelu(inputs, approximate=False)


def token_part(tokens, cot, attention, w_out, w_up, w_down, b_out, b_up, b_down, g_attn, s_attn, g_mlp, s_mlp):
    out_proj = product("td,de->te", attention, w_out) + b_out
    hidden, norm_one_back = jax.vjp(layer_norm, tokens.astype(f32) + out_proj, g_attn, s_attn)
    hidden_low = hidden.astype(bf16)
    up_pre = product("td,df->tf", hidden_low, w_up) + b_up
    gelu_val, gelu_back = jax.vjp(gelu_exact, up_pre)
    gelu_low = gelu_val.astype(bf16)
    down_pre = product("tf,fd->td", gelu_low, w_down) + b_down
    output, norm_two_back = jax.vjp(layer_norm, hidden + down_pre, g_mlp, s_mlp)
    d_r2, dg_mlp, ds_mlp = norm_two_back(cot.astype(f32))
    d_down = d_r2.astype(bf16)
    db_down = jnp.sum(d_down.astype(f32), axis=0)
    dw_down = product("tf,td->fd", gelu_low, d_down)
    d_gelu = product("td,fd->tf", d_down, w_down)
    d_up = gelu_back(d_gelu)[0].astype(bf16)
    db_up = jnp.sum(d_up.astype(f32), axis=0)
    dw_up = product("td,tf->df", hidden_low, d_up)
    d_hidden = product("tf,df->td", d_up, w_up) + d_r2
    d_r1, dg_attn, ds_attn = norm_one_back(d_hidden)
    d_out = d_r1.astype(bf16)
    db_out = jnp.sum(d_out.astype(f32), axis=0)
    dw_out = product("td,te->de", attention, d_out)
    d_attn = product("te,de->td", d_out, w_out)
    smalls = (db_out, db_up, db_down, dg_attn, ds_attn, dg_mlp, ds_mlp)
    return output.astype(bf16), d_r1, d_attn, dw_out, dw_up, dw_down, smalls
def local(sizes, *args):
    (tokens, cotangent, doc_lengths, w_query, b_query, w_key, w_value, b_value, w_out, b_out, w_up, b_up,
     w_down, b_down, g_attn, s_attn, g_mlp, s_mlp, conv_kernel) = args
    seq, fsdp = sizes
    devices = seq * fsdp
    fast = sizes == (8, 4)
    axes = ("seq", "fsdp")
    rows = D // devices
    hidden_rows = FF // devices
    own_tokens, own_cot, lengths = tokens[0], cotangent[0], doc_lengths[0]
    count = own_tokens.shape[0]
    total = count * seq
    heads = -(-HEADS // seq)
    width = heads * HD
    active = HEADS // heads
    s = lax.axis_index("seq")

    taps = conv_kernel.T
    if fast:
        vectors = (b_out, b_down, g_attn, s_attn, g_mlp, s_mlp, b_up, b_query, b_value)
        results = layer(
            heads, active, lengths, taps, own_tokens, own_cot, w_query, w_key, w_value, vectors, w_up, w_out, w_down)
        output, d_tokens, dw_query, dw_key, dw_value, s_up, s_out, s_down, *g, d_kernel = finish(results, hidden_rows)
        return (
            output[None], d_tokens[None], dw_query, g[7], dw_key, dw_value, g[8], s_out, g[0],
            s_up, g[6], s_down, g[1], g[2], g[3], g[4], g[5], d_kernel.T)

    own = (s * fsdp + lax.axis_index("fsdp")) * rows
    pack_rows = -(-rows // 8) * 8 + 8
    lead = pack_rows - 8

    def placed(vector, at, size):
        return lax.dynamic_update_slice(jnp.zeros((size,), bf16), vector, (at,))

    bias_q, bias_v = (placed(b, own, D).reshape(active, 1, width) for b in (b_query, b_value))
    bias = jnp.concatenate([bias_q, jnp.zeros((active, 1, width), bf16), bias_v], axis=2)
    bias = jnp.pad(bias, ((0, 0), (0, 7), (0, 0)))
    small = [placed(v, own, D) for v in (b_out, b_down, g_attn, s_attn, g_mlp, s_mlp)]
    small = jnp.concatenate(small + [placed(b_up, own * 4, FF), jnp.zeros((6 * D,), bf16)]).reshape(16, D)
    blocks = []
    for b in range(active):
        cols = slice(b * width, (b + 1) * width)
        blocks.append(jnp.concatenate([w_query[:, cols], w_key[:, cols], w_value[:, cols]], axis=1))
    pack = jnp.concatenate([jnp.pad(jnp.stack(blocks), ((0, 0), (0, lead - rows), (0, 0))), bias], axis=1)
    all_tokens = lax.all_gather(own_tokens, "seq").reshape(total, D)
    all_pack = lax.all_gather(lax.all_to_all(
        jnp.take(pack, jnp.arange(seq) % active, axis=0), "seq", 0, 0), "fsdp", axis=1).reshape(
            devices, pack_rows, 3 * width)
    qkv_weights = all_pack[:, :rows].reshape(D, 3 * width)
    full_up, full_small, full_down, full_out = (
        lax.all_gather(w, axes, tiled=True) for w in (w_up, small, w_down, w_out))
    mixed, *state = attention_forward(heads, active, all_tokens, qkv_weights, all_pack[:, lead:], lengths, taps)
    attention = lax.all_to_all(mixed.reshape(seq, count, width), "seq", 0, 0)
    vectors = jnp.sum(full_small.reshape(devices, 16, D).astype(f32), axis=0)
    attention = jnp.transpose(attention[:active], (1, 0, 2)).reshape(count, D)
    output, d_r1, d_attn, dw_out, dw_up, dw_down, smalls = token_part(
        own_tokens, own_cot, attention, full_out, full_up, full_down, vectors[0], vectors[6:10].reshape(FF),
        *(vectors[j] for j in range(1, 6)))
    d_attn = jnp.transpose(d_attn.astype(bf16).reshape(count, active, width), (1, 0, 2))
    d_mixed = lax.all_to_all(jnp.take(d_attn, jnp.arange(seq) % active, axis=0), "seq", 0, 0)
    s_up, s_out, s_down = (
        lax.psum_scatter(w, axes, scatter_dimension=0, tiled=True) for w in (dw_up, dw_out, dw_down))
    small = [lax.psum_scatter(v, axes, scatter_dimension=0, tiled=True) for v in smalls]
    part, dw, extra = attention_backward(
        heads, active, all_tokens, qkv_weights, d_mixed.reshape(total, width), lengths, taps, state)
    token_parts = lax.all_to_all(part.reshape(seq, count, D), "seq", 0, 0)
    d_tokens = (d_r1 + jnp.sum(token_parts.astype(f32), axis=0)).astype(bf16)
    extra = lax.psum(lax.all_gather(extra, "seq")[:active], "fsdp")
    dw = jnp.transpose(dw.reshape(width, 3, devices, rows), (2, 3, 1, 0)).reshape(devices, rows, 3 * width)
    dw = lax.all_to_all(dw, axes, 0, 0)
    dw = jnp.sum(dw.reshape(seq, fsdp, rows, 3, width)[:active], axis=1)
    dw_query, dw_key, dw_value = (jnp.transpose(dw[:, :, j], (1, 0, 2)).reshape(rows, D) for j in range(3))
    db_query = lax.dynamic_slice_in_dim(extra[:, 0, :width].reshape(D), own, rows)
    db_value = lax.dynamic_slice_in_dim(extra[:, 0, 2 * width :].reshape(D), own, rows)
    d_kernel = jnp.transpose(extra[:, 1 : 1 + heads, :CONV].reshape(active * heads, CONV), (1, 0))
    s_b_out, s_b_up, s_b_down, s_g_attn, s_s_attn, s_g_mlp, s_s_mlp = small
    return (
        output[None], d_tokens[None], dw_query, db_query, dw_key, dw_value, db_value, s_out, s_b_out,
        s_up, s_b_up, s_down, s_b_down, s_g_attn, s_s_attn, s_g_mlp, s_s_mlp, d_kernel)


def solution(mesh):
    sizes = (mesh.shape["seq"], mesh.shape["fsdp"])
    both = ("seq", "fsdp")
    wide, flat, stream = P(both, None), P(both), P("fsdp", "seq", None)
    in_specs = (stream, stream, P("fsdp", None), wide, flat, wide, wide, flat, wide, flat, wide, flat, wide, flat,
                flat, flat, flat, flat, P())
    out_specs = (stream, stream, wide, flat, wide, wide, flat, wide, flat, wide, flat, wide, flat, flat, flat, flat,
                 flat, P())
    return jax.shard_map(partial(local, sizes), mesh=mesh, in_specs=in_specs, out_specs=out_specs, check_vma=False)
```
